128 devices in a mesh: dp: 8 (over z, core), seq: 16 (over x, y).
Axes of the slice: x: 4, y: 4, z: 4, core: 2. Of those that a mesh axis runs over, the one named last changes fastest.
Arguments:
- dec_input: bfloat16 [128, 128, 768], P(('dp', 'seq')), may hold values from -6 to 6
- memory: bfloat16 [128, 3072, 768], P('dp', 'seq'), may hold values from -6 to 6
- mem_len: int32 [128], P(('dp', 'seq')), may hold values from 1 to 3072, 196608 in all
- grad_out: bfloat16 [128, 128, 768], P(('dp', 'seq')), may hold values from -6 to 6
- attn_master: float32 [8, 768, 768], P(None, ('dp', 'seq'))
- ffn_in_master: float32 [2, 768, 2048], P(None, ('dp', 'seq')), may hold values from -0.21875 to 0.21875
- ffn_out_master: float32 [2048, 768], P(('dp', 'seq')), may hold values from -0.125 to 0.125
- gain_master: float32 [3, 768], P(None, ('dp', 'seq')), may hold values from 0.5 to 1.5
- attn_first: float32 [8, 768, 768], P(None, ('dp', 'seq')), may hold values from -64 to 64
- ffn_in_first: float32 [2, 768, 2048], P(None, ('dp', 'seq')), may hold values from -40 to 40
- ffn_out_first: float32 [2048, 768], P(('dp', 'seq')), may hold values from -40 to 40
- gain_first: float32 [3, 768], P(None, ('dp', 'seq')), may hold values from -96 to 96
- attn_second: float32 [8, 768, 768], P(None, ('dp', 'seq'))
- ffn_in_second: float32 [2, 768, 2048], P(None, ('dp', 'seq')), may hold values from 4.096 to 16.384
- ffn_out_second: float32 [2048, 768], P(('dp', 'seq')), may hold values from 4.096 to 16.384
- gain_second: float32 [3, 768], P(None, ('dp', 'seq'))
Outputs:
- out_block: bfloat16 [128, 128, 768], P(('dp', 'seq'))
- grad_input: float32 [128, 128, 768], P(('dp', 'seq'))
- grad_memory: float32 [128, 3072, 768], P('dp', 'seq')
- attn_new: float32 [8, 768, 768], P(None, ('dp', 'seq'))
- attn_first_new: float32 [8, 768, 768], P(None, ('dp', 'seq'))
- attn_second_new: float32 [8, 768, 768], P(None, ('dp', 'seq'))
- attn_copy: bfloat16 [8, 768, 768], P(None, ('dp', 'seq'))
- ffn_in_new: float32 [2, 768, 2048], P(None, ('dp', 'seq'))
- ffn_in_first_new: float32 [2, 768, 2048], P(None, ('dp', 'seq'))
- ffn_in_second_new: float32 [2, 768, 2048], P(None, ('dp', 'seq'))
- ffn_in_copy: bfloat16 [2, 768, 2048], P(None, ('dp', 'seq'))
- ffn_out_new: float32 [2048, 768], P(('dp', 'seq'))
- ffn_out_first_new: float32 [2048, 768], P(('dp', 'seq'))
- ffn_out_second_new: float32 [2048, 768], P(('dp', 'seq'))
- ffn_out_copy: bfloat16 [2048, 768], P(('dp', 'seq'))
- gain_new: float32 [3, 768], P(None, ('dp', 'seq'))
- gain_first_new: float32 [3, 768], P(None, ('dp', 'seq'))
- gain_second_new: float32 [3, 768], P(None, ('dp', 'seq'))
- gain_copy: bfloat16 [3, 768], P(None, ('dp', 'seq'))
The draws below stay inside these ranges and needn't reach their ends.
Inputs may be any that keep to these rules, and one draw needn't show every extreme that they name: `mem_len`: each example's count of live memory positions; the largest is exactly 3072.
All inputs are finite; a program needn't handle non-finite values. No bound on the sum of `mem_len` on one device may be relied on, other than what follows from the above.
Results may differ from the reference program's by a relative error of at most 0.02.
The reference program's roundings to bfloat16 on the way count: a program that leaves them out, or rounds other values in their place, can miss the bound.
Values may be sent and summed in bfloat16 or wider, within the bound.
A program may use at most 256 MiB of HBM per device.

```python
import math
import jax
import jax.numpy as jnp
import numpy as np
from jax import lax

D = 768
H = 12
HEAD = 64
FF = 2048
TGT = 128
MEM = 3072
STEP = 10
EXAMPLES = 128
TOKENS = 16384


def draw_attn_master(key, part):
    base_draw = jax.random.normal(key, (8, D, D), jnp.float32) * D ** (-0.5)
    factors = jnp.array([1.0, 1.0, 1.0, 1.0, 1.3, 1.3, 1.0, 1.0], jnp.float32)
    return base_draw * factors[:, None, None]


def second_moment(key, array_shape, base_level):
    factor = jnp.exp(jax.random.uniform(jax.random.fold_in(key, 13), array_shape, jnp.float32) * math.log(4.0))
    return base_level * factor


def draw_attn_second(key, part):
    return second_moment(key, (8, D, D), 0.00049 * TOKENS)


def draw_gain_second(key, part):
    return second_moment(key, (3, D), 0.0012 * TOKENS)


def steps_of(key, shape, pieces, least, top_value):
    def one(axis_at, parts):
        heights = jax.random.uniform(jax.random.fold_in(jax.random.fold_in(key, 6), axis_at), (parts,), jnp.float32, least / len(pieces), top_value / len(pieces))
        return jnp.repeat(jnp.exp(heights), shape[axis_at] // parts).reshape((-1,) + (1,) * (len(shape) - axis_at - 1))

    gain = one(*pieces[0])
    for cut in pieces[1:]:
        gain = gain * one(*cut)
    return gain


def length_profile(number_of, total, most, skew):
    weights = [(1 << 20) // math.isqrt(grade ** skew) + 1 for grade in range(2, number_of + 1)]
    spare, holding = total - most - (number_of - 1), [1] * (number_of - 1)
    while spare > 0:
        free = [i for i in range(number_of - 1) if holding[i] < most]
        mass, budget = sum([weights[i] for i in free]), spare
        for i in free:
            more = min(most - holding[i], max(1, budget * weights[i] // mass), spare)
            holding[i] = holding[i] + more
            spare = spare - more
    return np.array([most] + holding)


def ragged_sizes(key, amount, total, bound, skew):
    if amount == 2:
        one = jax.random.randint(key, (), max(1, total - bound), min(bound, total - 1) + 1)
        return jnp.stack([one, total - one])
    tallies = jnp.asarray(length_profile(amount, total, bound, skew), jnp.int32)
    pairs = (amount - 1) // 2
    giver, receiver = tallies[1:1 + 2 * pairs:2], tallies[2:2 + 2 * pairs:2]
    room = jnp.minimum(giver - 1, bound - receiver)
    moved = jax.random.randint(jax.random.fold_in(key, 1), (pairs,), 0, 1 << 20) % (room + 1)
    tallies = tallies.at[1:1 + 2 * pairs:2].set(giver - moved).at[2:2 + 2 * pairs:2].set(receiver + moved)
    return tallies[jax.random.permutation(jax.random.fold_in(key, 2), amount)]


def centred(own_key, shape, scale, most, split=(), dtype=jnp.bfloat16):
    gain = steps_of(own_key, shape, split, -0.22, 0.18) if split else 1.0
    result = jax.random.normal(own_key, shape, jnp.float32) * scale * gain
    return jnp.minimum(jnp.maximum(result, -most), most).astype(dtype)


def setup_inputs(seed: int = 0) -> dict:
    arg_keys = jax.random.split(jax.random.key(seed), 17)
    dec_input = centred(arg_keys[0], (EXAMPLES, TGT, D), 1.0, 6.0, ((0, 128),))
    memory = centred(arg_keys[1], (EXAMPLES, MEM, D), 1.0, 6.0, ((0, 8), (1, 16)))
    mem_len = ragged_sizes(arg_keys[2], EXAMPLES, EXAMPLES * MEM // 2, MEM, 2).astype(jnp.int32)
    grad_out = centred(arg_keys[3], (EXAMPLES, TGT, D), 1.0, 6.0, ((0, 128),))
    attn_master = draw_attn_master(jax.random.fold_in(arg_keys[16], 71), 0)
    ffn_in_master = centred(arg_keys[5], (2, D, FF), D ** -0.5, 0.21875, ((1, 128),), jnp.float32)
    ffn_out_master = centred(arg_keys[6], (FF, D), FF ** -0.5, 0.125, ((0, 128),), jnp.float32)
    gain_master = jnp.clip(1.0 + 0.1 * jax.random.normal(arg_keys[7], (3, D), jnp.float32), 0.5, 1.5)
    attn_first = centred(arg_keys[8], (8, D, D), (0.078 * TOKENS ** 0.5), 64.0, ((1, 128),), jnp.float32)
    ffn_in_first = centred(arg_keys[9], (2, D, FF), (0.055 * TOKENS ** 0.5), 40.0, ((1, 128),), jnp.float32)
    ffn_out_first = centred(arg_keys[10], (FF, D), (0.055 * TOKENS ** 0.5), 40.0, ((0, 128),), jnp.float32)
    gain_first = centred(arg_keys[11], (3, D), (0.12 * TOKENS ** 0.5), 96.0, ((1, 128),), jnp.float32)
    attn_second = draw_attn_second(jax.random.fold_in(arg_keys[16], 71), 0)
    ffn_in_second = jnp.clip(jnp.exp(math.log(16.384) - 1.3862944 * jax.random.uniform(arg_keys[13], (2, D, FF), jnp.float32) ** steps_of(arg_keys[13], (2, D, FF), ((1, 128),), -0.2, 0.2)), 4.096, 16.384)
    ffn_out_second = jnp.clip(jnp.exp(math.log(16.384) - 1.3862944 * jax.random.uniform(arg_keys[14], (FF, D), jnp.float32) ** steps_of(arg_keys[14], (FF, D), ((0, 128),), -0.2, 0.2)), 4.096, 16.384)
    gain_second = draw_gain_second(jax.random.fold_in(arg_keys[16], 71), 0)
    return dict(dec_input=dec_input, memory=memory, mem_len=mem_len, grad_out=grad_out, attn_master=attn_master, ffn_in_master=ffn_in_master, ffn_out_master=ffn_out_master, gain_master=gain_master, attn_first=attn_first, ffn_in_first=ffn_in_first, ffn_out_first=ffn_out_first, gain_first=gain_first, attn_second=attn_second, ffn_in_second=ffn_in_second, ffn_out_second=ffn_out_second, gain_second=gain_second)


@jax.custom_vjp
def low(v):
    return lax.optimization_barrier(v.astype(jnp.bfloat16)).astype(jnp.float32)

@jax.custom_vjp
def low_back(v):
    return v

def low_keep(v):
    return (low(v), None)

def low_pass(kept, grad):
    return (grad,)

def back_keep(v):
    return (v, None)

def back_low(kept, grad):
    return (low(grad),)
low.defvjp(low_keep, low_pass)
low_back.defvjp(back_keep, back_low)
HIGHEST = lax.Precision.HIGHEST
eps_norm = 1e-06
score_scale = 0.125
beta_one = 0.9
beta_two = 0.999
adam_eps = 1e-08
decay_rate = 0.01
rate_matrix = 0.12
rate_gain = 3.0
neg_big = -1e+30

def matmul(left, right):
    return jnp.dot(left, right, precision=HIGHEST, preferred_element_type=jnp.float32)

def rounded(value):
    return low_back(low(value))

def rms_norm(tok_rows, gain_row):
    inverse = lax.rsqrt(lax.optimization_barrier(jnp.mean(tok_rows * tok_rows, axis=-1, keepdims=True)) + eps_norm)
    return tok_rows * inverse * gain_row

def gated_gelu(gate_part, up_part):
    return jax.nn.gelu(gate_part, approximate=True) * up_part

def attend(queries, key_set, values, is_valid):
    row_count = queries.shape[0]
    query_heads = queries.reshape(row_count, H, HEAD)
    key_heads = key_set.reshape(key_set.shape[0], H, HEAD)
    value_heads = values.reshape(values.shape[0], H, HEAD)
    scores = low_back(score_scale * jnp.einsum('qhc,khc->hqk', query_heads, key_heads, precision=HIGHEST))
    scores = jnp.where(is_valid, scores, neg_big)
    shifted = jnp.exp(scores - lax.optimization_barrier(jnp.max(scores, axis=-1, keepdims=True)))
    prob_rows = low(shifted / lax.optimization_barrier(jnp.sum(shifted, axis=-1, keepdims=True)))
    mixed = jnp.einsum('hqk,khc->qhc', prob_rows, value_heads, precision=HIGHEST)
    return mixed.reshape(row_count, H * HEAD)

def layer(hidden_in, memory_in, live_count, w_attn, w_in, w_out, gains):
    h_one = low(rms_norm(hidden_in, gains[0]))
    q_one = rounded(matmul(h_one, w_attn[0]))
    k_one = rounded(matmul(h_one, w_attn[1]))
    v_one = rounded(matmul(h_one, w_attn[2]))
    position = jnp.arange(hidden_in.shape[0])
    causal = (position[:, None] >= position[None, :])[None]
    o_one = rounded(attend(q_one, k_one, v_one, causal))
    after_one = hidden_in + low_back(matmul(o_one, w_attn[3]))
    h_two = low(rms_norm(after_one, gains[1]))
    q_two = rounded(matmul(h_two, w_attn[4]))
    k_two = rounded(matmul(memory_in, w_attn[5]))
    v_two = rounded(matmul(memory_in, w_attn[6]))
    reach = (jnp.arange(memory_in.shape[0]) < live_count)[None, None, :]
    o_two = rounded(attend(q_two, k_two, v_two, reach))
    after_two = after_one + low_back(matmul(o_two, w_attn[7]))
    h_three = low(rms_norm(after_two, gains[2]))
    gate_part = low_back(matmul(h_three, w_in[0]))
    up_part = low_back(matmul(h_three, w_in[1]))
    middle = low(gated_gelu(gate_part, up_part))
    return after_two + low_back(matmul(middle, w_out))

def adam_update(master, first, second, grad, rate):
    first_new = beta_one * first + (1.0 - beta_one) * grad
    second_new = beta_two * second + (1.0 - beta_two) * grad * grad
    fix_one = 1.0 - beta_one ** STEP
    fix_two = 1.0 - beta_two ** STEP
    master_new = master - rate * (first_new / fix_one / (jnp.sqrt(second_new / fix_two) + adam_eps) + decay_rate * master)
    return (master_new, first_new, second_new, master_new.astype(jnp.bfloat16))

def reference(dec_input, memory, mem_len, grad_out, attn_master, ffn_in_master, ffn_out_master, gain_master, attn_first, ffn_in_first, ffn_out_first, gain_first, attn_second, ffn_in_second, ffn_out_second, gain_second):
    masters = (attn_master, ffn_in_master, ffn_out_master, gain_master)
    weights = tuple((lax.optimization_barrier(master.astype(jnp.bfloat16)).astype(jnp.float32) for master in masters))

    def one_example(totals, item):
        hidden_in, memory_in, live_count, cotangent = item

        def run(x_in, m_in, w_attn, w_in, w_out, gains):
            return layer(x_in, m_in, live_count, w_attn, w_in, w_out, gains)
        output, pull = jax.vjp(run, hidden_in.astype(jnp.float32), memory_in.astype(jnp.float32), *weights)
        grads = pull(cotangent.astype(jnp.float32))
        totals = tuple((total + grad for total, grad in zip(totals, grads[2:])))
        return (totals, (output.astype(jnp.bfloat16), grads[0], grads[1]))
    zeros = tuple((jnp.zeros(weight.shape, jnp.float32) for weight in weights))
    totals, outputs = lax.scan(one_example, zeros, (dec_input, memory, mem_len, grad_out))
    out_block, grad_input, grad_memory = outputs
    attn_res = adam_update(attn_master, attn_first, attn_second, totals[0], rate_matrix)
    in_res = adam_update(ffn_in_master, ffn_in_first, ffn_in_second, totals[1], rate_matrix)
    out_res = adam_update(ffn_out_master, ffn_out_first, ffn_out_second, totals[2], rate_matrix)
    gain_res = adam_update(gain_master, gain_first, gain_second, totals[3], rate_gain)
    return (out_block, grad_input, grad_memory, attn_res[0], attn_res[1], attn_res[2], attn_res[3], in_res[0], in_res[1], in_res[2], in_res[3], out_res[0], out_res[1], out_res[2], out_res[3], gain_res[0], gain_res[1], gain_res[2], gain_res[3])
```

```python
import functools
import jax
import jax.numpy as jnp
from jax import lax
from jax.experimental import pallas as pl
from jax.experimental.pallas import tpu as pltpu
from jax.sharding import PartitionSpec as P

H = 12
HEAD = 64
STEP = 10


eps_norm = 1e-06
score_scale = 0.125
beta_one = 0.9
beta_two = 0.999
adam_eps = 1e-08
decay_rate = 0.01
rate_matrix = 0.12
rate_gain = 3.0
neg_big = -1e30


def dense(left, right):
    return jnp.dot(left, right, preferred_element_type=jnp.float32)


def weight_grad(left, right):
    return jnp.einsum("rd,re->de", left, right, preferred_element_type=jnp.float32)


def back_dense(incoming, weight):
    return jnp.einsum("re,de->rd", incoming, weight, preferred_element_type=jnp.float32)


def gated_gelu(gate_part, up_part):
    return jax.nn.gelu(gate_part, approximate=True) * up_part


def norm_forward(tok_rows, gain_row):
    inverse = lax.rsqrt(jnp.mean(tok_rows * tok_rows, axis=-1, keepdims=True) + eps_norm)
    return ((tok_rows * inverse * gain_row).astype(jnp.bfloat16), inverse)


def norm_backward(tok_rows, inverse, gain_row, incoming):
    scaled = incoming * gain_row
    gain_grad = jnp.sum(incoming * tok_rows * inverse, axis=0)
    inner_sum = jnp.mean(scaled * tok_rows, axis=-1, keepdims=True)
    return (inverse * scaled - tok_rows * inverse * inverse * inverse * inner_sum, gain_grad)


def scores_of(queries, key_set, is_valid):
    scores = (
        jnp.einsum("eqhc,ekhc->ehqk", queries, key_set, preferred_element_type=jnp.float32)
        * score_scale
    )
    return jnp.where(is_valid, scores, neg_big)


def attend_forward(queries, key_set, values, is_valid):
    scores = scores_of(queries, key_set, is_valid)
    row_top = jnp.max(scores, axis=-1, keepdims=True)
    logsum = row_top + jnp.log(jnp.sum(jnp.exp(scores - row_top), axis=-1, keepdims=True))
    prob_rows = jnp.exp(scores - logsum).astype(jnp.bfloat16)
    mixed = jnp.einsum("ehqk,ekhc->eqhc", prob_rows, values, preferred_element_type=jnp.float32)
    return (mixed.astype(jnp.bfloat16), logsum)


def attend_backward(queries, key_set, values, is_valid, logsum, incoming):
    prob_rows = jnp.exp(scores_of(queries, key_set, is_valid) - logsum)
    value_grad = jnp.einsum(
        "ehqk,eqhc->ekhc",
        prob_rows.astype(jnp.bfloat16),
        incoming,
        preferred_element_type=jnp.float32,
    )
    prob_grad = jnp.einsum("eqhc,ekhc->ehqk", incoming, values, preferred_element_type=jnp.float32)
    row_delta = jnp.sum(prob_grad * prob_rows, axis=-1, keepdims=True)
    score_grad = (prob_rows * (prob_grad - row_delta)).astype(jnp.bfloat16)
    query_grad = (
        jnp.einsum("ehqk,ekhc->eqhc", score_grad, key_set, preferred_element_type=jnp.float32)
        * score_scale
    )
    key_grad = (
        jnp.einsum("ehqk,eqhc->ekhc", score_grad, queries, preferred_element_type=jnp.float32)
        * score_scale
    )
    return (
        query_grad.astype(jnp.bfloat16),
        key_grad.astype(jnp.bfloat16),
        value_grad.astype(jnp.bfloat16),
    )


def adam_update(master, first, second, grad, rate):
    first_new = beta_one * first + (1.0 - beta_one) * grad
    second_new = beta_two * second + (1.0 - beta_two) * grad * grad
    fix_one = 1.0 - beta_one**STEP
    fix_two = 1.0 - beta_two**STEP
    master_new = master - rate * (
        first_new / fix_one / (jnp.sqrt(second_new / fix_two) + adam_eps) + decay_rate * master
    )
    return (master_new, first_new, second_new, master_new.astype(jnp.bfloat16))


MESH = pl.DeviceIdType.MESH
BF, F32 = jnp.bfloat16, jnp.float32
ALL = slice(None)
PARTS = (("A", 0, "xyz"), ("A", 1, "yzx"), ("A", 2, "zxy"), ("B", 0, "xyz"), ("B", 1, "yzx"), ("C", 0, "zxy"))

def where_am_i():
    dp, sq = lax.axis_index("dp"), lax.axis_index("seq")
    return {"x": sq // 4, "y": sq % 4, "z": dp // 2, "c": dp % 2}

def dev(at):
    return (at["z"] * 2 + at["c"], at["x"] * 4 + at["y"])

def moved(at, axis, step):
    return {**at, axis: (at[axis] + step + 4) % 4}

def gather_kernel(attn, wi, wo, info, A, B, C, infos, stage, recv, blk, blkA, blkB, blkC, irecv,
                  ss, rs, sib_s, sib_r, as_, ar_, is_, ir_, ds_, dr_, own_s):
    me = where_am_i()
    dp, sq = lax.axis_index("dp"), lax.axis_index("seq")
    bar = pltpu.get_barrier_semaphore()
    for i in range(1, 16):
        pl.semaphore_signal(bar, inc=1, device_id=(dp, (sq + i) % 16), device_id_type=MESH)
    for i in range(1, 8):
        pl.semaphore_signal(bar, inc=1, device_id=((dp + i) % 8, sq), device_id_type=MESH)
    stage[:, 6:8, :] = jnp.zeros((16, 2, 640), F32)
    for s in range(16):
        stage[s, 0:6, 0:384] = attn[s // 2, :, 384 * (s % 2):384 * (s % 2) + 384]
        stage[s, 0:6, 384:640] = wi[s // 8, :, 256 * (s % 8):256 * (s % 8) + 256]
    pl.semaphore_wait(bar, 22)
    def a2a(i):
        peer = (sq + i) % 16
        return pltpu.make_async_remote_copy(stage.at[peer], recv.at[sq], as_.at[i], ar_.at[i], device_id=(dp, peer), device_id_type=MESH)
    def inf(i):
        peer = (sq + i) % 16
        return pltpu.make_async_remote_copy(info, irecv.at[sq], is_.at[i], ir_.at[i], device_id=(dp, peer), device_id_type=MESH)
    for i in range(1, 16):
        a2a(i).start()
    for i in range(1, 16):
        inf(i).start()
    recv[sq] = stage[sq]
    irecv[sq] = info[...]
    blkC[...] = wo[...].astype(BF)
    for i in range(1, 16):
        a2a(i).wait_recv()
    for k in range(16):
        blk[6 * k:6 * k + 6, :] = recv[k, 0:6, :]
    for p in range(3):
        blkA[p] = blk[32 * p:32 * p + 32, 0:384].astype(BF)
    for p in range(2):
        blkB[p] = blk[48 * p:48 * p + 48, 384:640].astype(BF)

    def view(part, at):
        name, p, _ = part
        if name == "A":
            return A.at[at["x"], at["y"], at["z"], at["c"], p]
        if name == "B":
            return B.at[at["x"], at["y"], at["z"], at["c"], p]
        return C.at[at["z"], at["c"], at["x"], at["y"]]

    def mine(part):
        name, p, _ = part
        return blkA.at[p] if name == "A" else blkB.at[p] if name == "B" else blkC

    def group(part, t, step, half=None):
        order = part[2]
        at = moved(me, order[t], step)
        for j in range(t):
            at = {**at, order[j]: ALL}
        if half is not None and t:
            at = {**at, order[0]: pl.ds(2 * half, 2)}
        return at

    def send(n, t, kind):
        part = PARTS[n]
        axis = part[2][t]
        step = 1 if kind in (0, 2) else -1
        if kind < 2:
            dst = view(part, group(part, t, 0))
            src = mine(part) if t == 0 else dst
        else:
            dst = src = view(part, group(part, t, -step, kind - 2))
        return pltpu.make_async_remote_copy(src, dst, ss.at[n, t, kind], rs.at[n, t, kind], device_id=dev(moved(me, axis, step)), device_id_type=MESH)

    def arrival(n, t, kind):
        part = PARTS[n]
        axis = part[2][t]
        step = 1 if kind in (0, 2) else -1
        if kind < 2:
            dst = view(part, group(part, t, -step))
        else:
            dst = view(part, group(part, t, -2 * step, kind - 2))
        return pltpu.make_async_remote_copy(dst, dst, ss.at[n, t, kind], rs.at[n, t, kind], device_id=dev(moved(me, axis, step)), device_id_type=MESH)

    def kinds(n, t):
        return (0, 1, 2, 3) if t else (0, 1, 2 + n % 2)

    def sibling(n, j, c):
        part = PARTS[n]
        steps = (0, -1, 1, 2)
        at = {**group(part, 2, steps[j]), "c": c}
        v = view(part, at)
        return pltpu.make_async_remote_copy(v, v, sib_s.at[n, j], sib_r.at[n, j], device_id=dev({**me, "c": 1 - me["c"]}), device_id_type=MESH)

    owns = [pltpu.make_async_copy(mine(PARTS[n]), view(PARTS[n], me), own_s.at[n]) for n in range(6)]
    for o in owns:
        o.start()
    for t in range(3):
        for n in range(6):
            if t == 1:
                owns[n].wait()
            if t:
                for k in kinds(n, t - 1)[2:]:
                    arrival(n, t - 1, k).wait_recv()
            send(n, t, 0).start()
            send(n, t, 1).start()
            if t == 2:
                sibling(n, 0, me["c"]).start()
        for n in range(6):
            for k in (0, 1):
                arrival(n, t, k).wait_recv()
                if 2 + k in kinds(n, t):
                    send(n, t, 2 + k).start()
                if t == 2:
                    sibling(n, 1 + k, me["c"]).start()
    for i in range(1, 16):
        inf(i).wait_recv()
    tile = jnp.sum(irecv[...], axis=0)
    infos[dp] = tile
    def dpx(i):
        return pltpu.make_async_remote_copy(infos.at[dp], infos.at[dp], ds_.at[i], dr_.at[i], device_id=((dp + i) % 8, sq), device_id_type=MESH)
    def dpx_in(i):
        return pltpu.make_async_remote_copy(infos.at[(dp - i + 8) % 8], infos.at[(dp - i + 8) % 8], ds_.at[i], dr_.at[i], device_id=((dp + i) % 8, sq), device_id_type=MESH)
    for i in range(1, 8):
        dpx(i).start()
    for n in range(6):
        for k in (2, 3):
            arrival(n, 2, k).wait_recv()
        sibling(n, 3, me["c"]).start()
    for i in range(1, 8):
        dpx_in(i).wait_recv()
    for n in range(6):
        for j in range(4):
            sibling(n, j, 1 - me["c"]).wait_recv()
    for i in range(1, 16):
        a2a(i).wait_send()
        inf(i).wait_send()
    for i in range(1, 8):
        dpx(i).wait_send()
    for n in range(6):
        for t in range(3):
            for k in kinds(n, t):
                send(n, t, k).wait_send()
        for j in range(4):
            sibling(n, j, me["c"]).wait_send()

def gather(attn, wi, wo, info):
    V = pl.BlockSpec(memory_space=pltpu.VMEM)
    H = pl.BlockSpec(memory_space=pl.ANY)
    D = pltpu.SemaphoreType.DMA
    return pl.pallas_call(
        gather_kernel,
        out_shape=(jax.ShapeDtypeStruct((4, 4, 4, 2, 3, 32, 384), BF),
                   jax.ShapeDtypeStruct((4, 4, 4, 2, 2, 48, 256), BF),
                   jax.ShapeDtypeStruct((4, 2, 4, 4, 16, 768), BF),
                   jax.ShapeDtypeStruct((8, 8, 128), F32)),
        in_specs=[V] * 4, out_specs=(H, H, H, V),
        scratch_shapes=[pltpu.VMEM((16, 8, 640), F32), pltpu.VMEM((16, 8, 640), F32), pltpu.VMEM((96, 640), F32),
                        pltpu.VMEM((3, 32, 384), BF), pltpu.VMEM((2, 48, 256), BF), pltpu.VMEM((16, 768), BF),
                        pltpu.VMEM((16, 8, 128), F32),
                        D((6, 3, 4)), D((6, 3, 4)), D((6, 4)), D((6, 4)), D((16,)), D((16,)), D((16,)), D((16,)), D((8,)), D((8,)), D((6,))],
        compiler_params=pltpu.CompilerParams(collective_id=0, has_side_effects=True, vmem_limit_bytes=32 << 20),
        name="gather_weights",
    )(attn, wi, wo, info)

def info_tile(gain, mem_len):
    sq = lax.axis_index("seq")
    t = jnp.zeros((8, 128), F32)
    t = lax.dynamic_update_slice(t, gain.astype(BF).astype(F32), (0, 6 * sq))
    return lax.dynamic_update_slice(t, mem_len.astype(F32)[:, None], (3, sq))

def scatter_kernel(GA, GB, GC, gg, oA, oB, oC, oG, accA, accB, accC, sibA, sibB, sibC,
                   hA2, hB2, hC2, fA2, fB2, fC2, hA1, hB1, hC1, fA1, fB1, fC1, hA0, hB0, hC0, fA0, fB0, fC0,
                   blk, stage, recv, gdp, gsum, gsq,
                   ss, rs, sib_s, sib_r, loc_s, as_, ar_, is_, ir_, ds_, dr_):
    me = where_am_i()
    dp, sq = lax.axis_index("dp"), lax.axis_index("seq")
    acc = {"A": accA, "B": accB, "C": accC}
    sib = {"A": sibA, "B": sibB, "C": sibC}
    hop = {2: {"A": hA2, "B": hB2, "C": hC2}, 1: {"A": hA1, "B": hB1, "C": hC1}, 0: {"A": hA0, "B": hB0, "C": hC0}}
    fin = {2: {"A": fA2, "B": fB2, "C": fC2}, 1: {"A": fA1, "B": fB1, "C": fC1}, 0: {"A": fA0, "B": fB0, "C": fC0}}
    bar = pltpu.get_barrier_semaphore()
    for i in range(1, 16):
        pl.semaphore_signal(bar, inc=1, device_id=(dp, (sq + i) % 16), device_id_type=MESH)
    for i in range(1, 8):
        pl.semaphore_signal(bar, inc=1, device_id=((dp + i) % 8, sq), device_id_type=MESH)
    pl.semaphore_wait(bar, 22)

    def idx(part, at):
        name, p, _ = part
        if name == "C":
            return (at["z"], at["x"], at["y"])
        return (p, at["x"], at["y"], at["z"])

    def source(part, at, c):
        name, p, _ = part
        if name == "A":
            return GA.at[at["x"], at["y"], at["z"], c, p]
        if name == "B":
            return GB.at[at["x"], at["y"], at["z"], c, p]
        return GC.at[at["z"], c, at["x"], at["y"]]

    def names(part):
        return "zxy" if part[0] == "C" else "xyz"

    def group(part, t, step):
        order = part[2]
        at = moved(me, order[t], step)
        for j in range(t):
            at = {**at, order[j]: ALL}
        return at

    def halved(part, t, at, half):
        if t == 0:
            return at
        first = [a for a in names(part) if a in part[2][:t]][0]
        return {**at, first: pl.ds(2 * half, 2)}

    def done(part, t):
        return [a for a in names(part) if a in part[2][:t]]

    STEPS = (2, -1, 1, 0)
    other = dev({**me, "c": 1 - me["c"]})

    def sib_copy(n, j):
        part = PARTS[n]
        at = group(part, 2, STEPS[j])
        return pltpu.make_async_remote_copy(source(part, at, 1 - me["c"]), sib[part[0]].at[idx(part, at)], sib_s.at[n, j], sib_r.at[n, j], device_id=other, device_id_type=MESH)

    def loc_copy(n, j):
        part = PARTS[n]
        at = group(part, 2, STEPS[j])
        return pltpu.make_async_copy(source(part, at, me["c"]), acc[part[0]].at[idx(part, at)], loc_s.at[n, j])

    def slot(part):
        return () if part[0] == "C" else (part[1],)

    def kinds(n, t):
        return (0, 1) if t else (n % 2,)

    def hop_send(n, t, kind):
        part = PARTS[n]
        step = 1 if kind == 0 else -1
        at = halved(part, t, group(part, t, 2 * step), kind)
        return pltpu.make_async_remote_copy(acc[part[0]].at[idx(part, at)], hop[t][part[0]].at[slot(part) + (kind,)],
                                            ss.at[n, t, kind], rs.at[n, t, kind], device_id=dev(moved(me, part[2][t], step)), device_id_type=MESH)

    def fin_send(n, t, kind):
        part = PARTS[n]
        step = 1 if kind == 0 else -1
        at = group(part, t, step)
        return pltpu.make_async_remote_copy(acc[part[0]].at[idx(part, at)], fin[t][part[0]].at[slot(part) + (kind,)],
                                            ss.at[n, t, 2 + kind], rs.at[n, t, 2 + kind], device_id=dev(moved(me, part[2][t], step)), device_id_type=MESH)

    def each(part, t, at, fn, half=None):
        axes = done(part, t)
        sizes = [4] * len(axes)
        offs = [0] * len(axes)
        if half is not None and axes:
            sizes[0] = 2
            offs[0] = 2 * half
        total = 1
        for s in sizes:
            total *= s
        def one(i):
            pos = []
            rest = i
            for s in sizes[::-1]:
                pos.append(rest % s)
                rest = rest // s
            pos = pos[::-1]
            where = dict(at)
            for a, p, o in zip(axes, pos, offs):
                where[a] = p + o
            fn(idx(part, where), tuple(pos))
        if total == 1:
            one(0)
        else:
            pl.loop(0, total)(one)

    def merge_sibling(n, j):
        part = PARTS[n]
        sib_copy(n, j).wait_recv()
        loc_copy(n, j).wait()
        a, b = acc[part[0]], sib[part[0]]
        def fn(i, _):
            a[i] = (a[i].astype(F32) + b[i].astype(F32)).astype(BF)
        each(part, 2, group(part, 2, STEPS[j]), fn)

    for j in range(4):
        for n in range(6):
            sib_copy(n, j).start()
            loc_copy(n, j).start()
    def dpx(i):
        peer = (dp + i) % 8
        return pltpu.make_async_remote_copy(gg.at[peer], gdp.at[dp], ds_.at[i], dr_.at[i], device_id=(peer, sq), device_id_type=MESH)
    for i in range(1, 8):
        dpx(i).start()
    gdp[dp] = gg[dp]
    for t in (2, 1, 0):
        for n in range(6):
            if t == 2:
                merge_sibling(n, 0)
            else:
                finish(n, t + 1)
            for k in kinds(n, t):
                hop_send(n, t, k).start()
        if t == 2:
            for n in range(6):
                merge_sibling(n, 1)
                merge_sibling(n, 2)
        for n in range(6):
            part = PARTS[n]
            for k in (0, 1):
                if k in kinds(n, t):
                    hop_send(n, t, k).wait_recv()
                    a, b = acc[part[0]], hop[t][part[0]]
                    def fn(i, pos, a=a, b=b, part=part, k=k):
                        j = slot(part) + (k,) + pos
                        a[i] = (a[i].astype(F32) + b[j].astype(F32)).astype(BF)
                    each(part, t, group(part, t, 1 if k == 0 else -1), fn, k)
                fin_send(n, t, k).start()
        if t == 2:
            for n in range(6):
                merge_sibling(n, 3)

        def finish(n, t):
            part = PARTS[n]
            fin_send(n, t, 0).wait_recv()
            fin_send(n, t, 1).wait_recv()
            a, b = acc[part[0]], fin[t][part[0]]
            def fn(i, pos):
                s = slot(part)
                a[i] = (a[i].astype(F32) + b[s + (0,) + pos].astype(F32) + b[s + (1,) + pos].astype(F32)).astype(BF)
            each(part, t, group(part, t, 0), fn)

    for n in range(6):
        part = PARTS[n]
        fin_send(n, 0, 0).wait_recv()
        fin_send(n, 0, 1).wait_recv()
        a, b = acc[part[0]], fin[0][part[0]]
        s = slot(part)
        v = a[idx(part, me)].astype(F32) + b[s + (0,)].astype(F32) + b[s + (1,)].astype(F32)
        if part[0] == "A":
            blk[32 * part[1]:32 * part[1] + 32, 0:384] = v
        elif part[0] == "B":
            blk[48 * part[1]:48 * part[1] + 48, 384:640] = v
        else:
            oC[...] = v
    stage[:, 6:8, :] = jnp.zeros((16, 2, 640), F32)
    for k in range(16):
        stage[k, 0:6, :] = blk[6 * k:6 * k + 6, :]
    def a2a(i):
        peer = (sq + i) % 16
        return pltpu.make_async_remote_copy(stage.at[peer], recv.at[sq], as_.at[i], ar_.at[i], device_id=(dp, peer), device_id_type=MESH)
    for i in range(1, 16):
        a2a(i).start()
    recv[sq] = stage[sq]
    for i in range(1, 8):
        dpx(i).wait_recv()
    gsum[...] = jnp.sum(gdp[...], axis=0)
    def inf(i):
        peer = (sq + i) % 16
        return pltpu.make_async_remote_copy(gsum, gsq.at[sq], is_.at[i], ir_.at[i], device_id=(dp, peer), device_id_type=MESH)
    for i in range(1, 16):
        inf(i).start()
    gsq[sq] = gsum[...]
    for i in range(1, 16):
        a2a(i).wait_recv()
    for s in range(16):
        oA[s // 2, :, 384 * (s % 2):384 * (s % 2) + 384] = recv[s, 0:6, 0:384]
        oB[s // 8, :, 256 * (s % 8):256 * (s % 8) + 256] = recv[s, 0:6, 384:640]
    for i in range(1, 16):
        inf(i).wait_recv()
    oG[...] = jnp.sum(gsq[...], axis=0)
    for i in range(1, 8):
        dpx(i).wait_send()
    for i in range(1, 16):
        a2a(i).wait_send()
        inf(i).wait_send()
    for n in range(6):
        for j in range(4):
            sib_copy(n, j).wait_send()
        for t in range(3):
            for k in kinds(n, t):
                hop_send(n, t, k).wait_send()
            fin_send(n, t, 0).wait_send()
            fin_send(n, t, 1).wait_send()

def scatter(GA, GB, GC, gg):
    V = pl.BlockSpec(memory_space=pltpu.VMEM)
    H = pl.BlockSpec(memory_space=pl.ANY)
    D = pltpu.SemaphoreType.DMA
    bA, bB, bC = (32, 384), (48, 256), (16, 768)
    M = lambda *s: pltpu.VMEM(s, BF)
    trip = lambda pre: [M(3, *pre, *bA), M(2, *pre, *bB), M(*pre, *bC)]
    return pl.pallas_call(
        scatter_kernel,
        out_shape=(jax.ShapeDtypeStruct((8, 6, 768), F32), jax.ShapeDtypeStruct((2, 6, 2048), F32),
                   jax.ShapeDtypeStruct((16, 768), F32), jax.ShapeDtypeStruct((8, 128), F32)),
        in_specs=[H] * 3 + [V], out_specs=(V,) * 4,
        scratch_shapes=trip((4, 4, 4)) + trip((4, 4, 4)) + trip((2, 2, 4)) + trip((2, 4, 4)) + trip((2, 2)) + trip((2, 4)) + trip((2,)) + trip((2,))
        + [pltpu.VMEM((96, 640), F32), pltpu.VMEM((16, 8, 640), F32), pltpu.VMEM((16, 8, 640), F32),
           pltpu.VMEM((8, 8, 128), F32), pltpu.VMEM((8, 128), F32), pltpu.VMEM((16, 8, 128), F32),
           D((6, 3, 4)), D((6, 3, 4)), D((6, 4)), D((6, 4)), D((6, 4)), D((16,)), D((16,)), D((16,)), D((16,)), D((8,)), D((8,))],
        compiler_params=pltpu.CompilerParams(collective_id=1, has_side_effects=True, vmem_limit_bytes=56 << 20),
        name="scatter_grads",
    )(GA, GB, GC, gg)


def body(
    dec_input,
    memory,
    mem_len,
    grad_out,
    attn_master,
    ffn_in_master,
    ffn_out_master,
    gain_master,
    attn_first,
    ffn_in_first,
    ffn_out_first,
    gain_first,
    attn_second,
    ffn_in_second,
    ffn_out_second,
    gain_second,
):
    gath_a, gath_b, gath_c, infos = gather(
        attn_master, ffn_in_master, ffn_out_master, info_tile(gain_master, mem_len)
    )
    attn_w = gath_a.reshape(8, 2, 768, 384).transpose(0, 2, 1, 3).reshape(8, 768, 768)
    in_w = gath_b.reshape(2, 8, 768, 256).transpose(0, 2, 1, 3).reshape(2, 768, 2048)
    out_w = gath_c.reshape(2048, 768)
    gains = infos[:, :3, :96].transpose(1, 0, 2).reshape(3, 768)
    examples, tgt_len, width = dec_input.shape
    total_rows = examples * tgt_len

    def split_heads(block):
        return block.reshape(examples, -1, H, HEAD)

    tok_rows = dec_input.astype(jnp.float32).reshape(total_rows, width)
    h_one, inv_one = norm_forward(tok_rows, gains[0])
    triple = jnp.einsum(
        "rd,kde->kre", h_one, attn_w[0:3], preferred_element_type=jnp.float32
    ).astype(jnp.bfloat16)
    q_one = split_heads(triple[0])
    k_one = split_heads(triple[1])
    v_one = split_heads(triple[2])
    position = jnp.arange(tgt_len)
    causal = (position[:, None] >= position[None, :])[None, None]
    mixed_one, lse_one = attend_forward(q_one, k_one, v_one, causal)
    flat_one = mixed_one.reshape(total_rows, width)
    after_one = tok_rows + dense(flat_one, attn_w[3])
    h_two, inv_two = norm_forward(after_one, gains[1])
    q_two = split_heads(dense(h_two, attn_w[4]).astype(jnp.bfloat16))
    local_pair = jnp.einsum(
        "emd,kdf->kemf", memory, attn_w[5:7], preferred_element_type=jnp.float32
    ).astype(jnp.bfloat16)
    pair = lax.all_to_all(local_pair, "seq", split_axis=1, concat_axis=2, tiled=True)
    mem_pos = jnp.arange(pair.shape[2])
    reach = (mem_pos[None, :] < mem_len[:, None])[:, None, None, :]
    k_two = split_heads(pair[0])
    v_two = split_heads(pair[1])
    mixed_two, lse_two = attend_forward(q_two, k_two, v_two, reach)
    flat_two = mixed_two.reshape(total_rows, width)
    after_two = after_one + dense(flat_two, attn_w[7])
    h_three, inv_three = norm_forward(after_two, gains[2])
    gate_up = jnp.einsum("rd,kdf->krf", h_three, in_w, preferred_element_type=jnp.float32)
    middle = gated_gelu(gate_up[0], gate_up[1]).astype(jnp.bfloat16)
    result = after_two + dense(middle, out_w)
    out_block = result.astype(jnp.bfloat16).reshape(dec_input.shape)
    grad_rows = grad_out.astype(jnp.float32).reshape(total_rows, width)
    grad_low = grad_rows.astype(jnp.bfloat16)
    g_down = jnp.einsum("rf,rd->fd", middle, grad_low, preferred_element_type=jnp.float32)
    grad_mid = jnp.einsum("rd,fd->rf", grad_low, out_w, preferred_element_type=jnp.float32)
    unused_value, pull = jax.vjp(gated_gelu, gate_up[0], gate_up[1])
    grad_gate, grad_up = pull(grad_mid)
    grad_pair = jnp.stack([grad_gate, grad_up]).astype(jnp.bfloat16)
    g_up = jnp.einsum("rd,krf->kdf", h_three, grad_pair, preferred_element_type=jnp.float32)
    grad_h_three = jnp.einsum("krf,kdf->rd", grad_pair, in_w, preferred_element_type=jnp.float32)
    norm_three, gain_three = norm_backward(after_two, inv_three, gains[2], grad_h_three)
    grad_two = grad_rows + norm_three
    cross_low = grad_two.astype(jnp.bfloat16)
    g_cross_out = weight_grad(flat_two, cross_low)
    grad_mixed_two = split_heads(back_dense(cross_low, attn_w[7]).astype(jnp.bfloat16))
    dq_two, dk_two, dv_two = attend_backward(q_two, k_two, v_two, reach, lse_two, grad_mixed_two)
    dq_flat = dq_two.reshape(total_rows, width)
    g_cross_query = weight_grad(h_two, dq_flat)
    kv_grad = jnp.stack([dk_two.reshape(examples, -1, width), dv_two.reshape(examples, -1, width)])
    kv_back = lax.all_to_all(kv_grad, "seq", split_axis=2, concat_axis=1, tiled=True)
    g_cross_kv = jnp.einsum("emd,kemf->kdf", memory, kv_back, preferred_element_type=jnp.float32)
    grad_memory = jnp.einsum(
        "kemf,kdf->emd", kv_back, attn_w[5:7], preferred_element_type=jnp.float32
    )
    norm_two, gain_two = norm_backward(after_one, inv_two, gains[1], back_dense(dq_flat, attn_w[4]))
    grad_one = grad_two + norm_two
    self_low = grad_one.astype(jnp.bfloat16)
    g_self_out = weight_grad(flat_one, self_low)
    grad_mixed_one = split_heads(back_dense(self_low, attn_w[3]).astype(jnp.bfloat16))
    dq_one, dk_one, dv_one = attend_backward(q_one, k_one, v_one, causal, lse_one, grad_mixed_one)
    grad_triple = jnp.stack(
        [
            dq_one.reshape(total_rows, width),
            dk_one.reshape(total_rows, width),
            dv_one.reshape(total_rows, width),
        ]
    )
    g_self_qkv = jnp.einsum("rd,kre->kde", h_one, grad_triple, preferred_element_type=jnp.float32)
    grad_h_one = jnp.einsum(
        "kre,kde->rd", grad_triple, attn_w[0:3], preferred_element_type=jnp.float32
    )
    norm_one, gain_one = norm_backward(tok_rows, inv_one, gains[0], grad_h_one)
    grad_input = (grad_one + norm_one).reshape(dec_input.shape)
    g_attn = jnp.concatenate(
        [g_self_qkv, g_self_out[None], g_cross_query[None], g_cross_kv, g_cross_out[None]], axis=0
    )
    g_gain = jnp.stack([gain_one, gain_two, gain_three])
    low_a = g_attn.reshape(8, 768, 2, 384).transpose(0, 2, 1, 3).astype(jnp.bfloat16)
    low_b = g_up.reshape(2, 768, 8, 256).transpose(0, 2, 1, 3).astype(jnp.bfloat16)
    tile_g = jnp.pad(g_gain.reshape(3, 8, 96).transpose(1, 0, 2), ((0, 0), (0, 5), (0, 32)))
    share_a, share_b, share_c, share_g = scatter(
        low_a.reshape(4, 4, 4, 2, 3, 32, 384),
        low_b.reshape(4, 4, 4, 2, 2, 48, 256),
        g_down.astype(jnp.bfloat16).reshape(4, 2, 4, 4, 16, 768),
        tile_g,
    )
    share_g = lax.dynamic_slice_in_dim(share_g[:3], 6 * lax.axis_index("seq"), 6, 1)
    shares = (share_a, share_b, share_c, share_g)
    attn_res = adam_update(attn_master, attn_first, attn_second, shares[0], rate_matrix)
    in_res = adam_update(ffn_in_master, ffn_in_first, ffn_in_second, shares[1], rate_matrix)
    out_res = adam_update(ffn_out_master, ffn_out_first, ffn_out_second, shares[2], rate_matrix)
    gain_res = adam_update(gain_master, gain_first, gain_second, shares[3], rate_gain)
    return (
        out_block,
        grad_input,
        grad_memory,
        attn_res[0],
        attn_res[1],
        attn_res[2],
        attn_res[3],
        in_res[0],
        in_res[1],
        in_res[2],
        in_res[3],
        out_res[0],
        out_res[1],
        out_res[2],
        out_res[3],
        gain_res[0],
        gain_res[1],
        gain_res[2],
        gain_res[3],
    )


def solution(mesh):
    placed = (
        P(("dp", "seq"), None, None),
        P("dp", "seq", None),
        P(("dp", "seq")),
        P(("dp", "seq"), None, None),
        P(None, ("dp", "seq"), None),
        P(None, ("dp", "seq"), None),
        P(("dp", "seq"), None),
        P(None, ("dp", "seq")),
        P(None, ("dp", "seq"), None),
        P(None, ("dp", "seq"), None),
        P(("dp", "seq"), None),
        P(None, ("dp", "seq")),
        P(None, ("dp", "seq"), None),
        P(None, ("dp", "seq"), None),
        P(("dp", "seq"), None),
        P(None, ("dp", "seq")),
    )
    return jax.shard_map(
        body,
        mesh=mesh,
        in_specs=placed,
        out_specs=(
            P(("dp", "seq"), None, None),
            P(("dp", "seq"), None, None),
            P("dp", "seq", None),
            P(None, ("dp", "seq"), None),
            P(None, ("dp", "seq"), None),
            P(None, ("dp", "seq"), None),
            P(None, ("dp", "seq"), None),
            P(None, ("dp", "seq"), None),
            P(None, ("dp", "seq"), None),
            P(None, ("dp", "seq"), None),
            P(None, ("dp", "seq"), None),
            P(("dp", "seq"), None),
            P(("dp", "seq"), None),
            P(("dp", "seq"), None),
            P(("dp", "seq"), None),
            P(None, ("dp", "seq")),
            P(None, ("dp", "seq")),
            P(None, ("dp", "seq")),
            P(None, ("dp", "seq")),
        ),
        check_vma=False,
    )
```

```python
import jax
import jax.numpy as jnp
from jax import lax
from jax.experimental import pallas as pl
from jax.experimental.pallas import tpu as pltpu
from jax.sharding import PartitionSpec as P

H = 12
HEAD = 64
STEP = 10


eps_norm = 1e-06
score_scale = 0.125
beta_one = 0.9
beta_two = 0.999
adam_eps = 1e-08
decay_rate = 0.01
rate_matrix = 0.12
rate_gain = 3.0
neg_big = -1e30


def dense(left, right):
    return jnp.dot(left, right, preferred_element_type=jnp.float32)


def weight_grad(left, right):
    return jnp.einsum("rd,re->de", left, right, preferred_element_type=jnp.float32)


def back_dense(incoming, weight):
    return jnp.einsum("re,de->rd", incoming, weight, preferred_element_type=jnp.float32)


def gated_gelu(gate_part, up_part):
    return jax.nn.gelu(gate_part, approximate=True) * up_part


def norm_forward(tok_rows, gain_row):
    inverse = lax.rsqrt(jnp.mean(tok_rows * tok_rows, axis=-1, keepdims=True) + eps_norm)
    return ((tok_rows * inverse * gain_row).astype(jnp.bfloat16), inverse)


def norm_backward(tok_rows, inverse, gain_row, incoming):
    scaled = incoming * gain_row
    gain_grad = jnp.sum(incoming * tok_rows * inverse, axis=0)
    inner_sum = jnp.mean(scaled * tok_rows, axis=-1, keepdims=True)
    return (inverse * scaled - tok_rows * inverse * inverse * inverse * inner_sum, gain_grad)


def scores_of(queries, key_set, is_valid):
    scores = (
        jnp.einsum("eqhc,ekhc->ehqk", queries, key_set, preferred_element_type=jnp.float32)
        * score_scale
    )
    return jnp.where(is_valid, scores, neg_big)


def attend_forward(queries, key_set, values, is_valid):
    scores = scores_of(queries, key_set, is_valid)
    row_top = jnp.max(scores, axis=-1, keepdims=True)
    logsum = row_top + jnp.log(jnp.sum(jnp.exp(scores - row_top), axis=-1, keepdims=True))
    prob_rows = jnp.exp(scores - logsum).astype(jnp.bfloat16)
    mixed = jnp.einsum("ehqk,ekhc->eqhc", prob_rows, values, preferred_element_type=jnp.float32)
    return (mixed.astype(jnp.bfloat16), logsum)


def attend_backward(queries, key_set, values, is_valid, logsum, incoming):
    prob_rows = jnp.exp(scores_of(queries, key_set, is_valid) - logsum)
    value_grad = jnp.einsum(
        "ehqk,eqhc->ekhc",
        prob_rows.astype(jnp.bfloat16),
        incoming,
        preferred_element_type=jnp.float32,
    )
    prob_grad = jnp.einsum("eqhc,ekhc->ehqk", incoming, values, preferred_element_type=jnp.float32)
    row_delta = jnp.sum(prob_grad * prob_rows, axis=-1, keepdims=True)
    score_grad = (prob_rows * (prob_grad - row_delta)).astype(jnp.bfloat16)
    query_grad = (
        jnp.einsum("ehqk,ekhc->eqhc", score_grad, key_set, preferred_element_type=jnp.float32)
        * score_scale
    )
    key_grad = (
        jnp.einsum("ehqk,eqhc->ekhc", score_grad, queries, preferred_element_type=jnp.float32)
        * score_scale
    )
    return (
        query_grad.astype(jnp.bfloat16),
        key_grad.astype(jnp.bfloat16),
        value_grad.astype(jnp.bfloat16),
    )


def adam_update(master, first, second, grad, rate):
    first_new = beta_one * first + (1.0 - beta_one) * grad
    second_new = beta_two * second + (1.0 - beta_two) * grad * grad
    fix_one = 1.0 - beta_one**STEP
    fix_two = 1.0 - beta_two**STEP
    master_new = master - rate * (
        first_new / fix_one / (jnp.sqrt(second_new / fix_two) + adam_eps) + decay_rate * master
    )
    return (master_new, first_new, second_new, master_new.astype(jnp.bfloat16))


MESH = pl.DeviceIdType.MESH
BF, F32 = jnp.bfloat16, jnp.float32
ALL = slice(None)
PARTS = (("A", 0, "xyz"), ("A", 1, "yzx"), ("A", 2, "zxy"), ("B", 0, "xyz"), ("B", 1, "yzx"), ("C", 0, "zxy"))

def where_am_i():
    dp, sq = lax.axis_index("dp"), lax.axis_index("seq")
    return {"x": sq // 4, "y": sq % 4, "z": dp // 2, "c": dp % 2}

def dev(at):
    return (at["z"] * 2 + at["c"], at["x"] * 4 + at["y"])

def moved(at, axis, step):
    return {**at, axis: (at[axis] + step + 4) % 4}

def gather_kernel(attn, wi, wo, info, A, B, C, infos, stage, recv, blk, blkA, blkB, blkC, irecv,
                  ss, rs, sib_s, sib_r, as_, ar_, is_, ir_, ds_, dr_, own_s):
    me = where_am_i()
    dp, sq = lax.axis_index("dp"), lax.axis_index("seq")
    bar = pltpu.get_barrier_semaphore()
    for i in range(1, 16):
        pl.semaphore_signal(bar, inc=1, device_id=(dp, (sq + i) % 16), device_id_type=MESH)
    for i in range(1, 8):
        pl.semaphore_signal(bar, inc=1, device_id=((dp + i) % 8, sq), device_id_type=MESH)
    stage[:, 6:8, :] = jnp.zeros((16, 2, 640), F32)
    for s in range(16):
        stage[s, 0:6, 0:384] = attn[s // 2, :, 384 * (s % 2):384 * (s % 2) + 384]
        stage[s, 0:6, 384:640] = wi[s // 8, :, 256 * (s % 8):256 * (s % 8) + 256]
    pl.semaphore_wait(bar, 22)
    def a2a(i):
        peer = (sq + i) % 16
        return pltpu.make_async_remote_copy(stage.at[peer], recv.at[sq], as_.at[i], ar_.at[i], device_id=(dp, peer), device_id_type=MESH)
    def inf(i):
        peer = (sq + i) % 16
        return pltpu.make_async_remote_copy(info, irecv.at[sq], is_.at[i], ir_.at[i], device_id=(dp, peer), device_id_type=MESH)
    for i in range(1, 16):
        a2a(i).start()
    for i in range(1, 16):
        inf(i).start()
    recv[sq] = stage[sq]
    irecv[sq] = info[...]
    blkC[...] = wo[...].astype(BF)
    for i in range(1, 16):
        a2a(i).wait_recv()
    for k in range(16):
        blk[6 * k:6 * k + 6, :] = recv[k, 0:6, :]
    for p in range(3):
        blkA[p] = blk[32 * p:32 * p + 32, 0:384].astype(BF)
    for p in range(2):
        blkB[p] = blk[48 * p:48 * p + 48, 384:640].astype(BF)

    def view(part, at):
        name, p, _ = part
        if name == "A":
            return A.at[at["x"], at["y"], at["z"], at["c"], p]
        if name == "B":
            return B.at[at["x"], at["y"], at["z"], at["c"], p]
        return C.at[at["z"], at["c"], at["x"], at["y"]]

    def mine(part):
        name, p, _ = part
        return blkA.at[p] if name == "A" else blkB.at[p] if name == "B" else blkC

    def group(part, t, step, half=None):
        order = part[2]
        at = moved(me, order[t], step)
        for j in range(t):
            at = {**at, order[j]: ALL}
        if half is not None and t:
            at = {**at, order[0]: pl.ds(2 * half, 2)}
        return at

    def send(n, t, kind):
        part = PARTS[n]
        axis = part[2][t]
        step = 1 if kind in (0, 2) else -1
        if kind < 2:
            dst = view(part, group(part, t, 0))
            src = mine(part) if t == 0 else dst
        else:
            dst = src = view(part, group(part, t, -step, kind - 2))
        return pltpu.make_async_remote_copy(src, dst, ss.at[n, t, kind], rs.at[n, t, kind], device_id=dev(moved(me, axis, step)), device_id_type=MESH)

    def arrival(n, t, kind):
        part = PARTS[n]
        axis = part[2][t]
        step = 1 if kind in (0, 2) else -1
        if kind < 2:
            dst = view(part, group(part, t, -step))
        else:
            dst = view(part, group(part, t, -2 * step, kind - 2))
        return pltpu.make_async_remote_copy(dst, dst, ss.at[n, t, kind], rs.at[n, t, kind], device_id=dev(moved(me, axis, step)), device_id_type=MESH)

    def kinds(n, t):
        return (0, 1, 2, 3) if t else (0, 1, 2 + n % 2)

    def sibling(n, j, c):
        part = PARTS[n]
        steps = (0, -1, 1, 2)
        at = {**group(part, 2, steps[j]), "c": c}
        v = view(part, at)
        return pltpu.make_async_remote_copy(v, v, sib_s.at[n, j], sib_r.at[n, j], device_id=dev({**me, "c": 1 - me["c"]}), device_id_type=MESH)

    owns = [pltpu.make_async_copy(mine(PARTS[n]), view(PARTS[n], me), own_s.at[n]) for n in range(6)]
    for o in owns:
        o.start()
    for t in range(3):
        for n in range(6):
            if t == 1:
                owns[n].wait()
            if t:
                for k in kinds(n, t - 1)[2:]:
                    arrival(n, t - 1, k).wait_recv()
            send(n, t, 0).start()
            send(n, t, 1).start()
            if t == 2:
                sibling(n, 0, me["c"]).start()
        for n in range(6):
            for k in (0, 1):
                arrival(n, t, k).wait_recv()
                if 2 + k in kinds(n, t):
                    send(n, t, 2 + k).start()
                if t == 2:
                    sibling(n, 1 + k, me["c"]).start()
    for i in range(1, 16):
        inf(i).wait_recv()
    tile = jnp.sum(irecv[...], axis=0)
    infos[dp] = tile
    def dpx(i):
        return pltpu.make_async_remote_copy(infos.at[dp], infos.at[dp], ds_.at[i], dr_.at[i], device_id=((dp + i) % 8, sq), device_id_type=MESH)
    def dpx_in(i):
        return pltpu.make_async_remote_copy(infos.at[(dp - i + 8) % 8], infos.at[(dp - i + 8) % 8], ds_.at[i], dr_.at[i], device_id=((dp + i) % 8, sq), device_id_type=MESH)
    for i in range(1, 8):
        dpx(i).start()
    for n in range(6):
        for k in (2, 3):
            arrival(n, 2, k).wait_recv()
        sibling(n, 3, me["c"]).start()
    for i in range(1, 8):
        dpx_in(i).wait_recv()
    for n in range(6):
        for j in range(4):
            sibling(n, j, 1 - me["c"]).wait_recv()
    for i in range(1, 16):
        a2a(i).wait_send()
        inf(i).wait_send()
    for i in range(1, 8):
        dpx(i).wait_send()
    for n in range(6):
        for t in range(3):
            for k in kinds(n, t):
                send(n, t, k).wait_send()
        for j in range(4):
            sibling(n, j, me["c"]).wait_send()

def gather(attn, wi, wo, info):
    V = pl.BlockSpec(memory_space=pltpu.VMEM)
    H = pl.BlockSpec(memory_space=pl.ANY)
    D = pltpu.SemaphoreType.DMA
    return pl.pallas_call(
        gather_kernel,
        out_shape=(jax.ShapeDtypeStruct((4, 4, 4, 2, 3, 32, 384), BF),
                   jax.ShapeDtypeStruct((4, 4, 4, 2, 2, 48, 256), BF),
                   jax.ShapeDtypeStruct((4, 2, 4, 4, 16, 768), BF),
                   jax.ShapeDtypeStruct((8, 8, 128), F32)),
        in_specs=[V] * 4, out_specs=(H, H, H, V),
        scratch_shapes=[pltpu.VMEM((16, 8, 640), F32), pltpu.VMEM((16, 8, 640), F32), pltpu.VMEM((96, 640), F32),
                        pltpu.VMEM((3, 32, 384), BF), pltpu.VMEM((2, 48, 256), BF), pltpu.VMEM((16, 768), BF),
                        pltpu.VMEM((16, 8, 128), F32),
                        D((6, 3, 4)), D((6, 3, 4)), D((6, 4)), D((6, 4)), D((16,)), D((16,)), D((16,)), D((16,)), D((8,)), D((8,)), D((6,))],
        compiler_params=pltpu.CompilerParams(collective_id=0, has_side_effects=True, vmem_limit_bytes=32 << 20),
        name="gather_weights",
    )(attn, wi, wo, info)

def info_tile(gain, mem_len):
    sq = lax.axis_index("seq")
    t = jnp.zeros((8, 128), F32)
    t = lax.dynamic_update_slice(t, gain.astype(BF).astype(F32), (0, 6 * sq))
    return lax.dynamic_update_slice(t, mem_len.astype(F32)[:, None], (3, sq))

def scatter_kernel(GA, GB, GC, gg, oA, oB, oC, oG, accA, accB, accC, sibA, sibB, sibC,
                   hA2, hB2, hC2, fA2, fB2, fC2, hA1, hB1, hC1, fA1, fB1, fC1, hA0, hB0, hC0, fA0, fB0, fC0,
                   blk, stage, recv, gdp, gsum, gsq,
                   ss, rs, sib_s, sib_r, loc_s, as_, ar_, is_, ir_, ds_, dr_):
    me = where_am_i()
    dp, sq = lax.axis_index("dp"), lax.axis_index("seq")
    acc = {"A": accA, "B": accB, "C": accC}
    sib = {"A": sibA, "B": sibB, "C": sibC}
    hop = {2: {"A": hA2, "B": hB2, "C": hC2}, 1: {"A": hA1, "B": hB1, "C": hC1}, 0: {"A": hA0, "B": hB0, "C": hC0}}
    fin = {2: {"A": fA2, "B": fB2, "C": fC2}, 1: {"A": fA1, "B": fB1, "C": fC1}, 0: {"A": fA0, "B": fB0, "C": fC0}}
    bar = pltpu.get_barrier_semaphore()
    for i in range(1, 16):
        pl.semaphore_signal(bar, inc=1, device_id=(dp, (sq + i) % 16), device_id_type=MESH)
    for i in range(1, 8):
        pl.semaphore_signal(bar, inc=1, device_id=((dp + i) % 8, sq), device_id_type=MESH)
    pl.semaphore_wait(bar, 22)

    def idx(part, at):
        name, p, _ = part
        if name == "C":
            return (at["z"], at["x"], at["y"])
        return (p, at["x"], at["y"], at["z"])

    def source(part, at, c):
        name, p, _ = part
        if name == "A":
            return GA.at[at["x"], at["y"], at["z"], c, p]
        if name == "B":
            return GB.at[at["x"], at["y"], at["z"], c, p]
        return GC.at[at["z"], c, at["x"], at["y"]]

    def names(part):
        return "zxy" if part[0] == "C" else "xyz"

    def group(part, t, step):
        order = part[2]
        at = moved(me, order[t], step)
        for j in range(t):
            at = {**at, order[j]: ALL}
        return at

    def halved(part, t, at, half):
        if t == 0:
            return at
        first = [a for a in names(part) if a in part[2][:t]][0]
        return {**at, first: pl.ds(2 * half, 2)}

    def done(part, t):
        return [a for a in names(part) if a in part[2][:t]]

    STEPS = (2, -1, 1, 0)
    other = dev({**me, "c": 1 - me["c"]})

    def sib_copy(n, j):
        part = PARTS[n]
        at = group(part, 2, STEPS[j])
        return pltpu.make_async_remote_copy(source(part, at, 1 - me["c"]), sib[part[0]].at[idx(part, at)], sib_s.at[n, j], sib_r.at[n, j], device_id=other, device_id_type=MESH)

    def loc_copy(n, j):
        part = PARTS[n]
        at = group(part, 2, STEPS[j])
        return pltpu.make_async_copy(source(part, at, me["c"]), acc[part[0]].at[idx(part, at)], loc_s.at[n, j])

    def slot(part):
        return () if part[0] == "C" else (part[1],)

    def kinds(n, t):
        return (0, 1) if t else (n % 2,)

    def hop_send(n, t, kind):
        part = PARTS[n]
        step = 1 if kind == 0 else -1
        at = halved(part, t, group(part, t, 2 * step), kind)
        return pltpu.make_async_remote_copy(acc[part[0]].at[idx(part, at)], hop[t][part[0]].at[slot(part) + (kind,)],
                                            ss.at[n, t, kind], rs.at[n, t, kind], device_id=dev(moved(me, part[2][t], step)), device_id_type=MESH)

    def fin_send(n, t, kind):
        part = PARTS[n]
        step = 1 if kind == 0 else -1
        at = group(part, t, step)
        return pltpu.make_async_remote_copy(acc[part[0]].at[idx(part, at)], fin[t][part[0]].at[slot(part) + (kind,)],
                                            ss.at[n, t, 2 + kind], rs.at[n, t, 2 + kind], device_id=dev(moved(me, part[2][t], step)), device_id_type=MESH)

    def each(part, t, at, fn, half=None):
        axes = done(part, t)
        sizes = [4] * len(axes)
        offs = [0] * len(axes)
        if half is not None and axes:
            sizes[0] = 2
            offs[0] = 2 * half
        total = 1
        for s in sizes:
            total *= s
        def one(i):
            pos = []
            rest = i
            for s in sizes[::-1]:
                pos.append(rest % s)
                rest = rest // s
            pos = pos[::-1]
            where = dict(at)
            for a, p, o in zip(axes, pos, offs):
                where[a] = p + o
            fn(idx(part, where), tuple(pos))
        if total == 1:
            one(0)
        else:
            pl.loop(0, total)(one)

    def merge_sibling(n, j):
        part = PARTS[n]
        sib_copy(n, j).wait_recv()
        loc_copy(n, j).wait()
        a, b = acc[part[0]], sib[part[0]]
        def fn(i, _):
            a[i] = (a[i].astype(F32) + b[i].astype(F32)).astype(BF)
        each(part, 2, group(part, 2, STEPS[j]), fn)

    for j in range(4):
        for n in range(6):
            sib_copy(n, j).start()
            loc_copy(n, j).start()
    def dpx(i):
        peer = (dp + i) % 8
        return pltpu.make_async_remote_copy(gg.at[peer], gdp.at[dp], ds_.at[i], dr_.at[i], device_id=(peer, sq), device_id_type=MESH)
    for i in range(1, 8):
        dpx(i).start()
    gdp[dp] = gg[dp]
    for t in (2, 1, 0):
        for n in range(6):
            if t == 2:
                merge_sibling(n, 0)
            else:
                finish(n, t + 1)
            for k in kinds(n, t):
                hop_send(n, t, k).start()
        if t == 2:
            for n in range(6):
                merge_sibling(n, 1)
                merge_sibling(n, 2)
        for n in range(6):
            part = PARTS[n]
            for k in (0, 1):
                if k in kinds(n, t):
                    hop_send(n, t, k).wait_recv()
                    a, b = acc[part[0]], hop[t][part[0]]
                    def fn(i, pos, a=a, b=b, part=part, k=k):
                        j = slot(part) + (k,) + pos
                        a[i] = (a[i].astype(F32) + b[j].astype(F32)).astype(BF)
                    each(part, t, group(part, t, 1 if k == 0 else -1), fn, k)
                fin_send(n, t, k).start()
        if t == 2:
            for n in range(6):
                merge_sibling(n, 3)

        def finish(n, t):
            part = PARTS[n]
            fin_send(n, t, 0).wait_recv()
            fin_send(n, t, 1).wait_recv()
            a, b = acc[part[0]], fin[t][part[0]]
            def fn(i, pos):
                s = slot(part)
                a[i] = (a[i].astype(F32) + b[s + (0,) + pos].astype(F32) + b[s + (1,) + pos].astype(F32)).astype(BF)
            each(part, t, group(part, t, 0), fn)

    for n in range(6):
        part = PARTS[n]
        fin_send(n, 0, 0).wait_recv()
        fin_send(n, 0, 1).wait_recv()
        a, b = acc[part[0]], fin[0][part[0]]
        s = slot(part)
        v = a[idx(part, me)].astype(F32) + b[s + (0,)].astype(F32) + b[s + (1,)].astype(F32)
        if part[0] == "A":
            blk[32 * part[1]:32 * part[1] + 32, 0:384] = v
        elif part[0] == "B":
            blk[48 * part[1]:48 * part[1] + 48, 384:640] = v
        else:
            oC[...] = v
    stage[:, 6:8, :] = jnp.zeros((16, 2, 640), F32)
    for k in range(16):
        stage[k, 0:6, :] = blk[6 * k:6 * k + 6, :]
    def a2a(i):
        peer = (sq + i) % 16
        return pltpu.make_async_remote_copy(stage.at[peer], recv.at[sq], as_.at[i], ar_.at[i], device_id=(dp, peer), device_id_type=MESH)
    for i in range(1, 16):
        a2a(i).start()
    recv[sq] = stage[sq]
    for i in range(1, 8):
        dpx(i).wait_recv()
    gsum[...] = jnp.sum(gdp[...], axis=0)
    def inf(i):
        peer = (sq + i) % 16
        return pltpu.make_async_remote_copy(gsum, gsq.at[sq], is_.at[i], ir_.at[i], device_id=(dp, peer), device_id_type=MESH)
    for i in range(1, 16):
        inf(i).start()
    gsq[sq] = gsum[...]
    for i in range(1, 16):
        a2a(i).wait_recv()
    for s in range(16):
        oA[s // 2, :, 384 * (s % 2):384 * (s % 2) + 384] = recv[s, 0:6, 0:384]
        oB[s // 8, :, 256 * (s % 8):256 * (s % 8) + 256] = recv[s, 0:6, 384:640]
    for i in range(1, 16):
        inf(i).wait_recv()
    oG[...] = jnp.sum(gsq[...], axis=0)
    for i in range(1, 8):
        dpx(i).wait_send()
    for i in range(1, 16):
        a2a(i).wait_send()
        inf(i).wait_send()
    for n in range(6):
        for j in range(4):
            sib_copy(n, j).wait_send()
        for t in range(3):
            for k in kinds(n, t):
                hop_send(n, t, k).wait_send()
            fin_send(n, t, 0).wait_send()
            fin_send(n, t, 1).wait_send()

def scatter(GA, GB, GC, gg):
    V = pl.BlockSpec(memory_space=pltpu.VMEM)
    H = pl.BlockSpec(memory_space=pl.ANY)
    D = pltpu.SemaphoreType.DMA
    bA, bB, bC = (32, 384), (48, 256), (16, 768)
    M = lambda *s: pltpu.VMEM(s, BF)
    trip = lambda pre: [M(3, *pre, *bA), M(2, *pre, *bB), M(*pre, *bC)]
    return pl.pallas_call(
        scatter_kernel,
        out_shape=(jax.ShapeDtypeStruct((8, 6, 768), F32), jax.ShapeDtypeStruct((2, 6, 2048), F32),
                   jax.ShapeDtypeStruct((16, 768), F32), jax.ShapeDtypeStruct((8, 128), F32)),
        in_specs=[H] * 3 + [V], out_specs=(V,) * 4,
        scratch_shapes=trip((4, 4, 4)) + trip((4, 4, 4)) + trip((2, 2, 4)) + trip((2, 4, 4)) + trip((2, 2)) + trip((2, 4)) + trip((2,)) + trip((2,))
        + [pltpu.VMEM((96, 640), F32), pltpu.VMEM((16, 8, 640), F32), pltpu.VMEM((16, 8, 640), F32),
           pltpu.VMEM((8, 8, 128), F32), pltpu.VMEM((8, 128), F32), pltpu.VMEM((16, 8, 128), F32),
           D((6, 3, 4)), D((6, 3, 4)), D((6, 4)), D((6, 4)), D((6, 4)), D((16,)), D((16,)), D((16,)), D((16,)), D((8,)), D((8,))],
        compiler_params=pltpu.CompilerParams(collective_id=1, has_side_effects=True, vmem_limit_bytes=56 << 20),
        name="scatter_grads",
    )(GA, GB, GC, gg)
NEG = -1e30
PLANE = ((0, "xy"), (1, "yx"))

class Plane:
    def __init__(self, me, view, ss, rs):
        self.me, self.view, self.ss, self.rs = me, view, ss, rs
    def group(self, n, t, step, half=None):
        order = PLANE[n][1]
        at = moved(self.me, order[t], step)
        if t:
            at = {**at, order[0]: ALL if half is None else pl.ds(2 * half, 2)}
        return at
    def copy(self, n, t, kind, back=0):
        axis = PLANE[n][1][t]
        step = 1 if kind in (0, 2) else -1
        at = self.group(n, t, back) if kind < 2 else self.group(n, t, back - step, kind - 2)
        v = self.view(n, at)
        return pltpu.make_async_remote_copy(v, v, self.ss.at[n, t, kind], self.rs.at[n, t, kind], device_id=dev(moved(self.me, axis, step)), device_id_type=MESH)
    def arrived(self, n, t, kind):
        step = 1 if kind in (0, 2) else -1
        self.copy(n, t, kind, -step).wait_recv()
    def kinds(self, n, t):
        return (0, 1, 2, 3) if t else (0, 1, 2 + n)
    def send(self, t):
        for n in range(2):
            if t:
                for k in self.kinds(n, t - 1)[2:]:
                    self.arrived(n, t - 1, k)
            self.copy(n, t, 0).start()
            self.copy(n, t, 1).start()
    def forward(self, t):
        for n in range(2):
            for k in (0, 1):
                self.arrived(n, t, k)
                if 2 + k in self.kinds(n, t):
                    self.copy(n, t, 2 + k).start()
    def finish(self):
        for n in range(2):
            for k in (2, 3):
                self.arrived(n, 1, k)
    def drain(self):
        for n in range(2):
            for t in range(2):
                for k in self.kinds(n, t):
                    self.copy(n, t, k).wait_send()

def meet(dp, sq):
    bar = pltpu.get_barrier_semaphore()
    for i in range(1, 16):
        pl.semaphore_signal(bar, inc=1, device_id=(dp, (sq + i) % 16), device_id_type=MESH)
    return bar

def offset(me, j, sign=1):
    return {**me, "x": (me["x"] + sign * (j // 4) + 4) % 4, "y": (me["y"] + sign * (j % 4) + 4) % 4}

def head_masks():
    lane = lax.broadcasted_iota(jnp.int32, (1, 256), 1)
    return [jnp.where(lane // 64 == h, 1.0, 0.0).astype(BF) for h in range(4)]

def dot(a, b, ca=1, cb=0):
    return lax.dot_general(a, b, (((ca,), (cb,)), ((), ())), preferred_element_type=F32)

def cross_fwd_kernel(q, lens, mem_h, A, q_h, k_h, v_h, kt_h, o_ref, L_ref,
                     qall, mem, wk, wv, wkT, wvT, K, V, KT, VT, ost, lst, orc, lrc, acc,
                     mem_s, w_s, out_s, ss, rs, os_, or_, ls_, lr_):
    me = where_am_i()
    dp, sq = lax.axis_index("dp"), lax.axis_index("seq")
    bar = meet(dp, sq)
    def load_mem(e):
        return pltpu.make_async_copy(mem_h.at[e], mem.at[e], mem_s.at[e])
    loads = [pltpu.make_async_copy(A.at[10 + i], (wk if i < 2 else wv).at[:, pl.ds(384 * (i % 2), 384)], w_s.at[i]) for i in range(4)]
    for c in loads:
        c.start()
    @pl.loop(0, 16)
    def _(e):
        load_mem(e).start()
    qall[me["x"], me["y"]] = q[...]
    pl.semaphore_wait(bar, 15)
    plane = Plane(me, lambda n, at: qall.at[at["x"], at["y"], :, pl.ds(384 * n, 384)], ss, rs)
    plane.send(0)
    for c in loads:
        c.wait()
    for i in range(6):
        wkT[:, 128 * i:128 * i + 128] = wk[128 * i:128 * i + 128, :].T
        wvT[:, 128 * i:128 * i + 128] = wv[128 * i:128 * i + 128, :].T
    plane.forward(0)
    def project(a, b):
        @pl.loop(a, b)
        def _(e):
            load_mem(e).wait()
            m = mem[e]
            K[e] = dot(m, wk[...]).astype(BF)
            VT[e] = dot(wvT[...], m, 1, 1).astype(BF)
            V[e] = dot(m, wv[...]).astype(BF)
            KT[e] = dot(wkT[...], m, 1, 1).astype(BF)
    project(0, 4)
    plane.send(1)
    project(4, 12)
    plane.forward(1)
    project(12, 16)
    outs = [pltpu.make_async_copy(a, b, out_s.at[i]) for i, (a, b) in enumerate(((K, k_h), (V, v_h), (KT, kt_h), (qall, q_h)))]
    for c in outs[:3]:
        c.start()
    plane.finish()
    outs[3].start()
    masks = head_masks()
    pos = 192 * sq + lax.broadcasted_iota(jnp.int32, (192, 128), 0)
    def o_copy(j):
        return pltpu.make_async_remote_copy(ost.at[j], orc.at[j], os_.at[j], or_.at[j], device_id=dev(offset(me, j)), device_id_type=MESH)
    def l_copy(j):
        return pltpu.make_async_remote_copy(lst.at[j], lrc.at[j], ls_.at[j], lr_.at[j], device_id=dev(offset(me, j)), device_id_type=MESH)
    @pl.loop(0, 16)
    def _(i):
        j = (i + 1) % 16
        at = offset(me, j)
        e = at["x"] * 4 + at["y"]
        live = pos < lens[pl.ds(e, 1), :]
        for g in range(3):
            q4 = qall[at["x"], at["y"], :, 256 * g:256 * g + 256]
            q4s = jnp.concatenate([q4 * m for m in masks], axis=0)
            sT = dot(K[e, :, 256 * g:256 * g + 256], q4s, 1, 1)
            ps, inv = [], []
            for h in range(4):
                s = jnp.where(live, sT[:, 128 * h:128 * h + 128], NEG)
                top = jnp.max(s, axis=0, keepdims=True)
                p = jnp.exp(s - top)
                tot = jnp.sum(p, axis=0, keepdims=True)
                lst[j, 4 * g + h:4 * g + h + 1, :] = top + jnp.log(tot)
                ps.append(p.astype(BF))
                inv.append(1.0 / tot)
            oT = dot(VT[e, 256 * g:256 * g + 256, :], jnp.concatenate(ps, axis=1))
            for h in range(4):
                ost[j, 256 * g + 64 * h:256 * g + 64 * h + 64, :] = (oT[64 * h:64 * h + 64, 128 * h:128 * h + 128] * inv[h]).astype(BF)
        @pl.when(j > 0)
        def _():
            l_copy(j).start()
            o_copy(j).start()
    lrc[0] = lst[0]
    orc[0] = ost[0]
    @pl.loop(1, 16)
    def _(j):
        l_copy(j).wait_recv()
    l = lrc[:, 0:12, :]
    top = jnp.max(l, axis=0)
    total = top + jnp.log(jnp.sum(jnp.exp(l - top[None]), axis=0))
    L_ref[0:12, :] = total
    L_ref[12:16, :] = jnp.zeros((4, 128), F32)
    acc[...] = jnp.zeros_like(acc)
    @pl.loop(0, 16)
    def _(j):
        @pl.when(j > 0)
        def _():
            o_copy(j).wait_recv()
        w = jnp.exp(lrc[j, 0:12, :] - L_ref[0:12, :])
        for h in range(12):
            acc[64 * h:64 * h + 64, :] += orc[j, 64 * h:64 * h + 64, :].astype(F32) * w[h:h + 1, :]
    for i in range(6):
        o_ref[:, 128 * i:128 * i + 128] = acc[128 * i:128 * i + 128, :].T
    @pl.loop(1, 16)
    def _(j):
        l_copy(j).wait_send()
        o_copy(j).wait_send()
    plane.drain()
    for c in outs:
        c.wait()

def cross_fwd(q, lens, memory, A):
    V = pl.BlockSpec(memory_space=pltpu.VMEM)
    H = pl.BlockSpec(memory_space=pl.ANY)
    D = pltpu.SemaphoreType.DMA
    S = jax.ShapeDtypeStruct
    M = lambda *s: pltpu.VMEM(s, BF)
    return pl.pallas_call(
        cross_fwd_kernel,
        out_shape=(S((4, 4, 128, 768), BF), S((16, 192, 768), BF), S((16, 192, 768), BF), S((16, 768, 192), BF), S((128, 768), F32), S((16, 128), F32)),
        in_specs=[V, V, H, H], out_specs=(H, H, H, H, V, V),
        scratch_shapes=[M(4, 4, 128, 768), M(16, 192, 768), M(768, 768), M(768, 768), M(768, 768), M(768, 768),
                        M(16, 192, 768), M(16, 192, 768), M(16, 768, 192), M(16, 768, 192), M(16, 768, 128), pltpu.VMEM((16, 16, 128), F32),
                        M(16, 768, 128), pltpu.VMEM((16, 16, 128), F32), pltpu.VMEM((768, 128), F32),
                        D((16,)), D((4,)), D((4,)), D((2, 2, 4)), D((2, 2, 4)), D((16,)), D((16,)), D((16,)), D((16,))],
        compiler_params=pltpu.CompilerParams(collective_id=2, has_side_effects=True, vmem_limit_bytes=60 << 20),
        name="cross_forward",
    )(q, lens, memory, A)

def cross_bwd_kernel(do, st, lens, q_h, k_h, v_h, kt_h, mem_h, A, dq_ref, gm_h, dw_h,
                     qall, doall, stall, wk, wv, K, V, KT, mem, memT, dK, dV, gst, wst, dst, drc, acc,
                     ld_s, w_s, gm_s, dw_s, ss, rs, sss, srs, ds_, dr_):
    me = where_am_i()
    dp, sq = lax.axis_index("dp"), lax.axis_index("seq")
    bar = meet(dp, sq)
    lds = [pltpu.make_async_copy(a, b, ld_s.at[i]) for i, (a, b) in enumerate(((mem_h, mem), (q_h, qall), (k_h, K), (v_h, V), (kt_h, KT)))]
    lds += [pltpu.make_async_copy(A.at[10 + i], (wk if i < 2 else wv).at[:, pl.ds(384 * (i % 2), 384)], w_s.at[i]) for i in range(4)]
    for c in lds:
        c.start()
    doall[me["x"], me["y"]] = do[...]
    stall[0] = st[...]
    pl.semaphore_wait(bar, 15)
    plane = Plane(me, lambda n, at: doall.at[at["x"], at["y"], :, pl.ds(384 * n, 384)], ss, rs)
    plane.send(0)
    def st_copy(j):
        return pltpu.make_async_remote_copy(st, stall.at[j], sss.at[j], srs.at[j], device_id=dev(offset(me, j, -1)), device_id_type=MESH)
    @pl.loop(1, 16)
    def _(j):
        st_copy(j).start()
    lds[0].wait()
    def turn(a, b):
        @pl.loop(a, b)
        def _(e):
            memT[:, pl.ds(pl.multiple_of(256 * e, 256), 256)] = mem[pl.ds(pl.multiple_of(256 * e, 256), 256), :].T
    turn(0, 2)
    plane.forward(0)
    turn(2, 5)
    plane.send(1)
    turn(5, 9)
    plane.forward(1)
    turn(9, 12)
    for c in lds[1:]:
        c.wait()
    @pl.loop(1, 16)
    def _(j):
        st_copy(j).wait_recv()
    plane.finish()
    masks = head_masks()
    pos = 192 * sq + lax.broadcasted_iota(jnp.int32, (192, 128), 0)
    def d_copy(j):
        return pltpu.make_async_remote_copy(dst.at[j], drc.at[j], ds_.at[j], dr_.at[j], device_id=dev(offset(me, j)), device_id_type=MESH)
    @pl.loop(0, 16)
    def _(i):
        j = (i + 1) % 16
        at = offset(me, j)
        e = at["x"] * 4 + at["y"]
        live = pos < lens[pl.ds(e, 1), :]
        rows = pl.ds(pl.multiple_of(192 * e, 192), 192)
        for g in range(3):
            cols = slice(256 * g, 256 * g + 256)
            q4 = qall[at["x"], at["y"], :, cols]
            d4 = doall[at["x"], at["y"], :, cols]
            q4s = jnp.concatenate([q4 * m for m in masks], axis=0)
            d4s = jnp.concatenate([d4 * m for m in masks], axis=0)
            sT = dot(K[e, :, cols], q4s, 1, 1)
            gT = dot(V[e, :, cols], d4s, 1, 1)
            ps, gs = [], []
            for h in range(4):
                n = 4 * g + h
                s = jnp.where(live, sT[:, 128 * h:128 * h + 128], NEG)
                p = jnp.exp(s - stall[j, n:n + 1, :])
                ps.append(p.astype(BF))
                gs.append((p * (gT[:, 128 * h:128 * h + 128] - stall[j, 16 + n:17 + n, :])).astype(BF))
            pT = jnp.concatenate(ps, axis=1)
            sg = jnp.concatenate(gs, axis=1)
            dV[rows, cols] = dot(pT, d4s).astype(BF)
            dK[rows, cols] = dot(sg, q4s).astype(BF)
            qT = dot(KT[e, cols, :], sg)
            for h in range(4):
                dst[j, 256 * g + 64 * h:256 * g + 64 * h + 64, :] = qT[64 * h:64 * h + 64, 128 * h:128 * h + 128].astype(BF)
        @pl.when(j > 0)
        def _():
            d_copy(j).start()
    def gm_copy(e):
        return pltpu.make_async_copy(gst.at[e % 2], gm_h.at[e], gm_s.at[e % 2])
    @pl.loop(0, 16)
    def _(e):
        @pl.when(e > 1)
        def _():
            gm_copy(e - 2).wait()
        rows = pl.ds(pl.multiple_of(192 * e, 192), 192)
        gst[e % 2] = dot(dK[rows, :], wk[...], 1, 1) + dot(dV[rows, :], wv[...], 1, 1)
        gm_copy(e).start()
    def dw_copy(n, r):
        return pltpu.make_async_copy(wst.at[n % 2], dw_h.at[n, pl.ds(pl.multiple_of(128 * r, 128), 128)], dw_s.at[n % 2])
    for n in range(4):
        src = dK if n < 2 else dV
        @pl.loop(0, 6)
        def _(r):
            @pl.when(r > 0)
            def _():
                dw_copy(n, r - 1).wait()
            wst[n % 2] = dot(memT[pl.ds(pl.multiple_of(128 * r, 128), 128), :], src[:, 384 * (n % 2):384 * (n % 2) + 384]).astype(BF)
            dw_copy(n, r).start()
        dw_copy(n, 5).wait()
    acc[...] = dst[0].astype(F32)
    @pl.loop(1, 16)
    def _(j):
        d_copy(j).wait_recv()
        acc[...] += drc[j].astype(F32)
    for i in range(6):
        dq_ref[:, 128 * i:128 * i + 128] = 0.125 * acc[128 * i:128 * i + 128, :].T
    gm_copy(14).wait()
    gm_copy(15).wait()
    @pl.loop(1, 16)
    def _(j):
        st_copy(j).wait_send()
        d_copy(j).wait_send()
    plane.drain()

def cross_bwd(do, st, lens, q_h, k_h, v_h, kt_h, memory, A):
    V = pl.BlockSpec(memory_space=pltpu.VMEM)
    H = pl.BlockSpec(memory_space=pl.ANY)
    D = pltpu.SemaphoreType.DMA
    S = jax.ShapeDtypeStruct
    M = lambda *s: pltpu.VMEM(s, BF)
    return pl.pallas_call(
        cross_bwd_kernel,
        out_shape=(S((128, 768), F32), S((16, 192, 768), F32), S((4, 768, 384), BF)),
        in_specs=[V, V, V, H, H, H, H, H, H], out_specs=(V, H, H),
        scratch_shapes=[M(4, 4, 128, 768), M(4, 4, 128, 768), pltpu.VMEM((16, 32, 128), F32), M(768, 768), M(768, 768),
                        M(16, 192, 768), M(16, 192, 768), M(16, 768, 192), M(3072, 768), M(768, 3072), M(3072, 768), M(3072, 768),
                        pltpu.VMEM((2, 192, 768), F32), M(2, 128, 384), M(16, 768, 128), M(16, 768, 128), pltpu.VMEM((768, 128), F32),
                        D((5,)), D((4,)), D((2,)), D((2,)), D((2, 2, 4)), D((2, 2, 4)), D((16,)), D((16,)), D((16,)), D((16,))],
        compiler_params=pltpu.CompilerParams(collective_id=3, has_side_effects=True, vmem_limit_bytes=62 << 20),
        name="cross_backward",
    )(do, st, lens, q_h, k_h, v_h, kt_h, memory.reshape(3072, 768), A)


def body(
    dec_input,
    memory,
    mem_len,
    grad_out,
    attn_master,
    ffn_in_master,
    ffn_out_master,
    gain_master,
    attn_first,
    ffn_in_first,
    ffn_out_first,
    gain_first,
    attn_second,
    ffn_in_second,
    ffn_out_second,
    gain_second,
):
    sq = lax.axis_index("seq")
    gath_a, gath_b, gath_c, infos = gather(
        attn_master, ffn_in_master, ffn_out_master, info_tile(gain_master, mem_len)
    )
    aw = gath_a.reshape(16, 768, 384)
    iw = gath_b.reshape(16, 768, 256)
    out_w = gath_c.reshape(2048, 768)
    gains = infos[:, :3, :96].transpose(1, 0, 2).reshape(3, 768)
    own_info = lax.dynamic_slice_in_dim(infos, lax.axis_index("dp"), 1, 0)[0]
    lens = jnp.broadcast_to(own_info[3, :16].astype(jnp.int32)[:, None], (16, 128))
    rows, width = 128, 768

    def split_heads(block):
        return block.reshape(1, rows, H, HEAD)

    def times(left, k, n=1):
        return jnp.einsum("rd,sde->rse", left, aw[2 * k:2 * k + 2 * n], preferred_element_type=F32).reshape(rows, n * width)

    def times_back(inc, k, n=1):
        return jnp.einsum("rse,sde->rd", inc.reshape(rows, 2 * n, 384), aw[2 * k:2 * k + 2 * n], preferred_element_type=F32)

    def grad_blocks(left, inc, w=384):
        return jnp.einsum("rd,rse->sde", left, inc.reshape(rows, -1, w), preferred_element_type=F32).astype(BF)

    tok_rows = dec_input.astype(F32).reshape(rows, width)
    h_one, inv_one = norm_forward(tok_rows, gains[0])
    triple = times(h_one, 0, 3).astype(BF)
    q_one, k_one, v_one = (split_heads(triple[:, width * n:width * n + width]) for n in range(3))
    position = jnp.arange(rows)
    causal = (position[:, None] >= position[None, :])[None, None]
    mixed_one, lse_one = attend_forward(q_one, k_one, v_one, causal)
    flat_one = mixed_one.reshape(rows, width)
    after_one = tok_rows + times(flat_one, 3)
    h_two, inv_two = norm_forward(after_one, gains[1])
    q_two = times(h_two, 4).astype(BF) * jnp.asarray(score_scale, BF)
    q_all, k_two, v_two, kt_two, mixed_two, lse_two = cross_fwd(q_two, lens, memory, aw)
    flat_two = mixed_two.astype(BF)
    after_two = after_one + times(flat_two, 7)
    h_three, inv_three = norm_forward(after_two, gains[2])
    gate_up = jnp.einsum("rd,sdf->rsf", h_three, iw, preferred_element_type=F32).reshape(rows, 2, 2048)
    gate, up = gate_up[:, 0], gate_up[:, 1]
    middle = gated_gelu(gate, up).astype(BF)
    result = after_two + dense(middle, out_w)
    out_block = result.astype(BF).reshape(dec_input.shape)
    grad_low = grad_out.reshape(rows, width)
    grad_rows = grad_low.astype(F32)
    g_down = jnp.einsum("rf,rd->fd", middle, grad_low, preferred_element_type=F32).astype(BF)
    grad_mid = jnp.einsum("rd,fd->rf", grad_low, out_w, preferred_element_type=F32)
    _, pull = jax.vjp(gated_gelu, gate, up)
    grad_gate, grad_up = pull(grad_mid)
    grad_pair = jnp.concatenate([grad_gate, grad_up], axis=1).astype(BF)
    g_up = grad_blocks(h_three, grad_pair, 256)
    grad_h_three = jnp.einsum("rsf,sdf->rd", grad_pair.reshape(rows, 16, 256), iw, preferred_element_type=F32)
    norm_three, gain_three = norm_backward(after_two, inv_three, gains[2], grad_h_three)
    grad_two = grad_rows + norm_three
    cross_low = grad_two.astype(BF)
    g_cross_out = grad_blocks(flat_two, cross_low)
    do_two = times_back(cross_low, 7).astype(BF)
    delta = jnp.sum((do_two.astype(F32) * mixed_two).reshape(rows, H, HEAD), axis=-1).T
    stats = jnp.concatenate([lse_two, delta, jnp.zeros((4, 128), F32)], axis=0)
    dq_two, grad_memory, g_cross_kv = cross_bwd(do_two, stats, lens, q_all, k_two, v_two, kt_two, memory, aw)
    dq_flat = dq_two.astype(BF)
    g_cross_query = grad_blocks(h_two, dq_flat)
    norm_two, gain_two = norm_backward(after_one, inv_two, gains[1], times_back(dq_flat, 4))
    grad_one = grad_two + norm_two
    self_low = grad_one.astype(BF)
    g_self_out = grad_blocks(flat_one, self_low)
    grad_mixed_one = split_heads(times_back(self_low, 3).astype(BF))
    dq_one, dk_one, dv_one = attend_backward(q_one, k_one, v_one, causal, lse_one, grad_mixed_one)
    grad_triple = jnp.concatenate([part.reshape(rows, width) for part in (dq_one, dk_one, dv_one)], axis=1)
    g_self_qkv = grad_blocks(h_one, grad_triple)
    norm_one, gain_one = norm_backward(tok_rows, inv_one, gains[0], times_back(grad_triple, 0, 3))
    grad_input = (grad_one + norm_one).reshape(dec_input.shape)
    g_attn = jnp.concatenate([g_self_qkv, g_self_out, g_cross_query, g_cross_kv, g_cross_out], axis=0)
    g_gain = jnp.stack([gain_one, gain_two, gain_three])
    tile_g = jnp.pad(g_gain.reshape(3, 8, 96).transpose(1, 0, 2), ((0, 0), (0, 5), (0, 32)))
    share_a, share_b, share_c, share_g = scatter(
        g_attn.reshape(4, 4, 4, 2, 3, 32, 384),
        g_up.reshape(4, 4, 4, 2, 2, 48, 256),
        g_down.reshape(4, 2, 4, 4, 16, 768),
        tile_g,
    )
    share_g = lax.dynamic_slice_in_dim(share_g[:3], 6 * sq, 6, 1)
    shares = (share_a, share_b, share_c, share_g)
    attn_res = adam_update(attn_master, attn_first, attn_second, shares[0], rate_matrix)
    in_res = adam_update(ffn_in_master, ffn_in_first, ffn_in_second, shares[1], rate_matrix)
    out_res = adam_update(ffn_out_master, ffn_out_first, ffn_out_second, shares[2], rate_matrix)
    gain_res = adam_update(gain_master, gain_first, gain_second, shares[3], rate_gain)
    return (
        out_block,
        grad_input,
        grad_memory,
        attn_res[0],
        attn_res[1],
        attn_res[2],
        attn_res[3],
        in_res[0],
        in_res[1],
        in_res[2],
        in_res[3],
        out_res[0],
        out_res[1],
        out_res[2],
        out_res[3],
        gain_res[0],
        gain_res[1],
        gain_res[2],
        gain_res[3],
    )


def solution(mesh):
    placed = (
        P(("dp", "seq"), None, None),
        P("dp", "seq", None),
        P(("dp", "seq")),
        P(("dp", "seq"), None, None),
        P(None, ("dp", "seq"), None),
        P(None, ("dp", "seq"), None),
        P(("dp", "seq"), None),
        P(None, ("dp", "seq")),
        P(None, ("dp", "seq"), None),
        P(None, ("dp", "seq"), None),
        P(("dp", "seq"), None),
        P(None, ("dp", "seq")),
        P(None, ("dp", "seq"), None),
        P(None, ("dp", "seq"), None),
        P(("dp", "seq"), None),
        P(None, ("dp", "seq")),
    )
    return jax.shard_map(
        body,
        mesh=mesh,
        in_specs=placed,
        out_specs=(
            P(("dp", "seq"), None, None),
            P(("dp", "seq"), None, None),
            P("dp", "seq", None),
            P(None, ("dp", "seq"), None),
            P(None, ("dp", "seq"), None),
            P(None, ("dp", "seq"), None),
            P(None, ("dp", "seq"), None),
            P(None, ("dp", "seq"), None),
            P(None, ("dp", "seq"), None),
            P(None, ("dp", "seq"), None),
            P(None, ("dp", "seq"), None),
            P(("dp", "seq"), None),
            P(("dp", "seq"), None),
            P(("dp", "seq"), None),
            P(("dp", "seq"), None),
            P(None, ("dp", "seq")),
            P(None, ("dp", "seq")),
            P(None, ("dp", "seq")),
            P(None, ("dp", "seq")),
        ),
        check_vma=False,
    )
```

```python
import jax
import jax.numpy as jnp
from jax import lax
from jax.experimental import pallas as pl
from jax.experimental.pallas import tpu as pltpu
from jax.sharding import PartitionSpec as P

eps_norm = 1e-06
beta_one = 0.9
beta_two = 0.999
adam_eps = 1e-08
decay_rate = 0.01
rate_matrix = 0.12
rate_gain = 3.0
STEP = 10
MESH = pl.DeviceIdType.MESH
BF, F32 = jnp.bfloat16, jnp.float32
ALL = slice(None)
PARTS = (("A", 0, "xyz"), ("A", 1, "yzx"), ("A", 2, "zxy"), ("B", 0, "xyz"), ("B", 1, "yzx"), ("C", 0, "zxy"))

def where_am_i():
    dp, sq = lax.axis_index("dp"), lax.axis_index("seq")
    return {"x": sq // 4, "y": sq % 4, "z": dp // 2, "c": dp % 2}

def dev(at):
    return (at["z"] * 2 + at["c"], at["x"] * 4 + at["y"])

def moved(at, axis, step):
    return {**at, axis: (at[axis] + step + 4) % 4}

def gather_kernel(attn, wi, wo, info, A, B, C, gains, lens, infos, stage, recv, blk, blkA, blkB, blkC, irecv,
                  ss, rs, sib_s, sib_r, as_, ar_, is_, ir_, ds_, dr_, own_s):
    me = where_am_i()
    dp, sq = lax.axis_index("dp"), lax.axis_index("seq")
    bar = pltpu.get_barrier_semaphore()
    for i in range(1, 16):
        pl.semaphore_signal(bar, inc=1, device_id=(dp, (sq + i) % 16), device_id_type=MESH)
    for i in range(1, 8):
        pl.semaphore_signal(bar, inc=1, device_id=((dp + i) % 8, sq), device_id_type=MESH)
    stage[:, 6:8, :] = jnp.zeros((16, 2, 640), F32)
    for s in range(16):
        stage[s, 0:6, 0:384] = attn[:, s // 2, 384 * (s % 2):384 * (s % 2) + 384]
        stage[s, 0:6, 384:640] = wi[:, s // 8, 256 * (s % 8):256 * (s % 8) + 256]
    pl.semaphore_wait(bar, 22)
    def a2a(i):
        peer = (sq + i) % 16
        return pltpu.make_async_remote_copy(stage.at[peer], recv.at[sq], as_.at[i], ar_.at[i], device_id=(dp, peer), device_id_type=MESH)
    def inf(i):
        peer = (sq + i) % 16
        return pltpu.make_async_remote_copy(info, irecv.at[sq], is_.at[i], ir_.at[i], device_id=(dp, peer), device_id_type=MESH)
    for i in range(1, 16):
        a2a(i).start()
    for i in range(1, 16):
        inf(i).start()
    recv[sq] = stage[sq]
    irecv[sq] = info[...]
    blkC[...] = wo[...].astype(BF)
    for i in range(1, 16):
        a2a(i).wait_recv()
    for k in range(16):
        blk[6 * k:6 * k + 6, :] = recv[k, 0:6, :]
    for p in range(3):
        blkA[p] = blk[32 * p:32 * p + 32, 0:384].astype(BF)
    for p in range(2):
        blkB[p] = blk[48 * p:48 * p + 48, 384:640].astype(BF)

    def view(part, at):
        name, p, _ = part
        if name == "A":
            return A.at[at["x"], at["y"], at["z"], at["c"], p]
        if name == "B":
            return B.at[at["x"], at["y"], at["z"], at["c"], p]
        return C.at[at["z"], at["c"], at["x"], at["y"]]

    def mine(part):
        name, p, _ = part
        return blkA.at[p] if name == "A" else blkB.at[p] if name == "B" else blkC

    def group(part, t, step, half=None):
        order = part[2]
        at = moved(me, order[t], step)
        for j in range(t):
            at = {**at, order[j]: ALL}
        if half is not None and t:
            at = {**at, order[0]: pl.ds(2 * half, 2)}
        return at

    def send(n, t, kind):
        part = PARTS[n]
        axis = part[2][t]
        step = 1 if kind in (0, 2) else -1
        if kind < 2:
            dst = view(part, group(part, t, 0))
            src = mine(part) if t == 0 else dst
        else:
            dst = src = view(part, group(part, t, -step, kind - 2))
        return pltpu.make_async_remote_copy(src, dst, ss.at[n, t, kind], rs.at[n, t, kind], device_id=dev(moved(me, axis, step)), device_id_type=MESH)

    def arrival(n, t, kind):
        part = PARTS[n]
        axis = part[2][t]
        step = 1 if kind in (0, 2) else -1
        if kind < 2:
            dst = view(part, group(part, t, -step))
        else:
            dst = view(part, group(part, t, -2 * step, kind - 2))
        return pltpu.make_async_remote_copy(dst, dst, ss.at[n, t, kind], rs.at[n, t, kind], device_id=dev(moved(me, axis, step)), device_id_type=MESH)

    def kinds(n, t):
        return (0, 1, 2, 3) if t else (0, 1, 2 + n % 2)

    def sibling(n, j, c):
        part = PARTS[n]
        steps = (0, -1, 1, 2)
        at = {**group(part, 2, steps[j]), "c": c}
        v = view(part, at)
        return pltpu.make_async_remote_copy(v, v, sib_s.at[n, j], sib_r.at[n, j], device_id=dev({**me, "c": 1 - me["c"]}), device_id_type=MESH)

    owns = [pltpu.make_async_copy(mine(PARTS[n]), view(PARTS[n], me), own_s.at[n]) for n in range(6)]
    for o in owns:
        o.start()
    for t in range(3):
        for n in range(6):
            if t == 1:
                owns[n].wait()
            if t:
                for k in kinds(n, t - 1)[2:]:
                    arrival(n, t - 1, k).wait_recv()
            send(n, t, 0).start()
            send(n, t, 1).start()
            if t == 2:
                sibling(n, 0, me["c"]).start()
        for n in range(6):
            for k in (0, 1):
                arrival(n, t, k).wait_recv()
                if 2 + k in kinds(n, t):
                    send(n, t, 2 + k).start()
                if t == 2:
                    sibling(n, 1 + k, me["c"]).start()
    for i in range(1, 16):
        inf(i).wait_recv()
    tile = jnp.sum(irecv[...], axis=0)
    infos[dp] = tile
    def dpx(i):
        return pltpu.make_async_remote_copy(infos.at[dp], infos.at[dp], ds_.at[i], dr_.at[i], device_id=((dp + i) % 8, sq), device_id_type=MESH)
    def dpx_in(i):
        return pltpu.make_async_remote_copy(infos.at[(dp - i + 8) % 8], infos.at[(dp - i + 8) % 8], ds_.at[i], dr_.at[i], device_id=((dp + i) % 8, sq), device_id_type=MESH)
    for i in range(1, 8):
        dpx(i).start()
    for n in range(6):
        for k in (2, 3):
            arrival(n, 2, k).wait_recv()
        sibling(n, 3, me["c"]).start()
    for i in range(1, 8):
        dpx_in(i).wait_recv()
    lane = lax.broadcasted_iota(jnp.int32, (8, 128), 1)
    gains[...] = jnp.zeros((8, 768), F32)
    for d in range(8):
        lo, sh = 96 * d // 128, 96 * d % 128
        t = pltpu.roll(jnp.where(lane < 96, infos[d], 0.0), sh, 1)
        gains[:, 128 * lo:128 * lo + 128] += jnp.where(lane >= sh, t, 0.0)
        if sh > 32:
            gains[:, 128 * lo + 128:128 * lo + 256] += jnp.where(lane < sh, t, 0.0)
    pick = lax.broadcasted_iota(jnp.int32, (16, 128), 0) == lax.broadcasted_iota(jnp.int32, (16, 128), 1)
    lens[...] = jnp.broadcast_to(jnp.sum(jnp.where(pick, tile[3:4, :], 0.0), axis=1, keepdims=True), (16, 128))
    for n in range(6):
        for j in range(4):
            sibling(n, j, 1 - me["c"]).wait_recv()
    for i in range(1, 16):
        a2a(i).wait_send()
        inf(i).wait_send()
    for i in range(1, 8):
        dpx(i).wait_send()
    for n in range(6):
        for t in range(3):
            for k in kinds(n, t):
                send(n, t, k).wait_send()
        for j in range(4):
            sibling(n, j, me["c"]).wait_send()

def gather(attn, wi, wo, info):
    V = pl.BlockSpec(memory_space=pltpu.VMEM)
    H = pl.BlockSpec(memory_space=pltpu.HBM)
    D = pltpu.SemaphoreType.DMA
    return pl.pallas_call(
        gather_kernel,
        out_shape=(jax.ShapeDtypeStruct((4, 4, 4, 2, 3, 32, 384), BF),
                   jax.ShapeDtypeStruct((4, 4, 4, 2, 2, 48, 256), BF),
                   jax.ShapeDtypeStruct((4, 2, 4, 4, 16, 768), BF),
                   jax.ShapeDtypeStruct((8, 768), F32), jax.ShapeDtypeStruct((16, 128), F32)),
        in_specs=[V] * 4, out_specs=(H, H, H, V, V),
        scratch_shapes=[pltpu.VMEM((8, 8, 128), F32), pltpu.VMEM((16, 8, 640), F32), pltpu.VMEM((16, 8, 640), F32), pltpu.VMEM((96, 640), F32),
                        pltpu.VMEM((3, 32, 384), BF), pltpu.VMEM((2, 48, 256), BF), pltpu.VMEM((16, 768), BF),
                        pltpu.VMEM((16, 8, 128), F32),
                        D((6, 3, 4)), D((6, 3, 4)), D((6, 4)), D((6, 4)), D((16,)), D((16,)), D((16,)), D((16,)), D((8,)), D((8,)), D((6,))],
        compiler_params=pltpu.CompilerParams(collective_id=0, has_side_effects=True, vmem_limit_bytes=60 << 20),
        name="gather_weights",
    )(attn, wi, wo, info)

def info_tile(gain, mem_len):
    sq = lax.axis_index("seq")
    t = jnp.zeros((8, 128), F32)
    t = lax.dynamic_update_slice(t, gain.astype(BF).astype(F32), (0, 6 * sq))
    return lax.dynamic_update_slice(t, mem_len.astype(F32)[:, None], (3, sq))


def scatter_kernel(GA, GB, GC, gg, oA, oB, oC, oG, accA, accB, accC, sibA, sibB, sibC,
                   hA2, hB2, hC2, fA2, fB2, fC2, hA1, hB1, hC1, fA1, fB1, fC1, hA0, hB0, hC0, fA0, fB0, fC0,
                   blk, stage, recv, gdp, gsum, gsq,
                   ss, rs, sib_s, sib_r, loc_s, as_, ar_, is_, ir_, ds_, dr_):
    me = where_am_i()
    dp, sq = lax.axis_index("dp"), lax.axis_index("seq")
    acc = {"A": accA, "B": accB, "C": accC}
    sib = {"A": sibA, "B": sibB, "C": sibC}
    hop = {2: {"A": hA2, "B": hB2, "C": hC2}, 1: {"A": hA1, "B": hB1, "C": hC1}, 0: {"A": hA0, "B": hB0, "C": hC0}}
    fin = {2: {"A": fA2, "B": fB2, "C": fC2}, 1: {"A": fA1, "B": fB1, "C": fC1}, 0: {"A": fA0, "B": fB0, "C": fC0}}
    bar = pltpu.get_barrier_semaphore()
    for i in range(1, 16):
        pl.semaphore_signal(bar, inc=1, device_id=(dp, (sq + i) % 16), device_id_type=MESH)
    for i in range(1, 8):
        pl.semaphore_signal(bar, inc=1, device_id=((dp + i) % 8, sq), device_id_type=MESH)
    pl.semaphore_wait(bar, 22)

    def idx(part, at):
        name, p, _ = part
        if name == "C":
            return (at["z"], at["x"], at["y"])
        return (p, at["x"], at["y"], at["z"])

    def source(part, at, c):
        name, p, _ = part
        if name == "A":
            return GA.at[at["x"], at["y"], at["z"], c, p]
        if name == "B":
            return GB.at[at["x"], at["y"], at["z"], c, p]
        return GC.at[at["z"], c, at["x"], at["y"]]

    def names(part):
        return "zxy" if part[0] == "C" else "xyz"

    def group(part, t, step):
        order = part[2]
        at = moved(me, order[t], step)
        for j in range(t):
            at = {**at, order[j]: ALL}
        return at

    def halved(part, t, at, half):
        if t == 0:
            return at
        first = [a for a in names(part) if a in part[2][:t]][0]
        return {**at, first: pl.ds(2 * half, 2)}

    def done(part, t):
        return [a for a in names(part) if a in part[2][:t]]

    STEPS = (2, -1, 1, 0)
    other = dev({**me, "c": 1 - me["c"]})

    def sib_copy(n, j):
        part = PARTS[n]
        at = group(part, 2, STEPS[j])
        return pltpu.make_async_remote_copy(source(part, at, 1 - me["c"]), sib[part[0]].at[idx(part, at)], sib_s.at[n, j], sib_r.at[n, j], device_id=other, device_id_type=MESH)

    def loc_copy(n, j):
        part = PARTS[n]
        at = group(part, 2, STEPS[j])
        return pltpu.make_async_copy(source(part, at, me["c"]), acc[part[0]].at[idx(part, at)], loc_s.at[n, j])

    def slot(part):
        return () if part[0] == "C" else (part[1],)

    def kinds(n, t):
        return (0, 1) if t else (n % 2,)

    def hop_send(n, t, kind):
        part = PARTS[n]
        step = 1 if kind == 0 else -1
        at = halved(part, t, group(part, t, 2 * step), kind)
        return pltpu.make_async_remote_copy(acc[part[0]].at[idx(part, at)], hop[t][part[0]].at[slot(part) + (kind,)],
                                            ss.at[n, t, kind], rs.at[n, t, kind], device_id=dev(moved(me, part[2][t], step)), device_id_type=MESH)

    def fin_send(n, t, kind):
        part = PARTS[n]
        step = 1 if kind == 0 else -1
        at = group(part, t, step)
        return pltpu.make_async_remote_copy(acc[part[0]].at[idx(part, at)], fin[t][part[0]].at[slot(part) + (kind,)],
                                            ss.at[n, t, 2 + kind], rs.at[n, t, 2 + kind], device_id=dev(moved(me, part[2][t], step)), device_id_type=MESH)

    def each(part, t, at, fn, half=None):
        axes = done(part, t)
        sizes = [4] * len(axes)
        offs = [0] * len(axes)
        if half is not None and axes:
            sizes[0] = 2
            offs[0] = 2 * half
        total = 1
        for s in sizes:
            total *= s
        def one(i):
            pos = []
            rest = i
            for s in sizes[::-1]:
                pos.append(rest % s)
                rest = rest // s
            pos = pos[::-1]
            where = dict(at)
            for a, p, o in zip(axes, pos, offs):
                where[a] = p + o
            fn(idx(part, where), tuple(pos))
        if total == 1:
            one(0)
        else:
            pl.loop(0, total)(one)

    def merge_sibling(n, j):
        part = PARTS[n]
        sib_copy(n, j).wait_recv()
        loc_copy(n, j).wait()
        a, b = acc[part[0]], sib[part[0]]
        def fn(i, _):
            a[i] = (a[i].astype(F32) + b[i].astype(F32)).astype(BF)
        each(part, 2, group(part, 2, STEPS[j]), fn)

    for j in range(4):
        for n in range(6):
            sib_copy(n, j).start()
            loc_copy(n, j).start()
    def dpx(i):
        peer = (dp + i) % 8
        return pltpu.make_async_remote_copy(gg.at[peer], gdp.at[dp], ds_.at[i], dr_.at[i], device_id=(peer, sq), device_id_type=MESH)
    for i in range(1, 8):
        dpx(i).start()
    gdp[dp] = gg[dp]
    for t in (2, 1, 0):
        for n in range(6):
            if t == 2:
                merge_sibling(n, 0)
            else:
                finish(n, t + 1)
            for k in kinds(n, t):
                hop_send(n, t, k).start()
        if t == 2:
            for n in range(6):
                merge_sibling(n, 1)
                merge_sibling(n, 2)
        for n in range(6):
            part = PARTS[n]
            for k in (0, 1):
                if k in kinds(n, t):
                    hop_send(n, t, k).wait_recv()
                    a, b = acc[part[0]], hop[t][part[0]]
                    def fn(i, pos, a=a, b=b, part=part, k=k):
                        j = slot(part) + (k,) + pos
                        a[i] = (a[i].astype(F32) + b[j].astype(F32)).astype(BF)
                    each(part, t, group(part, t, 1 if k == 0 else -1), fn, k)
                fin_send(n, t, k).start()
        if t == 2:
            for n in range(6):
                merge_sibling(n, 3)

        def finish(n, t):
            part = PARTS[n]
            fin_send(n, t, 0).wait_recv()
            fin_send(n, t, 1).wait_recv()
            a, b = acc[part[0]], fin[t][part[0]]
            def fn(i, pos):
                s = slot(part)
                a[i] = (a[i].astype(F32) + b[s + (0,) + pos].astype(F32) + b[s + (1,) + pos].astype(F32)).astype(BF)
            each(part, t, group(part, t, 0), fn)

    for n in range(6):
        part = PARTS[n]
        fin_send(n, 0, 0).wait_recv()
        fin_send(n, 0, 1).wait_recv()
        a, b = acc[part[0]], fin[0][part[0]]
        s = slot(part)
        v = a[idx(part, me)].astype(F32) + b[s + (0,)].astype(F32) + b[s + (1,)].astype(F32)
        if part[0] == "A":
            blk[32 * part[1]:32 * part[1] + 32, 0:384] = v
        elif part[0] == "B":
            blk[48 * part[1]:48 * part[1] + 48, 384:640] = v
        else:
            oC[...] = v
    stage[:, 6:8, :] = jnp.zeros((16, 2, 640), F32)
    for k in range(16):
        stage[k, 0:6, :] = blk[6 * k:6 * k + 6, :]
    def a2a(i):
        peer = (sq + i) % 16
        return pltpu.make_async_remote_copy(stage.at[peer], recv.at[sq], as_.at[i], ar_.at[i], device_id=(dp, peer), device_id_type=MESH)
    for i in range(1, 16):
        a2a(i).start()
    recv[sq] = stage[sq]
    for i in range(1, 8):
        dpx(i).wait_recv()
    gsum[...] = jnp.sum(gdp[...], axis=0)
    def inf(i):
        peer = (sq + i) % 16
        return pltpu.make_async_remote_copy(gsum, gsq.at[sq], is_.at[i], ir_.at[i], device_id=(dp, peer), device_id_type=MESH)
    for i in range(1, 16):
        inf(i).start()
    gsq[sq] = gsum[...]
    for i in range(1, 16):
        a2a(i).wait_recv()
    for s in range(16):
        oA[:, s // 2, 384 * (s % 2):384 * (s % 2) + 384] = recv[s, 0:6, 0:384]
        oB[:, s // 8, 256 * (s % 8):256 * (s % 8) + 256] = recv[s, 0:6, 384:640]
    for i in range(1, 16):
        inf(i).wait_recv()
    oG[...] = pltpu.roll(jnp.sum(gsq[...], axis=0), (128 - 6 * sq) % 128, 1)
    for i in range(1, 8):
        dpx(i).wait_send()
    for i in range(1, 16):
        a2a(i).wait_send()
        inf(i).wait_send()
    for n in range(6):
        for j in range(4):
            sib_copy(n, j).wait_send()
        for t in range(3):
            for k in kinds(n, t):
                hop_send(n, t, k).wait_send()
            fin_send(n, t, 0).wait_send()
            fin_send(n, t, 1).wait_send()

def scatter(GA, GB, GC, gg):
    V = pl.BlockSpec(memory_space=pltpu.VMEM)
    H = pl.BlockSpec(memory_space=pltpu.HBM)
    D = pltpu.SemaphoreType.DMA
    bA, bB, bC = (32, 384), (48, 256), (16, 768)
    M = lambda *s: pltpu.VMEM(s, BF)
    trip = lambda pre: [M(3, *pre, *bA), M(2, *pre, *bB), M(*pre, *bC)]
    return pl.pallas_call(
        scatter_kernel,
        out_shape=(jax.ShapeDtypeStruct((6, 8, 768), F32), jax.ShapeDtypeStruct((6, 2, 2048), F32),
                   jax.ShapeDtypeStruct((16, 768), F32), jax.ShapeDtypeStruct((8, 128), F32)),
        in_specs=[H] * 3 + [V], out_specs=(V,) * 4,
        scratch_shapes=trip((4, 4, 4)) + trip((4, 4, 4)) + trip((2, 2, 4)) + trip((2, 4, 4)) + trip((2, 2)) + trip((2, 4)) + trip((2,)) + trip((2,))
        + [pltpu.VMEM((96, 640), F32), pltpu.VMEM((16, 8, 640), F32), pltpu.VMEM((16, 8, 640), F32),
           pltpu.VMEM((8, 8, 128), F32), pltpu.VMEM((8, 128), F32), pltpu.VMEM((16, 8, 128), F32),
           D((6, 3, 4)), D((6, 3, 4)), D((6, 4)), D((6, 4)), D((6, 4)), D((16,)), D((16,)), D((16,)), D((16,)), D((8,)), D((8,))],
        compiler_params=pltpu.CompilerParams(collective_id=1, has_side_effects=True, vmem_limit_bytes=60 << 20),
        name="scatter_grads",
    )(GA, GB, GC, gg)

NEG = -1e30
PLANE = ((0, "xy"), (1, "yx"))

class Plane:
    def __init__(self, me, view, ss, rs):
        self.me, self.view, self.ss, self.rs = me, view, ss, rs
    def group(self, n, t, step, half=None):
        order = PLANE[n][1]
        at = moved(self.me, order[t], step)
        if t:
            at = {**at, order[0]: ALL if half is None else pl.ds(2 * half, 2)}
        return at
    def copy(self, n, t, kind, back=0):
        axis = PLANE[n][1][t]
        step = 1 if kind in (0, 2) else -1
        at = self.group(n, t, back) if kind < 2 else self.group(n, t, back - step, kind - 2)
        v = self.view(n, at)
        return pltpu.make_async_remote_copy(v, v, self.ss.at[n, t, kind], self.rs.at[n, t, kind], device_id=dev(moved(self.me, axis, step)), device_id_type=MESH)
    def arrived(self, n, t, kind):
        step = 1 if kind in (0, 2) else -1
        self.copy(n, t, kind, -step).wait_recv()
    def kinds(self, n, t):
        return (0, 1, 2, 3) if t else (0, 1, 2 + n)
    def send(self, t):
        for n in range(2):
            if t:
                for k in self.kinds(n, t - 1)[2:]:
                    self.arrived(n, t - 1, k)
            self.copy(n, t, 0).start()
            self.copy(n, t, 1).start()
    def forward(self, t):
        for n in range(2):
            for k in (0, 1):
                self.arrived(n, t, k)
                if 2 + k in self.kinds(n, t):
                    self.copy(n, t, 2 + k).start()
    def finish(self):
        for n in range(2):
            for k in (2, 3):
                self.arrived(n, 1, k)
    def drain(self):
        for n in range(2):
            for t in range(2):
                for k in self.kinds(n, t):
                    self.copy(n, t, k).wait_send()

def meet(dp, sq):
    bar = pltpu.get_barrier_semaphore()
    for i in range(1, 16):
        pl.semaphore_signal(bar, inc=1, device_id=(dp, (sq + i) % 16), device_id_type=MESH)
    return bar

def offset(me, j, sign=1):
    return {**me, "x": (me["x"] + sign * (j // 4) + 4) % 4, "y": (me["y"] + sign * (j % 4) + 4) % 4}

def head_masks(value=1.0):
    lane = lax.broadcasted_iota(jnp.int32, (1, 256), 1)
    return [jnp.where(lane // 64 == h, value, 0.0).astype(BF) for h in range(4)]

def dot(a, b, ca=1, cb=0):
    return lax.dot_general(a, b, (((ca,), (cb,)), ((), ())), preferred_element_type=F32)

def cross_fwd_kernel(q, lens, mem_h, A, q_h, k_h, v_h, kt_h, o_ref, L_ref,
                     qall, mem, wk, wv, wkT, wvT, K, V, KT, VT, ost, lst, orc, lrc, acc,
                     mem_s, w_s, out_s, ss, rs, os_, or_, ls_, lr_):
    me = where_am_i()
    dp, sq = lax.axis_index("dp"), lax.axis_index("seq")
    bar = meet(dp, sq)
    def load_mem(e):
        return pltpu.make_async_copy(mem_h.at[e], mem.at[e], mem_s.at[e])
    loads = [pltpu.make_async_copy(A.at[10 + i], (wk if i < 2 else wv).at[:, pl.ds(384 * (i % 2), 384)], w_s.at[i]) for i in range(4)]
    for c in loads:
        c.start()
    @pl.loop(0, 16)
    def _(e):
        load_mem(e).start()
    qall[me["x"], me["y"]] = q[...]
    pl.semaphore_wait(bar, 15)
    plane = Plane(me, lambda n, at: qall.at[at["x"], at["y"], :, pl.ds(384 * n, 384)], ss, rs)
    plane.send(0)
    for c in loads:
        c.wait()
    for i in range(6):
        wkT[:, 128 * i:128 * i + 128] = wk[128 * i:128 * i + 128, :].T
        wvT[:, 128 * i:128 * i + 128] = wv[128 * i:128 * i + 128, :].T
    plane.forward(0)
    def project(a, b):
        @pl.loop(a, b)
        def _(e):
            load_mem(e).wait()
            m = mem[e]
            K[e] = dot(m, wk[...]).astype(BF)
            VT[e] = dot(wvT[...], m, 1, 1).astype(BF)
            V[e] = dot(m, wv[...]).astype(BF)
            KT[e] = dot(wkT[...], m, 1, 1).astype(BF)
    project(0, 4)
    plane.send(1)
    project(4, 12)
    plane.forward(1)
    project(12, 16)
    outs = [pltpu.make_async_copy(a, b, out_s.at[i]) for i, (a, b) in enumerate(((K, k_h), (V, v_h), (KT, kt_h), (qall, q_h)))]
    for c in outs[:3]:
        c.start()
    plane.finish()
    outs[3].start()
    masks = head_masks()
    pos = (192 * sq + lax.broadcasted_iota(jnp.int32, (192, 128), 0)).astype(F32)
    def o_copy(j):
        return pltpu.make_async_remote_copy(ost.at[j], orc.at[j], os_.at[j], or_.at[j], device_id=dev(offset(me, j)), device_id_type=MESH)
    def l_copy(j):
        return pltpu.make_async_remote_copy(lst.at[j], lrc.at[j], ls_.at[j], lr_.at[j], device_id=dev(offset(me, j)), device_id_type=MESH)
    @pl.loop(0, 16)
    def _(i):
        j = (i + 1) % 16
        at = offset(me, j)
        e = at["x"] * 4 + at["y"]
        live = pos < lens[pl.ds(e, 1), :]
        for g in range(3):
            q4 = qall[at["x"], at["y"], :, 256 * g:256 * g + 256]
            q4s = jnp.concatenate([q4 * m for m in masks], axis=0)
            sT = dot(K[e, :, 256 * g:256 * g + 256], q4s, 1, 1)
            ps, inv = [], []
            for h in range(4):
                s = jnp.where(live, sT[:, 128 * h:128 * h + 128], NEG)
                top = jnp.max(s, axis=0, keepdims=True)
                p = jnp.exp(s - top)
                tot = jnp.sum(p, axis=0, keepdims=True)
                lst[j, 4 * g + h:4 * g + h + 1, :] = top + jnp.log(tot)
                ps.append(p.astype(BF))
                inv.append(1.0 / tot)
            oT = dot(VT[e, 256 * g:256 * g + 256, :], jnp.concatenate(ps, axis=1))
            for h in range(4):
                ost[j, 256 * g + 64 * h:256 * g + 64 * h + 64, :] = (oT[64 * h:64 * h + 64, 128 * h:128 * h + 128] * inv[h]).astype(BF)
        @pl.when(j > 0)
        def _():
            l_copy(j).start()
            o_copy(j).start()
    lrc[0] = lst[0]
    orc[0] = ost[0]
    @pl.loop(1, 16)
    def _(j):
        l_copy(j).wait_recv()
    l = lrc[:, 0:12, :]
    top = jnp.max(l, axis=0)
    total = top + jnp.log(jnp.sum(jnp.exp(l - top[None]), axis=0))
    L_ref[0:12, :] = total
    L_ref[12:16, :] = jnp.zeros((4, 128), F32)
    acc[...] = jnp.zeros_like(acc)
    @pl.loop(0, 16)
    def _(j):
        @pl.when(j > 0)
        def _():
            o_copy(j).wait_recv()
        w = jnp.exp(lrc[j, 0:12, :] - L_ref[0:12, :])
        for h in range(12):
            acc[64 * h:64 * h + 64, :] += orc[j, 64 * h:64 * h + 64, :].astype(F32) * w[h:h + 1, :]
    for i in range(6):
        o_ref[:, 128 * i:128 * i + 128] = acc[128 * i:128 * i + 128, :].T
    @pl.loop(1, 16)
    def _(j):
        l_copy(j).wait_send()
        o_copy(j).wait_send()
    plane.drain()
    for c in outs:
        c.wait()

def cross_fwd(q, lens, memory, A):
    V = pl.BlockSpec(memory_space=pltpu.VMEM)
    H = pl.BlockSpec(memory_space=pltpu.HBM)
    D = pltpu.SemaphoreType.DMA
    S = jax.ShapeDtypeStruct
    M = lambda *s: pltpu.VMEM(s, BF)
    return pl.pallas_call(
        cross_fwd_kernel,
        out_shape=(S((4, 4, 128, 768), BF), S((16, 192, 768), BF), S((16, 192, 768), BF), S((16, 768, 192), BF), S((128, 768), F32), S((16, 128), F32)),
        in_specs=[V, V, H, H], out_specs=(H, H, H, H, V, V),
        scratch_shapes=[M(4, 4, 128, 768), M(16, 192, 768), M(768, 768), M(768, 768), M(768, 768), M(768, 768),
                        M(16, 192, 768), M(16, 192, 768), M(16, 768, 192), M(16, 768, 192), M(16, 768, 128), pltpu.VMEM((16, 16, 128), F32),
                        M(16, 768, 128), pltpu.VMEM((16, 16, 128), F32), pltpu.VMEM((768, 128), F32),
                        D((16,)), D((4,)), D((4,)), D((2, 2, 4)), D((2, 2, 4)), D((16,)), D((16,)), D((16,)), D((16,))],
        compiler_params=pltpu.CompilerParams(collective_id=2, has_side_effects=True, vmem_limit_bytes=60 << 20),
        name="cross_forward",
    )(q, lens, memory, A)

def cross_bwd_kernel(do, st, lens, q_h, k_h, v_h, kt_h, mem_h, A, G_in, dq_ref, gm_h, dw_h,
                     qall, doall, stall, wk, wv, K, V, KT, mem, memT, dK, dV, gst, wst, dst, drc, acc,
                     ld_s, w_s, gm_s, dw_s, ss, rs, sss, srs, ds_, dr_):
    me = where_am_i()
    dp, sq = lax.axis_index("dp"), lax.axis_index("seq")
    bar = meet(dp, sq)
    lds = [pltpu.make_async_copy(a, b, ld_s.at[i]) for i, (a, b) in enumerate(((mem_h, mem), (q_h, qall), (k_h, K), (v_h, V), (kt_h, KT)))]
    lds += [pltpu.make_async_copy(A.at[10 + i], (wk if i < 2 else wv).at[:, pl.ds(384 * (i % 2), 384)], w_s.at[i]) for i in range(4)]
    for c in lds:
        c.start()
    doall[me["x"], me["y"]] = do[...]
    stall[0] = st[...]
    pl.semaphore_wait(bar, 15)
    plane = Plane(me, lambda n, at: doall.at[at["x"], at["y"], :, pl.ds(384 * n, 384)], ss, rs)
    plane.send(0)
    def st_copy(j):
        return pltpu.make_async_remote_copy(st, stall.at[j], sss.at[j], srs.at[j], device_id=dev(offset(me, j, -1)), device_id_type=MESH)
    @pl.loop(1, 16)
    def _(j):
        st_copy(j).start()
    lds[0].wait()
    def turn(a, b):
        @pl.loop(a, b)
        def _(e):
            memT[:, pl.ds(pl.multiple_of(256 * e, 256), 256)] = mem[pl.ds(pl.multiple_of(256 * e, 256), 256), :].T
    turn(0, 2)
    plane.forward(0)
    turn(2, 5)
    plane.send(1)
    turn(5, 9)
    plane.forward(1)
    turn(9, 12)
    for c in lds[1:]:
        c.wait()
    @pl.loop(1, 16)
    def _(j):
        st_copy(j).wait_recv()
    plane.finish()
    masks = head_masks()
    pos = (192 * sq + lax.broadcasted_iota(jnp.int32, (192, 128), 0)).astype(F32)
    def d_copy(j):
        return pltpu.make_async_remote_copy(dst.at[j], drc.at[j], ds_.at[j], dr_.at[j], device_id=dev(offset(me, j)), device_id_type=MESH)
    @pl.loop(0, 16)
    def _(i):
        j = (i + 1) % 16
        at = offset(me, j)
        e = at["x"] * 4 + at["y"]
        live = pos < lens[pl.ds(e, 1), :]
        rows = pl.ds(pl.multiple_of(192 * e, 192), 192)
        for g in range(3):
            cols = slice(256 * g, 256 * g + 256)
            q4 = qall[at["x"], at["y"], :, cols]
            d4 = doall[at["x"], at["y"], :, cols]
            q4s = jnp.concatenate([q4 * m for m in masks], axis=0)
            d4s = jnp.concatenate([d4 * m for m in masks], axis=0)
            sT = dot(K[e, :, cols], q4s, 1, 1)
            gT = dot(V[e, :, cols], d4s, 1, 1)
            ps, gs = [], []
            for h in range(4):
                n = 4 * g + h
                s = jnp.where(live, sT[:, 128 * h:128 * h + 128], NEG)
                p = jnp.exp(s - stall[j, n:n + 1, :])
                ps.append(p.astype(BF))
                gs.append((p * (gT[:, 128 * h:128 * h + 128] - stall[j, 16 + n:17 + n, :])).astype(BF))
            pT = jnp.concatenate(ps, axis=1)
            sg = jnp.concatenate(gs, axis=1)
            dV[rows, cols] = dot(pT, d4s).astype(BF)
            dK[rows, cols] = dot(sg, q4s).astype(BF)
            qT = dot(KT[e, cols, :], sg)
            for h in range(4):
                dst[j, 256 * g + 64 * h:256 * g + 64 * h + 64, :] = qT[64 * h:64 * h + 64, 128 * h:128 * h + 128].astype(BF)
        @pl.when(j > 0)
        def _():
            d_copy(j).start()
    def gm_copy(e):
        return pltpu.make_async_copy(gst.at[e % 2], gm_h.at[e], gm_s.at[e % 2])
    @pl.loop(0, 16)
    def _(e):
        @pl.when(e > 1)
        def _():
            gm_copy(e - 2).wait()
        rows = pl.ds(pl.multiple_of(192 * e, 192), 192)
        gst[e % 2] = dot(dK[rows, :], wk[...], 1, 1) + dot(dV[rows, :], wv[...], 1, 1)
        gm_copy(e).start()
    def dw_copy(n, r):
        return pltpu.make_async_copy(wst.at[n % 2], dw_h.at[10 + n, pl.ds(pl.multiple_of(128 * r, 128), 128)], dw_s.at[n % 2])
    for n in range(4):
        src = dK if n < 2 else dV
        @pl.loop(0, 6)
        def _(r):
            @pl.when(r > 0)
            def _():
                dw_copy(n, r - 1).wait()
            wst[n % 2] = dot(memT[pl.ds(pl.multiple_of(128 * r, 128), 128), :], src[:, 384 * (n % 2):384 * (n % 2) + 384]).astype(BF)
            dw_copy(n, r).start()
        dw_copy(n, 5).wait()
    acc[...] = dst[0].astype(F32)
    @pl.loop(1, 16)
    def _(j):
        d_copy(j).wait_recv()
        acc[...] += drc[j].astype(F32)
    for i in range(6):
        dq_ref[:, 128 * i:128 * i + 128] = 0.125 * acc[128 * i:128 * i + 128, :].T
    gm_copy(14).wait()
    gm_copy(15).wait()
    @pl.loop(1, 16)
    def _(j):
        st_copy(j).wait_send()
        d_copy(j).wait_send()
    plane.drain()

def cross_bwd(do, st, lens, q_h, k_h, v_h, kt_h, memory, A, GA):
    V = pl.BlockSpec(memory_space=pltpu.VMEM)
    H = pl.BlockSpec(memory_space=pltpu.HBM)
    D = pltpu.SemaphoreType.DMA
    S = jax.ShapeDtypeStruct
    M = lambda *s: pltpu.VMEM(s, BF)
    return pl.pallas_call(
        cross_bwd_kernel,
        out_shape=(S((128, 768), F32), S((16, 192, 768), F32), S((16, 768, 384), BF)),
        in_specs=[V, V, V, H, H, H, H, H, H, H], out_specs=(V, H, H), input_output_aliases={9: 2},
        scratch_shapes=[M(4, 4, 128, 768), M(4, 4, 128, 768), pltpu.VMEM((16, 32, 128), F32), M(768, 768), M(768, 768),
                        M(16, 192, 768), M(16, 192, 768), M(16, 768, 192), M(3072, 768), M(768, 3072), M(3072, 768), M(3072, 768),
                        pltpu.VMEM((2, 192, 768), F32), M(2, 128, 384), M(16, 768, 128), M(16, 768, 128), pltpu.VMEM((768, 128), F32),
                        D((5,)), D((4,)), D((2,)), D((2,)), D((2, 2, 4)), D((2, 2, 4)), D((16,)), D((16,)), D((16,)), D((16,))],
        compiler_params=pltpu.CompilerParams(collective_id=3, has_side_effects=True, vmem_limit_bytes=60 << 20),
        name="cross_backward",
    )(do, st, lens, q_h, k_h, v_h, kt_h, memory.reshape(3072, 768), A, GA)


def adam_update(master, first, second, grad, rate):
    first_new = beta_one * first + (1.0 - beta_one) * grad
    second_new = beta_two * second + (1.0 - beta_two) * grad * grad
    fix_one = 1.0 - beta_one**STEP
    fix_two = 1.0 - beta_two**STEP
    master_new = master - rate * (
        first_new / fix_one / (jnp.sqrt(second_new / fix_two) + adam_eps) + decay_rate * master
    )
    return (master_new, first_new, second_new, master_new.astype(jnp.bfloat16))


def rms(x):
    return lax.rsqrt(jnp.mean(x * x, axis=-1, keepdims=True) + eps_norm)

def rms_back(x, inv, gain, u):
    scaled = u * gain
    inner = jnp.mean(scaled * x, axis=-1, keepdims=True)
    return inv * scaled - x * inv * inv * inv * inner, jnp.sum(u * x * inv, axis=0, keepdims=True)

def flip(x):
    return jnp.concatenate([x[:, 128 * i:128 * i + 128].T for i in range(x.shape[1] // 128)], axis=0)

def unflip(x):
    return jnp.concatenate([x[128 * i:128 * i + 128, :].T for i in range(x.shape[0] // 128)], axis=1)

def apply_w(h, W, k):
    return jnp.concatenate([dot(h, W[2 * k]), dot(h, W[2 * k + 1])], axis=1)

def apply_wt(u, W, k):
    return dot(u[:, 0:384], W[2 * k], 1, 1) + dot(u[:, 384:768], W[2 * k + 1], 1, 1)

def causal_mask():
    return lax.broadcasted_iota(jnp.int32, (128, 128), 0) <= lax.broadcasted_iota(jnp.int32, (128, 128), 1)

def self_fwd_kernel(x_ref, gains, A, q2, h1, qkv, o1, x1, h2, L1, W, sem):
    loads = [pltpu.make_async_copy(A.at[i], W.at[i], sem.at[i]) for i in range(10)]
    for c in loads:
        c.start()
    x = x_ref[...].astype(F32)
    h = (x * rms(x) * gains[0:1, :]).astype(BF)
    h1[...] = h
    for k in range(3):
        loads[2 * k].wait()
        loads[2 * k + 1].wait()
        full = apply_w(h, W, k)
        qkv[k] = full.astype(BF)
    vT = flip(full).astype(BF)
    masks = head_masks(0.125)
    live = causal_mask()
    outs = []
    for g in range(3):
        cols = slice(256 * g, 256 * g + 256)
        q4 = qkv[0, :, cols]
        sT = dot(qkv[1, :, cols], jnp.concatenate([q4 * m for m in masks], axis=0), 1, 1)
        ps = []
        for n in range(4):
            s = jnp.where(live, sT[:, 128 * n:128 * n + 128], NEG)
            top = jnp.max(s, axis=0, keepdims=True)
            lse = top + jnp.log(jnp.sum(jnp.exp(s - top), axis=0, keepdims=True))
            L1[4 * g + n:4 * g + n + 1, :] = lse
            ps.append(jnp.exp(s - lse).astype(BF))
        oT = dot(vT[256 * g:256 * g + 256, :], jnp.concatenate(ps, axis=1))
        outs += [oT[64 * n:64 * n + 64, 128 * n:128 * n + 128] for n in range(4)]
    o = unflip(jnp.concatenate(outs, axis=0)).astype(BF)
    o1[...] = o
    for c in loads[6:]:
        c.wait()
    x = x + apply_w(o, W, 3)
    x1[...] = x
    h = (x * rms(x) * gains[1:2, :]).astype(BF)
    h2[...] = h
    q2[...] = apply_w(h, W, 4).astype(BF) * jnp.asarray(0.125, BF)

VS = pl.BlockSpec(memory_space=pltpu.VMEM)
HS = pl.BlockSpec(memory_space=pltpu.HBM)
SDS = jax.ShapeDtypeStruct

def self_fwd(x, gains, A):
    row = SDS((128, 768), BF)
    return pl.pallas_call(
        self_fwd_kernel,
        out_shape=(row, row, SDS((3, 128, 768), BF), row, SDS((128, 768), F32), row, SDS((16, 128), F32)),
        in_specs=[VS, VS, HS], out_specs=(VS,) * 7,
        scratch_shapes=[pltpu.VMEM((10, 768, 384), BF), pltpu.SemaphoreType.DMA((10,))],
        compiler_params=pltpu.CompilerParams(vmem_limit_bytes=60 << 20),
        name="self_forward",
    )(x, gains, A)

def ffn_kernel(x1, o2, L2, dy_ref, gains, A, B, C, out, do2, st, dx2, gg, GA, GB, GC,
               W7, WB, WC, gA, gB, gC, sw, sb, sc, tb, tc, ta):
    lA = [pltpu.make_async_copy(A.at[14 + i], W7.at[i], sw.at[i]) for i in range(2)]
    lB = [pltpu.make_async_copy(B.at[i], WB.at[i], sb.at[i]) for i in range(16)]
    lC = [pltpu.make_async_copy(C.at[i], WC.at[i], sc.at[i]) for i in range(8)]
    for c in lA:
        c.start()
    for j in range(8):
        lB[j].start()
        lB[8 + j].start()
        lC[j].start()
    o = o2[...]
    ob = o.astype(BF)
    for c in lA:
        c.wait()
    x = x1[...] + apply_w(ob, W7, 0)
    inv = rms(x)
    h = (x * inv * gains[2:3, :]).astype(BF)
    hT = flip(h.astype(F32)).astype(BF)
    df = dy_ref[...]
    y = jnp.zeros((128, 768), F32)
    dh = jnp.zeros((128, 768), F32)
    c0 = 0.7978845608028654
    sB, sC = [], []
    for j in range(8):
        lB[j].wait()
        lB[8 + j].wait()
        lC[j].wait()
        a = dot(h, WB[j])
        up = dot(h, WB[8 + j])
        t = jnp.tanh(c0 * (a + 0.044715 * a * a * a))
        half = 0.5 * (1.0 + t)
        gel = a * half
        der = half + 0.5 * a * (1.0 - t * t) * (c0 * (1.0 + 0.134145 * a * a))
        mid32 = gel * up
        mid = mid32.astype(BF)
        y += dot(mid, WC[j])
        dm = dot(df, WC[j], 1, 1)
        dga = (dm * up * der).astype(BF)
        dup = (dm * gel).astype(BF)
        dh += dot(dga, WB[j], 1, 1) + dot(dup, WB[8 + j], 1, 1)
        gB[j] = dot(hT, dga).astype(BF)
        gB[8 + j] = dot(hT, dup).astype(BF)
        gC[j] = dot(flip(mid32).astype(BF), df).astype(BF)
        sB += [pltpu.make_async_copy(gB.at[j], GB.at[j], tb.at[j]), pltpu.make_async_copy(gB.at[8 + j], GB.at[8 + j], tb.at[8 + j])]
        sC += [pltpu.make_async_copy(gC.at[j], GC.at[j], tc.at[j])]
        for c in sB[-2:] + sC[-1:]:
            c.start()
    out[...] = (x + y).astype(BF)
    dz, gain = rms_back(x, inv, gains[2:3, :], dh)
    gg[...] = gain
    d = df.astype(F32) + dz
    dx2[...] = d
    dc = d.astype(BF)
    dof = apply_wt(dc, W7, 0).astype(BF)
    do2[...] = dof
    prod = flip(dof.astype(F32) * o)
    st[...] = jnp.zeros((32, 128), F32)
    st[0:12, :] = L2[0:12, :]
    for n in range(12):
        st[16 + n:17 + n, :] = jnp.sum(prod[64 * n:64 * n + 64, :], axis=0, keepdims=True)
    oT = flip(o).astype(BF)
    sA = []
    for i in range(2):
        gA[i] = dot(oT, dc[:, 384 * i:384 * i + 384]).astype(BF)
        sA.append(pltpu.make_async_copy(gA.at[i], GA.at[14 + i], ta.at[i]))
        sA[-1].start()
    for c in sA + sB + sC:
        c.wait()

def ffn(x1, o2, L2, dy, gains, A, B, C):
    M = lambda *s: pltpu.VMEM(s, BF)
    D = pltpu.SemaphoreType.DMA
    return pl.pallas_call(
        ffn_kernel,
        out_shape=(SDS((128, 768), BF), SDS((128, 768), BF), SDS((32, 128), F32), SDS((128, 768), F32), SDS((1, 768), F32),
                   SDS((16, 768, 384), BF), SDS((16, 768, 256), BF), SDS((8, 256, 768), BF)),
        in_specs=[VS] * 5 + [HS] * 3, out_specs=(VS,) * 5 + (HS,) * 3,
        scratch_shapes=[M(2, 768, 384), M(16, 768, 256), M(8, 256, 768), M(2, 768, 384), M(16, 768, 256), M(8, 256, 768),
                        D((2,)), D((16,)), D((8,)), D((16,)), D((8,)), D((2,))],
        compiler_params=pltpu.CompilerParams(vmem_limit_bytes=60 << 20),
        name="feed_forward",
    )(x1, o2, L2, dy, gains, A, B, C)

def self_bwd_kernel(dq2, h2, x1, dx2, qkv, o1, L1, x_ref, h1, gains, g3, A, GA_in, gm_in, gin, tile, GA, gm,
                    W, G, gb, gmv, sem, gsem, msem):
    loads = [pltpu.make_async_copy(A.at[i], W.at[i], sem.at[i]) for i in range(10)]
    for i in (8, 9, 6, 7, 0, 1, 2, 3, 4, 5):
        loads[i].start()
    def gm_load(e):
        return pltpu.make_async_copy(gm_in.at[e], gmv.at[e], msem.at[e])
    def gm_store(e):
        return pltpu.make_async_copy(gmv.at[e], gm.at[e], msem.at[16 + e])
    for e in range(16):
        gm_load(e).start()
    stores = []
    def weight_grad(k, left, inc):
        for i in range(2):
            n = 2 * k + i
            G[n] = dot(left, inc[:, 384 * i:384 * i + 384]).astype(BF)
            stores.append(pltpu.make_async_copy(G.at[n], GA.at[n], gsem.at[n]))
            stores[-1].start()
    dqb = dq2[...].astype(BF)
    for i in (8, 9, 6, 7):
        loads[i].wait()
    u = apply_wt(dqb, W, 4)
    x = x1[...]
    inv = rms(x)
    dz, gain = rms_back(x, inv, gains[1:2, :], u)
    gb[...] = jnp.zeros((8, 768), F32)
    gb[1:2, :] = gain
    gb[2:3, :] = g3[...]
    d1 = dx2[...] + dz
    da = d1.astype(BF)
    do1 = apply_wt(da, W, 3).astype(BF)
    weight_grad(4, flip(h2[...].astype(F32)).astype(BF), dqb)
    masks = head_masks(0.125)
    ones = head_masks(1.0)
    live = causal_mask()
    kT = flip(qkv[1].astype(F32)).astype(BF)
    qs, ks, vs = [], [], []
    for g in range(3):
        cols = slice(256 * g, 256 * g + 256)
        q4 = qkv[0, :, cols]
        d4 = do1[:, cols]
        q4s = jnp.concatenate([q4 * m for m in masks], axis=0)
        d4s = jnp.concatenate([d4 * m for m in ones], axis=0)
        sT = dot(qkv[1, :, cols], q4s, 1, 1)
        gT = dot(qkv[2, :, cols], d4s, 1, 1)
        ps, gs = [], []
        for n in range(4):
            s = jnp.where(live, sT[:, 128 * n:128 * n + 128], NEG)
            p = jnp.exp(s - L1[4 * g + n:4 * g + n + 1, :])
            gt = gT[:, 128 * n:128 * n + 128]
            ps.append(p.astype(BF))
            gs.append((p * (gt - jnp.sum(p * gt, axis=0, keepdims=True))).astype(BF))
        sg = jnp.concatenate(gs, axis=1)
        vs.append(dot(jnp.concatenate(ps, axis=1), d4s).astype(BF))
        ks.append(dot(sg, q4s).astype(BF))
        qT = dot(kT[256 * g:256 * g + 256, :], sg)
        qs += [qT[64 * n:64 * n + 64, 128 * n:128 * n + 128] for n in range(4)]
    for e in range(16):
        gm_load(e).wait()
        gm_store(e).start()
    inc = [(0.125 * unflip(jnp.concatenate(qs, axis=0))).astype(BF), jnp.concatenate(ks, axis=1), jnp.concatenate(vs, axis=1)]
    weight_grad(3, flip(o1[...].astype(F32)).astype(BF), da)
    for c in loads[:6]:
        c.wait()
    u = apply_wt(inc[0], W, 0) + apply_wt(inc[1], W, 1) + apply_wt(inc[2], W, 2)
    x = x_ref[...].astype(F32)
    inv = rms(x)
    dz, gain = rms_back(x, inv, gains[0:1, :], u)
    gb[0:1, :] = gain
    gin[...] = d1 + dz
    hT = flip(h1[...].astype(F32)).astype(BF)
    for k in range(3):
        weight_grad(k, hT, inc[k])
    lane = lax.broadcasted_iota(jnp.int32, (8, 128), 1)
    for d in range(8):
        lo, sh = 96 * d // 128, 96 * d % 128
        t = pltpu.roll(gb[:, 128 * lo:128 * lo + 128], (128 - sh) % 128, 1)
        if sh > 32:
            nxt = pltpu.roll(gb[:, 128 * lo + 128:128 * lo + 256], (128 - sh) % 128, 1)
            t = jnp.where(lane < 128 - sh, t, nxt)
        tile[d] = jnp.where(lane < 96, t, 0.0)
    for c in stores:
        c.wait()
    for e in range(16):
        gm_store(e).wait()

def self_bwd(dq2, h2, x1, dx2, qkv, o1, L1, x, h1, gains, g3, A, GA, gm):
    D = pltpu.SemaphoreType.DMA
    return pl.pallas_call(
        self_bwd_kernel,
        out_shape=(SDS((128, 768), F32), SDS((8, 8, 128), F32), SDS((16, 768, 384), BF), SDS((16, 192, 768), F32)),
        in_specs=[VS] * 11 + [HS] * 3, out_specs=(VS, VS, HS, HS),
        input_output_aliases={12: 2},
        scratch_shapes=[pltpu.VMEM((10, 768, 384), BF), pltpu.VMEM((10, 768, 384), BF), pltpu.VMEM((8, 768), F32), pltpu.VMEM((16, 192, 768), F32), D((10,)), D((10,)), D((32,))],
        compiler_params=pltpu.CompilerParams(vmem_limit_bytes=60 << 20),
        name="self_backward",
    )(dq2, h2, x1, dx2, qkv, o1, L1, x, h1, gains, g3, A, GA, gm)

def adam_kernel(*refs):
    ins, outs = refs[:16], refs[16:]
    for n in range(4):
        w, m, v, g = ins[4 * n:4 * n + 4]
        grad = g[0:3, 0:6] if n == 3 else g[...]
        for o, val in zip(outs[4 * n:4 * n + 4], adam_update(w[...], m[...], v[...], grad, rate_gain if n == 3 else rate_matrix)):
            o[...] = val

def adam(*args):
    shapes = []
    for n in range(4):
        s = args[4 * n].shape
        shapes += [SDS(s, F32)] * 3 + [SDS(s, BF)]
    return pl.pallas_call(adam_kernel, out_shape=tuple(shapes), in_specs=[VS] * 16, out_specs=(VS,) * 16,
                          compiler_params=pltpu.CompilerParams(vmem_limit_bytes=60 << 20), name="adam")(*args)


def body(
    dec_input,
    memory,
    mem_len,
    grad_out,
    attn_master,
    ffn_in_master,
    ffn_out_master,
    gain_master,
    attn_first,
    ffn_in_first,
    ffn_out_first,
    gain_first,
    attn_second,
    ffn_in_second,
    ffn_out_second,
    gain_second,
):
    swap = lambda a: a.transpose(1, 0, 2)
    attn_t, in_t = swap(attn_master), swap(ffn_in_master)
    gath_a, gath_b, gath_c, gains, lens = gather(attn_t, in_t, ffn_out_master, info_tile(gain_master, mem_len))
    aw = gath_a.reshape(16, 768, 384)
    x = dec_input[0]
    q2, h1, qkv, o1, x1, h2, L1 = self_fwd(x, gains, aw)
    q_all, k_two, v_two, kt_two, o2, L2 = cross_fwd(q2, lens, memory, aw)
    out_block, do2, st, dx2, g3, GA, GB, GC = ffn(x1, o2, L2, grad_out[0], gains, aw, gath_b.reshape(16, 768, 256), gath_c.reshape(8, 256, 768))
    dq2, gm, GA = cross_bwd(do2, st, lens, q_all, k_two, v_two, kt_two, memory, aw, GA)
    grad_input, tile_g, GA, grad_memory = self_bwd(dq2, h2, x1, dx2, qkv, o1, L1, x, h1, gains, g3, aw, GA, gm)
    share_a, share_b, share_c, share_g = scatter(
        GA.reshape(4, 4, 4, 2, 3, 32, 384), GB.reshape(4, 4, 4, 2, 2, 48, 256), GC.reshape(4, 2, 4, 4, 16, 768), tile_g
    )
    new = adam(
        attn_t, swap(attn_first), swap(attn_second), share_a,
        in_t, swap(ffn_in_first), swap(ffn_in_second), share_b,
        ffn_out_master, ffn_out_first, ffn_out_second, share_c,
        gain_master, gain_first, gain_second, share_g,
    )
    return (out_block[None], grad_input[None], grad_memory, *[swap(a) for a in new[:8]], *new[8:])


def solution(mesh):
    placed = (
        P(("dp", "seq"), None, None),
        P("dp", "seq", None),
        P(("dp", "seq")),
        P(("dp", "seq"), None, None),
        P(None, ("dp", "seq"), None),
        P(None, ("dp", "seq"), None),
        P(("dp", "seq"), None),
        P(None, ("dp", "seq")),
        P(None, ("dp", "seq"), None),
        P(None, ("dp", "seq"), None),
        P(("dp", "seq"), None),
        P(None, ("dp", "seq")),
        P(None, ("dp", "seq"), None),
        P(None, ("dp", "seq"), None),
        P(("dp", "seq"), None),
        P(None, ("dp", "seq")),
    )
    return jax.shard_map(
        body,
        mesh=mesh,
        in_specs=placed,
        out_specs=(
            P(("dp", "seq"), None, None),
            P(("dp", "seq"), None, None),
            P("dp", "seq", None),
            P(None, ("dp", "seq"), None),
            P(None, ("dp", "seq"), None),
            P(None, ("dp", "seq"), None),
            P(None, ("dp", "seq"), None),
            P(None, ("dp", "seq"), None),
            P(None, ("dp", "seq"), None),
            P(None, ("dp", "seq"), None),
            P(None, ("dp", "seq"), None),
            P(("dp", "seq"), None),
            P(("dp", "seq"), None),
            P(("dp", "seq"), None),
            P(("dp", "seq"), None),
            P(None, ("dp", "seq")),
            P(None, ("dp", "seq")),
            P(None, ("dp", "seq")),
            P(None, ("dp", "seq")),
        ),
        check_vma=False,
    )
```

```python
import jax
import jax.numpy as jnp
from jax import lax
from jax.experimental import pallas as pl
from jax.experimental.pallas import tpu as pltpu
from jax.sharding import PartitionSpec as P

eps_norm = 1e-06
beta_one = 0.9
beta_two = 0.999
adam_eps = 1e-08
decay_rate = 0.01
rate_matrix = 0.12
rate_gain = 3.0
STEP = 10
MESH = pl.DeviceIdType.MESH
BF, F32 = jnp.bfloat16, jnp.float32
ALL = slice(None)
NEG = -1e30
PARTS_A = (("A", 0, "xyz"), ("A", 1, "yzx"), ("A", 2, "zxy"))
PARTS_F = (("B", 0, "xyz"), ("B", 1, "yxz"), ("C", 0, "xyz"))
PARTS_D = (("D", 0, "xy"), ("D", 1, "yx"))
AXES = {"A": "xyz", "B": "xyz", "C": "zxy", "D": "xy"}
STEPS = (2, -1, 1, 0)
VS = pl.BlockSpec(memory_space=pltpu.VMEM)
HS = pl.BlockSpec(memory_space=pltpu.HBM)
SDS = jax.ShapeDtypeStruct
DMA = pltpu.SemaphoreType.DMA


def vm(*shape):
    return pltpu.VMEM(shape, BF)


def vf(*shape):
    return pltpu.VMEM(shape, F32)


def where_am_i():
    dp, sq = lax.axis_index("dp"), lax.axis_index("seq")
    return {"x": sq // 4, "y": sq % 4, "z": dp // 2, "c": dp % 2}


def dev(at):
    return (at["z"] * 2 + at["c"], at["x"] * 4 + at["y"])


def moved(at, axis, step):
    return {**at, axis: (at[axis] + step + 4) % 4}


def offset(me, j, sign=1):
    return {**me, "x": (me["x"] + sign * (j // 4) + 4) % 4, "y": (me["y"] + sign * (j % 4) + 4) % 4}


def sibling_of(me):
    return {**me, "c": 1 - me["c"]}


def remote(src, dst, send, recv, to):
    return pltpu.make_async_remote_copy(src, dst, send, recv, device_id=dev(to), device_id_type=MESH)


def meet(me, column):
    dp, sq = lax.axis_index("dp"), lax.axis_index("seq")
    bar = pltpu.get_barrier_semaphore()
    for i in range(1, 16):
        pl.semaphore_signal(bar, inc=1, device_id=(dp, (sq + i) % 16), device_id_type=MESH)
    if column == "dp":
        for i in range(1, 8):
            pl.semaphore_signal(bar, inc=1, device_id=((dp + i) % 8, sq), device_id_type=MESH)
        return bar, 22
    if column == "z":
        for to in (moved(me, "z", 1), moved(me, "z", -1), sibling_of(me)):
            pl.semaphore_signal(bar, inc=1, device_id=dev(to), device_id_type=MESH)
        return bar, 18
    return bar, 15


def dot(a, b, ca=1, cb=0):
    return lax.dot_general(a, b, (((ca,), (cb,)), ((), ())), preferred_element_type=F32)


class Gather:
    def __init__(self, me, orders, view, own, ss, rs, sib_s=None, sib_r=None):
        self.me, self.orders, self.view, self.own = me, orders, view, own
        self.ss, self.rs, self.sib_s, self.sib_r = ss, rs, sib_s, sib_r
        self.count, self.last = len(orders), len(orders[0]) - 1

    def group(self, n, t, step, half=None):
        order = self.orders[n]
        at = moved(self.me, order[t], step)
        for j in range(t):
            at = {**at, order[j]: ALL}
        if half is not None and t:
            at = {**at, order[0]: pl.ds(2 * half, 2)}
        return at

    def kinds(self, n, t):
        return (0, 1, 2, 3) if t else (0, 1, 2 + n % 2)

    def copy(self, n, t, kind, back=0):
        axis = self.orders[n][t]
        step = 1 if kind in (0, 2) else -1
        dst = self.view(n, self.group(n, t, back) if kind < 2 else self.group(n, t, back - step, kind - 2))
        src = self.own(n) if t == 0 and kind < 2 and back == 0 else dst
        return remote(src, dst, self.ss.at[n, t, kind], self.rs.at[n, t, kind], moved(self.me, axis, step))

    def arrived(self, n, t, kind):
        self.copy(n, t, kind, -1 if kind in (0, 2) else 1).wait_recv()

    def sibling(self, n, j, c):
        v = self.view(n, {**self.group(n, self.last, (0, -1, 1, 2)[j]), "c": c})
        return remote(v, v, self.sib_s.at[n, j], self.sib_r.at[n, j], sibling_of(self.me))

    def send(self, t):
        for n in range(self.count):
            if t:
                for k in self.kinds(n, t - 1)[2:]:
                    self.arrived(n, t - 1, k)
            self.copy(n, t, 0).start()
            self.copy(n, t, 1).start()
            if self.sib_s is not None and t == self.last:
                self.sibling(n, 0, self.me["c"]).start()

    def forward(self, t):
        for n in range(self.count):
            for k in (0, 1):
                self.arrived(n, t, k)
                if 2 + k in self.kinds(n, t):
                    self.copy(n, t, 2 + k).start()
                if self.sib_s is not None and t == self.last:
                    self.sibling(n, 1 + k, self.me["c"]).start()

    def finish(self):
        for n in range(self.count):
            for k in (2, 3):
                self.arrived(n, self.last, k)
            if self.sib_s is not None:
                self.sibling(n, 3, self.me["c"]).start()

    def siblings_in(self):
        for n in range(self.count):
            for j in range(4):
                self.sibling(n, j, 1 - self.me["c"]).wait_recv()

    def drain(self):
        for n in range(self.count):
            for t in range(self.last + 1):
                for k in self.kinds(n, t):
                    self.copy(n, t, k).wait_send()
            if self.sib_s is not None:
                for j in range(4):
                    self.sibling(n, j, self.me["c"]).wait_send()


class Scatter:
    def __init__(self, me, parts, acc, hop, fin, ss, rs, sib=None, source=None, sib_s=None, sib_r=None, loc_s=None):
        self.me, self.parts, self.acc, self.hop_b, self.fin_b = me, parts, acc, hop, fin
        self.ss, self.rs, self.sib, self.source = ss, rs, sib, source
        self.sib_s, self.sib_r, self.loc_s = sib_s, sib_r, loc_s
        self.count, self.last = len(parts), len(parts[0][2]) - 1

    def idx(self, n, at):
        name, p, _ = self.parts[n]
        place = tuple(at[a] for a in AXES[name])
        return place if name == "C" else (p,) + place

    def slot(self, n):
        name, p, _ = self.parts[n]
        return () if name == "C" else (p,)

    def done(self, n, t):
        name, _, order = self.parts[n]
        return [a for a in AXES[name] if a in order[:t]]

    def group(self, n, t, step, half=None):
        order = self.parts[n][2]
        at = moved(self.me, order[t], step)
        for j in range(t):
            at = {**at, order[j]: ALL}
        if half is not None and t:
            at = {**at, self.done(n, t)[0]: pl.ds(2 * half, 2)}
        return at

    def kinds(self, n, t):
        return (0, 1) if t else (n % 2,)

    def refs(self, n, t):
        name = self.parts[n][0]
        return self.acc[name], self.hop_b[t][name], self.fin_b[t][name]

    def hop_copy(self, n, t, kind):
        step = 1 if kind == 0 else -1
        a, h, _ = self.refs(n, t)
        return remote(a.at[self.idx(n, self.group(n, t, 2 * step, kind))], h.at[self.slot(n) + (kind,)],
                      self.ss.at[n, t, kind], self.rs.at[n, t, kind], moved(self.me, self.parts[n][2][t], step))

    def fin_copy(self, n, t, kind):
        step = 1 if kind == 0 else -1
        a, _, f = self.refs(n, t)
        return remote(a.at[self.idx(n, self.group(n, t, step))], f.at[self.slot(n) + (kind,)],
                      self.ss.at[n, t, 2 + kind], self.rs.at[n, t, 2 + kind], moved(self.me, self.parts[n][2][t], step))

    def each(self, n, t, at, fn, half=None):
        axes = self.done(n, t)
        sizes, offs = [4] * len(axes), [0] * len(axes)
        if half is not None and axes:
            sizes[0], offs[0] = 2, 2 * half
        total = 1
        for s in sizes:
            total *= s

        def one(i):
            pos, rest = [], i
            for s in sizes[::-1]:
                pos.append(rest % s)
                rest = rest // s
            pos = pos[::-1]
            where = dict(at)
            for a, p, o in zip(axes, pos, offs):
                where[a] = p + o
            fn(self.idx(n, where), tuple(pos))

        if total == 1:
            one(0)
        else:
            pl.loop(0, total)(one)

    def sib_copy(self, n, j):
        at = self.group(n, self.last, STEPS[j])
        return remote(self.source(n, at, 1 - self.me["c"]), self.sib[self.parts[n][0]].at[self.idx(n, at)],
                      self.sib_s.at[n, j], self.sib_r.at[n, j], sibling_of(self.me))

    def loc_copy(self, n, j):
        at = self.group(n, self.last, STEPS[j])
        return pltpu.make_async_copy(self.source(n, at, self.me["c"]), self.acc[self.parts[n][0]].at[self.idx(n, at)], self.loc_s.at[n, j])

    def start(self):
        for j in range(4):
            for n in range(self.count):
                self.sib_copy(n, j).start()
                self.loc_copy(n, j).start()

    def merge(self, j):
        for n in range(self.count):
            self.sib_copy(n, j).wait_recv()
            self.loc_copy(n, j).wait()
            a, b = self.acc[self.parts[n][0]], self.sib[self.parts[n][0]]

            def fn(i, _):
                a[i] = (a[i].astype(F32) + b[i].astype(F32)).astype(BF)

            self.each(n, self.last, self.group(n, self.last, STEPS[j]), fn)

    def hop(self, t):
        for n in range(self.count):
            for k in self.kinds(n, t):
                self.hop_copy(n, t, k).start()

    def pass_on(self, t):
        for n in range(self.count):
            a, h, _ = self.refs(n, t)
            for k in (0, 1):
                if k in self.kinds(n, t):
                    self.hop_copy(n, t, k).wait_recv()

                    def fn(i, pos):
                        j = self.slot(n) + (k,) + pos
                        a[i] = (a[i].astype(F32) + h[j].astype(F32)).astype(BF)

                    self.each(n, t, self.group(n, t, 1 if k == 0 else -1), fn, k)
                self.fin_copy(n, t, k).start()

    def close(self, t):
        for n in range(self.count):
            self.fin_copy(n, t, 0).wait_recv()
            self.fin_copy(n, t, 1).wait_recv()
            a, _, f = self.refs(n, t)

            def fn(i, pos):
                s = self.slot(n)
                a[i] = (a[i].astype(F32) + f[s + (0,) + pos].astype(F32) + f[s + (1,) + pos].astype(F32)).astype(BF)

            self.each(n, t, self.group(n, t, 0), fn)

    def result(self, n):
        self.fin_copy(n, 0, 0).wait_recv()
        self.fin_copy(n, 0, 1).wait_recv()
        a, _, f = self.refs(n, 0)
        s = self.slot(n)
        return a[self.idx(n, self.me)].astype(F32) + f[s + (0,)].astype(F32) + f[s + (1,)].astype(F32)

    def drain(self):
        for n in range(self.count):
            if self.sib is not None:
                for j in range(4):
                    self.sib_copy(n, j).wait_send()
            for t in range(self.last + 1):
                for k in self.kinds(n, t):
                    self.hop_copy(n, t, k).wait_send()
                self.fin_copy(n, t, 0).wait_send()
                self.fin_copy(n, t, 1).wait_send()


def places(names, refs):
    return dict(zip(names, refs))


def stage_buffers(*shapes):
    out = []
    for lead in ((2, 2, 4), (2, 4, 4), (2, 2), (2, 4), (2,), (2,)):
        out += [vm(*pre, *lead, *block) for pre, block in shapes]
    return out


def staged(names, refs):
    k = len(names)
    got = [places(names, refs[k * i:k * i + k]) for i in range(6)]
    return {2: got[0], 1: got[2], 0: got[4]}, {2: got[1], 1: got[3], 0: got[5]}


def gather_kernel(attn, wi, wo, info, A, gains, lens, outB, outC, infos, stage, recv, blk, blkA, irecv,
                  ss, rs, sib_s, sib_r, as_, ar_, is_, ir_, ds_, dr_, own_s):
    me = where_am_i()
    dp, sq = lax.axis_index("dp"), lax.axis_index("seq")
    bar, count = meet(me, "dp")
    stage[:, 6:8, :] = jnp.zeros((16, 2, 640), F32)
    for s in range(16):
        stage[s, 0:6, 0:384] = attn[:, s // 2, 384 * (s % 2):384 * (s % 2) + 384]
        stage[s, 0:6, 384:640] = wi[:, s // 8, 256 * (s % 8):256 * (s % 8) + 256]
    pl.semaphore_wait(bar, count)

    def a2a(i):
        peer = (sq + i) % 16
        return pltpu.make_async_remote_copy(stage.at[peer], recv.at[sq], as_.at[i], ar_.at[i], device_id=(dp, peer), device_id_type=MESH)

    def inf(i):
        peer = (sq + i) % 16
        return pltpu.make_async_remote_copy(info, irecv.at[sq], is_.at[i], ir_.at[i], device_id=(dp, peer), device_id_type=MESH)

    for i in range(1, 16):
        a2a(i).start()
    for i in range(1, 16):
        inf(i).start()
    recv[sq] = stage[sq]
    irecv[sq] = info[...]
    outC[...] = wo[...].astype(BF)
    for i in range(1, 16):
        a2a(i).wait_recv()
    for k in range(16):
        blk[6 * k:6 * k + 6, :] = recv[k, 0:6, :]
    for p in range(3):
        blkA[p] = blk[32 * p:32 * p + 32, 0:384].astype(BF)
    for p in range(2):
        outB[p] = blk[48 * p:48 * p + 48, 384:640].astype(BF)
    place = lambda n, at: A.at[at["x"], at["y"], at["z"], at["c"], PARTS_A[n][1]]
    ring = Gather(me, [p[2] for p in PARTS_A], place, lambda n: blkA.at[n], ss, rs, sib_s, sib_r)
    owns = [pltpu.make_async_copy(blkA.at[n], place(n, me), own_s.at[n]) for n in range(3)]
    for o in owns:
        o.start()
    ring.send(0)
    ring.forward(0)
    for o in owns:
        o.wait()
    ring.send(1)
    ring.forward(1)
    ring.send(2)
    for i in range(1, 16):
        inf(i).wait_recv()
    tile = jnp.sum(irecv[...], axis=0)
    infos[dp] = tile

    def dpx(i, back=0):
        v = infos.at[(dp - back + 8) % 8]
        return pltpu.make_async_remote_copy(v, v, ds_.at[i], dr_.at[i], device_id=((dp + i) % 8, sq), device_id_type=MESH)

    for i in range(1, 8):
        dpx(i).start()
    ring.forward(2)
    for i in range(1, 8):
        dpx(i, i).wait_recv()
    lane = lax.broadcasted_iota(jnp.int32, (8, 128), 1)
    gains[...] = jnp.zeros((8, 768), F32)
    for d in range(8):
        lo, sh = 96 * d // 128, 96 * d % 128
        t = pltpu.roll(jnp.where(lane < 96, infos[d], 0.0), sh, 1)
        gains[:, 128 * lo:128 * lo + 128] += jnp.where(lane >= sh, t, 0.0)
        if sh > 32:
            gains[:, 128 * lo + 128:128 * lo + 256] += jnp.where(lane < sh, t, 0.0)
    pick = lax.broadcasted_iota(jnp.int32, (16, 128), 0) == lax.broadcasted_iota(jnp.int32, (16, 128), 1)
    lens[...] = jnp.broadcast_to(jnp.sum(jnp.where(pick, tile[3:4, :], 0.0), axis=1, keepdims=True), (16, 128))
    ring.finish()
    ring.siblings_in()
    for i in range(1, 16):
        a2a(i).wait_send()
        inf(i).wait_send()
    for i in range(1, 8):
        dpx(i).wait_send()
    ring.drain()


def gather(attn, wi, wo, info):
    return pl.pallas_call(
        gather_kernel,
        out_shape=(SDS((4, 4, 4, 2, 3, 32, 384), BF), SDS((8, 768), F32), SDS((16, 128), F32), SDS((2, 48, 256), BF), SDS((16, 768), BF)),
        in_specs=[VS] * 4, out_specs=(HS,) + (VS,) * 4,
        scratch_shapes=[vf(8, 8, 128), vf(16, 8, 640), vf(16, 8, 640), vf(96, 640), vm(3, 32, 384), vf(16, 8, 128),
                        DMA((3, 3, 4)), DMA((3, 3, 4)), DMA((3, 4)), DMA((3, 4)), DMA((16,)), DMA((16,)), DMA((16,)), DMA((16,)), DMA((8,)), DMA((8,)), DMA((3,))],
        compiler_params=pltpu.CompilerParams(collective_id=0, has_side_effects=True, vmem_limit_bytes=60 << 20),
        name="gather_attention_weights",
    )(attn, wi, wo, info)


def info_tile(gain, mem_len):
    sq = lax.axis_index("seq")
    t = jnp.zeros((8, 128), F32)
    t = lax.dynamic_update_slice(t, gain.astype(BF).astype(F32), (0, 6 * sq))
    return lax.dynamic_update_slice(t, mem_len.astype(F32)[:, None], (3, sq))


def scatter_kernel(GA, blkF, gg, oA, oB, oG, accA, sibA, h2, f2, h1, f1, h0, f0, blk, stage, recv, gdp, gsum, gsq,
                   ss, rs, sib_s, sib_r, loc_s, as_, ar_, is_, ir_, ds_, dr_):
    me = where_am_i()
    dp, sq = lax.axis_index("dp"), lax.axis_index("seq")
    bar, count = meet(me, "dp")
    pl.semaphore_wait(bar, count)
    hop, fin = staged("A", (h2, f2, h1, f1, h0, f0))
    ring = Scatter(me, PARTS_A, {"A": accA}, hop, fin, ss, rs, {"A": sibA},
                   lambda n, at, c: GA.at[at["x"], at["y"], at["z"], c, n], sib_s, sib_r, loc_s)
    ring.start()

    def dpx(i):
        peer = (dp + i) % 8
        return pltpu.make_async_remote_copy(gg.at[peer], gdp.at[dp], ds_.at[i], dr_.at[i], device_id=(peer, sq), device_id_type=MESH)

    for i in range(1, 8):
        dpx(i).start()
    gdp[dp] = gg[dp]
    ring.merge(0)
    ring.hop(2)
    ring.merge(1)
    ring.merge(2)
    ring.pass_on(2)
    ring.merge(3)
    for i in range(1, 8):
        dpx(i).wait_recv()
    gsum[...] = jnp.sum(gdp[...], axis=0)

    def inf(i):
        peer = (sq + i) % 16
        return pltpu.make_async_remote_copy(gsum, gsq.at[sq], is_.at[i], ir_.at[i], device_id=(dp, peer), device_id_type=MESH)

    for i in range(1, 16):
        inf(i).start()
    gsq[sq] = gsum[...]
    blk[:, 384:640] = blkF[...]
    stage[:, 6:8, :] = jnp.zeros((16, 2, 640), F32)
    ring.close(2)
    ring.hop(1)
    ring.pass_on(1)
    ring.close(1)
    ring.hop(0)
    ring.pass_on(0)
    for n in range(3):
        blk[32 * n:32 * n + 32, 0:384] = ring.result(n)
    for k in range(16):
        stage[k, 0:6, :] = blk[6 * k:6 * k + 6, :]

    def a2a(i):
        peer = (sq + i) % 16
        return pltpu.make_async_remote_copy(stage.at[peer], recv.at[sq], as_.at[i], ar_.at[i], device_id=(dp, peer), device_id_type=MESH)

    for i in range(1, 16):
        a2a(i).start()
    recv[sq] = stage[sq]
    for i in range(1, 16):
        inf(i).wait_recv()
    oG[...] = pltpu.roll(jnp.sum(gsq[...], axis=0), (128 - 6 * sq) % 128, 1)
    for i in range(1, 16):
        a2a(i).wait_recv()
    for s in range(16):
        oA[:, s // 2, 384 * (s % 2):384 * (s % 2) + 384] = recv[s, 0:6, 0:384]
        oB[:, s // 8, 256 * (s % 8):256 * (s % 8) + 256] = recv[s, 0:6, 384:640]
    for i in range(1, 8):
        dpx(i).wait_send()
    for i in range(1, 16):
        a2a(i).wait_send()
        inf(i).wait_send()
    ring.drain()


def scatter(GA, blkF, gg):
    return pl.pallas_call(
        scatter_kernel,
        out_shape=(SDS((6, 8, 768), F32), SDS((6, 2, 2048), F32), SDS((8, 128), F32)),
        in_specs=[HS, VS, VS], out_specs=(VS,) * 3,
        scratch_shapes=[vm(3, 4, 4, 4, 32, 384), vm(3, 4, 4, 4, 32, 384), *stage_buffers(((3,), (32, 384))),
                        vf(96, 640), vf(16, 8, 640), vf(16, 8, 640), vf(8, 8, 128), vf(8, 128), vf(16, 8, 128),
                        DMA((3, 3, 4)), DMA((3, 3, 4)), DMA((3, 4)), DMA((3, 4)), DMA((3, 4)),
                        DMA((16,)), DMA((16,)), DMA((16,)), DMA((16,)), DMA((8,)), DMA((8,))],
        compiler_params=pltpu.CompilerParams(collective_id=1, has_side_effects=True, vmem_limit_bytes=60 << 20),
        name="scatter_attention_grads",
    )(GA, blkF, gg)


def head_masks(value=1.0):
    lane = lax.broadcasted_iota(jnp.int32, (1, 256), 1)
    return [jnp.where(lane // 64 == h, value, 0.0).astype(BF) for h in range(4)]


def stack_heads(block, masks):
    return jnp.concatenate([block * m for m in masks], axis=0)


def key_positions():
    sq = lax.axis_index("seq")
    return (192 * sq + lax.broadcasted_iota(jnp.int32, (192, 128), 0)).astype(F32)


def ffn_place(B, C):
    def place(n, at):
        if n < 2:
            return B.at[at["x"], at["y"], at["z"], at["c"], n]
        return C.at[at["z"], at["c"], at["x"], at["y"]]
    return place


def cross_fwd_kernel(q, lens, blkB, blkC, mem_h, A, q_h, k_h, v_h, kt_h, B, C, o_ref, L_ref,
                     qall, mem, wk, wv, wkT, wvT, K, V, KT, VT, ost, lst, orc, lrc, acc,
                     mem_s, w_s, out_s, ss, rs, os_, or_, ls_, lr_, fs, fr, fsib_s, fsib_r, own_s):
    me = where_am_i()
    bar, count = meet(me, "z")

    def load_mem(e):
        return pltpu.make_async_copy(mem_h.at[e], mem.at[e], mem_s.at[e])

    loads = [pltpu.make_async_copy(A.at[10 + i], (wk if i < 2 else wv).at[:, pl.ds(384 * (i % 2), 384)], w_s.at[i]) for i in range(4)]
    for c in loads:
        c.start()

    @pl.loop(0, 16)
    def _(e):
        load_mem(e).start()

    qall[me["x"], me["y"]] = q[...]
    place = ffn_place(B, C)
    mine = lambda n: blkB.at[n] if n < 2 else blkC
    owns = [pltpu.make_async_copy(mine(n), place(n, me), own_s.at[n]) for n in range(3)]
    for c in owns:
        c.start()
    pl.semaphore_wait(bar, count)
    plane = Gather(me, ("xy", "yx"), lambda n, at: qall.at[at["x"], at["y"], :, pl.ds(384 * n, 384)],
                   lambda n: qall.at[me["x"], me["y"], :, pl.ds(384 * n, 384)], ss, rs)
    ring = Gather(me, [p[2] for p in PARTS_F], place, mine, fs, fr, fsib_s, fsib_r)
    plane.send(0)
    ring.send(0)
    for c in loads:
        c.wait()
    for i in range(6):
        wkT[:, 128 * i:128 * i + 128] = wk[128 * i:128 * i + 128, :].T
        wvT[:, 128 * i:128 * i + 128] = wv[128 * i:128 * i + 128, :].T
    plane.forward(0)
    ring.forward(0)
    for c in owns:
        c.wait()

    def project(a, b):
        @pl.loop(a, b)
        def _(e):
            load_mem(e).wait()
            m = mem[e]
            K[e] = dot(m, wk[...]).astype(BF)
            VT[e] = dot(wvT[...], m, 1, 1).astype(BF)
            V[e] = dot(m, wv[...]).astype(BF)
            KT[e] = dot(wkT[...], m, 1, 1).astype(BF)

    project(0, 3)
    plane.send(1)
    ring.send(1)
    project(3, 8)
    ring.forward(1)
    project(8, 11)
    ring.send(2)
    plane.forward(1)
    project(11, 16)
    outs = [pltpu.make_async_copy(a, b, out_s.at[i]) for i, (a, b) in enumerate(((K, k_h), (V, v_h), (KT, kt_h), (qall, q_h)))]
    for c in outs[:3]:
        c.start()
    plane.finish()
    outs[3].start()
    masks = head_masks()
    pos = key_positions()

    def o_copy(j):
        return remote(ost.at[j], orc.at[j], os_.at[j], or_.at[j], offset(me, j))

    def l_copy(j):
        return remote(lst.at[j], lrc.at[j], ls_.at[j], lr_.at[j], offset(me, j))

    def attend(a, b):
        @pl.loop(a, b)
        def _(i):
            j = (i + 1) % 16
            at = offset(me, j)
            e = at["x"] * 4 + at["y"]
            live = pos < lens[pl.ds(e, 1), :]
            for g in range(3):
                cols = slice(256 * g, 256 * g + 256)
                sT = dot(K[e, :, cols], stack_heads(qall[at["x"], at["y"], :, cols], masks), 1, 1)
                ps, inv = [], []
                for h in range(4):
                    s = jnp.where(live, sT[:, 128 * h:128 * h + 128], NEG)
                    top = jnp.max(s, axis=0, keepdims=True)
                    p = jnp.exp(s - top)
                    tot = jnp.sum(p, axis=0, keepdims=True)
                    lst[j, 4 * g + h:4 * g + h + 1, :] = top + jnp.log(tot)
                    ps.append(p.astype(BF))
                    inv.append(1.0 / tot)
                oT = dot(VT[e, cols, :], jnp.concatenate(ps, axis=1))
                for h in range(4):
                    ost[j, 256 * g + 64 * h:256 * g + 64 * h + 64, :] = (oT[64 * h:64 * h + 64, 128 * h:128 * h + 128] * inv[h]).astype(BF)

            @pl.when(j > 0)
            def _():
                l_copy(j).start()
                o_copy(j).start()

    attend(0, 8)
    ring.forward(2)
    attend(8, 16)
    lrc[0] = lst[0]
    orc[0] = ost[0]
    ring.finish()

    @pl.loop(1, 16)
    def _(j):
        l_copy(j).wait_recv()

    l = lrc[:, 0:12, :]
    top = jnp.max(l, axis=0)
    L_ref[0:12, :] = top + jnp.log(jnp.sum(jnp.exp(l - top[None]), axis=0))
    L_ref[12:16, :] = jnp.zeros((4, 128), F32)
    acc[...] = jnp.zeros_like(acc)

    @pl.loop(0, 16)
    def _(j):
        @pl.when(j > 0)
        def _():
            o_copy(j).wait_recv()

        w = jnp.exp(lrc[j, 0:12, :] - L_ref[0:12, :])
        for h in range(12):
            acc[64 * h:64 * h + 64, :] += orc[j, 64 * h:64 * h + 64, :].astype(F32) * w[h:h + 1, :]

    for i in range(6):
        o_ref[:, 128 * i:128 * i + 128] = acc[128 * i:128 * i + 128, :].T

    @pl.loop(1, 16)
    def _(j):
        l_copy(j).wait_send()
        o_copy(j).wait_send()

    plane.drain()
    for c in outs:
        c.wait()
    ring.siblings_in()
    ring.drain()


def cross_fwd(q, lens, blkB, blkC, memory, A):
    return pl.pallas_call(
        cross_fwd_kernel,
        out_shape=(SDS((4, 4, 128, 768), BF), SDS((16, 192, 768), BF), SDS((16, 192, 768), BF), SDS((16, 768, 192), BF),
                   SDS((4, 4, 4, 2, 2, 48, 256), BF), SDS((4, 2, 4, 4, 16, 768), BF), SDS((128, 768), F32), SDS((16, 128), F32)),
        in_specs=[VS] * 4 + [HS] * 2, out_specs=(HS,) * 6 + (VS,) * 2,
        scratch_shapes=[vm(4, 4, 128, 768), vm(16, 192, 768), vm(768, 768), vm(768, 768), vm(768, 768), vm(768, 768),
                        vm(16, 192, 768), vm(16, 192, 768), vm(16, 768, 192), vm(16, 768, 192), vm(16, 768, 128), vf(16, 16, 128),
                        vm(16, 768, 128), vf(16, 16, 128), vf(768, 128),
                        DMA((16,)), DMA((4,)), DMA((4,)), DMA((2, 2, 4)), DMA((2, 2, 4)), DMA((16,)), DMA((16,)), DMA((16,)), DMA((16,)),
                        DMA((3, 3, 4)), DMA((3, 3, 4)), DMA((3, 4)), DMA((3, 4)), DMA((3,))],
        compiler_params=pltpu.CompilerParams(collective_id=2, has_side_effects=True, vmem_limit_bytes=60 << 20),
        name="cross_forward",
    )(q, lens, blkB, blkC, memory, A)


def cross_bwd_kernel(do, st, lens, q_h, k_h, v_h, kt_h, mem_h, A, GB, GC, G_in, dq_ref, fB, fC, gm_h, dw_h,
                     qall, doall, stall, wk, wv, K, V, KT, mem, memT, dK, dV, gst, wst, dst, dh1, df1, dh0, df0,
                     accB, accC, sibB, sibC, hB2, hC2, fB2, fC2, hB1, hC1, fB1, fC1, hB0, hC0, fB0, fC0,
                     q_s, kv_s, mem_s, w_s, gm_s, dw_s, ss, rs, ds_, dr_, fs, fr, fsib_s, fsib_r, floc):
    me = where_am_i()
    bar, count = meet(me, "z")

    def load_mem(e):
        return pltpu.make_async_copy(mem_h.at[pl.ds(pl.multiple_of(256 * e, 256), 256)], mem.at[e % 2], mem_s.at[e % 2])

    load_mem(0).start()
    load_mem(1).start()
    loads = [pltpu.make_async_copy(A.at[10 + i], (wk if i < 2 else wv).at[:, pl.ds(384 * (i % 2), 384)], w_s.at[i]) for i in range(4)]
    loads.append(pltpu.make_async_copy(q_h, qall, q_s))
    doall[me["x"], me["y"]] = do[...]
    stall[me["x"], me["y"]] = st[...]
    pl.semaphore_wait(bar, count)

    def place(n, at):
        return stall.at[at["x"], at["y"]] if n == 2 else doall.at[at["x"], at["y"], :, pl.ds(384 * n, 384)]

    plane = Gather(me, ("xy", "yx", "xy"), place, lambda n: place(n, me), ss, rs)
    fhop, ffin = staged("BC", (hB2, hC2, fB2, fC2, hB1, hC1, fB1, fC1, hB0, hC0, fB0, fC0))
    grads = ffn_place(GB, GC)
    ring = Scatter(me, PARTS_F, {"B": accB, "C": accC}, fhop, ffin, fs, fr, {"B": sibB, "C": sibC},
                   lambda n, at, c: grads(n, {**at, "c": c}), fsib_s, fsib_r, floc)
    back = Scatter(me, PARTS_D, {"D": dst}, {1: {"D": dh1}, 0: {"D": dh0}}, {1: {"D": df1}, 0: {"D": df0}}, ds_, dr_)
    plane.send(0)
    ring.start()
    for c in loads:
        c.start()

    def turn(a, b):
        @pl.loop(a, b)
        def _(e):
            load_mem(e).wait()
            memT[:, pl.ds(pl.multiple_of(256 * e, 256), 256)] = mem[e % 2].T

            @pl.when(e < 10)
            def _():
                load_mem(e + 2).start()

    turn(0, 2)
    plane.forward(0)
    ring.merge(0)
    ring.hop(2)
    plane.send(1)
    turn(2, 7)
    ring.merge(1)
    ring.merge(2)
    plane.forward(1)
    ring.pass_on(2)
    turn(7, 12)
    ring.merge(3)
    masks = head_masks()
    pos = key_positions()

    def where(i):
        return {**me, "x": (me["x"] + 2 + i // 4) % 4, "y": (me["y"] + 2 + i % 4) % 4}

    def load_kv(i, which):
        at = where(i)
        e = at["x"] * 4 + at["y"]
        src, to = ((k_h, K), (v_h, V), (kt_h, KT))[which]
        return pltpu.make_async_copy(src.at[e], to.at[i % 2], kv_s.at[which, i % 2])

    for w in range(3):
        load_kv(0, w).start()
    for c in loads:
        c.wait()
    plane.finish()

    @pl.loop(0, 16)
    def _(i):
        at = where(i)
        e = at["x"] * 4 + at["y"]

        @pl.when(i < 15)
        def _():
            for w in range(3):
                load_kv(i + 1, w).start()

        for w in range(3):
            load_kv(i, w).wait()
        live = pos < lens[pl.ds(e, 1), :]
        rows = pl.ds(pl.multiple_of(192 * e, 192), 192)
        for g in range(3):
            cols = slice(256 * g, 256 * g + 256)
            q4s = stack_heads(qall[at["x"], at["y"], :, cols], masks)
            d4s = stack_heads(doall[at["x"], at["y"], :, cols], masks)
            sT = dot(K[i % 2, :, cols], q4s, 1, 1)
            gT = dot(V[i % 2, :, cols], d4s, 1, 1)
            ps, gs = [], []
            for h in range(4):
                n = 4 * g + h
                s = jnp.where(live, sT[:, 128 * h:128 * h + 128], NEG)
                p = jnp.exp(s - stall[at["x"], at["y"], n:n + 1, :])
                ps.append(p.astype(BF))
                gs.append((p * (gT[:, 128 * h:128 * h + 128] - stall[at["x"], at["y"], 12 + n:13 + n, :])).astype(BF))
            sg = jnp.concatenate(gs, axis=1)
            dV[rows, cols] = dot(jnp.concatenate(ps, axis=1), d4s).astype(BF)
            dK[rows, cols] = dot(sg, q4s).astype(BF)
            qT = dot(KT[i % 2, cols, :], sg)
            for h in range(4):
                r = 256 * g + 64 * h
                dst[r // 384, at["x"], at["y"], r % 384:r % 384 + 64, :] = qT[64 * h:64 * h + 64, 128 * h:128 * h + 128].astype(BF)

    back.hop(1)

    def gm_copy(e):
        return pltpu.make_async_copy(gst.at[e % 2], gm_h.at[e], gm_s.at[e % 2])

    def mem_grad(a, b):
        @pl.loop(a, b)
        def _(e):
            @pl.when(e > 1)
            def _():
                gm_copy(e - 2).wait()

            rows = pl.ds(pl.multiple_of(192 * e, 192), 192)
            gst[e % 2] = dot(dK[rows, :], wk[...], 1, 1) + dot(dV[rows, :], wv[...], 1, 1)
            gm_copy(e).start()

    def dw_copy(n, r):
        return pltpu.make_async_copy(wst.at[n % 2], dw_h.at[10 + n, pl.ds(pl.multiple_of(128 * r, 128), 128)], dw_s.at[n % 2])

    def weight_grad(n):
        src = dK if n < 2 else dV

        @pl.loop(0, 6)
        def _(r):
            @pl.when(r > 0)
            def _():
                dw_copy(n, r - 1).wait()

            wst[n % 2] = dot(memT[pl.ds(pl.multiple_of(128 * r, 128), 128), :], src[:, 384 * (n % 2):384 * (n % 2) + 384]).astype(BF)
            dw_copy(n, r).start()

        dw_copy(n, 5).wait()

    mem_grad(0, 5)
    back.pass_on(1)
    ring.close(2)
    ring.hop(1)
    mem_grad(5, 16)
    ring.pass_on(1)
    weight_grad(0)
    back.close(1)
    back.hop(0)
    ring.close(1)
    ring.hop(0)
    weight_grad(1)
    back.pass_on(0)
    ring.pass_on(0)
    weight_grad(2)
    weight_grad(3)
    for n in range(2):
        v = 0.125 * back.result(n)
        for i in range(3):
            dq_ref[:, 384 * n + 128 * i:384 * n + 128 * i + 128] = v[128 * i:128 * i + 128, :].T
    fB[0:48, :] = ring.result(0)
    fB[48:96, :] = ring.result(1)
    fC[...] = ring.result(2)
    gm_copy(14).wait()
    gm_copy(15).wait()
    plane.drain()
    ring.drain()
    back.drain()


def cross_bwd(do, st, lens, q_h, k_h, v_h, kt_h, memory, A, GB, GC, GA):
    bB, bC = (48, 256), (16, 768)
    return pl.pallas_call(
        cross_bwd_kernel,
        out_shape=(SDS((128, 768), F32), SDS((96, 256), F32), SDS((16, 768), F32), SDS((16, 192, 768), F32), SDS((16, 768, 384), BF)),
        in_specs=[VS] * 3 + [HS] * 9, out_specs=(VS,) * 3 + (HS,) * 2, input_output_aliases={11: 4},
        scratch_shapes=[vm(4, 4, 128, 768), vm(4, 4, 128, 768), vf(4, 4, 24, 128), vm(768, 768), vm(768, 768),
                        vm(2, 192, 768), vm(2, 192, 768), vm(2, 768, 192), vm(2, 256, 768), vm(768, 3072), vm(3072, 768), vm(3072, 768),
                        vf(2, 192, 768), vm(2, 128, 384), vm(2, 4, 4, 384, 128), vm(2, 2, 2, 384, 128), vm(2, 2, 4, 384, 128), vm(2, 2, 384, 128), vm(2, 2, 384, 128),
                        vm(2, 4, 4, 4, *bB), vm(4, 4, 4, *bC), vm(2, 4, 4, 4, *bB), vm(4, 4, 4, *bC), *stage_buffers(((2,), bB), ((), bC)),
                        DMA, DMA((3, 2)), DMA((2,)), DMA((4,)), DMA((2,)), DMA((2,)), DMA((3, 2, 4)), DMA((3, 2, 4)), DMA((2, 2, 4)), DMA((2, 2, 4)),
                        DMA((3, 3, 4)), DMA((3, 3, 4)), DMA((3, 4)), DMA((3, 4)), DMA((3, 4))],
        compiler_params=pltpu.CompilerParams(collective_id=3, has_side_effects=True, vmem_limit_bytes=60 << 20),
        name="cross_backward",
    )(do, st, lens, q_h, k_h, v_h, kt_h, memory.reshape(3072, 768), A, GB, GC, GA)


def adam_update(master, first, second, grad, rate):
    first_new = beta_one * first + (1.0 - beta_one) * grad
    second_new = beta_two * second + (1.0 - beta_two) * grad * grad
    fix_one = 1.0 - beta_one**STEP
    fix_two = 1.0 - beta_two**STEP
    master_new = master - rate * (
        first_new / fix_one / (jnp.sqrt(second_new / fix_two) + adam_eps) + decay_rate * master
    )
    return (master_new, first_new, second_new, master_new.astype(jnp.bfloat16))


def rms(x):
    return lax.rsqrt(jnp.mean(x * x, axis=-1, keepdims=True) + eps_norm)

def rms_back(x, inv, gain, u):
    scaled = u * gain
    inner = jnp.mean(scaled * x, axis=-1, keepdims=True)
    return inv * scaled - x * inv * inv * inv * inner, jnp.sum(u * x * inv, axis=0, keepdims=True)

def flip(x):
    return jnp.concatenate([x[:, 128 * i:128 * i + 128].T for i in range(x.shape[1] // 128)], axis=0)

def unflip(x):
    return jnp.concatenate([x[128 * i:128 * i + 128, :].T for i in range(x.shape[0] // 128)], axis=1)

def apply_w(h, W, k):
    return jnp.concatenate([dot(h, W[2 * k]), dot(h, W[2 * k + 1])], axis=1)

def apply_wt(u, W, k):
    return dot(u[:, 0:384], W[2 * k], 1, 1) + dot(u[:, 384:768], W[2 * k + 1], 1, 1)

def causal_mask():
    return lax.broadcasted_iota(jnp.int32, (128, 128), 0) <= lax.broadcasted_iota(jnp.int32, (128, 128), 1)

def self_fwd_kernel(x_ref, gains, A, q2, h1, qkv, o1, x1, h2, L1, W, sem):
    loads = [pltpu.make_async_copy(A.at[i], W.at[i], sem.at[i]) for i in range(10)]
    for c in loads:
        c.start()
    x = x_ref[...].astype(F32)
    h = (x * rms(x) * gains[0:1, :]).astype(BF)
    h1[...] = h
    for k in range(3):
        loads[2 * k].wait()
        loads[2 * k + 1].wait()
        full = apply_w(h, W, k)
        qkv[k] = full.astype(BF)
    vT = flip(full).astype(BF)
    masks = head_masks(0.125)
    live = causal_mask()
    outs = []
    for g in range(3):
        cols = slice(256 * g, 256 * g + 256)
        q4 = qkv[0, :, cols]
        sT = dot(qkv[1, :, cols], jnp.concatenate([q4 * m for m in masks], axis=0), 1, 1)
        ps = []
        for n in range(4):
            s = jnp.where(live, sT[:, 128 * n:128 * n + 128], NEG)
            top = jnp.max(s, axis=0, keepdims=True)
            lse = top + jnp.log(jnp.sum(jnp.exp(s - top), axis=0, keepdims=True))
            L1[4 * g + n:4 * g + n + 1, :] = lse
            ps.append(jnp.exp(s - lse).astype(BF))
        oT = dot(vT[256 * g:256 * g + 256, :], jnp.concatenate(ps, axis=1))
        outs += [oT[64 * n:64 * n + 64, 128 * n:128 * n + 128] for n in range(4)]
    o = unflip(jnp.concatenate(outs, axis=0)).astype(BF)
    o1[...] = o
    for c in loads[6:]:
        c.wait()
    x = x + apply_w(o, W, 3)
    x1[...] = x
    h = (x * rms(x) * gains[1:2, :]).astype(BF)
    h2[...] = h
    q2[...] = apply_w(h, W, 4).astype(BF) * jnp.asarray(0.125, BF)

def self_fwd(x, gains, A):
    row = SDS((128, 768), BF)
    return pl.pallas_call(
        self_fwd_kernel,
        out_shape=(row, row, SDS((3, 128, 768), BF), row, SDS((128, 768), F32), row, SDS((16, 128), F32)),
        in_specs=[VS, VS, HS], out_specs=(VS,) * 7,
        scratch_shapes=[pltpu.VMEM((10, 768, 384), BF), pltpu.SemaphoreType.DMA((10,))],
        compiler_params=pltpu.CompilerParams(vmem_limit_bytes=60 << 20),
        name="self_forward",
    )(x, gains, A)

def ffn_kernel(x1, o2, L2, dy_ref, gains, A, B, C, out, do2, st, dx2, gg, GA, GB, GC,
               W7, WB, WC, gA, gB, gC, sw, sb, sc, tb, tc, ta):
    lA = [pltpu.make_async_copy(A.at[14 + i], W7.at[i], sw.at[i]) for i in range(2)]
    lB = [pltpu.make_async_copy(B.at[i], WB.at[i], sb.at[i]) for i in range(16)]
    lC = [pltpu.make_async_copy(C.at[i], WC.at[i], sc.at[i]) for i in range(8)]
    for c in lA:
        c.start()
    for j in range(8):
        lB[j].start()
        lB[8 + j].start()
        lC[j].start()
    o = o2[...]
    ob = o.astype(BF)
    for c in lA:
        c.wait()
    x = x1[...] + apply_w(ob, W7, 0)
    inv = rms(x)
    h = (x * inv * gains[2:3, :]).astype(BF)
    hT = flip(h.astype(F32)).astype(BF)
    df = dy_ref[...]
    y = jnp.zeros((128, 768), F32)
    dh = jnp.zeros((128, 768), F32)
    c0 = 0.7978845608028654
    sB, sC = [], []
    for j in range(8):
        lB[j].wait()
        lB[8 + j].wait()
        lC[j].wait()
        a = dot(h, WB[j])
        up = dot(h, WB[8 + j])
        t = jnp.tanh(c0 * (a + 0.044715 * a * a * a))
        half = 0.5 * (1.0 + t)
        gel = a * half
        der = half + 0.5 * a * (1.0 - t * t) * (c0 * (1.0 + 0.134145 * a * a))
        mid32 = gel * up
        mid = mid32.astype(BF)
        y += dot(mid, WC[j])
        dm = dot(df, WC[j], 1, 1)
        dga = (dm * up * der).astype(BF)
        dup = (dm * gel).astype(BF)
        dh += dot(dga, WB[j], 1, 1) + dot(dup, WB[8 + j], 1, 1)
        gB[j] = dot(hT, dga).astype(BF)
        gB[8 + j] = dot(hT, dup).astype(BF)
        gC[j] = dot(flip(mid32).astype(BF), df).astype(BF)
        sB += [pltpu.make_async_copy(gB.at[j], GB.at[j], tb.at[j]), pltpu.make_async_copy(gB.at[8 + j], GB.at[8 + j], tb.at[8 + j])]
        sC += [pltpu.make_async_copy(gC.at[j], GC.at[j], tc.at[j])]
        for c in sB[-2:] + sC[-1:]:
            c.start()
    out[...] = (x + y).astype(BF)
    dz, gain = rms_back(x, inv, gains[2:3, :], dh)
    gg[...] = gain
    d = df.astype(F32) + dz
    dx2[...] = d
    dc = d.astype(BF)
    dof = apply_wt(dc, W7, 0).astype(BF)
    do2[...] = dof
    prod = flip(dof.astype(F32) * o)
    st[0:12, :] = L2[0:12, :]
    for n in range(12):
        st[12 + n:13 + n, :] = jnp.sum(prod[64 * n:64 * n + 64, :], axis=0, keepdims=True)
    oT = flip(o).astype(BF)
    sA = []
    for i in range(2):
        gA[i] = dot(oT, dc[:, 384 * i:384 * i + 384]).astype(BF)
        sA.append(pltpu.make_async_copy(gA.at[i], GA.at[14 + i], ta.at[i]))
        sA[-1].start()
    for c in sA + sB + sC:
        c.wait()

def ffn(x1, o2, L2, dy, gains, A, B, C):
    M = lambda *s: pltpu.VMEM(s, BF)
    D = pltpu.SemaphoreType.DMA
    return pl.pallas_call(
        ffn_kernel,
        out_shape=(SDS((128, 768), BF), SDS((128, 768), BF), SDS((24, 128), F32), SDS((128, 768), F32), SDS((1, 768), F32),
                   SDS((16, 768, 384), BF), SDS((16, 768, 256), BF), SDS((8, 256, 768), BF)),
        in_specs=[VS] * 5 + [HS] * 3, out_specs=(VS,) * 5 + (HS,) * 3,
        scratch_shapes=[M(2, 768, 384), M(16, 768, 256), M(8, 256, 768), M(2, 768, 384), M(16, 768, 256), M(8, 256, 768),
                        D((2,)), D((16,)), D((8,)), D((16,)), D((8,)), D((2,))],
        compiler_params=pltpu.CompilerParams(vmem_limit_bytes=60 << 20),
        name="feed_forward",
    )(x1, o2, L2, dy, gains, A, B, C)

def self_bwd_kernel(dq2, h2, x1, dx2, qkv, o1, L1, x_ref, h1, gains, g3, A, GA_in, gm_in, gin, tile, GA, gm,
                    W, G, gb, gmv, sem, gsem, msem):
    loads = [pltpu.make_async_copy(A.at[i], W.at[i], sem.at[i]) for i in range(10)]
    for i in (8, 9, 6, 7, 0, 1, 2, 3, 4, 5):
        loads[i].start()
    def gm_load(e):
        return pltpu.make_async_copy(gm_in.at[e], gmv.at[e], msem.at[e])
    def gm_store(e):
        return pltpu.make_async_copy(gmv.at[e], gm.at[e], msem.at[16 + e])
    for e in range(16):
        gm_load(e).start()
    stores = []
    def weight_grad(k, left, inc):
        for i in range(2):
            n = 2 * k + i
            G[n] = dot(left, inc[:, 384 * i:384 * i + 384]).astype(BF)
            stores.append(pltpu.make_async_copy(G.at[n], GA.at[n], gsem.at[n]))
            stores[-1].start()
    dqb = dq2[...].astype(BF)
    for i in (8, 9, 6, 7):
        loads[i].wait()
    u = apply_wt(dqb, W, 4)
    x = x1[...]
    inv = rms(x)
    dz, gain = rms_back(x, inv, gains[1:2, :], u)
    gb[...] = jnp.zeros((8, 768), F32)
    gb[1:2, :] = gain
    gb[2:3, :] = g3[...]
    d1 = dx2[...] + dz
    da = d1.astype(BF)
    do1 = apply_wt(da, W, 3).astype(BF)
    weight_grad(4, flip(h2[...].astype(F32)).astype(BF), dqb)
    masks = head_masks(0.125)
    ones = head_masks(1.0)
    live = causal_mask()
    kT = flip(qkv[1].astype(F32)).astype(BF)
    qs, ks, vs = [], [], []
    for g in range(3):
        cols = slice(256 * g, 256 * g + 256)
        q4 = qkv[0, :, cols]
        d4 = do1[:, cols]
        q4s = jnp.concatenate([q4 * m for m in masks], axis=0)
        d4s = jnp.concatenate([d4 * m for m in ones], axis=0)
        sT = dot(qkv[1, :, cols], q4s, 1, 1)
        gT = dot(qkv[2, :, cols], d4s, 1, 1)
        ps, gs = [], []
        for n in range(4):
            s = jnp.where(live, sT[:, 128 * n:128 * n + 128], NEG)
            p = jnp.exp(s - L1[4 * g + n:4 * g + n + 1, :])
            gt = gT[:, 128 * n:128 * n + 128]
            ps.append(p.astype(BF))
            gs.append((p * (gt - jnp.sum(p * gt, axis=0, keepdims=True))).astype(BF))
        sg = jnp.concatenate(gs, axis=1)
        vs.append(dot(jnp.concatenate(ps, axis=1), d4s).astype(BF))
        ks.append(dot(sg, q4s).astype(BF))
        qT = dot(kT[256 * g:256 * g + 256, :], sg)
        qs += [qT[64 * n:64 * n + 64, 128 * n:128 * n + 128] for n in range(4)]
    for e in range(16):
        gm_load(e).wait()
        gm_store(e).start()
    inc = [(0.125 * unflip(jnp.concatenate(qs, axis=0))).astype(BF), jnp.concatenate(ks, axis=1), jnp.concatenate(vs, axis=1)]
    weight_grad(3, flip(o1[...].astype(F32)).astype(BF), da)
    for c in loads[:6]:
        c.wait()
    u = apply_wt(inc[0], W, 0) + apply_wt(inc[1], W, 1) + apply_wt(inc[2], W, 2)
    x = x_ref[...].astype(F32)
    inv = rms(x)
    dz, gain = rms_back(x, inv, gains[0:1, :], u)
    gb[0:1, :] = gain
    gin[...] = d1 + dz
    hT = flip(h1[...].astype(F32)).astype(BF)
    for k in range(3):
        weight_grad(k, hT, inc[k])
    lane = lax.broadcasted_iota(jnp.int32, (8, 128), 1)
    for d in range(8):
        lo, sh = 96 * d // 128, 96 * d % 128
        t = pltpu.roll(gb[:, 128 * lo:128 * lo + 128], (128 - sh) % 128, 1)
        if sh > 32:
            nxt = pltpu.roll(gb[:, 128 * lo + 128:128 * lo + 256], (128 - sh) % 128, 1)
            t = jnp.where(lane < 128 - sh, t, nxt)
        tile[d] = jnp.where(lane < 96, t, 0.0)
    for c in stores:
        c.wait()
    for e in range(16):
        gm_store(e).wait()

def self_bwd(dq2, h2, x1, dx2, qkv, o1, L1, x, h1, gains, g3, A, GA, gm):
    D = pltpu.SemaphoreType.DMA
    return pl.pallas_call(
        self_bwd_kernel,
        out_shape=(SDS((128, 768), F32), SDS((8, 8, 128), F32), SDS((16, 768, 384), BF), SDS((16, 192, 768), F32)),
        in_specs=[VS] * 11 + [HS] * 3, out_specs=(VS, VS, HS, HS),
        input_output_aliases={12: 2},
        scratch_shapes=[pltpu.VMEM((10, 768, 384), BF), pltpu.VMEM((10, 768, 384), BF), pltpu.VMEM((8, 768), F32), pltpu.VMEM((16, 192, 768), F32), D((10,)), D((10,)), D((32,))],
        compiler_params=pltpu.CompilerParams(vmem_limit_bytes=60 << 20),
        name="self_backward",
    )(dq2, h2, x1, dx2, qkv, o1, L1, x, h1, gains, g3, A, GA, gm)

def adam_kernel(*refs):
    ins, outs = refs[:16], refs[16:]
    for n in range(4):
        w, m, v, g = ins[4 * n:4 * n + 4]
        grad = g[0:3, 0:6] if n == 3 else g[...]
        for o, val in zip(outs[4 * n:4 * n + 4], adam_update(w[...], m[...], v[...], grad, rate_gain if n == 3 else rate_matrix)):
            o[...] = val

def adam(*args):
    shapes = []
    for n in range(4):
        s = args[4 * n].shape
        shapes += [SDS(s, F32)] * 3 + [SDS(s, BF)]
    return pl.pallas_call(adam_kernel, out_shape=tuple(shapes), in_specs=[VS] * 16, out_specs=(VS,) * 16,
                          compiler_params=pltpu.CompilerParams(vmem_limit_bytes=60 << 20), name="adam")(*args)


def body(
    dec_input,
    memory,
    mem_len,
    grad_out,
    attn_master,
    ffn_in_master,
    ffn_out_master,
    gain_master,
    attn_first,
    ffn_in_first,
    ffn_out_first,
    gain_first,
    attn_second,
    ffn_in_second,
    ffn_out_second,
    gain_second,
):
    swap = lambda a: a.transpose(1, 0, 2)
    attn_t, in_t = swap(attn_master), swap(ffn_in_master)
    gath_a, gains, lens, blk_b, blk_c = gather(attn_t, in_t, ffn_out_master, info_tile(gain_master, mem_len))
    aw = gath_a.reshape(16, 768, 384)
    x = dec_input[0]
    q2, h1, qkv, o1, x1, h2, L1 = self_fwd(x, gains, aw)
    q_all, k_two, v_two, kt_two, gath_b, gath_c, o2, L2 = cross_fwd(q2, lens, blk_b, blk_c, memory, aw)
    out_block, do2, st, dx2, g3, GA, GB, GC = ffn(x1, o2, L2, grad_out[0], gains, aw, gath_b.reshape(16, 768, 256), gath_c.reshape(8, 256, 768))
    dq2, blk_f, share_c, gm, GA = cross_bwd(
        do2, st, lens, q_all, k_two, v_two, kt_two, memory, aw,
        GB.reshape(4, 4, 4, 2, 2, 48, 256), GC.reshape(4, 2, 4, 4, 16, 768), GA,
    )
    grad_input, tile_g, GA, grad_memory = self_bwd(dq2, h2, x1, dx2, qkv, o1, L1, x, h1, gains, g3, aw, GA, gm)
    share_a, share_b, share_g = scatter(GA.reshape(4, 4, 4, 2, 3, 32, 384), blk_f, tile_g)
    new = adam(
        attn_t, swap(attn_first), swap(attn_second), share_a,
        in_t, swap(ffn_in_first), swap(ffn_in_second), share_b,
        ffn_out_master, ffn_out_first, ffn_out_second, share_c,
        gain_master, gain_first, gain_second, share_g,
    )
    return (out_block[None], grad_input[None], grad_memory, *[swap(a) for a in new[:8]], *new[8:])


def solution(mesh):
    placed = (
        P(("dp", "seq"), None, None),
        P("dp", "seq", None),
        P(("dp", "seq")),
        P(("dp", "seq"), None, None),
        P(None, ("dp", "seq"), None),
        P(None, ("dp", "seq"), None),
        P(("dp", "seq"), None),
        P(None, ("dp", "seq")),
        P(None, ("dp", "seq"), None),
        P(None, ("dp", "seq"), None),
        P(("dp", "seq"), None),
        P(None, ("dp", "seq")),
        P(None, ("dp", "seq"), None),
        P(None, ("dp", "seq"), None),
        P(("dp", "seq"), None),
        P(None, ("dp", "seq")),
    )
    return jax.shard_map(
        body,
        mesh=mesh,
        in_specs=placed,
        out_specs=(
            P(("dp", "seq"), None, None),
            P(("dp", "seq"), None, None),
            P("dp", "seq", None),
            P(None, ("dp", "seq"), None),
            P(None, ("dp", "seq"), None),
            P(None, ("dp", "seq"), None),
            P(None, ("dp", "seq"), None),
            P(None, ("dp", "seq"), None),
            P(None, ("dp", "seq"), None),
            P(None, ("dp", "seq"), None),
            P(None, ("dp", "seq"), None),
            P(("dp", "seq"), None),
            P(("dp", "seq"), None),
            P(("dp", "seq"), None),
            P(("dp", "seq"), None),
            P(None, ("dp", "seq")),
            P(None, ("dp", "seq")),
            P(None, ("dp", "seq")),
            P(None, ("dp", "seq")),
        ),
        check_vma=False,
    )
```

```python
import jax
import jax.numpy as jnp
from jax import lax
from jax.experimental import pallas as pl
from jax.experimental.pallas import tpu as pltpu
from jax.sharding import PartitionSpec as P

eps_norm = 1e-06
beta_one = 0.9
beta_two = 0.999
adam_eps = 1e-08
decay_rate = 0.01
rate_matrix = 0.12
rate_gain = 3.0
STEP = 10
MESH = pl.DeviceIdType.MESH
BF, F32 = jnp.bfloat16, jnp.float32
ALL = slice(None)
NEG = -1e30
PARTS_A = (("A", 0, "xyz"), ("A", 1, "yzx"), ("A", 2, "zxy"))
PARTS_F = (("B", 0, "xyz"), ("B", 1, "yxz"), ("C", 0, "xyz"))
PLANE = ("xy", "yx") * 3
PARTS_D = tuple(("D", n, PLANE[n]) for n in range(6))
AXES = {"A": "xyz", "B": "xyz", "C": "zxy", "D": "xy"}
STEPS = (2, -1, 1, 0)
VS = pl.BlockSpec(memory_space=pltpu.VMEM)
HS = pl.BlockSpec(memory_space=pltpu.HBM)
SDS = jax.ShapeDtypeStruct
DMA = pltpu.SemaphoreType.DMA


def vm(*shape):
    return pltpu.VMEM(shape, BF)


def vf(*shape):
    return pltpu.VMEM(shape, F32)


def where_am_i():
    dp, sq = lax.axis_index("dp"), lax.axis_index("seq")
    return {"x": sq // 4, "y": sq % 4, "z": dp // 2, "c": dp % 2}


def dev(at):
    return (at["z"] * 2 + at["c"], at["x"] * 4 + at["y"])


def moved(at, axis, step):
    return {**at, axis: (at[axis] + step + 4) % 4}


def offset(me, j, sign=1):
    return {**me, "x": (me["x"] + sign * (j // 4) + 4) % 4, "y": (me["y"] + sign * (j % 4) + 4) % 4}


def sibling_of(me):
    return {**me, "c": 1 - me["c"]}


def remote(src, dst, send, recv, to):
    return pltpu.make_async_remote_copy(src, dst, send, recv, device_id=dev(to), device_id_type=MESH)


def meet(me, column):
    dp, sq = lax.axis_index("dp"), lax.axis_index("seq")
    bar = pltpu.get_barrier_semaphore()
    for i in range(1, 16):
        pl.semaphore_signal(bar, inc=1, device_id=(dp, (sq + i) % 16), device_id_type=MESH)
    if column == "dp":
        for i in range(1, 8):
            pl.semaphore_signal(bar, inc=1, device_id=((dp + i) % 8, sq), device_id_type=MESH)
        return bar, 22
    if column == "z":
        for to in (moved(me, "z", 1), moved(me, "z", -1), sibling_of(me)):
            pl.semaphore_signal(bar, inc=1, device_id=dev(to), device_id_type=MESH)
        return bar, 18
    return bar, 15


def dot(a, b, ca=1, cb=0):
    return lax.dot_general(a, b, (((ca,), (cb,)), ((), ())), preferred_element_type=F32)


class Gather:
    def __init__(self, me, orders, view, own, ss, rs, sib_s=None, sib_r=None):
        self.me, self.orders, self.view, self.own = me, orders, view, own
        self.ss, self.rs, self.sib_s, self.sib_r = ss, rs, sib_s, sib_r
        self.count, self.last = len(orders), len(orders[0]) - 1

    def group(self, n, t, step, half=None):
        order = self.orders[n]
        at = moved(self.me, order[t], step)
        for j in range(t):
            at = {**at, order[j]: ALL}
        if half is not None and t:
            at = {**at, order[0]: pl.ds(2 * half, 2)}
        return at

    def kinds(self, n, t):
        return (0, 1, 2, 3) if t else (0, 1, 2 + n % 2)

    def copy(self, n, t, kind, back=0):
        axis = self.orders[n][t]
        step = 1 if kind in (0, 2) else -1
        dst = self.view(n, self.group(n, t, back) if kind < 2 else self.group(n, t, back - step, kind - 2))
        src = self.own(n) if t == 0 and kind < 2 and back == 0 else dst
        return remote(src, dst, self.ss.at[n, t, kind], self.rs.at[n, t, kind], moved(self.me, axis, step))

    def arrived(self, n, t, kind):
        self.copy(n, t, kind, -1 if kind in (0, 2) else 1).wait_recv()

    def sibling(self, n, j, c):
        v = self.view(n, {**self.group(n, self.last, (0, -1, 1, 2)[j]), "c": c})
        return remote(v, v, self.sib_s.at[n, j], self.sib_r.at[n, j], sibling_of(self.me))

    def send(self, t, ns=None):
        for n in ns or range(self.count):
            if t:
                for k in self.kinds(n, t - 1)[2:]:
                    self.arrived(n, t - 1, k)
            self.copy(n, t, 0).start()
            self.copy(n, t, 1).start()
            if self.sib_s is not None and t == self.last:
                self.sibling(n, 0, self.me["c"]).start()

    def forward(self, t, ns=None):
        for n in ns or range(self.count):
            for k in (0, 1):
                self.arrived(n, t, k)
                if 2 + k in self.kinds(n, t):
                    self.copy(n, t, 2 + k).start()
                if self.sib_s is not None and t == self.last:
                    self.sibling(n, 1 + k, self.me["c"]).start()

    def finish(self, ns=None):
        for n in ns or range(self.count):
            for k in (2, 3):
                self.arrived(n, self.last, k)
            if self.sib_s is not None:
                self.sibling(n, 3, self.me["c"]).start()

    def siblings_in(self):
        for n in range(self.count):
            for j in range(4):
                self.sibling(n, j, 1 - self.me["c"]).wait_recv()

    def drain(self):
        for n in range(self.count):
            for t in range(self.last + 1):
                for k in self.kinds(n, t):
                    self.copy(n, t, k).wait_send()
            if self.sib_s is not None:
                for j in range(4):
                    self.sibling(n, j, self.me["c"]).wait_send()


class Scatter:
    def __init__(self, me, parts, acc, hop, fin, ss, rs, sib=None, source=None, sib_s=None, sib_r=None, loc_s=None):
        self.me, self.parts, self.acc, self.hop_b, self.fin_b = me, parts, acc, hop, fin
        self.ss, self.rs, self.sib, self.source = ss, rs, sib, source
        self.sib_s, self.sib_r, self.loc_s = sib_s, sib_r, loc_s
        self.count, self.last = len(parts), len(parts[0][2]) - 1

    def idx(self, n, at):
        name, p, _ = self.parts[n]
        place = tuple(at[a] for a in AXES[name])
        return place if name == "C" else (p,) + place

    def slot(self, n):
        name, p, _ = self.parts[n]
        return () if name == "C" else (p,)

    def done(self, n, t):
        name, _, order = self.parts[n]
        return [a for a in AXES[name] if a in order[:t]]

    def group(self, n, t, step, half=None):
        order = self.parts[n][2]
        at = moved(self.me, order[t], step)
        for j in range(t):
            at = {**at, order[j]: ALL}
        if half is not None and t:
            at = {**at, self.done(n, t)[0]: pl.ds(2 * half, 2)}
        return at

    def kinds(self, n, t):
        return (0, 1) if t else (n % 2,)

    def refs(self, n, t):
        name = self.parts[n][0]
        return self.acc[name], self.hop_b[t][name], self.fin_b[t][name]

    def hop_copy(self, n, t, kind):
        step = 1 if kind == 0 else -1
        a, h, _ = self.refs(n, t)
        return remote(a.at[self.idx(n, self.group(n, t, 2 * step, kind))], h.at[self.slot(n) + (kind,)],
                      self.ss.at[n, t, kind], self.rs.at[n, t, kind], moved(self.me, self.parts[n][2][t], step))

    def fin_copy(self, n, t, kind):
        step = 1 if kind == 0 else -1
        a, _, f = self.refs(n, t)
        return remote(a.at[self.idx(n, self.group(n, t, step))], f.at[self.slot(n) + (kind,)],
                      self.ss.at[n, t, 2 + kind], self.rs.at[n, t, 2 + kind], moved(self.me, self.parts[n][2][t], step))

    def each(self, n, t, at, fn, half=None):
        axes = self.done(n, t)
        sizes, offs = [4] * len(axes), [0] * len(axes)
        if half is not None and axes:
            sizes[0], offs[0] = 2, 2 * half
        total = 1
        for s in sizes:
            total *= s

        def one(i):
            pos, rest = [], i
            for s in sizes[::-1]:
                pos.append(rest % s)
                rest = rest // s
            pos = pos[::-1]
            where = dict(at)
            for a, p, o in zip(axes, pos, offs):
                where[a] = p + o
            fn(self.idx(n, where), tuple(pos))

        if total == 1:
            one(0)
        else:
            pl.loop(0, total)(one)

    def sib_copy(self, n, j):
        at = self.group(n, self.last, STEPS[j])
        return remote(self.source(n, at, 1 - self.me["c"]), self.sib[self.parts[n][0]].at[self.idx(n, at)],
                      self.sib_s.at[n, j], self.sib_r.at[n, j], sibling_of(self.me))

    def loc_copy(self, n, j):
        at = self.group(n, self.last, STEPS[j])
        return pltpu.make_async_copy(self.source(n, at, self.me["c"]), self.acc[self.parts[n][0]].at[self.idx(n, at)], self.loc_s.at[n, j])

    def start(self):
        for j in range(4):
            for n in range(self.count):
                self.sib_copy(n, j).start()
                self.loc_copy(n, j).start()

    def merge(self, j):
        for n in range(self.count):
            self.sib_copy(n, j).wait_recv()
            self.loc_copy(n, j).wait()
            a, b = self.acc[self.parts[n][0]], self.sib[self.parts[n][0]]

            def fn(i, _):
                a[i] = (a[i].astype(F32) + b[i].astype(F32)).astype(BF)

            self.each(n, self.last, self.group(n, self.last, STEPS[j]), fn)

    def hop(self, t, ns=None):
        for n in ns or range(self.count):
            for k in self.kinds(n, t):
                self.hop_copy(n, t, k).start()

    def pass_on(self, t, ns=None):
        for n in ns or range(self.count):
            a, h, _ = self.refs(n, t)
            for k in (0, 1):
                if k in self.kinds(n, t):
                    self.hop_copy(n, t, k).wait_recv()

                    def fn(i, pos):
                        j = self.slot(n) + (k,) + pos
                        a[i] = (a[i].astype(F32) + h[j].astype(F32)).astype(BF)

                    self.each(n, t, self.group(n, t, 1 if k == 0 else -1), fn, k)
                self.fin_copy(n, t, k).start()

    def close(self, t, ns=None):
        for n in ns or range(self.count):
            self.fin_copy(n, t, 0).wait_recv()
            self.fin_copy(n, t, 1).wait_recv()
            a, _, f = self.refs(n, t)

            def fn(i, pos):
                s = self.slot(n)
                a[i] = (a[i].astype(F32) + f[s + (0,) + pos].astype(F32) + f[s + (1,) + pos].astype(F32)).astype(BF)

            self.each(n, t, self.group(n, t, 0), fn)

    def result(self, n):
        self.fin_copy(n, 0, 0).wait_recv()
        self.fin_copy(n, 0, 1).wait_recv()
        a, _, f = self.refs(n, 0)
        s = self.slot(n)
        return a[self.idx(n, self.me)].astype(F32) + f[s + (0,)].astype(F32) + f[s + (1,)].astype(F32)

    def drain(self):
        for n in range(self.count):
            if self.sib is not None:
                for j in range(4):
                    self.sib_copy(n, j).wait_send()
            for t in range(self.last + 1):
                for k in self.kinds(n, t):
                    self.hop_copy(n, t, k).wait_send()
                self.fin_copy(n, t, 0).wait_send()
                self.fin_copy(n, t, 1).wait_send()


def places(names, refs):
    return dict(zip(names, refs))


def stage_buffers(*shapes):
    out = []
    for lead in ((2, 2, 4), (2, 4, 4), (2, 2), (2, 4), (2,), (2,)):
        out += [vm(*pre, *lead, *block) for pre, block in shapes]
    return out


def staged(names, refs):
    k = len(names)
    got = [places(names, refs[k * i:k * i + k]) for i in range(6)]
    return {2: got[0], 1: got[2], 0: got[4]}, {2: got[1], 1: got[3], 0: got[5]}


def gather_kernel(attn, wi, wo, info, A, gains, lens, outB, outC, infos, stage, recv, blk, blkA, irecv,
                  ss, rs, sib_s, sib_r, as_, ar_, is_, ir_, ds_, dr_, own_s):
    me = where_am_i()
    dp, sq = lax.axis_index("dp"), lax.axis_index("seq")
    bar, count = meet(me, "dp")
    stage[:, 6:8, :] = jnp.zeros((16, 2, 640), F32)
    for s in range(16):
        stage[s, 0:6, 0:384] = attn[:, s // 2, 384 * (s % 2):384 * (s % 2) + 384]
        stage[s, 0:6, 384:640] = wi[:, s // 8, 256 * (s % 8):256 * (s % 8) + 256]
    pl.semaphore_wait(bar, count)

    def a2a(i):
        peer = (sq + i) % 16
        return pltpu.make_async_remote_copy(stage.at[peer], recv.at[sq], as_.at[i], ar_.at[i], device_id=(dp, peer), device_id_type=MESH)

    def inf(i):
        peer = (sq + i) % 16
        return pltpu.make_async_remote_copy(info, irecv.at[sq], is_.at[i], ir_.at[i], device_id=(dp, peer), device_id_type=MESH)

    for i in range(1, 16):
        a2a(i).start()
    for i in range(1, 16):
        inf(i).start()
    recv[sq] = stage[sq]
    irecv[sq] = info[...]
    outC[...] = wo[...].astype(BF)
    for i in range(1, 16):
        a2a(i).wait_recv()
    for k in range(16):
        blk[6 * k:6 * k + 6, :] = recv[k, 0:6, :]
    for p in range(3):
        blkA[p] = blk[32 * p:32 * p + 32, 0:384].astype(BF)
    for p in range(2):
        outB[p] = blk[48 * p:48 * p + 48, 384:640].astype(BF)
    place = lambda n, at: A.at[at["x"], at["y"], at["z"], at["c"], PARTS_A[n][1]]
    ring = Gather(me, [p[2] for p in PARTS_A], place, lambda n: blkA.at[n], ss, rs, sib_s, sib_r)
    owns = [pltpu.make_async_copy(blkA.at[n], place(n, me), own_s.at[n]) for n in range(3)]
    for o in owns:
        o.start()
    ring.send(0)
    ring.forward(0)
    for o in owns:
        o.wait()
    ring.send(1)
    ring.forward(1)
    ring.send(2)
    for i in range(1, 16):
        inf(i).wait_recv()
    tile = jnp.sum(irecv[...], axis=0)
    infos[dp] = tile

    def dpx(i, back=0):
        v = infos.at[(dp - back + 8) % 8]
        return pltpu.make_async_remote_copy(v, v, ds_.at[i], dr_.at[i], device_id=((dp + i) % 8, sq), device_id_type=MESH)

    for i in range(1, 8):
        dpx(i).start()
    ring.forward(2)
    for i in range(1, 8):
        dpx(i, i).wait_recv()
    lane = lax.broadcasted_iota(jnp.int32, (8, 128), 1)
    gains[...] = jnp.zeros((8, 768), F32)
    for d in range(8):
        lo, sh = 96 * d // 128, 96 * d % 128
        t = pltpu.roll(jnp.where(lane < 96, infos[d], 0.0), sh, 1)
        gains[:, 128 * lo:128 * lo + 128] += jnp.where(lane >= sh, t, 0.0)
        if sh > 32:
            gains[:, 128 * lo + 128:128 * lo + 256] += jnp.where(lane < sh, t, 0.0)
    pick = lax.broadcasted_iota(jnp.int32, (16, 128), 0) == lax.broadcasted_iota(jnp.int32, (16, 128), 1)
    lens[...] = jnp.broadcast_to(jnp.sum(jnp.where(pick, tile[3:4, :], 0.0), axis=1, keepdims=True), (16, 128))
    ring.finish()
    ring.siblings_in()
    for i in range(1, 16):
        a2a(i).wait_send()
        inf(i).wait_send()
    for i in range(1, 8):
        dpx(i).wait_send()
    ring.drain()


def gather(attn, wi, wo, info):
    return pl.pallas_call(
        gather_kernel,
        out_shape=(SDS((4, 4, 4, 2, 3, 32, 384), BF), SDS((8, 768), F32), SDS((16, 128), F32), SDS((2, 48, 256), BF), SDS((16, 768), BF)),
        in_specs=[VS] * 4, out_specs=(HS,) + (VS,) * 4,
        scratch_shapes=[vf(8, 8, 128), vf(16, 8, 640), vf(16, 8, 640), vf(96, 640), vm(3, 32, 384), vf(16, 8, 128),
                        DMA((3, 3, 4)), DMA((3, 3, 4)), DMA((3, 4)), DMA((3, 4)), DMA((16,)), DMA((16,)), DMA((16,)), DMA((16,)), DMA((8,)), DMA((8,)), DMA((3,))],
        compiler_params=pltpu.CompilerParams(collective_id=0, has_side_effects=True, vmem_limit_bytes=60 << 20),
        name="gather_attention_weights",
    )(attn, wi, wo, info)


def info_tile(gain, mem_len):
    sq = lax.axis_index("seq")
    t = jnp.zeros((8, 128), F32)
    t = lax.dynamic_update_slice(t, gain.astype(BF).astype(F32), (0, 6 * sq))
    return lax.dynamic_update_slice(t, mem_len.astype(F32)[:, None], (3, sq))


def scatter_kernel(GA, blkF, gg, oA, oB, oG, accA, sibA, h2, f2, h1, f1, h0, f0, blk, stage, recv, gdp, gsum, gsq,
                   ss, rs, sib_s, sib_r, loc_s, as_, ar_, is_, ir_, ds_, dr_):
    me = where_am_i()
    dp, sq = lax.axis_index("dp"), lax.axis_index("seq")
    bar, count = meet(me, "dp")
    pl.semaphore_wait(bar, count)
    hop, fin = staged("A", (h2, f2, h1, f1, h0, f0))
    ring = Scatter(me, PARTS_A, {"A": accA}, hop, fin, ss, rs, {"A": sibA},
                   lambda n, at, c: GA.at[at["x"], at["y"], at["z"], c, n], sib_s, sib_r, loc_s)
    ring.start()

    def dpx(i):
        peer = (dp + i) % 8
        return pltpu.make_async_remote_copy(gg.at[peer], gdp.at[dp], ds_.at[i], dr_.at[i], device_id=(peer, sq), device_id_type=MESH)

    for i in range(1, 8):
        dpx(i).start()
    gdp[dp] = gg[dp]
    ring.merge(0)
    ring.hop(2)
    ring.merge(1)
    ring.merge(2)
    ring.pass_on(2)
    ring.merge(3)
    for i in range(1, 8):
        dpx(i).wait_recv()
    gsum[...] = jnp.sum(gdp[...], axis=0)

    def inf(i):
        peer = (sq + i) % 16
        return pltpu.make_async_remote_copy(gsum, gsq.at[sq], is_.at[i], ir_.at[i], device_id=(dp, peer), device_id_type=MESH)

    for i in range(1, 16):
        inf(i).start()
    gsq[sq] = gsum[...]
    blk[:, 384:640] = blkF[...]
    stage[:, 6:8, :] = jnp.zeros((16, 2, 640), F32)
    ring.close(2)
    ring.hop(1)
    ring.pass_on(1)
    ring.close(1)
    ring.hop(0)
    ring.pass_on(0)
    for n in range(3):
        blk[32 * n:32 * n + 32, 0:384] = ring.result(n)
    for k in range(16):
        stage[k, 0:6, :] = blk[6 * k:6 * k + 6, :]

    def a2a(i):
        peer = (sq + i) % 16
        return pltpu.make_async_remote_copy(stage.at[peer], recv.at[sq], as_.at[i], ar_.at[i], device_id=(dp, peer), device_id_type=MESH)

    for i in range(1, 16):
        a2a(i).start()
    recv[sq] = stage[sq]
    for i in range(1, 16):
        inf(i).wait_recv()
    oG[...] = pltpu.roll(jnp.sum(gsq[...], axis=0), (128 - 6 * sq) % 128, 1)
    for i in range(1, 16):
        a2a(i).wait_recv()
    for s in range(16):
        oA[:, s // 2, 384 * (s % 2):384 * (s % 2) + 384] = recv[s, 0:6, 0:384]
        oB[:, s // 8, 256 * (s % 8):256 * (s % 8) + 256] = recv[s, 0:6, 384:640]
    for i in range(1, 8):
        dpx(i).wait_send()
    for i in range(1, 16):
        a2a(i).wait_send()
        inf(i).wait_send()
    ring.drain()


def scatter(GA, blkF, gg):
    return pl.pallas_call(
        scatter_kernel,
        out_shape=(SDS((6, 8, 768), F32), SDS((6, 2, 2048), F32), SDS((8, 128), F32)),
        in_specs=[HS, VS, VS], out_specs=(VS,) * 3,
        scratch_shapes=[vm(3, 4, 4, 4, 32, 384), vm(3, 4, 4, 4, 32, 384), *stage_buffers(((3,), (32, 384))),
                        vf(96, 640), vf(16, 8, 640), vf(16, 8, 640), vf(8, 8, 128), vf(8, 128), vf(16, 8, 128),
                        DMA((3, 3, 4)), DMA((3, 3, 4)), DMA((3, 4)), DMA((3, 4)), DMA((3, 4)),
                        DMA((16,)), DMA((16,)), DMA((16,)), DMA((16,)), DMA((8,)), DMA((8,))],
        compiler_params=pltpu.CompilerParams(collective_id=1, has_side_effects=True, vmem_limit_bytes=60 << 20),
        name="scatter_attention_grads",
    )(GA, blkF, gg)


def head_masks(value=1.0):
    lane = lax.broadcasted_iota(jnp.int32, (1, 256), 1)
    return [jnp.where(lane // 64 == h, value, 0.0).astype(BF) for h in range(4)]


def stack_heads(block, masks):
    return jnp.concatenate([block * m for m in masks], axis=0)


def key_positions():
    sq = lax.axis_index("seq")
    return (192 * sq + lax.broadcasted_iota(jnp.int32, (192, 128), 0)).astype(F32)


def ffn_place(B, C):
    def place(n, at):
        if n < 2:
            return B.at[at["x"], at["y"], at["z"], at["c"], n]
        return C.at[at["z"], at["c"], at["x"], at["y"]]
    return place


class Merge:
    def __init__(self, me, src, mid, one, two, ss, rs):
        self.me, self.src, self.mid, self.bufs, self.ss, self.rs = me, src, mid, (one, two), ss, rs

    def block(self, n, a, b):
        return (n, a, b) if n % 2 == 0 else (n, b, a)

    def copy(self, n, t, k):
        axis = PLANE[n][t]
        to = moved(self.me, axis, (1, -1, 2)[k])
        src = self.src.at[self.block(n, to[axis], ALL)] if t == 0 else self.mid.at[n, to[axis]]
        return remote(src, self.bufs[t].at[n, k], self.ss.at[n, t, k], self.rs.at[n, t, k], to)

    def send(self, t, ns):
        for n in ns:
            for k in (2, 0, 1):
                self.copy(n, t, k).start()

    def join(self, blocks):
        rows = [b[128:144, :].astype(F32)[0:8, :] for b in blocks]
        logs = [r + pltpu.roll(r, 6, 0) + pltpu.roll(r, 4, 0) for r in rows]
        top = logs[0]
        for l in logs[1:]:
            top = jnp.maximum(top, l)
        ws = [jnp.exp(l - top) for l in logs]
        total = ws[0] + ws[1] + ws[2] + ws[3]
        inv = 1.0 / total
        out = []
        for h in range(2):
            o = sum(b[64 * h:64 * h + 64, :].astype(F32) * (w * inv)[h:h + 1, :] for b, w in zip(blocks, ws))
            out.append(o)
        return jnp.concatenate(out, axis=0), top + jnp.log(total)

    def middle(self, ns):
        for n in ns:
            for k in range(3):
                self.copy(n, 0, k).wait_recv()
            a = self.me[PLANE[n][0]]

            @pl.loop(0, 4)
            def _(b):
                o, l = self.join([self.src.at[self.block(n, a, b)]] + [self.bufs[0].at[n, k, b] for k in range(3)])
                self.mid[n, b, 0:128, :] = o.astype(BF)
                self.mid[n, b, 128:144, :] = log_tile(l)

    def result(self, n):
        for k in range(3):
            self.copy(n, 1, k).wait_recv()
        return self.join([self.mid.at[n, self.me[PLANE[n][1]]]] + [self.bufs[1].at[n, k] for k in range(3)])

    def drain(self):
        for n in range(6):
            for t in range(2):
                for k in range(3):
                    self.copy(n, t, k).wait_send()


def log_tile(l):
    l = jnp.where(lax.broadcasted_iota(jnp.int32, (8, 128), 0) < 2, l, 0.0)
    high = l.astype(BF).astype(F32)
    middle = (l - high).astype(BF).astype(F32)
    low = l - high - middle
    return jnp.concatenate([high + pltpu.roll(middle, 2, 0) + pltpu.roll(low, 4, 0), jnp.zeros((8, 128), F32)], axis=0).astype(BF)


def pair_of(ref, g, at):
    return jnp.concatenate([ref[2 * g, at["x"], at["y"]], ref[2 * g + 1, at["x"], at["y"]]], axis=1)


def cross_fwd_kernel(q, lens, blkB, blkC, mem_h, A, q_h, k_h, v_h, kt_h, B, C, o_ref, L_ref,
                     qall, mem, wk, wv, wkT, wvT, K, V, KT, VT, ost, mid, one, two, lrow,
                     mem_s, w_s, out_s, ss, rs, os_, or_, fs, fr, fsib_s, fsib_r, own_s):
    me = where_am_i()
    bar, count = meet(me, "z")

    def load_mem(e):
        return pltpu.make_async_copy(mem_h.at[e], mem.at[e], mem_s.at[e])

    loads = [pltpu.make_async_copy(A.at[10 + i], (wk if i < 2 else wv).at[:, pl.ds(384 * (i % 2), 384)], w_s.at[i]) for i in range(4)]
    for c in loads:
        c.start()

    @pl.loop(0, 16)
    def _(e):
        load_mem(e).start()

    for n in range(6):
        qall[n, me["x"], me["y"]] = q[:, 128 * n:128 * n + 128]
    place = ffn_place(B, C)
    mine = lambda n: blkB.at[n] if n < 2 else blkC
    owns = [pltpu.make_async_copy(mine(n), place(n, me), own_s.at[n]) for n in range(3)]
    for c in owns:
        c.start()
    lrow[...] = jnp.zeros((2, 8, 128), F32)
    pl.semaphore_wait(bar, count)
    view = lambda n, at: qall.at[n, at["x"], at["y"]]
    plane = Gather(me, PLANE, view, lambda n: view(n, me), ss, rs)
    ring = Gather(me, [p[2] for p in PARTS_F], place, mine, fs, fr, fsib_s, fsib_r)
    fold = Merge(me, ost, mid, one, two, os_, or_)
    plane.send(0)
    ring.send(0)
    for c in loads:
        c.wait()
    for i in range(6):
        wvT[:, 128 * i:128 * i + 128] = wv[128 * i:128 * i + 128, :].T
    plane.forward(0)
    ring.forward(0)
    for c in owns:
        c.wait()

    def project(a, b):
        @pl.loop(a, b)
        def _(e):
            load_mem(e).wait()
            K[e] = dot(mem[e], wk[...]).astype(BF)
            VT[e] = dot(wvT[...], mem[e], 1, 1).astype(BF)

    def project_more(a, b):
        @pl.loop(a, b)
        def _(e):
            V[e] = dot(mem[e], wv[...]).astype(BF)
            KT[e] = dot(wkT[...], mem[e], 1, 1).astype(BF)

    plane.send(1, (0, 1))
    project(0, 4)
    plane.send(1, (2, 3))
    plane.send(1, (4, 5))
    ring.send(1)
    project(4, 10)
    plane.forward(1, (0, 1))
    plane.forward(1, (2, 3))
    project(10, 16)
    ring.forward(1)
    plane.forward(1, (4, 5))
    ring.send(2)
    masks = head_masks()
    pos = key_positions()

    def attend(g):
        cols = slice(256 * g, 256 * g + 256)

        @pl.loop(0, 16)
        def _(j):
            at = offset(me, j)
            e = at["x"] * 4 + at["y"]
            live = pos < lens[pl.ds(e, 1), :]
            sT = dot(K[e, :, cols], stack_heads(pair_of(qall, g, at), masks), 1, 1)
            ps, inv = [], []
            for h in range(4):
                s = jnp.where(live, sT[:, 128 * h:128 * h + 128], NEG)
                top = jnp.max(s, axis=0, keepdims=True)
                p = jnp.exp(s - top)
                tot = jnp.sum(p, axis=0, keepdims=True)
                lrow[h // 2, h % 2:h % 2 + 1, :] = top + jnp.log(tot)
                ps.append(p.astype(BF))
                inv.append(1.0 / tot)
            oT = dot(VT[e, cols, :], jnp.concatenate(ps, axis=1))
            for h in range(4):
                ost[2 * g + h // 2, at["x"], at["y"], 64 * (h % 2):64 * (h % 2) + 64, :] = (
                    oT[64 * h:64 * h + 64, 128 * h:128 * h + 128] * inv[h]).astype(BF)
            for h in range(2):
                ost[2 * g + h, at["x"], at["y"], 128:144, :] = log_tile(lrow[h])

        fold.send(0, (2 * g, 2 * g + 1))

    def deliver(g):
        for n in (2 * g, 2 * g + 1):
            o, l = fold.result(n)
            o_ref[:, 128 * n:128 * n + 128] = o.T
            L_ref[2 * n:2 * n + 2, :] = l[0:2, :]

    plane.finish((0, 1))
    attend(0)
    plane.finish((2, 3))
    attend(1)
    fold.middle((0, 1))
    fold.send(1, (0, 1))
    plane.finish((4, 5))
    out_q = pltpu.make_async_copy(qall, q_h, out_s.at[0])
    out_q.start()
    attend(2)
    ring.forward(2)
    fold.middle((2, 3))
    fold.send(1, (2, 3))
    for i in range(6):
        wkT[:, 128 * i:128 * i + 128] = wk[128 * i:128 * i + 128, :].T
    project_more(0, 8)
    fold.middle((4, 5))
    fold.send(1, (4, 5))
    ring.finish()
    project_more(8, 16)
    outs = [pltpu.make_async_copy(a, b, out_s.at[1 + i]) for i, (a, b) in enumerate(((K, k_h), (V, v_h), (KT, kt_h)))]
    for c in outs:
        c.start()
    L_ref[12:16, :] = jnp.zeros((4, 128), F32)
    for g in range(3):
        deliver(g)
    plane.drain()
    fold.drain()
    for c in [out_q] + outs:
        c.wait()
    ring.siblings_in()
    ring.drain()


def cross_fwd(q, lens, blkB, blkC, memory, A):
    return pl.pallas_call(
        cross_fwd_kernel,
        out_shape=(SDS((6, 4, 4, 128, 128), BF), SDS((16, 192, 768), BF), SDS((16, 192, 768), BF), SDS((16, 768, 192), BF),
                   SDS((4, 4, 4, 2, 2, 48, 256), BF), SDS((4, 2, 4, 4, 16, 768), BF), SDS((128, 768), F32), SDS((16, 128), F32)),
        in_specs=[VS] * 4 + [HS] * 2, out_specs=(HS,) * 6 + (VS,) * 2,
        scratch_shapes=[vm(6, 4, 4, 128, 128), vm(16, 192, 768), vm(768, 768), vm(768, 768), vm(768, 768), vm(768, 768),
                        vm(16, 192, 768), vm(16, 192, 768), vm(16, 768, 192), vm(16, 768, 192),
                        vm(6, 4, 4, 144, 128), vm(6, 4, 144, 128), vm(6, 3, 4, 144, 128), vm(6, 3, 144, 128), vf(2, 8, 128),
                        DMA((16,)), DMA((4,)), DMA((4,)), DMA((6, 2, 4)), DMA((6, 2, 4)), DMA((6, 2, 3)), DMA((6, 2, 3)),
                        DMA((3, 3, 4)), DMA((3, 3, 4)), DMA((3, 4)), DMA((3, 4)), DMA((3,))],
        compiler_params=pltpu.CompilerParams(collective_id=2, has_side_effects=True, vmem_limit_bytes=60 << 20),
        name="cross_forward",
    )(q, lens, blkB, blkC, memory, A)


def cross_bwd_kernel(do, st, lens, q_h, k_h, v_h, kt_h, mem_h, A, GB, GC, G_in, dq_ref, fB, fC, gm_h, dw_h,
                     qall, doall, stall, wk, wv, K, V, KT, mem, memT, dK, dV, gst, wst, dst, dh1, df1, dh0, df0,
                     accB, accC, sibB, sibC, hB2, hC2, fB2, fC2, hB1, hC1, fB1, fC1, hB0, hC0, fB0, fC0,
                     q_s, kv_s, mem_s, w_s, gm_s, dw_s, ss, rs, ds_, dr_, fs, fr, fsib_s, fsib_r, floc):
    me = where_am_i()
    bar, count = meet(me, "z")

    def load_mem(e):
        return pltpu.make_async_copy(mem_h.at[pl.ds(pl.multiple_of(256 * e, 256), 256)], mem.at[e % 2], mem_s.at[e % 2])

    load_mem(0).start()
    load_mem(1).start()
    loads = [pltpu.make_async_copy(A.at[10 + i], (wk if i < 2 else wv).at[:, pl.ds(384 * (i % 2), 384)], w_s.at[i]) for i in range(4)]
    loads.append(pltpu.make_async_copy(q_h, qall, q_s))
    for n in range(6):
        doall[n, me["x"], me["y"]] = do[:, 128 * n:128 * n + 128]
    stall[me["x"], me["y"]] = st[...]
    pl.semaphore_wait(bar, count)

    def place(n, at):
        return stall.at[at["x"], at["y"]] if n == 6 else doall.at[n, at["x"], at["y"]]

    plane = Gather(me, PLANE + ("xy",), place, lambda n: place(n, me), ss, rs)
    fhop, ffin = staged("BC", (hB2, hC2, fB2, fC2, hB1, hC1, fB1, fC1, hB0, hC0, fB0, fC0))
    grads = ffn_place(GB, GC)
    ring = Scatter(me, PARTS_F, {"B": accB, "C": accC}, fhop, ffin, fs, fr, {"B": sibB, "C": sibC},
                   lambda n, at, c: grads(n, {**at, "c": c}), fsib_s, fsib_r, floc)
    back = Scatter(me, PARTS_D, {"D": dst}, {1: {"D": dh1}, 0: {"D": dh0}}, {1: {"D": df1}, 0: {"D": df0}}, ds_, dr_)
    plane.send(0, (6, 0, 1, 2, 3, 4, 5))
    ring.start()
    for c in loads:
        c.start()

    def turn(a, b):
        @pl.loop(a, b)
        def _(e):
            load_mem(e).wait()
            memT[:, pl.ds(pl.multiple_of(256 * e, 256), 256)] = mem[e % 2].T

            @pl.when(e < 10)
            def _():
                load_mem(e + 2).start()

    turn(0, 1)
    plane.forward(0, (6, 0, 1, 2, 3, 4, 5))
    turn(1, 3)
    plane.send(1, (6, 0, 1))
    plane.send(1, (2, 3))
    plane.send(1, (4, 5))
    ring.merge(0)
    ring.hop(2)
    turn(3, 6)
    plane.forward(1, (6, 0, 1))
    ring.merge(1)
    ring.merge(2)
    plane.forward(1, (2, 3))
    ring.pass_on(2)
    masks = head_masks()
    pos = key_positions()

    def where(i):
        return {**me, "x": (me["x"] + 2 + i // 4) % 4, "y": (me["y"] + 2 + i % 4) % 4}

    def load_kv(g, i, which):
        at = where(i)
        e = at["x"] * 4 + at["y"]
        cols = pl.ds(256 * g, 256)
        src = (k_h.at[e, :, cols], v_h.at[e, :, cols], kt_h.at[e, cols])[which]
        return pltpu.make_async_copy(src, (K, V, KT)[which].at[i % 2], kv_s.at[which, i % 2])

    for w in range(3):
        load_kv(0, 0, w).start()
    for c in loads:
        c.wait()

    def attend(g):
        cols = slice(256 * g, 256 * g + 256)

        @pl.loop(0, 16)
        def _(i):
            at = where(i)
            e = at["x"] * 4 + at["y"]

            @pl.when(i < 15)
            def _():
                for w in range(3):
                    load_kv(g, i + 1, w).start()

            for w in range(3):
                load_kv(g, i, w).wait()
            live = pos < lens[pl.ds(e, 1), :]
            rows = pl.ds(pl.multiple_of(192 * e, 192), 192)
            q4s = stack_heads(pair_of(qall, g, at), masks)
            d4s = stack_heads(pair_of(doall, g, at), masks)
            sT = dot(K[i % 2], q4s, 1, 1)
            gT = dot(V[i % 2], d4s, 1, 1)
            ps, gs = [], []
            for h in range(4):
                n = 4 * g + h
                s = jnp.where(live, sT[:, 128 * h:128 * h + 128], NEG)
                p = jnp.exp(s - stall[at["x"], at["y"], n:n + 1, :])
                ps.append(p.astype(BF))
                gs.append((p * (gT[:, 128 * h:128 * h + 128] - stall[at["x"], at["y"], 12 + n:13 + n, :])).astype(BF))
            sg = jnp.concatenate(gs, axis=1)
            dV[rows, cols] = dot(jnp.concatenate(ps, axis=1), d4s).astype(BF)
            dK[rows, cols] = dot(sg, q4s).astype(BF)
            qT = dot(KT[i % 2], sg)
            for h in range(4):
                dst[2 * g + h // 2, at["x"], at["y"], 64 * (h % 2):64 * (h % 2) + 64, :] = qT[64 * h:64 * h + 64, 128 * h:128 * h + 128].astype(BF)

        if g < 2:
            for w in range(3):
                load_kv(g + 1, 0, w).start()
        back.hop(1, (2 * g, 2 * g + 1))

    plane.finish((6, 0, 1))
    attend(0)
    plane.forward(1, (4, 5))
    plane.finish((2, 3))
    attend(1)
    back.pass_on(1, (0, 1))
    ring.merge(3)
    plane.finish((4, 5))
    attend(2)
    back.pass_on(1, (2, 3))
    back.close(1, (0, 1))
    back.hop(0, (0, 1))

    def gm_copy(e):
        return pltpu.make_async_copy(gst.at[e % 2], gm_h.at[e], gm_s.at[e % 2])

    def mem_grad(a, b):
        @pl.loop(a, b)
        def _(e):
            @pl.when(e > 1)
            def _():
                gm_copy(e - 2).wait()

            rows = pl.ds(pl.multiple_of(384 * e, 384), 384)
            gst[e % 2] = dot(dK[rows, :], wk[...], 1, 1) + dot(dV[rows, :], wv[...], 1, 1)
            gm_copy(e).start()

    def dw_copy(n, r):
        return pltpu.make_async_copy(wst.at[n % 2], dw_h.at[10 + n, pl.ds(pl.multiple_of(384 * r, 384), 384)], dw_s.at[n % 2])

    def weight_grad(n):
        src = dK if n < 2 else dV

        @pl.loop(0, 2)
        def _(r):
            @pl.when(r > 0)
            def _():
                dw_copy(n, r - 1).wait()

            wst[n % 2] = dot(memT[pl.ds(pl.multiple_of(384 * r, 384), 384), :], src[:, 384 * (n % 2):384 * (n % 2) + 384]).astype(BF)
            dw_copy(n, r).start()

        dw_copy(n, 1).wait()

    turn(6, 12)
    ring.close(2)
    ring.hop(1)
    back.pass_on(1, (4, 5))
    back.close(1, (2, 3))
    back.hop(0, (2, 3))
    back.pass_on(0, (0, 1))
    mem_grad(0, 4)
    back.close(1, (4, 5))
    back.hop(0, (4, 5))
    back.pass_on(0, (2, 3))
    ring.pass_on(1)
    mem_grad(4, 8)
    back.pass_on(0, (4, 5))
    ring.close(1)
    ring.hop(0)
    weight_grad(0)
    weight_grad(1)
    ring.pass_on(0)
    weight_grad(2)
    weight_grad(3)
    for n in range(6):
        dq_ref[:, 128 * n:128 * n + 128] = (0.125 * back.result(n)).T
    fB[0:48, :] = ring.result(0)
    fB[48:96, :] = ring.result(1)
    fC[...] = ring.result(2)
    gm_copy(6).wait()
    gm_copy(7).wait()
    plane.drain()
    ring.drain()
    back.drain()


def cross_bwd(do, st, lens, q_h, k_h, v_h, kt_h, memory, A, GB, GC, GA):
    bB, bC = (48, 256), (16, 768)
    return pl.pallas_call(
        cross_bwd_kernel,
        out_shape=(SDS((128, 768), F32), SDS((96, 256), F32), SDS((16, 768), F32), SDS((8, 384, 768), F32), SDS((16, 768, 384), BF)),
        in_specs=[VS] * 3 + [HS] * 9, out_specs=(VS,) * 3 + (HS,) * 2, input_output_aliases={11: 4},
        scratch_shapes=[vm(6, 4, 4, 128, 128), vm(6, 4, 4, 128, 128), vf(4, 4, 24, 128), vm(768, 768), vm(768, 768),
                        vm(2, 192, 256), vm(2, 192, 256), vm(2, 256, 192), vm(2, 256, 768), vm(768, 3072), vm(3072, 768), vm(3072, 768),
                        vf(2, 384, 768), vm(2, 384, 384), vm(6, 4, 4, 128, 128), vm(6, 2, 2, 128, 128), vm(6, 2, 4, 128, 128), vm(6, 2, 128, 128), vm(6, 2, 128, 128),
                        vm(2, 4, 4, 4, *bB), vm(4, 4, 4, *bC), vm(2, 4, 4, 4, *bB), vm(4, 4, 4, *bC), *stage_buffers(((2,), bB), ((), bC)),
                        DMA, DMA((3, 2)), DMA((2,)), DMA((4,)), DMA((2,)), DMA((2,)), DMA((7, 2, 4)), DMA((7, 2, 4)), DMA((6, 2, 4)), DMA((6, 2, 4)),
                        DMA((3, 3, 4)), DMA((3, 3, 4)), DMA((3, 4)), DMA((3, 4)), DMA((3, 4))],
        compiler_params=pltpu.CompilerParams(collective_id=3, has_side_effects=True, vmem_limit_bytes=60 << 20),
        name="cross_backward",
    )(do, st, lens, q_h, k_h, v_h, kt_h, memory.reshape(3072, 768), A, GB, GC, GA)


def adam_update(master, first, second, grad, rate):
    first_new = beta_one * first + (1.0 - beta_one) * grad
    second_new = beta_two * second + (1.0 - beta_two) * grad * grad
    fix_one = 1.0 - beta_one**STEP
    fix_two = 1.0 - beta_two**STEP
    master_new = master - rate * (
        first_new / fix_one / (jnp.sqrt(second_new / fix_two) + adam_eps) + decay_rate * master
    )
    return (master_new, first_new, second_new, master_new.astype(jnp.bfloat16))


def rms(x):
    return lax.rsqrt(jnp.mean(x * x, axis=-1, keepdims=True) + eps_norm)

def rms_back(x, inv, gain, u):
    scaled = u * gain
    inner = jnp.mean(scaled * x, axis=-1, keepdims=True)
    return inv * scaled - x * inv * inv * inv * inner, jnp.sum(u * x * inv, axis=0, keepdims=True)

def flip(x):
    return jnp.concatenate([x[:, 128 * i:128 * i + 128].T for i in range(x.shape[1] // 128)], axis=0)

def unflip(x):
    return jnp.concatenate([x[128 * i:128 * i + 128, :].T for i in range(x.shape[0] // 128)], axis=1)

def apply_w(h, W, k):
    return jnp.concatenate([dot(h, W[2 * k]), dot(h, W[2 * k + 1])], axis=1)

def apply_wt(u, W, k):
    return dot(u[:, 0:384], W[2 * k], 1, 1) + dot(u[:, 384:768], W[2 * k + 1], 1, 1)

def causal_mask():
    return lax.broadcasted_iota(jnp.int32, (128, 128), 0) <= lax.broadcasted_iota(jnp.int32, (128, 128), 1)

def self_fwd_kernel(x_ref, gains, A, q2, h1, qkv, o1, x1, h2, L1, W, sem):
    loads = [pltpu.make_async_copy(A.at[i], W.at[i], sem.at[i]) for i in range(10)]
    for c in loads:
        c.start()
    x = x_ref[...].astype(F32)
    h = (x * rms(x) * gains[0:1, :]).astype(BF)
    h1[...] = h
    for k in range(3):
        loads[2 * k].wait()
        loads[2 * k + 1].wait()
        full = apply_w(h, W, k)
        qkv[k] = full.astype(BF)
    vT = flip(full).astype(BF)
    masks = head_masks(0.125)
    live = causal_mask()
    outs = []
    for g in range(3):
        cols = slice(256 * g, 256 * g + 256)
        q4 = qkv[0, :, cols]
        sT = dot(qkv[1, :, cols], jnp.concatenate([q4 * m for m in masks], axis=0), 1, 1)
        ps = []
        for n in range(4):
            s = jnp.where(live, sT[:, 128 * n:128 * n + 128], NEG)
            top = jnp.max(s, axis=0, keepdims=True)
            lse = top + jnp.log(jnp.sum(jnp.exp(s - top), axis=0, keepdims=True))
            L1[4 * g + n:4 * g + n + 1, :] = lse
            ps.append(jnp.exp(s - lse).astype(BF))
        oT = dot(vT[256 * g:256 * g + 256, :], jnp.concatenate(ps, axis=1))
        outs += [oT[64 * n:64 * n + 64, 128 * n:128 * n + 128] for n in range(4)]
    o = unflip(jnp.concatenate(outs, axis=0)).astype(BF)
    o1[...] = o
    for c in loads[6:]:
        c.wait()
    x = x + apply_w(o, W, 3)
    x1[...] = x
    h = (x * rms(x) * gains[1:2, :]).astype(BF)
    h2[...] = h
    q2[...] = apply_w(h, W, 4).astype(BF) * jnp.asarray(0.125, BF)

def self_fwd(x, gains, A):
    row = SDS((128, 768), BF)
    return pl.pallas_call(
        self_fwd_kernel,
        out_shape=(row, row, SDS((3, 128, 768), BF), row, SDS((128, 768), F32), row, SDS((16, 128), F32)),
        in_specs=[VS, VS, HS], out_specs=(VS,) * 7,
        scratch_shapes=[pltpu.VMEM((10, 768, 384), BF), pltpu.SemaphoreType.DMA((10,))],
        compiler_params=pltpu.CompilerParams(vmem_limit_bytes=60 << 20),
        name="self_forward",
    )(x, gains, A)

def ffn_kernel(x1, o2, L2, dy_ref, gains, A, B, C, out, do2, st, dx2, gg, GA, GB, GC,
               W7, WB, WC, gA, gB, gC, sw, sb, sc, tb, tc, ta):
    lA = [pltpu.make_async_copy(A.at[14 + i], W7.at[i], sw.at[i]) for i in range(2)]
    lB = [pltpu.make_async_copy(B.at[i], WB.at[i], sb.at[i]) for i in range(16)]
    lC = [pltpu.make_async_copy(C.at[i], WC.at[i], sc.at[i]) for i in range(8)]
    for c in lA:
        c.start()
    for j in range(8):
        lB[j].start()
        lB[8 + j].start()
        lC[j].start()
    o = o2[...]
    ob = o.astype(BF)
    for c in lA:
        c.wait()
    x = x1[...] + apply_w(ob, W7, 0)
    inv = rms(x)
    h = (x * inv * gains[2:3, :]).astype(BF)
    hT = flip(h.astype(F32)).astype(BF)
    df = dy_ref[...]
    y = jnp.zeros((128, 768), F32)
    dh = jnp.zeros((128, 768), F32)
    c0 = 0.7978845608028654
    sB, sC = [], []
    for j in range(8):
        lB[j].wait()
        lB[8 + j].wait()
        lC[j].wait()
        a = dot(h, WB[j])
        up = dot(h, WB[8 + j])
        t = jnp.tanh(c0 * (a + 0.044715 * a * a * a))
        half = 0.5 * (1.0 + t)
        gel = a * half
        der = half + 0.5 * a * (1.0 - t * t) * (c0 * (1.0 + 0.134145 * a * a))
        mid32 = gel * up
        mid = mid32.astype(BF)
        y += dot(mid, WC[j])
        dm = dot(df, WC[j], 1, 1)
        dga = (dm * up * der).astype(BF)
        dup = (dm * gel).astype(BF)
        dh += dot(dga, WB[j], 1, 1) + dot(dup, WB[8 + j], 1, 1)
        gB[j] = dot(hT, dga).astype(BF)
        gB[8 + j] = dot(hT, dup).astype(BF)
        gC[j] = dot(flip(mid32).astype(BF), df).astype(BF)
        sB += [pltpu.make_async_copy(gB.at[j], GB.at[j], tb.at[j]), pltpu.make_async_copy(gB.at[8 + j], GB.at[8 + j], tb.at[8 + j])]
        sC += [pltpu.make_async_copy(gC.at[j], GC.at[j], tc.at[j])]
        for c in sB[-2:] + sC[-1:]:
            c.start()
    out[...] = (x + y).astype(BF)
    dz, gain = rms_back(x, inv, gains[2:3, :], dh)
    gg[...] = gain
    d = df.astype(F32) + dz
    dx2[...] = d
    dc = d.astype(BF)
    dof = apply_wt(dc, W7, 0).astype(BF)
    do2[...] = dof
    prod = flip(dof.astype(F32) * o)
    st[0:12, :] = L2[0:12, :]
    for n in range(12):
        st[12 + n:13 + n, :] = jnp.sum(prod[64 * n:64 * n + 64, :], axis=0, keepdims=True)
    oT = flip(o).astype(BF)
    sA = []
    for i in range(2):
        gA[i] = dot(oT, dc[:, 384 * i:384 * i + 384]).astype(BF)
        sA.append(pltpu.make_async_copy(gA.at[i], GA.at[14 + i], ta.at[i]))
        sA[-1].start()
    for c in sA + sB + sC:
        c.wait()

def ffn(x1, o2, L2, dy, gains, A, B, C):
    M = lambda *s: pltpu.VMEM(s, BF)
    D = pltpu.SemaphoreType.DMA
    return pl.pallas_call(
        ffn_kernel,
        out_shape=(SDS((128, 768), BF), SDS((128, 768), BF), SDS((24, 128), F32), SDS((128, 768), F32), SDS((1, 768), F32),
                   SDS((16, 768, 384), BF), SDS((16, 768, 256), BF), SDS((8, 256, 768), BF)),
        in_specs=[VS] * 5 + [HS] * 3, out_specs=(VS,) * 5 + (HS,) * 3,
        scratch_shapes=[M(2, 768, 384), M(16, 768, 256), M(8, 256, 768), M(2, 768, 384), M(16, 768, 256), M(8, 256, 768),
                        D((2,)), D((16,)), D((8,)), D((16,)), D((8,)), D((2,))],
        compiler_params=pltpu.CompilerParams(vmem_limit_bytes=60 << 20),
        name="feed_forward",
    )(x1, o2, L2, dy, gains, A, B, C)

def self_bwd_kernel(dq2, h2, x1, dx2, qkv, o1, L1, x_ref, h1, gains, g3, A, GA_in, gm_in, gin, tile, GA, gm,
                    W, G, gb, gmv, sem, gsem, msem):
    loads = [pltpu.make_async_copy(A.at[i], W.at[i], sem.at[i]) for i in range(10)]
    for i in (8, 9, 6, 7, 0, 1, 2, 3, 4, 5):
        loads[i].start()
    def gm_load(e):
        return pltpu.make_async_copy(gm_in.at[e], gmv.at[e], msem.at[e])
    def gm_store(e):
        return pltpu.make_async_copy(gmv.at[e], gm.at[e], msem.at[16 + e])
    for e in range(16):
        gm_load(e).start()
    stores = []
    def weight_grad(k, left, inc):
        for i in range(2):
            n = 2 * k + i
            G[n] = dot(left, inc[:, 384 * i:384 * i + 384]).astype(BF)
            stores.append(pltpu.make_async_copy(G.at[n], GA.at[n], gsem.at[n]))
            stores[-1].start()
    dqb = dq2[...].astype(BF)
    for i in (8, 9, 6, 7):
        loads[i].wait()
    u = apply_wt(dqb, W, 4)
    x = x1[...]
    inv = rms(x)
    dz, gain = rms_back(x, inv, gains[1:2, :], u)
    gb[...] = jnp.zeros((8, 768), F32)
    gb[1:2, :] = gain
    gb[2:3, :] = g3[...]
    d1 = dx2[...] + dz
    da = d1.astype(BF)
    do1 = apply_wt(da, W, 3).astype(BF)
    weight_grad(4, flip(h2[...].astype(F32)).astype(BF), dqb)
    masks = head_masks(0.125)
    ones = head_masks(1.0)
    live = causal_mask()
    kT = flip(qkv[1].astype(F32)).astype(BF)
    qs, ks, vs = [], [], []
    for g in range(3):
        cols = slice(256 * g, 256 * g + 256)
        q4 = qkv[0, :, cols]
        d4 = do1[:, cols]
        q4s = jnp.concatenate([q4 * m for m in masks], axis=0)
        d4s = jnp.concatenate([d4 * m for m in ones], axis=0)
        sT = dot(qkv[1, :, cols], q4s, 1, 1)
        gT = dot(qkv[2, :, cols], d4s, 1, 1)
        ps, gs = [], []
        for n in range(4):
            s = jnp.where(live, sT[:, 128 * n:128 * n + 128], NEG)
            p = jnp.exp(s - L1[4 * g + n:4 * g + n + 1, :])
            gt = gT[:, 128 * n:128 * n + 128]
            ps.append(p.astype(BF))
            gs.append((p * (gt - jnp.sum(p * gt, axis=0, keepdims=True))).astype(BF))
        sg = jnp.concatenate(gs, axis=1)
        vs.append(dot(jnp.concatenate(ps, axis=1), d4s).astype(BF))
        ks.append(dot(sg, q4s).astype(BF))
        qT = dot(kT[256 * g:256 * g + 256, :], sg)
        qs += [qT[64 * n:64 * n + 64, 128 * n:128 * n + 128] for n in range(4)]
    for e in range(16):
        gm_load(e).wait()
        gm_store(e).start()
    inc = [(0.125 * unflip(jnp.concatenate(qs, axis=0))).astype(BF), jnp.concatenate(ks, axis=1), jnp.concatenate(vs, axis=1)]
    weight_grad(3, flip(o1[...].astype(F32)).astype(BF), da)
    for c in loads[:6]:
        c.wait()
    u = apply_wt(inc[0], W, 0) + apply_wt(inc[1], W, 1) + apply_wt(inc[2], W, 2)
    x = x_ref[...].astype(F32)
    inv = rms(x)
    dz, gain = rms_back(x, inv, gains[0:1, :], u)
    gb[0:1, :] = gain
    gin[...] = d1 + dz
    hT = flip(h1[...].astype(F32)).astype(BF)
    for k in range(3):
        weight_grad(k, hT, inc[k])
    lane = lax.broadcasted_iota(jnp.int32, (8, 128), 1)
    for d in range(8):
        lo, sh = 96 * d // 128, 96 * d % 128
        t = pltpu.roll(gb[:, 128 * lo:128 * lo + 128], (128 - sh) % 128, 1)
        if sh > 32:
            nxt = pltpu.roll(gb[:, 128 * lo + 128:128 * lo + 256], (128 - sh) % 128, 1)
            t = jnp.where(lane < 128 - sh, t, nxt)
        tile[d] = jnp.where(lane < 96, t, 0.0)
    for c in stores:
        c.wait()
    for e in range(16):
        gm_store(e).wait()

def self_bwd(dq2, h2, x1, dx2, qkv, o1, L1, x, h1, gains, g3, A, GA, gm):
    D = pltpu.SemaphoreType.DMA
    return pl.pallas_call(
        self_bwd_kernel,
        out_shape=(SDS((128, 768), F32), SDS((8, 8, 128), F32), SDS((16, 768, 384), BF), SDS((16, 192, 768), F32)),
        in_specs=[VS] * 11 + [HS] * 3, out_specs=(VS, VS, HS, HS),
        input_output_aliases={12: 2},
        scratch_shapes=[pltpu.VMEM((10, 768, 384), BF), pltpu.VMEM((10, 768, 384), BF), pltpu.VMEM((8, 768), F32), pltpu.VMEM((16, 192, 768), F32), D((10,)), D((10,)), D((32,))],
        compiler_params=pltpu.CompilerParams(vmem_limit_bytes=60 << 20),
        name="self_backward",
    )(dq2, h2, x1, dx2, qkv, o1, L1, x, h1, gains, g3, A, GA, gm)

def adam_kernel(*refs):
    ins, outs = refs[:16], refs[16:]
    for n in range(4):
        w, m, v, g = ins[4 * n:4 * n + 4]
        grad = g[0:3, 0:6] if n == 3 else g[...]
        for o, val in zip(outs[4 * n:4 * n + 4], adam_update(w[...], m[...], v[...], grad, rate_gain if n == 3 else rate_matrix)):
            o[...] = val

def adam(*args):
    shapes = []
    for n in range(4):
        s = args[4 * n].shape
        shapes += [SDS(s, F32)] * 3 + [SDS(s, BF)]
    return pl.pallas_call(adam_kernel, out_shape=tuple(shapes), in_specs=[VS] * 16, out_specs=(VS,) * 16,
                          compiler_params=pltpu.CompilerParams(vmem_limit_bytes=60 << 20), name="adam")(*args)


def body(
    dec_input,
    memory,
    mem_len,
    grad_out,
    attn_master,
    ffn_in_master,
    ffn_out_master,
    gain_master,
    attn_first,
    ffn_in_first,
    ffn_out_first,
    gain_first,
    attn_second,
    ffn_in_second,
    ffn_out_second,
    gain_second,
):
    swap = lambda a: a.transpose(1, 0, 2)
    attn_t, in_t = swap(attn_master), swap(ffn_in_master)
    gath_a, gains, lens, blk_b, blk_c = gather(attn_t, in_t, ffn_out_master, info_tile(gain_master, mem_len))
    aw = gath_a.reshape(16, 768, 384)
    x = dec_input[0]
    q2, h1, qkv, o1, x1, h2, L1 = self_fwd(x, gains, aw)
    q_all, k_two, v_two, kt_two, gath_b, gath_c, o2, L2 = cross_fwd(q2, lens, blk_b, blk_c, memory, aw)
    out_block, do2, st, dx2, g3, GA, GB, GC = ffn(x1, o2, L2, grad_out[0], gains, aw, gath_b.reshape(16, 768, 256), gath_c.reshape(8, 256, 768))
    dq2, blk_f, share_c, gm, GA = cross_bwd(
        do2, st, lens, q_all, k_two, v_two, kt_two, memory, aw,
        GB.reshape(4, 4, 4, 2, 2, 48, 256), GC.reshape(4, 2, 4, 4, 16, 768), GA,
    )
    grad_input, tile_g, GA, grad_memory = self_bwd(dq2, h2, x1, dx2, qkv, o1, L1, x, h1, gains, g3, aw, GA, gm.reshape(16, 192, 768))
    share_a, share_b, share_g = scatter(GA.reshape(4, 4, 4, 2, 3, 32, 384), blk_f, tile_g)
    new = adam(
        attn_t, swap(attn_first), swap(attn_second), share_a,
        in_t, swap(ffn_in_first), swap(ffn_in_second), share_b,
        ffn_out_master, ffn_out_first, ffn_out_second, share_c,
        gain_master, gain_first, gain_second, share_g,
    )
    return (out_block[None], grad_input[None], grad_memory, *[swap(a) for a in new[:8]], *new[8:])


def solution(mesh):
    placed = (
        P(("dp", "seq"), None, None),
        P("dp", "seq", None),
        P(("dp", "seq")),
        P(("dp", "seq"), None, None),
        P(None, ("dp", "seq"), None),
        P(None, ("dp", "seq"), None),
        P(("dp", "seq"), None),
        P(None, ("dp", "seq")),
        P(None, ("dp", "seq"), None),
        P(None, ("dp", "seq"), None),
        P(("dp", "seq"), None),
        P(None, ("dp", "seq")),
        P(None, ("dp", "seq"), None),
        P(None, ("dp", "seq"), None),
        P(("dp", "seq"), None),
        P(None, ("dp", "seq")),
    )
    return jax.shard_map(
        body,
        mesh=mesh,
        in_specs=placed,
        out_specs=(
            P(("dp", "seq"), None, None),
            P(("dp", "seq"), None, None),
            P("dp", "seq", None),
            P(None, ("dp", "seq"), None),
            P(None, ("dp", "seq"), None),
            P(None, ("dp", "seq"), None),
            P(None, ("dp", "seq"), None),
            P(None, ("dp", "seq"), None),
            P(None, ("dp", "seq"), None),
            P(None, ("dp", "seq"), None),
            P(None, ("dp", "seq"), None),
            P(("dp", "seq"), None),
            P(("dp", "seq"), None),
            P(("dp", "seq"), None),
            P(("dp", "seq"), None),
            P(None, ("dp", "seq")),
            P(None, ("dp", "seq")),
            P(None, ("dp", "seq")),
            P(None, ("dp", "seq")),
        ),
        check_vma=False,
    )
```

```python
import jax
import jax.numpy as jnp
from jax import lax
from jax.experimental import pallas as pl
from jax.experimental.pallas import tpu as pltpu
from jax.sharding import PartitionSpec as P

eps_norm = 1e-06
beta_one = 0.9
beta_two = 0.999
adam_eps = 1e-08
decay_rate = 0.01
rate_matrix = 0.12
rate_gain = 3.0
STEP = 10
MESH = pl.DeviceIdType.MESH
BF, F32 = jnp.bfloat16, jnp.float32
ALL = slice(None)
NEG = -1e30
PARTS_A = (("A", 0, "xyz"), ("A", 1, "yzx"), ("A", 2, "zxy"))
PARTS_F = (("B", 0, "xyz"), ("B", 1, "yxz"), ("C", 0, "xyz"))
PLANE = ("xy", "yx") * 3
PARTS_D = tuple(("D", n, PLANE[n]) for n in range(6))
AXES = {"A": "xyz", "B": "xyz", "C": "zxy", "D": "xy"}
STEPS = (2, -1, 1, 0)
VS = pl.BlockSpec(memory_space=pltpu.VMEM)
HS = pl.BlockSpec(memory_space=pltpu.HBM)
SDS = jax.ShapeDtypeStruct
DMA = pltpu.SemaphoreType.DMA


def vm(*shape):
    return pltpu.VMEM(shape, BF)


def vf(*shape):
    return pltpu.VMEM(shape, F32)


def where_am_i():
    dp, sq = lax.axis_index("dp"), lax.axis_index("seq")
    return {"x": sq // 4, "y": sq % 4, "z": dp // 2, "c": dp % 2}


def dev(at):
    return (at["z"] * 2 + at["c"], at["x"] * 4 + at["y"])


def moved(at, axis, step):
    return {**at, axis: (at[axis] + step + 4) % 4}


def offset(me, j, sign=1):
    return {**me, "x": (me["x"] + sign * (j // 4) + 4) % 4, "y": (me["y"] + sign * (j % 4) + 4) % 4}


def sibling_of(me):
    return {**me, "c": 1 - me["c"]}


def remote(src, dst, send, recv, to):
    return pltpu.make_async_remote_copy(src, dst, send, recv, device_id=dev(to), device_id_type=MESH)


def meet(me, column):
    dp, sq = lax.axis_index("dp"), lax.axis_index("seq")
    bar = pltpu.get_barrier_semaphore()
    for i in range(1, 16):
        pl.semaphore_signal(bar, inc=1, device_id=(dp, (sq + i) % 16), device_id_type=MESH)
    if column == "dp":
        for i in range(1, 8):
            pl.semaphore_signal(bar, inc=1, device_id=((dp + i) % 8, sq), device_id_type=MESH)
        return bar, 22
    if column == "z":
        for to in (moved(me, "z", 1), moved(me, "z", -1), sibling_of(me)):
            pl.semaphore_signal(bar, inc=1, device_id=dev(to), device_id_type=MESH)
        return bar, 18
    return bar, 15


def dot(a, b, ca=1, cb=0):
    return lax.dot_general(a, b, (((ca,), (cb,)), ((), ())), preferred_element_type=F32)


class Gather:
    def __init__(self, me, orders, view, own, ss, rs, sib_s=None, sib_r=None):
        self.me, self.orders, self.view, self.own = me, orders, view, own
        self.ss, self.rs, self.sib_s, self.sib_r = ss, rs, sib_s, sib_r
        self.count, self.last = len(orders), len(orders[0]) - 1

    def group(self, n, t, step, half=None):
        order = self.orders[n]
        at = moved(self.me, order[t], step)
        for j in range(t):
            at = {**at, order[j]: ALL}
        if half is not None and t:
            at = {**at, order[0]: pl.ds(2 * half, 2)}
        return at

    def kinds(self, n, t):
        return (0, 1, 2, 3) if t else (0, 1, 2 + n % 2)

    def copy(self, n, t, kind, back=0):
        axis = self.orders[n][t]
        step = 1 if kind in (0, 2) else -1
        dst = self.view(n, self.group(n, t, back) if kind < 2 else self.group(n, t, back - step, kind - 2))
        src = self.own(n) if t == 0 and kind < 2 and back == 0 else dst
        return remote(src, dst, self.ss.at[n, t, kind], self.rs.at[n, t, kind], moved(self.me, axis, step))

    def arrived(self, n, t, kind):
        self.copy(n, t, kind, -1 if kind in (0, 2) else 1).wait_recv()

    def sibling(self, n, j, c):
        v = self.view(n, {**self.group(n, self.last, (0, -1, 1, 2)[j]), "c": c})
        return remote(v, v, self.sib_s.at[n, j], self.sib_r.at[n, j], sibling_of(self.me))

    def send(self, t, ns=None):
        for n in ns or range(self.count):
            if t:
                for k in self.kinds(n, t - 1)[2:]:
                    self.arrived(n, t - 1, k)
            self.copy(n, t, 0).start()
            self.copy(n, t, 1).start()
            if self.sib_s is not None and t == self.last:
                self.sibling(n, 0, self.me["c"]).start()

    def forward(self, t, ns=None):
        for n in ns or range(self.count):
            for k in (0, 1):
                self.arrived(n, t, k)
                if 2 + k in self.kinds(n, t):
                    self.copy(n, t, 2 + k).start()
                if self.sib_s is not None and t == self.last:
                    self.sibling(n, 1 + k, self.me["c"]).start()

    def finish(self, ns=None):
        for n in ns or range(self.count):
            for k in (2, 3):
                self.arrived(n, self.last, k)
            if self.sib_s is not None:
                self.sibling(n, 3, self.me["c"]).start()

    def siblings_in(self):
        for n in range(self.count):
            for j in range(4):
                self.sibling(n, j, 1 - self.me["c"]).wait_recv()

    def drain(self):
        for n in range(self.count):
            for t in range(self.last + 1):
                for k in self.kinds(n, t):
                    self.copy(n, t, k).wait_send()
            if self.sib_s is not None:
                for j in range(4):
                    self.sibling(n, j, self.me["c"]).wait_send()


class Scatter:
    def __init__(self, me, parts, acc, hop, fin, ss, rs, sib=None, source=None, sib_s=None, sib_r=None, loc_s=None):
        self.me, self.parts, self.acc, self.hop_b, self.fin_b = me, parts, acc, hop, fin
        self.ss, self.rs, self.sib, self.source = ss, rs, sib, source
        self.sib_s, self.sib_r, self.loc_s = sib_s, sib_r, loc_s
        self.count, self.last = len(parts), len(parts[0][2]) - 1

    def idx(self, n, at):
        name, p, _ = self.parts[n]
        place = tuple(at[a] for a in AXES[name])
        return place if name == "C" else (p,) + place

    def slot(self, n):
        name, p, _ = self.parts[n]
        return () if name == "C" else (p,)

    def done(self, n, t):
        name, _, order = self.parts[n]
        return [a for a in AXES[name] if a in order[:t]]

    def group(self, n, t, step, half=None):
        order = self.parts[n][2]
        at = moved(self.me, order[t], step)
        for j in range(t):
            at = {**at, order[j]: ALL}
        if half is not None and t:
            at = {**at, self.done(n, t)[0]: pl.ds(2 * half, 2)}
        return at

    def kinds(self, n, t):
        return (0, 1) if t else (n % 2,)

    def refs(self, n, t):
        name = self.parts[n][0]
        return self.acc[name], self.hop_b[t][name], self.fin_b[t][name]

    def hop_copy(self, n, t, kind):
        step = 1 if kind == 0 else -1
        a, h, _ = self.refs(n, t)
        return remote(a.at[self.idx(n, self.group(n, t, 2 * step, kind))], h.at[self.slot(n) + (kind,)],
                      self.ss.at[n, t, kind], self.rs.at[n, t, kind], moved(self.me, self.parts[n][2][t], step))

    def fin_copy(self, n, t, kind):
        step = 1 if kind == 0 else -1
        a, _, f = self.refs(n, t)
        return remote(a.at[self.idx(n, self.group(n, t, step))], f.at[self.slot(n) + (kind,)],
                      self.ss.at[n, t, 2 + kind], self.rs.at[n, t, 2 + kind], moved(self.me, self.parts[n][2][t], step))

    def each(self, n, t, at, fn, half=None):
        axes = self.done(n, t)
        sizes, offs = [4] * len(axes), [0] * len(axes)
        if half is not None and axes:
            sizes[0], offs[0] = 2, 2 * half
        total = 1
        for s in sizes:
            total *= s

        def one(i):
            pos, rest = [], i
            for s in sizes[::-1]:
                pos.append(rest % s)
                rest = rest // s
            pos = pos[::-1]
            where = dict(at)
            for a, p, o in zip(axes, pos, offs):
                where[a] = p + o
            fn(self.idx(n, where), tuple(pos))

        if total == 1:
            one(0)
        else:
            pl.loop(0, total, unroll=4)(one)

    def sib_copy(self, n, j):
        at = self.group(n, self.last, STEPS[j])
        return remote(self.source(n, at, 1 - self.me["c"]), self.sib[self.parts[n][0]].at[self.idx(n, at)],
                      self.sib_s.at[n, j], self.sib_r.at[n, j], sibling_of(self.me))

    def loc_copy(self, n, j):
        at = self.group(n, self.last, STEPS[j])
        return pltpu.make_async_copy(self.source(n, at, self.me["c"]), self.acc[self.parts[n][0]].at[self.idx(n, at)], self.loc_s.at[n, j])

    def start(self):
        for j in range(4):
            for n in range(self.count):
                self.sib_copy(n, j).start()
                self.loc_copy(n, j).start()

    def merge(self, j):
        for n in range(self.count):
            self.sib_copy(n, j).wait_recv()
            self.loc_copy(n, j).wait()
            a, b = self.acc[self.parts[n][0]], self.sib[self.parts[n][0]]

            def fn(i, _):
                a[i] = (a[i].astype(F32) + b[i].astype(F32)).astype(BF)

            self.each(n, self.last, self.group(n, self.last, STEPS[j]), fn)

    def hop(self, t, ns=None):
        for n in ns or range(self.count):
            for k in self.kinds(n, t):
                self.hop_copy(n, t, k).start()

    def pass_on(self, t, ns=None):
        for n in ns or range(self.count):
            a, h, _ = self.refs(n, t)
            for k in (0, 1):
                if k in self.kinds(n, t):
                    self.hop_copy(n, t, k).wait_recv()

                    def fn(i, pos):
                        j = self.slot(n) + (k,) + pos
                        a[i] = (a[i].astype(F32) + h[j].astype(F32)).astype(BF)

                    self.each(n, t, self.group(n, t, 1 if k == 0 else -1), fn, k)
                self.fin_copy(n, t, k).start()

    def close(self, t, ns=None):
        for n in ns or range(self.count):
            self.fin_copy(n, t, 0).wait_recv()
            self.fin_copy(n, t, 1).wait_recv()
            a, _, f = self.refs(n, t)

            def fn(i, pos):
                s = self.slot(n)
                a[i] = (a[i].astype(F32) + f[s + (0,) + pos].astype(F32) + f[s + (1,) + pos].astype(F32)).astype(BF)

            self.each(n, t, self.group(n, t, 0), fn)

    def result(self, n):
        self.fin_copy(n, 0, 0).wait_recv()
        self.fin_copy(n, 0, 1).wait_recv()
        a, _, f = self.refs(n, 0)
        s = self.slot(n)
        return a[self.idx(n, self.me)].astype(F32) + f[s + (0,)].astype(F32) + f[s + (1,)].astype(F32)

    def drain(self):
        for n in range(self.count):
            if self.sib is not None:
                for j in range(4):
                    self.sib_copy(n, j).wait_send()
            for t in range(self.last + 1):
                for k in self.kinds(n, t):
                    self.hop_copy(n, t, k).wait_send()
                self.fin_copy(n, t, 0).wait_send()
                self.fin_copy(n, t, 1).wait_send()


def places(names, refs):
    return dict(zip(names, refs))


def stage_buffers(*shapes):
    out = []
    for lead in ((2, 2, 4), (2, 4, 4), (2, 2), (2, 4), (2,), (2,)):
        out += [vm(*pre, *lead, *block) for pre, block in shapes]
    return out


def staged(names, refs):
    k = len(names)
    got = [places(names, refs[k * i:k * i + k]) for i in range(6)]
    return {2: got[0], 1: got[2], 0: got[4]}, {2: got[1], 1: got[3], 0: got[5]}


def gather_kernel(attn, wi, wo, info, A, gains, lens, outB, outC, infos, stage, recv, blk, blkA, irecv,
                  ss, rs, sib_s, sib_r, as_, ar_, is_, ir_, ds_, dr_, own_s):
    me = where_am_i()
    dp, sq = lax.axis_index("dp"), lax.axis_index("seq")
    bar, count = meet(me, "dp")
    stage[:, 6:8, :] = jnp.zeros((16, 2, 640), F32)
    for s in range(16):
        stage[s, 0:6, 0:384] = attn[:, s // 2, 384 * (s % 2):384 * (s % 2) + 384]
        stage[s, 0:6, 384:640] = wi[:, s // 8, 256 * (s % 8):256 * (s % 8) + 256]
    pl.semaphore_wait(bar, count)

    def a2a(i):
        peer = (sq + i) % 16
        return pltpu.make_async_remote_copy(stage.at[peer], recv.at[sq], as_.at[i], ar_.at[i], device_id=(dp, peer), device_id_type=MESH)

    def inf(i):
        peer = (sq + i) % 16
        return pltpu.make_async_remote_copy(info, irecv.at[sq], is_.at[i], ir_.at[i], device_id=(dp, peer), device_id_type=MESH)

    for i in range(1, 16):
        a2a(i).start()
    for i in range(1, 16):
        inf(i).start()
    recv[sq] = stage[sq]
    irecv[sq] = info[...]
    outC[...] = wo[...].astype(BF)
    for i in range(1, 16):
        a2a(i).wait_recv()
    for k in range(16):
        blk[6 * k:6 * k + 6, :] = recv[k, 0:6, :]
    for p in range(3):
        blkA[p] = blk[32 * p:32 * p + 32, 0:384].astype(BF)
    for p in range(2):
        outB[p] = blk[48 * p:48 * p + 48, 384:640].astype(BF)
    place = lambda n, at: A.at[at["x"], at["y"], at["z"], at["c"], PARTS_A[n][1]]
    ring = Gather(me, [p[2] for p in PARTS_A], place, lambda n: blkA.at[n], ss, rs, sib_s, sib_r)
    owns = [pltpu.make_async_copy(blkA.at[n], place(n, me), own_s.at[n]) for n in range(3)]
    for o in owns:
        o.start()
    ring.send(0)
    ring.forward(0)
    for o in owns:
        o.wait()
    ring.send(1)
    ring.forward(1)
    ring.send(2)
    for i in range(1, 16):
        inf(i).wait_recv()
    tile = jnp.sum(irecv[...], axis=0)
    infos[dp] = tile

    def dpx(i, back=0):
        v = infos.at[(dp - back + 8) % 8]
        return pltpu.make_async_remote_copy(v, v, ds_.at[i], dr_.at[i], device_id=((dp + i) % 8, sq), device_id_type=MESH)

    for i in range(1, 8):
        dpx(i).start()
    ring.forward(2)
    for i in range(1, 8):
        dpx(i, i).wait_recv()
    lane = lax.broadcasted_iota(jnp.int32, (8, 128), 1)
    gains[...] = jnp.zeros((8, 768), F32)
    for d in range(8):
        lo, sh = 96 * d // 128, 96 * d % 128
        t = pltpu.roll(jnp.where(lane < 96, infos[d], 0.0), sh, 1)
        gains[:, 128 * lo:128 * lo + 128] += jnp.where(lane >= sh, t, 0.0)
        if sh > 32:
            gains[:, 128 * lo + 128:128 * lo + 256] += jnp.where(lane < sh, t, 0.0)
    pick = lax.broadcasted_iota(jnp.int32, (16, 128), 0) == lax.broadcasted_iota(jnp.int32, (16, 128), 1)
    lens[...] = jnp.broadcast_to(jnp.sum(jnp.where(pick, tile[3:4, :], 0.0), axis=1, keepdims=True), (16, 128))
    ring.finish()
    ring.siblings_in()
    for i in range(1, 16):
        a2a(i).wait_send()
        inf(i).wait_send()
    for i in range(1, 8):
        dpx(i).wait_send()
    ring.drain()


def gather(attn, wi, wo, info):
    return pl.pallas_call(
        gather_kernel,
        out_shape=(SDS((4, 4, 4, 2, 3, 32, 384), BF), SDS((8, 768), F32), SDS((16, 128), F32), SDS((2, 48, 256), BF), SDS((16, 768), BF)),
        in_specs=[VS] * 4, out_specs=(HS,) + (VS,) * 4,
        scratch_shapes=[vf(8, 8, 128), vf(16, 8, 640), vf(16, 8, 640), vf(96, 640), vm(3, 32, 384), vf(16, 8, 128),
                        DMA((3, 3, 4)), DMA((3, 3, 4)), DMA((3, 4)), DMA((3, 4)), DMA((16,)), DMA((16,)), DMA((16,)), DMA((16,)), DMA((8,)), DMA((8,)), DMA((3,))],
        compiler_params=pltpu.CompilerParams(collective_id=0, has_side_effects=True, vmem_limit_bytes=60 << 20),
        name="gather_attention_weights",
    )(attn, wi, wo, info)


def info_tile(gain, mem_len):
    sq = lax.axis_index("seq")
    t = jnp.zeros((8, 128), F32)
    t = lax.dynamic_update_slice(t, gain.astype(BF).astype(F32), (0, 6 * sq))
    return lax.dynamic_update_slice(t, mem_len.astype(F32)[:, None], (3, sq))


def scatter_kernel(GA, blkF, gg, oA, oB, oG, accA, sibA, h2, f2, h1, f1, h0, f0, blk, stage, recv, gdp, gsum, gsq,
                   ss, rs, sib_s, sib_r, loc_s, as_, ar_, is_, ir_, ds_, dr_):
    me = where_am_i()
    dp, sq = lax.axis_index("dp"), lax.axis_index("seq")
    bar, count = meet(me, "dp")
    pl.semaphore_wait(bar, count)
    hop, fin = staged("A", (h2, f2, h1, f1, h0, f0))
    ring = Scatter(me, PARTS_A, {"A": accA}, hop, fin, ss, rs, {"A": sibA},
                   lambda n, at, c: GA.at[at["x"], at["y"], at["z"], c, n], sib_s, sib_r, loc_s)
    ring.start()

    def dpx(i):
        peer = (dp + i) % 8
        return pltpu.make_async_remote_copy(gg.at[peer], gdp.at[dp], ds_.at[i], dr_.at[i], device_id=(peer, sq), device_id_type=MESH)

    for i in range(1, 8):
        dpx(i).start()
    gdp[dp] = gg[dp]
    ring.merge(0)
    ring.hop(2)
    ring.merge(1)
    ring.merge(2)
    ring.pass_on(2)
    ring.merge(3)
    for i in range(1, 8):
        dpx(i).wait_recv()
    gsum[...] = jnp.sum(gdp[...], axis=0)

    def inf(i):
        peer = (sq + i) % 16
        return pltpu.make_async_remote_copy(gsum, gsq.at[sq], is_.at[i], ir_.at[i], device_id=(dp, peer), device_id_type=MESH)

    for i in range(1, 16):
        inf(i).start()
    gsq[sq] = gsum[...]
    blk[:, 384:640] = blkF[...]
    stage[:, 6:8, :] = jnp.zeros((16, 2, 640), F32)
    ring.close(2)
    ring.hop(1)
    ring.pass_on(1)
    ring.close(1)
    ring.hop(0)
    ring.pass_on(0)
    for n in range(3):
        blk[32 * n:32 * n + 32, 0:384] = ring.result(n)
    for k in range(16):
        stage[k, 0:6, :] = blk[6 * k:6 * k + 6, :]

    def a2a(i):
        peer = (sq + i) % 16
        return pltpu.make_async_remote_copy(stage.at[peer], recv.at[sq], as_.at[i], ar_.at[i], device_id=(dp, peer), device_id_type=MESH)

    for i in range(1, 16):
        a2a(i).start()
    recv[sq] = stage[sq]
    for i in range(1, 16):
        inf(i).wait_recv()
    oG[...] = pltpu.roll(jnp.sum(gsq[...], axis=0), (128 - 6 * sq) % 128, 1)
    for i in range(1, 16):
        a2a(i).wait_recv()
    for s in range(16):
        oA[:, s // 2, 384 * (s % 2):384 * (s % 2) + 384] = recv[s, 0:6, 0:384]
        oB[:, s // 8, 256 * (s % 8):256 * (s % 8) + 256] = recv[s, 0:6, 384:640]
    for i in range(1, 8):
        dpx(i).wait_send()
    for i in range(1, 16):
        a2a(i).wait_send()
        inf(i).wait_send()
    ring.drain()


def scatter(GA, blkF, gg):
    return pl.pallas_call(
        scatter_kernel,
        out_shape=(SDS((6, 8, 768), F32), SDS((6, 2, 2048), F32), SDS((8, 128), F32)),
        in_specs=[HS, VS, VS], out_specs=(VS,) * 3,
        scratch_shapes=[vm(3, 4, 4, 4, 32, 384), vm(3, 4, 4, 4, 32, 384), *stage_buffers(((3,), (32, 384))),
                        vf(96, 640), vf(16, 8, 640), vf(16, 8, 640), vf(8, 8, 128), vf(8, 128), vf(16, 8, 128),
                        DMA((3, 3, 4)), DMA((3, 3, 4)), DMA((3, 4)), DMA((3, 4)), DMA((3, 4)),
                        DMA((16,)), DMA((16,)), DMA((16,)), DMA((16,)), DMA((8,)), DMA((8,))],
        compiler_params=pltpu.CompilerParams(collective_id=1, has_side_effects=True, vmem_limit_bytes=60 << 20),
        name="scatter_attention_grads",
    )(GA, blkF, gg)


def head_masks(value=1.0):
    lane = lax.broadcasted_iota(jnp.int32, (1, 256), 1)
    return [jnp.where(lane // 64 == h, value, 0.0).astype(BF) for h in range(4)]


def stack_heads(block, masks):
    return jnp.concatenate([block * m for m in masks], axis=0)


def key_positions():
    sq = lax.axis_index("seq")
    return (192 * sq + lax.broadcasted_iota(jnp.int32, (192, 128), 0)).astype(F32)


def ffn_place(B, C):
    def place(n, at):
        if n < 2:
            return B.at[at["x"], at["y"], at["z"], at["c"], n]
        return C.at[at["z"], at["c"], at["x"], at["y"]]
    return place


class Merge:
    def __init__(self, me, src, mid, one, two, ss, rs):
        self.me, self.src, self.mid, self.bufs, self.ss, self.rs = me, src, mid, (one, two), ss, rs

    def block(self, n, a, b):
        return (n, a, b) if n % 2 == 0 else (n, b, a)

    def copy(self, n, t, k):
        axis = PLANE[n][t]
        to = moved(self.me, axis, (1, -1, 2)[k])
        src = self.src.at[self.block(n, to[axis], ALL)] if t == 0 else self.mid.at[n, to[axis]]
        return remote(src, self.bufs[t].at[n, k], self.ss.at[n, t, k], self.rs.at[n, t, k], to)

    def send(self, t, ns):
        for n in ns:
            for k in (2, 0, 1):
                self.copy(n, t, k).start()

    def join(self, blocks):
        rows = [b[128:144, :].astype(F32)[0:8, :] for b in blocks]
        logs = [r + pltpu.roll(r, 6, 0) + pltpu.roll(r, 4, 0) for r in rows]
        top = logs[0]
        for l in logs[1:]:
            top = jnp.maximum(top, l)
        ws = [jnp.exp(l - top) for l in logs]
        total = ws[0] + ws[1] + ws[2] + ws[3]
        inv = 1.0 / total
        out = []
        for h in range(2):
            o = sum(b[64 * h:64 * h + 64, :].astype(F32) * (w * inv)[h:h + 1, :] for b, w in zip(blocks, ws))
            out.append(o)
        return jnp.concatenate(out, axis=0), top + jnp.log(total)

    def middle(self, ns):
        for n in ns:
            for k in range(3):
                self.copy(n, 0, k).wait_recv()
            a = self.me[PLANE[n][0]]

            for b in range(4):
                o, l = self.join([self.src.at[self.block(n, a, b)]] + [self.bufs[0].at[n, k, b] for k in range(3)])
                self.mid[n, b, 0:128, :] = o.astype(BF)
                self.mid[n, b, 128:144, :] = log_tile(l)

    def result(self, n):
        for k in range(3):
            self.copy(n, 1, k).wait_recv()
        return self.join([self.mid.at[n, self.me[PLANE[n][1]]]] + [self.bufs[1].at[n, k] for k in range(3)])

    def drain(self):
        for n in range(6):
            for t in range(2):
                for k in range(3):
                    self.copy(n, t, k).wait_send()


def log_tile(l):
    l = jnp.where(lax.broadcasted_iota(jnp.int32, (8, 128), 0) < 2, l, 0.0)
    high = l.astype(BF).astype(F32)
    middle = (l - high).astype(BF).astype(F32)
    low = l - high - middle
    return jnp.concatenate([high + pltpu.roll(middle, 2, 0) + pltpu.roll(low, 4, 0), jnp.zeros((8, 128), F32)], axis=0).astype(BF)


def pair_of(ref, g, at):
    return jnp.concatenate([ref[2 * g, at["x"], at["y"]], ref[2 * g + 1, at["x"], at["y"]]], axis=1)


def cross_fwd_kernel(q, lens, blkB, blkC, mem_h, A, q_h, k_h, v_h, kt_h, B, C, o_ref, L_ref,
                     qall, mem, wk, wv, wkT, wvT, K, V, KT, VT, ost, mid, one, two, lrow,
                     mem_s, w_s, out_s, ss, rs, os_, or_, fs, fr, fsib_s, fsib_r, own_s):
    me = where_am_i()
    bar, count = meet(me, "z")

    def load_mem(e):
        return pltpu.make_async_copy(mem_h.at[e], mem.at[e], mem_s.at[e])

    loads = [pltpu.make_async_copy(A.at[10 + i], (wk if i < 2 else wv).at[:, pl.ds(384 * (i % 2), 384)], w_s.at[i]) for i in range(4)]
    for c in loads:
        c.start()

    @pl.loop(0, 16)
    def _(e):
        load_mem(e).start()

    for n in range(6):
        qall[n, me["x"], me["y"]] = q[:, 128 * n:128 * n + 128]
    place = ffn_place(B, C)
    mine = lambda n: blkB.at[n] if n < 2 else blkC
    owns = [pltpu.make_async_copy(mine(n), place(n, me), own_s.at[n]) for n in range(3)]
    for c in owns:
        c.start()
    lrow[...] = jnp.zeros((4, 2, 8, 128), F32)
    pl.semaphore_wait(bar, count)
    view = lambda n, at: qall.at[n, at["x"], at["y"]]
    plane = Gather(me, PLANE, view, lambda n: view(n, me), ss, rs)
    ring = Gather(me, [p[2] for p in PARTS_F], place, mine, fs, fr, fsib_s, fsib_r)
    fold = Merge(me, ost, mid, one, two, os_, or_)
    plane.send(0)
    ring.send(0)
    for c in loads:
        c.wait()
    for i in range(6):
        wvT[:, 128 * i:128 * i + 128] = wv[128 * i:128 * i + 128, :].T
    plane.forward(0)
    ring.forward(0)
    for c in owns:
        c.wait()

    def project(a, b):
        @pl.loop(a // 2, b // 2)
        def _(i):
            for e in (2 * i, 2 * i + 1):
                load_mem(e).wait()
            K[pl.ds(2 * i, 2)] = dot(mem[pl.ds(2 * i, 2)].reshape(384, 768), wk[...]).astype(BF).reshape(2, 192, 768)
            for e in (2 * i, 2 * i + 1):
                VT[e] = dot(wvT[...], mem[e], 1, 1).astype(BF)

    def project_more(a, b):
        @pl.loop(a // 2, b // 2)
        def _(i):
            V[pl.ds(2 * i, 2)] = dot(mem[pl.ds(2 * i, 2)].reshape(384, 768), wv[...]).astype(BF).reshape(2, 192, 768)
            for e in (2 * i, 2 * i + 1):
                KT[e] = dot(wkT[...], mem[e], 1, 1).astype(BF)

    plane.send(1, (0, 1))
    project(0, 4)
    plane.send(1, (2, 3))
    plane.send(1, (4, 5))
    ring.send(1)
    project(4, 10)
    plane.forward(1, (0, 1))
    plane.forward(1, (2, 3))
    project(10, 16)
    ring.forward(1)
    plane.forward(1, (4, 5))
    ring.send(2)
    masks = head_masks()
    pos = key_positions()

    def attend(g):
        cols = slice(256 * g, 256 * g + 256)

        @pl.loop(0, 4)
        def _(i):
            four = [(x, x * 4 + y, {"x": x, "y": y}) for x, y in [(i, y) for y in range(4)]]
            sT = [dot(K[e, :, cols], stack_heads(pair_of(qall, g, at), masks), 1, 1) for _, e, at in four]
            pT, inv = [], []
            for u, (_, e, at) in enumerate(four):
                live = pos < lens[pl.ds(e, 1), :]
                ps = []
                for h in range(4):
                    s = jnp.where(live, sT[u][:, 128 * h:128 * h + 128], NEG)
                    top = jnp.max(s, axis=0, keepdims=True)
                    p = jnp.exp(s - top)
                    tot = jnp.sum(p, axis=0, keepdims=True)
                    lrow[u, h // 2, h % 2:h % 2 + 1, :] = top + jnp.log(tot)
                    ps.append(p.astype(BF))
                    inv.append(1.0 / tot)
                pT.append(jnp.concatenate(ps, axis=1))
            oT = [dot(VT[e, cols, :], p) for (_, e, _), p in zip(four, pT)]
            for u, (_, e, at) in enumerate(four):
                for h in range(4):
                    ost[2 * g + h // 2, at["x"], at["y"], 64 * (h % 2):64 * (h % 2) + 64, :] = (
                        oT[u][64 * h:64 * h + 64, 128 * h:128 * h + 128] * inv[4 * u + h]).astype(BF)
                for h in range(2):
                    ost[2 * g + h, at["x"], at["y"], 128:144, :] = log_tile(lrow[u, h])

        fold.send(0, (2 * g, 2 * g + 1))

    def deliver(g):
        for n in (2 * g, 2 * g + 1):
            o, l = fold.result(n)
            o_ref[:, 128 * n:128 * n + 128] = o.T
            L_ref[2 * n:2 * n + 2, :] = l[0:2, :]

    plane.finish((0, 1))
    attend(0)
    plane.finish((2, 3))
    attend(1)
    fold.middle((0, 1))
    fold.send(1, (0, 1))
    plane.finish((4, 5))
    out_q = pltpu.make_async_copy(qall, q_h, out_s.at[0])
    out_k = pltpu.make_async_copy(K, k_h, out_s.at[1])
    out_q.start()
    out_k.start()
    attend(2)
    ring.forward(2)
    fold.middle((2, 3))
    fold.send(1, (2, 3))
    for i in range(6):
        wkT[:, 128 * i:128 * i + 128] = wk[128 * i:128 * i + 128, :].T
    project_more(0, 8)
    fold.middle((4, 5))
    fold.send(1, (4, 5))
    low, high = pl.ds(0, 8), pl.ds(8, 8)
    outs = [pltpu.make_async_copy(a.at[k], b.at[k], out_s.at[2 + 2 * i + j])
            for j, k in enumerate((low, high)) for i, (a, b) in enumerate(((V, v_h), (KT, kt_h)))]
    for c in outs[:2]:
        c.start()
    ring.finish()
    project_more(8, 16)
    for c in outs[2:]:
        c.start()
    L_ref[12:16, :] = jnp.zeros((4, 128), F32)
    for g in range(3):
        deliver(g)
    plane.drain()
    fold.drain()
    for c in [out_q, out_k] + outs:
        c.wait()
    ring.siblings_in()
    ring.drain()


def cross_fwd(q, lens, blkB, blkC, memory, A):
    return pl.pallas_call(
        cross_fwd_kernel,
        out_shape=(SDS((6, 4, 4, 128, 128), BF), SDS((16, 192, 768), BF), SDS((16, 192, 768), BF), SDS((16, 768, 192), BF),
                   SDS((4, 4, 4, 2, 2, 48, 256), BF), SDS((4, 2, 4, 4, 16, 768), BF), SDS((128, 768), F32), SDS((16, 128), F32)),
        in_specs=[VS] * 4 + [HS] * 2, out_specs=(HS,) * 6 + (VS,) * 2,
        scratch_shapes=[vm(6, 4, 4, 128, 128), vm(16, 192, 768), vm(768, 768), vm(768, 768), vm(768, 768), vm(768, 768),
                        vm(16, 192, 768), vm(16, 192, 768), vm(16, 768, 192), vm(16, 768, 192),
                        vm(6, 4, 4, 144, 128), vm(6, 4, 144, 128), vm(6, 3, 4, 144, 128), vm(6, 3, 144, 128), vf(4, 2, 8, 128),
                        DMA((16,)), DMA((4,)), DMA((6,)), DMA((6, 2, 4)), DMA((6, 2, 4)), DMA((6, 2, 3)), DMA((6, 2, 3)),
                        DMA((3, 3, 4)), DMA((3, 3, 4)), DMA((3, 4)), DMA((3, 4)), DMA((3,))],
        compiler_params=pltpu.CompilerParams(collective_id=2, has_side_effects=True, vmem_limit_bytes=60 << 20),
        name="cross_forward",
    )(q, lens, blkB, blkC, memory, A)


def cross_bwd_kernel(do, st, lens, q_h, k_h, v_h, kt_h, mem_h, A, GB, GC, G_in, dq_ref, fB, fC, gm_h, dw_h,
                     qall, doall, stall, wk, wv, K, V, KT, mem, memT, dK, dV, gst, wst, dst, dh1, df1, dh0, df0,
                     accB, accC, sibB, sibC, hB2, hC2, fB2, fC2, hB1, hC1, fB1, fC1, hB0, hC0, fB0, fC0,
                     q_s, kv_s, mem_s, w_s, gm_s, dw_s, ss, rs, ds_, dr_, fs, fr, fsib_s, fsib_r, floc):
    me = where_am_i()
    bar, count = meet(me, "z")

    def load_mem(e):
        return pltpu.make_async_copy(mem_h.at[pl.ds(pl.multiple_of(256 * e, 256), 256)], mem.at[e % 4], mem_s.at[e % 4])

    for e in range(4):
        load_mem(e).start()
    loads = [pltpu.make_async_copy(A.at[10 + i], (wk if i < 2 else wv).at[:, pl.ds(384 * (i % 2), 384)], w_s.at[i]) for i in range(4)]
    loads.append(pltpu.make_async_copy(q_h, qall, q_s))
    for n in range(6):
        doall[n, me["x"], me["y"]] = do[:, 128 * n:128 * n + 128]
    stall[me["x"], me["y"]] = st[...]
    pl.semaphore_wait(bar, count)

    def place(n, at):
        return stall.at[at["x"], at["y"]] if n == 6 else doall.at[n, at["x"], at["y"]]

    plane = Gather(me, PLANE + ("xy",), place, lambda n: place(n, me), ss, rs)
    fhop, ffin = staged("BC", (hB2, hC2, fB2, fC2, hB1, hC1, fB1, fC1, hB0, hC0, fB0, fC0))
    grads = ffn_place(GB, GC)
    ring = Scatter(me, PARTS_F, {"B": accB, "C": accC}, fhop, ffin, fs, fr, {"B": sibB, "C": sibC},
                   lambda n, at, c: grads(n, {**at, "c": c}), fsib_s, fsib_r, floc)
    back = Scatter(me, PARTS_D, {"D": dst}, {1: {"D": dh1}, 0: {"D": dh0}}, {1: {"D": df1}, 0: {"D": df0}}, ds_, dr_)
    plane.send(0, (6, 0, 1, 2, 3, 4, 5))
    ring.start()
    for c in loads:
        c.start()

    def turn(a, b):
        @pl.loop(a, b)
        def _(e):
            load_mem(e).wait()
            memT[:, pl.ds(pl.multiple_of(256 * e, 256), 256)] = mem[e % 4].T

            @pl.when(e < 8)
            def _():
                load_mem(e + 4).start()

    turn(0, 1)
    plane.forward(0, (6, 0, 1, 2, 3, 4, 5))
    turn(1, 3)
    plane.send(1, (6, 0, 1))
    plane.send(1, (2, 3))
    plane.send(1, (4, 5))
    ring.merge(0)
    ring.hop(2)
    turn(3, 6)
    plane.forward(1, (6, 0, 1))
    ring.merge(1)
    ring.merge(2)
    plane.forward(1, (2, 3))
    ring.pass_on(2)
    masks = head_masks()
    pos = key_positions()

    def load_kv(g, i, u, which):
        e = ((me["x"] + 2 + i) % 4) * 4 + u
        cols = pl.ds(256 * g, 256)
        src = (k_h.at[e, :, cols], v_h.at[e, :, cols], kt_h.at[e, cols])[which]
        return pltpu.make_async_copy(src, (K, V, KT)[which].at[i % 2, u], kv_s.at[which, i % 2, u])

    def fetch_kv(g, i):
        for u in range(4):
            for w in range(3):
                load_kv(g, i, u, w).start()

    fetch_kv(0, 0)
    for c in loads:
        c.wait()

    def attend(g):
        cols = slice(256 * g, 256 * g + 256)

        @pl.loop(0, 4)
        def _(i):
            @pl.when(i < 3)
            def _():
                fetch_kv(g, i + 1)

            for u in range(4):
                for w in range(3):
                    load_kv(g, i, u, w).wait()
            x = (me["x"] + 2 + i) % 4
            four = [(x * 4 + y, {"x": x, "y": y}) for y in range(4)]
            q4s = [stack_heads(pair_of(qall, g, at), masks) for _, at in four]
            d4s = [stack_heads(pair_of(doall, g, at), masks) for _, at in four]
            sT = [dot(K[i % 2, u], q4s[u], 1, 1) for u in range(4)]
            gT = [dot(V[i % 2, u], d4s[u], 1, 1) for u in range(4)]
            pT, sg = [], []
            for u, (e, at) in enumerate(four):
                live = pos < lens[pl.ds(e, 1), :]
                ps, gs = [], []
                for h in range(4):
                    n = 4 * g + h
                    s = jnp.where(live, sT[u][:, 128 * h:128 * h + 128], NEG)
                    p = jnp.exp(s - stall[at["x"], at["y"], n:n + 1, :])
                    ps.append(p.astype(BF))
                    gs.append((p * (gT[u][:, 128 * h:128 * h + 128] - stall[at["x"], at["y"], 12 + n:13 + n, :])).astype(BF))
                pT.append(jnp.concatenate(ps, axis=1))
                sg.append(jnp.concatenate(gs, axis=1))
            for u, (e, at) in enumerate(four):
                dV[pl.ds(pl.multiple_of(192 * e, 192), 192), cols] = dot(pT[u], d4s[u]).astype(BF)
            for u, (e, at) in enumerate(four):
                dK[pl.ds(pl.multiple_of(192 * e, 192), 192), cols] = dot(sg[u], q4s[u]).astype(BF)
            for u, (e, at) in enumerate(four):
                qT = dot(KT[i % 2, u], sg[u])
                for h in range(4):
                    dst[2 * g + h // 2, at["x"], at["y"], 64 * (h % 2):64 * (h % 2) + 64, :] = qT[64 * h:64 * h + 64, 128 * h:128 * h + 128].astype(BF)

        if g < 2:
            fetch_kv(g + 1, 0)
        back.hop(1, (2 * g, 2 * g + 1))

    plane.finish((6, 0, 1))
    attend(0)
    plane.forward(1, (4, 5))
    plane.finish((2, 3))
    attend(1)
    back.pass_on(1, (0, 1))
    ring.merge(3)
    plane.finish((4, 5))
    attend(2)
    back.pass_on(1, (2, 3))
    back.close(1, (0, 1))
    back.hop(0, (0, 1))

    def gm_copy(e):
        return pltpu.make_async_copy(gst.at[e % 2], gm_h.at[e], gm_s.at[e % 2])

    def mem_grad(a, b):
        @pl.loop(a, b)
        def _(e):
            @pl.when(e > 1)
            def _():
                gm_copy(e - 2).wait()

            rows = pl.ds(pl.multiple_of(384 * e, 384), 384)
            gst[e % 2] = dot(dK[rows, :], wk[...], 1, 1) + dot(dV[rows, :], wv[...], 1, 1)
            gm_copy(e).start()

    def dw_copy(k, r, half):
        rows = pl.ds(pl.multiple_of(256 * r, 256), 256)
        return pltpu.make_async_copy(wst.at[k, :, pl.ds(384 * half, 384)], dw_h.at[10 + 2 * k + half, rows], dw_s.at[k, half])

    def weight_grad(a, b):
        @pl.loop(a, b)
        def _(r):
            for k in range(2):
                @pl.when(r > 0)
                def _():
                    dw_copy(k, r - 1, 0).wait()
                    dw_copy(k, r - 1, 1).wait()

                wst[k] = dot(memT[pl.ds(pl.multiple_of(256 * r, 256), 256), :], (dV if k else dK)[...]).astype(BF)
                dw_copy(k, r, 0).start()
                dw_copy(k, r, 1).start()

    turn(6, 12)
    ring.close(2)
    ring.hop(1)
    back.pass_on(1, (4, 5))
    back.close(1, (2, 3))
    back.hop(0, (2, 3))
    back.pass_on(0, (0, 1))
    mem_grad(0, 4)
    back.close(1, (4, 5))
    back.hop(0, (4, 5))
    back.pass_on(0, (2, 3))
    ring.pass_on(1)
    mem_grad(4, 8)
    back.pass_on(0, (4, 5))
    ring.close(1)
    ring.hop(0)
    weight_grad(0, 1)
    ring.pass_on(0)
    weight_grad(1, 3)
    for n in range(6):
        dq_ref[:, 128 * n:128 * n + 128] = (0.125 * back.result(n)).T
    fB[0:48, :] = ring.result(0)
    fB[48:96, :] = ring.result(1)
    fC[...] = ring.result(2)
    gm_copy(6).wait()
    gm_copy(7).wait()
    for k in range(2):
        dw_copy(k, 2, 0).wait()
        dw_copy(k, 2, 1).wait()
    plane.drain()
    ring.drain()
    back.drain()


def cross_bwd(do, st, lens, q_h, k_h, v_h, kt_h, memory, A, GB, GC, GA):
    bB, bC = (48, 256), (16, 768)
    return pl.pallas_call(
        cross_bwd_kernel,
        out_shape=(SDS((128, 768), F32), SDS((96, 256), F32), SDS((16, 768), F32), SDS((8, 384, 768), F32), SDS((16, 768, 384), BF)),
        in_specs=[VS] * 3 + [HS] * 9, out_specs=(VS,) * 3 + (HS,) * 2, input_output_aliases={11: 4},
        scratch_shapes=[vm(6, 4, 4, 128, 128), vm(6, 4, 4, 128, 128), vf(4, 4, 24, 128), vm(768, 768), vm(768, 768),
                        vm(2, 4, 192, 256), vm(2, 4, 192, 256), vm(2, 4, 256, 192), vm(4, 256, 768), vm(768, 3072), vm(3072, 768), vm(3072, 768),
                        vf(2, 384, 768), vm(2, 256, 768), vm(6, 4, 4, 128, 128), vm(6, 2, 2, 128, 128), vm(6, 2, 4, 128, 128), vm(6, 2, 128, 128), vm(6, 2, 128, 128),
                        vm(2, 4, 4, 4, *bB), vm(4, 4, 4, *bC), vm(2, 4, 4, 4, *bB), vm(4, 4, 4, *bC), *stage_buffers(((2,), bB), ((), bC)),
                        DMA, DMA((3, 2, 4)), DMA((4,)), DMA((4,)), DMA((2,)), DMA((2, 2)), DMA((7, 2, 4)), DMA((7, 2, 4)), DMA((6, 2, 4)), DMA((6, 2, 4)),
                        DMA((3, 3, 4)), DMA((3, 3, 4)), DMA((3, 4)), DMA((3, 4)), DMA((3, 4))],
        compiler_params=pltpu.CompilerParams(collective_id=3, has_side_effects=True, vmem_limit_bytes=60 << 20),
        name="cross_backward",
    )(do, st, lens, q_h, k_h, v_h, kt_h, memory.reshape(3072, 768), A, GB, GC, GA)


def adam_update(master, first, second, grad, rate):
    first_new = beta_one * first + (1.0 - beta_one) * grad
    second_new = beta_two * second + (1.0 - beta_two) * grad * grad
    fix_one = 1.0 - beta_one**STEP
    fix_two = 1.0 - beta_two**STEP
    master_new = master - rate * (
        first_new / fix_one / (jnp.sqrt(second_new / fix_two) + adam_eps) + decay_rate * master
    )
    return (master_new, first_new, second_new, master_new.astype(jnp.bfloat16))


def rms(x):
    return lax.rsqrt(jnp.mean(x * x, axis=-1, keepdims=True) + eps_norm)

def rms_back(x, inv, gain, u):
    scaled = u * gain
    inner = jnp.mean(scaled * x, axis=-1, keepdims=True)
    return inv * scaled - x * inv * inv * inv * inner, jnp.sum(u * x * inv, axis=0, keepdims=True)

def flip(x):
    return jnp.concatenate([x[:, 128 * i:128 * i + 128].T for i in range(x.shape[1] // 128)], axis=0)

def unflip(x):
    return jnp.concatenate([x[128 * i:128 * i + 128, :].T for i in range(x.shape[0] // 128)], axis=1)

def apply_w(h, W, k):
    return jnp.concatenate([dot(h, W[2 * k]), dot(h, W[2 * k + 1])], axis=1)

def apply_wt(u, W, k):
    return dot(u[:, 0:384], W[2 * k], 1, 1) + dot(u[:, 384:768], W[2 * k + 1], 1, 1)

def causal_mask():
    return lax.broadcasted_iota(jnp.int32, (128, 128), 0) <= lax.broadcasted_iota(jnp.int32, (128, 128), 1)

def self_fwd_kernel(x_ref, gains, A, q2, h1, qkv, o1, x1, h2, L1, W, sem):
    loads = [pltpu.make_async_copy(A.at[i], W.at[i], sem.at[i]) for i in range(10)]
    for c in loads:
        c.start()
    x = x_ref[...].astype(F32)
    h = (x * rms(x) * gains[0:1, :]).astype(BF)
    h1[...] = h
    for k in range(3):
        loads[2 * k].wait()
        loads[2 * k + 1].wait()
        full = apply_w(h, W, k)
        qkv[k] = full.astype(BF)
    vT = flip(full).astype(BF)
    masks = head_masks(0.125)
    live = causal_mask()
    outs = []
    for g in range(3):
        cols = slice(256 * g, 256 * g + 256)
        q4 = qkv[0, :, cols]
        sT = dot(qkv[1, :, cols], jnp.concatenate([q4 * m for m in masks], axis=0), 1, 1)
        ps = []
        for n in range(4):
            s = jnp.where(live, sT[:, 128 * n:128 * n + 128], NEG)
            top = jnp.max(s, axis=0, keepdims=True)
            lse = top + jnp.log(jnp.sum(jnp.exp(s - top), axis=0, keepdims=True))
            L1[4 * g + n:4 * g + n + 1, :] = lse
            ps.append(jnp.exp(s - lse).astype(BF))
        oT = dot(vT[256 * g:256 * g + 256, :], jnp.concatenate(ps, axis=1))
        outs += [oT[64 * n:64 * n + 64, 128 * n:128 * n + 128] for n in range(4)]
    o = unflip(jnp.concatenate(outs, axis=0)).astype(BF)
    o1[...] = o
    for c in loads[6:]:
        c.wait()
    x = x + apply_w(o, W, 3)
    x1[...] = x
    h = (x * rms(x) * gains[1:2, :]).astype(BF)
    h2[...] = h
    q2[...] = apply_w(h, W, 4).astype(BF) * jnp.asarray(0.125, BF)

def self_fwd(x, gains, A):
    row = SDS((128, 768), BF)
    return pl.pallas_call(
        self_fwd_kernel,
        out_shape=(row, row, SDS((3, 128, 768), BF), row, SDS((128, 768), F32), row, SDS((16, 128), F32)),
        in_specs=[VS, VS, HS], out_specs=(VS,) * 7,
        scratch_shapes=[pltpu.VMEM((10, 768, 384), BF), pltpu.SemaphoreType.DMA((10,))],
        compiler_params=pltpu.CompilerParams(vmem_limit_bytes=60 << 20),
        name="self_forward",
    )(x, gains, A)

def ffn_kernel(x1, o2, L2, dy_ref, gains, A, B, C, out, do2, st, dx2, gg, GA, GB, GC,
               W7, WB, WC, gA, gB, gC, sw, sb, sc, tb, tc, ta):
    lA = [pltpu.make_async_copy(A.at[14 + i], W7.at[i], sw.at[i]) for i in range(2)]
    lB = [pltpu.make_async_copy(B.at[i], WB.at[i], sb.at[i]) for i in range(16)]
    lC = [pltpu.make_async_copy(C.at[i], WC.at[i], sc.at[i]) for i in range(8)]
    for c in lA:
        c.start()
    for j in range(8):
        lB[j].start()
        lB[8 + j].start()
        lC[j].start()
    o = o2[...]
    ob = o.astype(BF)
    for c in lA:
        c.wait()
    x = x1[...] + apply_w(ob, W7, 0)
    inv = rms(x)
    h = (x * inv * gains[2:3, :]).astype(BF)
    hT = flip(h.astype(F32)).astype(BF)
    df = dy_ref[...]
    y = jnp.zeros((128, 768), F32)
    dh = jnp.zeros((128, 768), F32)
    c0 = 0.7978845608028654
    sB, sC = [], []
    for j in range(8):
        lB[j].wait()
        lB[8 + j].wait()
        lC[j].wait()
        a = dot(h, WB[j])
        up = dot(h, WB[8 + j])
        t = jnp.tanh(c0 * (a + 0.044715 * a * a * a))
        half = 0.5 * (1.0 + t)
        gel = a * half
        der = half + 0.5 * a * (1.0 - t * t) * (c0 * (1.0 + 0.134145 * a * a))
        mid32 = gel * up
        mid = mid32.astype(BF)
        y += dot(mid, WC[j])
        dm = dot(df, WC[j], 1, 1)
        dga = (dm * up * der).astype(BF)
        dup = (dm * gel).astype(BF)
        dh += dot(dga, WB[j], 1, 1) + dot(dup, WB[8 + j], 1, 1)
        gB[j] = dot(hT, dga).astype(BF)
        gB[8 + j] = dot(hT, dup).astype(BF)
        gC[j] = dot(flip(mid32).astype(BF), df).astype(BF)
        sB += [pltpu.make_async_copy(gB.at[j], GB.at[j], tb.at[j]), pltpu.make_async_copy(gB.at[8 + j], GB.at[8 + j], tb.at[8 + j])]
        sC += [pltpu.make_async_copy(gC.at[j], GC.at[j], tc.at[j])]
        for c in sB[-2:] + sC[-1:]:
            c.start()
    out[...] = (x + y).astype(BF)
    dz, gain = rms_back(x, inv, gains[2:3, :], dh)
    gg[...] = gain
    d = df.astype(F32) + dz
    dx2[...] = d
    dc = d.astype(BF)
    dof = apply_wt(dc, W7, 0).astype(BF)
    do2[...] = dof
    prod = flip(dof.astype(F32) * o)
    st[0:12, :] = L2[0:12, :]
    for n in range(12):
        st[12 + n:13 + n, :] = jnp.sum(prod[64 * n:64 * n + 64, :], axis=0, keepdims=True)
    oT = flip(o).astype(BF)
    sA = []
    for i in range(2):
        gA[i] = dot(oT, dc[:, 384 * i:384 * i + 384]).astype(BF)
        sA.append(pltpu.make_async_copy(gA.at[i], GA.at[14 + i], ta.at[i]))
        sA[-1].start()
    for c in sA + sB + sC:
        c.wait()

def ffn(x1, o2, L2, dy, gains, A, B, C):
    M = lambda *s: pltpu.VMEM(s, BF)
    D = pltpu.SemaphoreType.DMA
    return pl.pallas_call(
        ffn_kernel,
        out_shape=(SDS((128, 768), BF), SDS((128, 768), BF), SDS((24, 128), F32), SDS((128, 768), F32), SDS((1, 768), F32),
                   SDS((16, 768, 384), BF), SDS((16, 768, 256), BF), SDS((8, 256, 768), BF)),
        in_specs=[VS] * 5 + [HS] * 3, out_specs=(VS,) * 5 + (HS,) * 3,
        scratch_shapes=[M(2, 768, 384), M(16, 768, 256), M(8, 256, 768), M(2, 768, 384), M(16, 768, 256), M(8, 256, 768),
                        D((2,)), D((16,)), D((8,)), D((16,)), D((8,)), D((2,))],
        compiler_params=pltpu.CompilerParams(vmem_limit_bytes=60 << 20),
        name="feed_forward",
    )(x1, o2, L2, dy, gains, A, B, C)

def self_bwd_kernel(dq2, h2, x1, dx2, qkv, o1, L1, x_ref, h1, gains, g3, A, GA_in, gm_in, gin, tile, GA, gm,
                    W, G, gb, gmv, sem, gsem, msem):
    loads = [pltpu.make_async_copy(A.at[i], W.at[i], sem.at[i]) for i in range(10)]
    for i in (8, 9, 6, 7, 0, 1, 2, 3, 4, 5):
        loads[i].start()
    def gm_load(e):
        return pltpu.make_async_copy(gm_in.at[e], gmv.at[e], msem.at[e])
    def gm_store(e):
        return pltpu.make_async_copy(gmv.at[e], gm.at[e], msem.at[16 + e])
    for e in range(16):
        gm_load(e).start()
    stores = []
    def weight_grad(k, left, inc):
        for i in range(2):
            n = 2 * k + i
            G[n] = dot(left, inc[:, 384 * i:384 * i + 384]).astype(BF)
            stores.append(pltpu.make_async_copy(G.at[n], GA.at[n], gsem.at[n]))
            stores[-1].start()
    dqb = dq2[...].astype(BF)
    for i in (8, 9, 6, 7):
        loads[i].wait()
    u = apply_wt(dqb, W, 4)
    x = x1[...]
    inv = rms(x)
    dz, gain = rms_back(x, inv, gains[1:2, :], u)
    gb[...] = jnp.zeros((8, 768), F32)
    gb[1:2, :] = gain
    gb[2:3, :] = g3[...]
    d1 = dx2[...] + dz
    da = d1.astype(BF)
    do1 = apply_wt(da, W, 3).astype(BF)
    weight_grad(4, flip(h2[...].astype(F32)).astype(BF), dqb)
    masks = head_masks(0.125)
    ones = head_masks(1.0)
    live = causal_mask()
    kT = flip(qkv[1].astype(F32)).astype(BF)
    qs, ks, vs = [], [], []
    for g in range(3):
        cols = slice(256 * g, 256 * g + 256)
        q4 = qkv[0, :, cols]
        d4 = do1[:, cols]
        q4s = jnp.concatenate([q4 * m for m in masks], axis=0)
        d4s = jnp.concatenate([d4 * m for m in ones], axis=0)
        sT = dot(qkv[1, :, cols], q4s, 1, 1)
        gT = dot(qkv[2, :, cols], d4s, 1, 1)
        ps, gs = [], []
        for n in range(4):
            s = jnp.where(live, sT[:, 128 * n:128 * n + 128], NEG)
            p = jnp.exp(s - L1[4 * g + n:4 * g + n + 1, :])
            gt = gT[:, 128 * n:128 * n + 128]
            ps.append(p.astype(BF))
            gs.append((p * (gt - jnp.sum(p * gt, axis=0, keepdims=True))).astype(BF))
        sg = jnp.concatenate(gs, axis=1)
        vs.append(dot(jnp.concatenate(ps, axis=1), d4s).astype(BF))
        ks.append(dot(sg, q4s).astype(BF))
        qT = dot(kT[256 * g:256 * g + 256, :], sg)
        qs += [qT[64 * n:64 * n + 64, 128 * n:128 * n + 128] for n in range(4)]
    for e in range(16):
        gm_load(e).wait()
        gm_store(e).start()
    inc = [(0.125 * unflip(jnp.concatenate(qs, axis=0))).astype(BF), jnp.concatenate(ks, axis=1), jnp.concatenate(vs, axis=1)]
    weight_grad(3, flip(o1[...].astype(F32)).astype(BF), da)
    for c in loads[:6]:
        c.wait()
    u = apply_wt(inc[0], W, 0) + apply_wt(inc[1], W, 1) + apply_wt(inc[2], W, 2)
    x = x_ref[...].astype(F32)
    inv = rms(x)
    dz, gain = rms_back(x, inv, gains[0:1, :], u)
    gb[0:1, :] = gain
    gin[...] = d1 + dz
    hT = flip(h1[...].astype(F32)).astype(BF)
    for k in range(3):
        weight_grad(k, hT, inc[k])
    lane = lax.broadcasted_iota(jnp.int32, (8, 128), 1)
    for d in range(8):
        lo, sh = 96 * d // 128, 96 * d % 128
        t = pltpu.roll(gb[:, 128 * lo:128 * lo + 128], (128 - sh) % 128, 1)
        if sh > 32:
            nxt = pltpu.roll(gb[:, 128 * lo + 128:128 * lo + 256], (128 - sh) % 128, 1)
            t = jnp.where(lane < 128 - sh, t, nxt)
        tile[d] = jnp.where(lane < 96, t, 0.0)
    for c in stores:
        c.wait()
    for e in range(16):
        gm_store(e).wait()

def self_bwd(dq2, h2, x1, dx2, qkv, o1, L1, x, h1, gains, g3, A, GA, gm):
    D = pltpu.SemaphoreType.DMA
    return pl.pallas_call(
        self_bwd_kernel,
        out_shape=(SDS((128, 768), F32), SDS((8, 8, 128), F32), SDS((16, 768, 384), BF), SDS((16, 192, 768), F32)),
        in_specs=[VS] * 11 + [HS] * 3, out_specs=(VS, VS, HS, HS),
        input_output_aliases={12: 2},
        scratch_shapes=[pltpu.VMEM((10, 768, 384), BF), pltpu.VMEM((10, 768, 384), BF), pltpu.VMEM((8, 768), F32), pltpu.VMEM((16, 192, 768), F32), D((10,)), D((10,)), D((32,))],
        compiler_params=pltpu.CompilerParams(vmem_limit_bytes=60 << 20),
        name="self_backward",
    )(dq2, h2, x1, dx2, qkv, o1, L1, x, h1, gains, g3, A, GA, gm)

def adam_kernel(*refs):
    ins, outs = refs[:16], refs[16:]
    for n in range(4):
        w, m, v, g = ins[4 * n:4 * n + 4]
        grad = g[0:3, 0:6] if n == 3 else g[...]
        for o, val in zip(outs[4 * n:4 * n + 4], adam_update(w[...], m[...], v[...], grad, rate_gain if n == 3 else rate_matrix)):
            o[...] = val

def adam(*args):
    shapes = []
    for n in range(4):
        s = args[4 * n].shape
        shapes += [SDS(s, F32)] * 3 + [SDS(s, BF)]
    return pl.pallas_call(adam_kernel, out_shape=tuple(shapes), in_specs=[VS] * 16, out_specs=(VS,) * 16,
                          compiler_params=pltpu.CompilerParams(vmem_limit_bytes=60 << 20), name="adam")(*args)


def body(
    dec_input,
    memory,
    mem_len,
    grad_out,
    attn_master,
    ffn_in_master,
    ffn_out_master,
    gain_master,
    attn_first,
    ffn_in_first,
    ffn_out_first,
    gain_first,
    attn_second,
    ffn_in_second,
    ffn_out_second,
    gain_second,
):
    swap = lambda a: a.transpose(1, 0, 2)
    attn_t, in_t = swap(attn_master), swap(ffn_in_master)
    gath_a, gains, lens, blk_b, blk_c = gather(attn_t, in_t, ffn_out_master, info_tile(gain_master, mem_len))
    aw = gath_a.reshape(16, 768, 384)
    x = dec_input[0]
    q2, h1, qkv, o1, x1, h2, L1 = self_fwd(x, gains, aw)
    q_all, k_two, v_two, kt_two, gath_b, gath_c, o2, L2 = cross_fwd(q2, lens, blk_b, blk_c, memory, aw)
    out_block, do2, st, dx2, g3, GA, GB, GC = ffn(x1, o2, L2, grad_out[0], gains, aw, gath_b.reshape(16, 768, 256), gath_c.reshape(8, 256, 768))
    dq2, blk_f, share_c, gm, GA = cross_bwd(
        do2, st, lens, q_all, k_two, v_two, kt_two, memory, aw,
        GB.reshape(4, 4, 4, 2, 2, 48, 256), GC.reshape(4, 2, 4, 4, 16, 768), GA,
    )
    grad_input, tile_g, GA, grad_memory = self_bwd(dq2, h2, x1, dx2, qkv, o1, L1, x, h1, gains, g3, aw, GA, gm.reshape(16, 192, 768))
    share_a, share_b, share_g = scatter(GA.reshape(4, 4, 4, 2, 3, 32, 384), blk_f, tile_g)
    new = adam(
        attn_t, swap(attn_first), swap(attn_second), share_a,
        in_t, swap(ffn_in_first), swap(ffn_in_second), share_b,
        ffn_out_master, ffn_out_first, ffn_out_second, share_c,
        gain_master, gain_first, gain_second, share_g,
    )
    return (out_block[None], grad_input[None], grad_memory, *[swap(a) for a in new[:8]], *new[8:])


def solution(mesh):
    placed = (
        P(("dp", "seq"), None, None),
        P("dp", "seq", None),
        P(("dp", "seq")),
        P(("dp", "seq"), None, None),
        P(None, ("dp", "seq"), None),
        P(None, ("dp", "seq"), None),
        P(("dp", "seq"), None),
        P(None, ("dp", "seq")),
        P(None, ("dp", "seq"), None),
        P(None, ("dp", "seq"), None),
        P(("dp", "seq"), None),
        P(None, ("dp", "seq")),
        P(None, ("dp", "seq"), None),
        P(None, ("dp", "seq"), None),
        P(("dp", "seq"), None),
        P(None, ("dp", "seq")),
    )
    return jax.shard_map(
        body,
        mesh=mesh,
        in_specs=placed,
        out_specs=(
            P(("dp", "seq"), None, None),
            P(("dp", "seq"), None, None),
            P("dp", "seq", None),
            P(None, ("dp", "seq"), None),
            P(None, ("dp", "seq"), None),
            P(None, ("dp", "seq"), None),
            P(None, ("dp", "seq"), None),
            P(None, ("dp", "seq"), None),
            P(None, ("dp", "seq"), None),
            P(None, ("dp", "seq"), None),
            P(None, ("dp", "seq"), None),
            P(("dp", "seq"), None),
            P(("dp", "seq"), None),
            P(("dp", "seq"), None),
            P(("dp", "seq"), None),
            P(None, ("dp", "seq")),
            P(None, ("dp", "seq")),
            P(None, ("dp", "seq")),
            P(None, ("dp", "seq")),
        ),
        check_vma=False,
    )
```

```python
import jax
import jax.numpy as jnp
from jax import lax
from jax.experimental import pallas as pl
from jax.experimental.pallas import tpu as pltpu
from jax.sharding import PartitionSpec as P

eps_norm = 1e-06
beta_one = 0.9
beta_two = 0.999
adam_eps = 1e-08
decay_rate = 0.01
rate_matrix = 0.12
rate_gain = 3.0
STEP = 10
MESH = pl.DeviceIdType.MESH
BF, F32 = jnp.bfloat16, jnp.float32
ALL = slice(None)
NEG = -1e30
PARTS_A = (("A", 0, "xyz"), ("A", 1, "yzx"), ("A", 2, "zxy"))
PARTS_F = (("B", 0, "z"), ("B", 1, "z"), ("C", 0, "z"))
PARTS_G = (("E", 0, "xy"), ("E", 1, "yx"), ("F", 0, "xy"))
PLANE = ("xy", "yx") * 3
PARTS_D = tuple(("D", n, PLANE[n]) for n in range(6))
AXES = {"A": "xyz", "B": "xyz", "C": "zxy", "D": "xy", "E": "xy", "F": "xy"}
STEPS = (2, -1, 1, 0)
VS = pl.BlockSpec(memory_space=pltpu.VMEM)
HS = pl.BlockSpec(memory_space=pltpu.HBM)
SDS = jax.ShapeDtypeStruct
DMA = pltpu.SemaphoreType.DMA


def vm(*shape):
    return pltpu.VMEM(shape, BF)


def vf(*shape):
    return pltpu.VMEM(shape, F32)


def where_am_i():
    dp, sq = lax.axis_index("dp"), lax.axis_index("seq")
    return {"x": sq // 4, "y": sq % 4, "z": dp // 2, "c": dp % 2}


def dev(at):
    return (at["z"] * 2 + at["c"], at["x"] * 4 + at["y"])


def moved(at, axis, step):
    return {**at, axis: (at[axis] + step + 4) % 4}


def offset(me, j, sign=1):
    return {**me, "x": (me["x"] + sign * (j // 4) + 4) % 4, "y": (me["y"] + sign * (j % 4) + 4) % 4}


def sibling_of(me):
    return {**me, "c": 1 - me["c"]}


def remote(src, dst, send, recv, to):
    return pltpu.make_async_remote_copy(src, dst, send, recv, device_id=dev(to), device_id_type=MESH)


def meet(me, column):
    dp, sq = lax.axis_index("dp"), lax.axis_index("seq")
    bar = pltpu.get_barrier_semaphore()
    for i in range(1, 16):
        pl.semaphore_signal(bar, inc=1, device_id=(dp, (sq + i) % 16), device_id_type=MESH)
    if column == "dp":
        for i in range(1, 8):
            pl.semaphore_signal(bar, inc=1, device_id=((dp + i) % 8, sq), device_id_type=MESH)
        return bar, 22
    if column == "z":
        for to in (moved(me, "z", 1), moved(me, "z", -1), sibling_of(me)):
            pl.semaphore_signal(bar, inc=1, device_id=dev(to), device_id_type=MESH)
        return bar, 18
    return bar, 15


def dot(a, b, ca=1, cb=0):
    return lax.dot_general(a, b, (((ca,), (cb,)), ((), ())), preferred_element_type=F32)


class Gather:
    def __init__(self, me, orders, view, own, ss, rs, sib_s=None, sib_r=None, whole=""):
        self.me, self.orders, self.view, self.own, self.whole = me, orders, view, own, whole
        self.ss, self.rs, self.sib_s, self.sib_r = ss, rs, sib_s, sib_r
        self.count, self.last = len(orders), len(orders[0]) - 1

    def group(self, n, t, step, half=None):
        axes = self.whole + self.orders[n][:t]
        at = {**moved(self.me, self.orders[n][t], step), **{a: ALL for a in axes}}
        if half is not None and axes:
            at[axes[0]] = pl.ds(2 * half, 2)
        return at

    def kinds(self, n, t):
        return (0, 1, 2, 3) if t or self.whole else (0, 1, 2 + n % 2)

    def copy(self, n, t, kind, back=0):
        axis = self.orders[n][t]
        step = 1 if kind in (0, 2) else -1
        dst = self.view(n, self.group(n, t, back) if kind < 2 else self.group(n, t, back - step, kind - 2))
        src = self.own(n) if self.own and t == 0 and kind < 2 and back == 0 else dst
        return remote(src, dst, self.ss.at[n, t, kind], self.rs.at[n, t, kind], moved(self.me, axis, step))

    def arrived(self, n, t, kind):
        self.copy(n, t, kind, -1 if kind in (0, 2) else 1).wait_recv()

    def sibling(self, n, j, c):
        v = self.view(n, {**self.group(n, self.last, (0, -1, 1, 2)[j]), "c": c})
        return remote(v, v, self.sib_s.at[n, j], self.sib_r.at[n, j], sibling_of(self.me))

    def send(self, t, ns=None):
        for n in ns or range(self.count):
            if t:
                for k in self.kinds(n, t - 1)[2:]:
                    self.arrived(n, t - 1, k)
            self.copy(n, t, 0).start()
            self.copy(n, t, 1).start()
            if self.sib_s is not None and t == self.last:
                self.sibling(n, 0, self.me["c"]).start()

    def forward(self, t, ns=None):
        for n in ns or range(self.count):
            for k in (0, 1):
                self.arrived(n, t, k)
                if 2 + k in self.kinds(n, t):
                    self.copy(n, t, 2 + k).start()
                if self.sib_s is not None and t == self.last:
                    self.sibling(n, 1 + k, self.me["c"]).start()

    def finish(self, ns=None):
        for n in ns or range(self.count):
            for k in (2, 3):
                self.arrived(n, self.last, k)
            if self.sib_s is not None:
                self.sibling(n, 3, self.me["c"]).start()

    def siblings_in(self):
        for n in range(self.count):
            for j in range(4):
                self.sibling(n, j, 1 - self.me["c"]).wait_recv()

    def drain(self):
        for n in range(self.count):
            for t in range(self.last + 1):
                for k in self.kinds(n, t):
                    self.copy(n, t, k).wait_send()
            if self.sib_s is not None:
                for j in range(4):
                    self.sibling(n, j, self.me["c"]).wait_send()


class Scatter:
    def __init__(self, me, parts, acc, hop, fin, ss, rs, sib=None, source=None, sib_s=None, sib_r=None, loc_s=None, whole=""):
        self.whole = whole
        self.me, self.parts, self.acc, self.hop_b, self.fin_b = me, parts, acc, hop, fin
        self.ss, self.rs, self.sib, self.source = ss, rs, sib, source
        self.sib_s, self.sib_r, self.loc_s = sib_s, sib_r, loc_s
        self.count, self.last = len(parts), len(parts[0][2]) - 1

    def idx(self, n, at):
        name, p, _ = self.parts[n]
        place = tuple(at[a] for a in AXES[name])
        return place if name in "CF" else (p,) + place

    def slot(self, n):
        name, p, _ = self.parts[n]
        return () if name in "CF" else (p,)

    def done(self, n, t):
        name, _, order = self.parts[n]
        return [a for a in AXES[name] if a in self.whole + order[:t]]

    def group(self, n, t, step, half=None):
        axes = self.done(n, t)
        at = {**moved(self.me, self.parts[n][2][t], step), **{a: ALL for a in axes}}
        if half is not None and axes:
            at[axes[0]] = pl.ds(2 * half, 2)
        return at

    def kinds(self, n, t):
        return (0, 1) if t or self.whole else (n % 2,)

    def refs(self, n, t):
        name = self.parts[n][0]
        return self.acc[name], self.hop_b[t][name], self.fin_b[t][name]

    def hop_copy(self, n, t, kind):
        step = 1 if kind == 0 else -1
        a, h, _ = self.refs(n, t)
        return remote(a.at[self.idx(n, self.group(n, t, 2 * step, kind))], h.at[self.slot(n) + (kind,)],
                      self.ss.at[n, t, kind], self.rs.at[n, t, kind], moved(self.me, self.parts[n][2][t], step))

    def fin_copy(self, n, t, kind):
        step = 1 if kind == 0 else -1
        a, _, f = self.refs(n, t)
        return remote(a.at[self.idx(n, self.group(n, t, step))], f.at[self.slot(n) + (kind,)],
                      self.ss.at[n, t, 2 + kind], self.rs.at[n, t, 2 + kind], moved(self.me, self.parts[n][2][t], step))

    def each(self, n, t, at, fn, half=None):
        axes = self.done(n, t)
        sizes, offs = [4] * len(axes), [0] * len(axes)
        if half is not None and axes:
            sizes[0], offs[0] = 2, 2 * half
        total = 1
        for s in sizes:
            total *= s

        def one(i):
            pos, rest = [], i
            for s in sizes[::-1]:
                pos.append(rest % s)
                rest = rest // s
            pos = pos[::-1]
            where = dict(at)
            for a, p, o in zip(axes, pos, offs):
                where[a] = p + o
            fn(self.idx(n, where), tuple(pos))

        if total == 1:
            one(0)
        else:
            pl.loop(0, total, unroll=4)(one)

    def sib_copy(self, n, j):
        at = self.group(n, self.last, STEPS[j])
        return remote(self.source(n, at, 1 - self.me["c"]), self.sib[self.parts[n][0]].at[self.idx(n, at)],
                      self.sib_s.at[n, j], self.sib_r.at[n, j], sibling_of(self.me))

    def loc_copy(self, n, j):
        at = self.group(n, self.last, STEPS[j])
        return pltpu.make_async_copy(self.source(n, at, self.me["c"]), self.acc[self.parts[n][0]].at[self.idx(n, at)], self.loc_s.at[n, j])

    def start(self):
        for j in range(4):
            for n in range(self.count):
                self.sib_copy(n, j).start()
                self.loc_copy(n, j).start()

    def merge(self, j):
        for n in range(self.count):
            self.sib_copy(n, j).wait_recv()
            self.loc_copy(n, j).wait()
            a, b = self.acc[self.parts[n][0]], self.sib[self.parts[n][0]]

            def fn(i, _):
                a[i] = (a[i].astype(F32) + b[i].astype(F32)).astype(BF)

            self.each(n, self.last, self.group(n, self.last, STEPS[j]), fn)

    def hop(self, t, ns=None):
        for n in ns or range(self.count):
            for k in self.kinds(n, t):
                self.hop_copy(n, t, k).start()

    def pass_on(self, t, ns=None):
        for n in ns or range(self.count):
            a, h, _ = self.refs(n, t)
            for k in (0, 1):
                if k in self.kinds(n, t):
                    self.hop_copy(n, t, k).wait_recv()

                    def fn(i, pos):
                        j = self.slot(n) + (k,) + pos
                        a[i] = (a[i].astype(F32) + h[j].astype(F32)).astype(BF)

                    self.each(n, t, self.group(n, t, 1 if k == 0 else -1), fn, k)
                self.fin_copy(n, t, k).start()

    def close(self, t, ns=None):
        for n in ns or range(self.count):
            self.fin_copy(n, t, 0).wait_recv()
            self.fin_copy(n, t, 1).wait_recv()
            a, _, f = self.refs(n, t)

            def fn(i, pos):
                s = self.slot(n)
                a[i] = (a[i].astype(F32) + f[s + (0,) + pos].astype(F32) + f[s + (1,) + pos].astype(F32)).astype(BF)

            self.each(n, t, self.group(n, t, 0), fn)

    def result(self, n):
        self.fin_copy(n, 0, 0).wait_recv()
        self.fin_copy(n, 0, 1).wait_recv()
        a, _, f = self.refs(n, 0)
        s = self.slot(n)
        return a[self.idx(n, self.me)].astype(F32) + f[s + (0,)].astype(F32) + f[s + (1,)].astype(F32)

    def drain(self):
        for n in range(self.count):
            if self.sib is not None:
                for j in range(4):
                    self.sib_copy(n, j).wait_send()
            for t in range(self.last + 1):
                for k in self.kinds(n, t):
                    self.hop_copy(n, t, k).wait_send()
                self.fin_copy(n, t, 0).wait_send()
                self.fin_copy(n, t, 1).wait_send()


def stage_buffers(leads, *shapes):
    return [vm(*pre, *lead, *block) for lead in leads for pre, block in shapes]


LEADS = ((2, 2, 4), (2, 4, 4), (2, 2), (2, 4), (2,), (2,))


def staged(names, refs):
    k = len(names)
    got = [dict(zip(names, refs[k * i:k * i + k])) for i in range(len(refs) // k)]
    last = len(got) // 2 - 1
    return {last - t: got[2 * t] for t in range(last + 1)}, {last - t: got[2 * t + 1] for t in range(last + 1)}


def ffn_place(B, C):
    def place(n, at):
        if n < 2:
            return B.at[at["x"], at["y"], at["z"], at["c"], n]
        return C.at[at["z"], at["c"], at["x"], at["y"]]
    return place


def gather_kernel(attn, wi, wo, info, A, B, C, gains, lens, infos, stage, recv, blk, blkA, blkB, blkC, irecv,
                  fs, fr, ss, rs, sib_s, sib_r, as_, ar_, is_, ir_, ds_, dr_, own_s):
    me = where_am_i()
    dp, sq = lax.axis_index("dp"), lax.axis_index("seq")
    bar, count = meet(me, "dp")
    stage[:, 6:8, :] = jnp.zeros((16, 2, 640), F32)
    for s in range(16):
        stage[s, 0:6, 0:384] = attn[:, s // 2, 384 * (s % 2):384 * (s % 2) + 384]
        stage[s, 0:6, 384:640] = wi[:, s // 8, 256 * (s % 8):256 * (s % 8) + 256]
    pl.semaphore_wait(bar, count)

    def a2a(i):
        peer = (sq + i) % 16
        return pltpu.make_async_remote_copy(stage.at[peer], recv.at[sq], as_.at[i], ar_.at[i], device_id=(dp, peer), device_id_type=MESH)

    def inf(i):
        peer = (sq + i) % 16
        return pltpu.make_async_remote_copy(info, irecv.at[sq], is_.at[i], ir_.at[i], device_id=(dp, peer), device_id_type=MESH)

    for i in range(1, 16):
        a2a(i).start()
    for i in range(1, 16):
        inf(i).start()
    recv[sq] = stage[sq]
    irecv[sq] = info[...]
    blkC[...] = wo[...].astype(BF)
    for i in range(1, 16):
        a2a(i).wait_recv()
    for k in range(16):
        blk[6 * k:6 * k + 6, :] = recv[k, 0:6, :]
    for p in range(3):
        blkA[p] = blk[32 * p:32 * p + 32, 0:384].astype(BF)
    for p in range(2):
        blkB[p] = blk[48 * p:48 * p + 48, 384:640].astype(BF)
    place = lambda n, at: A.at[at["x"], at["y"], at["z"], at["c"], PARTS_A[n][1]]
    ring = Gather(me, [p[2] for p in PARTS_A], place, lambda n: blkA.at[n], ss, rs, sib_s, sib_r)
    place_f = ffn_place(B, C)
    mine = lambda n: blkB.at[n] if n < 2 else blkC
    ring_f = Gather(me, [p[2] for p in PARTS_G], place_f, mine, fs, fr)
    owns = [pltpu.make_async_copy(blkA.at[n], place(n, me), own_s.at[n]) for n in range(3)]
    owns += [pltpu.make_async_copy(mine(n), place_f(n, me), own_s.at[3 + n]) for n in range(3)]
    for o in owns:
        o.start()
    ring.send(0)
    ring_f.send(0)
    ring.forward(0)
    ring_f.forward(0)
    for o in owns:
        o.wait()
    ring.send(1)
    ring_f.send(1)
    ring.forward(1)
    ring.send(2)
    ring_f.forward(1)
    for i in range(1, 16):
        inf(i).wait_recv()
    tile = jnp.sum(irecv[...], axis=0)
    infos[dp] = tile

    def dpx(i, back=0):
        v = infos.at[(dp - back + 8) % 8]
        return pltpu.make_async_remote_copy(v, v, ds_.at[i], dr_.at[i], device_id=((dp + i) % 8, sq), device_id_type=MESH)

    for i in range(1, 8):
        dpx(i).start()
    ring.forward(2)
    for i in range(1, 8):
        dpx(i, i).wait_recv()
    lane = lax.broadcasted_iota(jnp.int32, (8, 128), 1)
    gains[...] = jnp.zeros((8, 768), F32)
    for d in range(8):
        lo, sh = 96 * d // 128, 96 * d % 128
        t = pltpu.roll(jnp.where(lane < 96, infos[d], 0.0), sh, 1)
        gains[:, 128 * lo:128 * lo + 128] += jnp.where(lane >= sh, t, 0.0)
        if sh > 32:
            gains[:, 128 * lo + 128:128 * lo + 256] += jnp.where(lane < sh, t, 0.0)
    pick = lax.broadcasted_iota(jnp.int32, (16, 128), 0) == lax.broadcasted_iota(jnp.int32, (16, 128), 1)
    lens[...] = jnp.broadcast_to(jnp.sum(jnp.where(pick, tile[3:4, :], 0.0), axis=1, keepdims=True), (16, 128))
    ring_f.finish()
    ring.finish()
    ring.siblings_in()
    ring_f.drain()
    for i in range(1, 16):
        a2a(i).wait_send()
        inf(i).wait_send()
    for i in range(1, 8):
        dpx(i).wait_send()
    ring.drain()


def gather(attn, wi, wo, info):
    return pl.pallas_call(
        gather_kernel,
        out_shape=(SDS((4, 4, 4, 2, 3, 32, 384), BF), SDS((4, 4, 4, 2, 2, 48, 256), BF), SDS((4, 2, 4, 4, 16, 768), BF), SDS((8, 768), F32), SDS((16, 128), F32)),
        in_specs=[VS] * 4, out_specs=(HS,) * 3 + (VS,) * 2,
        scratch_shapes=[vf(8, 8, 128), vf(16, 8, 640), vf(16, 8, 640), vf(96, 640), vm(3, 32, 384), vm(2, 48, 256), vm(16, 768), vf(16, 8, 128),
                        DMA((3, 2, 4)), DMA((3, 2, 4)), DMA((3, 3, 4)), DMA((3, 3, 4)), DMA((3, 4)), DMA((3, 4)), DMA((16,)), DMA((16,)), DMA((16,)), DMA((16,)), DMA((8,)), DMA((8,)), DMA((6,))],
        compiler_params=pltpu.CompilerParams(collective_id=0, has_side_effects=True, vmem_limit_bytes=60 << 20),
        name="gather_attention_weights",
    )(attn, wi, wo, info)


def info_tile(gain, mem_len):
    sq = lax.axis_index("seq")
    t = jnp.zeros((8, 128), F32)
    t = lax.dynamic_update_slice(t, gain.astype(BF).astype(F32), (0, 6 * sq))
    return lax.dynamic_update_slice(t, mem_len.astype(F32)[:, None], (3, sq))


def scatter_kernel(GA, sumE, sumF, gg, oA, oB, oC, oG, accA, sibA, h2, f2, h1, f1, h0, f0,
                   accE, accF, hE1, hF1, fE1, fF1, hE0, hF0, fE0, fF0, blk, stage, recv, gdp, gsum, gsq,
                   ss, rs, sib_s, sib_r, loc_s, as_, ar_, is_, ir_, ds_, dr_, es, er, ld_s):
    me = where_am_i()
    dp, sq = lax.axis_index("dp"), lax.axis_index("seq")
    bar, count = meet(me, "dp")
    loads = [pltpu.make_async_copy(a, b, ld_s.at[i]) for i, (a, b) in enumerate(((sumE, accE), (sumF, accF)))]
    for c in loads:
        c.start()
    pl.semaphore_wait(bar, count)
    hop, fin = staged("A", (h2, f2, h1, f1, h0, f0))
    ring = Scatter(me, PARTS_A, {"A": accA}, hop, fin, ss, rs, {"A": sibA},
                   lambda n, at, c: GA.at[at["x"], at["y"], at["z"], c, n], sib_s, sib_r, loc_s)
    fhop, ffin = staged("EF", (hE1, hF1, fE1, fF1, hE0, hF0, fE0, fF0))
    ring_f = Scatter(me, PARTS_G, {"E": accE, "F": accF}, fhop, ffin, es, er)
    ring.start()
    for c in loads:
        c.wait()
    ring_f.hop(1)

    def dpx(i):
        peer = (dp + i) % 8
        return pltpu.make_async_remote_copy(gg.at[peer], gdp.at[dp], ds_.at[i], dr_.at[i], device_id=(peer, sq), device_id_type=MESH)

    for i in range(1, 8):
        dpx(i).start()
    gdp[dp] = gg[dp]
    ring.merge(0)
    ring.hop(2)
    ring.merge(1)
    ring.merge(2)
    ring_f.pass_on(1)
    ring.pass_on(2)
    ring.merge(3)
    ring_f.close(1)
    ring_f.hop(0)
    for i in range(1, 8):
        dpx(i).wait_recv()
    gsum[...] = jnp.sum(gdp[...], axis=0)

    def inf(i):
        peer = (sq + i) % 16
        return pltpu.make_async_remote_copy(gsum, gsq.at[sq], is_.at[i], ir_.at[i], device_id=(dp, peer), device_id_type=MESH)

    for i in range(1, 16):
        inf(i).start()
    gsq[sq] = gsum[...]
    stage[:, 6:8, :] = jnp.zeros((16, 2, 640), F32)
    ring_f.pass_on(0)
    ring.close(2)
    ring.hop(1)
    for n in range(2):
        blk[48 * n:48 * n + 48, 384:640] = ring_f.result(n)
    oC[...] = ring_f.result(2)
    ring.pass_on(1)
    ring.close(1)
    ring.hop(0)
    ring.pass_on(0)
    for n in range(3):
        blk[32 * n:32 * n + 32, 0:384] = ring.result(n)
    for k in range(16):
        stage[k, 0:6, :] = blk[6 * k:6 * k + 6, :]

    def a2a(i):
        peer = (sq + i) % 16
        return pltpu.make_async_remote_copy(stage.at[peer], recv.at[sq], as_.at[i], ar_.at[i], device_id=(dp, peer), device_id_type=MESH)

    for i in range(1, 16):
        a2a(i).start()
    recv[sq] = stage[sq]
    for i in range(1, 16):
        inf(i).wait_recv()
    oG[...] = pltpu.roll(jnp.sum(gsq[...], axis=0), (128 - 6 * sq) % 128, 1)
    for i in range(1, 16):
        a2a(i).wait_recv()
    for s in range(16):
        oA[:, s // 2, 384 * (s % 2):384 * (s % 2) + 384] = recv[s, 0:6, 0:384]
        oB[:, s // 8, 256 * (s % 8):256 * (s % 8) + 256] = recv[s, 0:6, 384:640]
    for i in range(1, 8):
        dpx(i).wait_send()
    for i in range(1, 16):
        a2a(i).wait_send()
        inf(i).wait_send()
    ring.drain()
    ring_f.drain()


def scatter(GA, sumE, sumF, gg):
    return pl.pallas_call(
        scatter_kernel,
        out_shape=(SDS((6, 8, 768), F32), SDS((6, 2, 2048), F32), SDS((16, 768), F32), SDS((8, 128), F32)),
        in_specs=[HS, HS, HS, VS], out_specs=(VS,) * 4,
        scratch_shapes=[vm(3, 4, 4, 4, 32, 384), vm(3, 4, 4, 4, 32, 384), *stage_buffers(LEADS, ((3,), (32, 384))),
                        vm(2, 4, 4, 48, 256), vm(4, 4, 16, 768), *stage_buffers(LEADS[2:], ((2,), (48, 256)), ((), (16, 768))),
                        vf(96, 640), vf(16, 8, 640), vf(16, 8, 640), vf(8, 8, 128), vf(8, 128), vf(16, 8, 128),
                        DMA((3, 3, 4)), DMA((3, 3, 4)), DMA((3, 4)), DMA((3, 4)), DMA((3, 4)),
                        DMA((16,)), DMA((16,)), DMA((16,)), DMA((16,)), DMA((8,)), DMA((8,)), DMA((3, 2, 4)), DMA((3, 2, 4)), DMA((2,))],
        compiler_params=pltpu.CompilerParams(collective_id=1, has_side_effects=True, vmem_limit_bytes=60 << 20),
        name="scatter_attention_grads",
    )(GA, sumE, sumF, gg)


def head_masks(value=1.0):
    lane = lax.broadcasted_iota(jnp.int32, (1, 256), 1)
    return [jnp.where(lane // 64 == h, value, 0.0).astype(BF) for h in range(4)]


def stack_heads(block, masks):
    return jnp.concatenate([block * m for m in masks], axis=0)


def key_positions():
    sq = lax.axis_index("seq")
    return (192 * sq + lax.broadcasted_iota(jnp.int32, (192, 128), 0)).astype(F32)


class Merge:
    def __init__(self, me, src, mid, one, two, ss, rs):
        self.me, self.src, self.mid, self.bufs, self.ss, self.rs = me, src, mid, (one, two), ss, rs

    def block(self, n, a, b):
        return (n, a, b) if n % 2 == 0 else (n, b, a)

    def copy(self, n, t, k):
        axis = PLANE[n][t]
        to = moved(self.me, axis, (1, -1, 2)[k])
        src = self.src.at[self.block(n, to[axis], ALL)] if t == 0 else self.mid.at[n, to[axis]]
        return remote(src, self.bufs[t].at[n, k], self.ss.at[n, t, k], self.rs.at[n, t, k], to)

    def send(self, t, ns):
        for n in ns:
            for k in (2, 0, 1):
                self.copy(n, t, k).start()

    def join(self, blocks):
        rows = [b[128:144, :].astype(F32)[0:8, :] for b in blocks]
        logs = [r + pltpu.roll(r, 6, 0) + pltpu.roll(r, 4, 0) for r in rows]
        top = logs[0]
        for l in logs[1:]:
            top = jnp.maximum(top, l)
        ws = [jnp.exp(l - top) for l in logs]
        total = ws[0] + ws[1] + ws[2] + ws[3]
        inv = 1.0 / total
        out = []
        for h in range(2):
            o = sum(b[64 * h:64 * h + 64, :].astype(F32) * (w * inv)[h:h + 1, :] for b, w in zip(blocks, ws))
            out.append(o)
        return jnp.concatenate(out, axis=0), top + jnp.log(total)

    def middle(self, ns):
        for n in ns:
            for k in range(3):
                self.copy(n, 0, k).wait_recv()
            a = self.me[PLANE[n][0]]

            for b in range(4):
                o, l = self.join([self.src.at[self.block(n, a, b)]] + [self.bufs[0].at[n, k, b] for k in range(3)])
                self.mid[n, b, 0:128, :] = o.astype(BF)
                self.mid[n, b, 128:144, :] = log_tile(l)

    def result(self, n):
        for k in range(3):
            self.copy(n, 1, k).wait_recv()
        return self.join([self.mid.at[n, self.me[PLANE[n][1]]]] + [self.bufs[1].at[n, k] for k in range(3)])

    def drain(self):
        for n in range(6):
            for t in range(2):
                for k in range(3):
                    self.copy(n, t, k).wait_send()


def log_tile(l):
    l = jnp.where(lax.broadcasted_iota(jnp.int32, (8, 128), 0) < 2, l, 0.0)
    high = l.astype(BF).astype(F32)
    middle = (l - high).astype(BF).astype(F32)
    low = l - high - middle
    return jnp.concatenate([high + pltpu.roll(middle, 2, 0) + pltpu.roll(low, 4, 0), jnp.zeros((8, 128), F32)], axis=0).astype(BF)


def pair_of(ref, g, at):
    return jnp.concatenate([ref[2 * g, at["x"], at["y"]], ref[2 * g + 1, at["x"], at["y"]]], axis=1)


def cross_fwd_kernel(q, lens, mem_h, A, B_in, C_in, q_h, k_h, v_h, kt_h, B, C, o_ref, L_ref,
                     qall, mem, wk, wv, wkT, wvT, K, V, KT, VT, ost, mid, one, two, lrow,
                     mem_s, w_s, out_s, ss, rs, os_, or_, fs, fr, fsib_s, fsib_r):
    me = where_am_i()
    bar, count = meet(me, "z")

    def load_mem(e):
        return pltpu.make_async_copy(mem_h.at[e], mem.at[e], mem_s.at[e])

    loads = [pltpu.make_async_copy(A.at[10 + i], (wk if i < 2 else wv).at[:, pl.ds(384 * (i % 2), 384)], w_s.at[i]) for i in range(4)]
    for c in loads:
        c.start()

    @pl.loop(0, 16)
    def _(e):
        load_mem(e).start()

    for n in range(6):
        qall[n, me["x"], me["y"]] = q[:, 128 * n:128 * n + 128]
    lrow[...] = jnp.zeros((4, 2, 8, 128), F32)
    pl.semaphore_wait(bar, count)
    view = lambda n, at: qall.at[n, at["x"], at["y"]]
    plane = Gather(me, PLANE, view, lambda n: view(n, me), ss, rs)
    ring = Gather(me, ("z",) * 3, ffn_place(B, C), None, fs, fr, fsib_s, fsib_r, "xy")
    fold = Merge(me, ost, mid, one, two, os_, or_)
    plane.send(0)
    ring.send(0)
    for c in loads:
        c.wait()
    for i in range(6):
        wvT[:, 128 * i:128 * i + 128] = wv[128 * i:128 * i + 128, :].T
    plane.forward(0)

    def project(a, b):
        @pl.loop(a // 2, b // 2)
        def _(i):
            for e in (2 * i, 2 * i + 1):
                load_mem(e).wait()
            K[pl.ds(2 * i, 2)] = dot(mem[pl.ds(2 * i, 2)].reshape(384, 768), wk[...]).astype(BF).reshape(2, 192, 768)
            for e in (2 * i, 2 * i + 1):
                VT[e] = dot(wvT[...], mem[e], 1, 1).astype(BF)

    def project_more(a, b):
        @pl.loop(a // 2, b // 2)
        def _(i):
            V[pl.ds(2 * i, 2)] = dot(mem[pl.ds(2 * i, 2)].reshape(384, 768), wv[...]).astype(BF).reshape(2, 192, 768)
            for e in (2 * i, 2 * i + 1):
                KT[e] = dot(wkT[...], mem[e], 1, 1).astype(BF)

    plane.send(1, (0, 1))
    project(0, 4)
    plane.send(1, (2, 3))
    plane.send(1, (4, 5))
    project(4, 10)
    plane.forward(1, (0, 1))
    plane.forward(1, (2, 3))
    project(10, 16)
    plane.forward(1, (4, 5))
    masks = head_masks()
    pos = key_positions()

    def attend(g):
        cols = slice(256 * g, 256 * g + 256)

        @pl.loop(0, 4)
        def _(i):
            four = [(x, x * 4 + y, {"x": x, "y": y}) for x, y in [(i, y) for y in range(4)]]
            sT = [dot(K[e, :, cols], stack_heads(pair_of(qall, g, at), masks), 1, 1) for _, e, at in four]
            pT, inv = [], []
            for u, (_, e, at) in enumerate(four):
                live = pos < lens[pl.ds(e, 1), :]
                ps = []
                for h in range(4):
                    s = jnp.where(live, sT[u][:, 128 * h:128 * h + 128], NEG)
                    top = jnp.max(s, axis=0, keepdims=True)
                    p = jnp.exp(s - top)
                    tot = jnp.sum(p, axis=0, keepdims=True)
                    lrow[u, h // 2, h % 2:h % 2 + 1, :] = top + jnp.log(tot)
                    ps.append(p.astype(BF))
                    inv.append(1.0 / tot)
                pT.append(jnp.concatenate(ps, axis=1))
            oT = [dot(VT[e, cols, :], p) for (_, e, _), p in zip(four, pT)]
            for u, (_, e, at) in enumerate(four):
                for h in range(4):
                    ost[2 * g + h // 2, at["x"], at["y"], 64 * (h % 2):64 * (h % 2) + 64, :] = (
                        oT[u][64 * h:64 * h + 64, 128 * h:128 * h + 128] * inv[4 * u + h]).astype(BF)
                for h in range(2):
                    ost[2 * g + h, at["x"], at["y"], 128:144, :] = log_tile(lrow[u, h])

        fold.send(0, (2 * g, 2 * g + 1))

    def deliver(g):
        for n in (2 * g, 2 * g + 1):
            o, l = fold.result(n)
            o_ref[:, 128 * n:128 * n + 128] = o.T
            L_ref[2 * n:2 * n + 2, :] = l[0:2, :]

    plane.finish((0, 1))
    attend(0)
    plane.finish((2, 3))
    attend(1)
    fold.middle((0, 1))
    fold.send(1, (0, 1))
    plane.finish((4, 5))
    out_q = pltpu.make_async_copy(qall, q_h, out_s.at[0])
    out_k = pltpu.make_async_copy(K, k_h, out_s.at[1])
    out_q.start()
    out_k.start()
    ring.forward(0)
    attend(2)
    fold.middle((2, 3))
    fold.send(1, (2, 3))
    for i in range(6):
        wkT[:, 128 * i:128 * i + 128] = wk[128 * i:128 * i + 128, :].T
    project_more(0, 8)
    fold.middle((4, 5))
    fold.send(1, (4, 5))
    low, high = pl.ds(0, 8), pl.ds(8, 8)
    outs = [pltpu.make_async_copy(a.at[k], b.at[k], out_s.at[2 + 2 * i + j])
            for j, k in enumerate((low, high)) for i, (a, b) in enumerate(((V, v_h), (KT, kt_h)))]
    for c in outs[:2]:
        c.start()
    ring.finish()
    project_more(8, 16)
    for c in outs[2:]:
        c.start()
    L_ref[12:16, :] = jnp.zeros((4, 128), F32)
    for g in range(3):
        deliver(g)
    plane.drain()
    fold.drain()
    for c in [out_q, out_k] + outs:
        c.wait()
    ring.siblings_in()
    ring.drain()


def cross_fwd(q, lens, memory, A, B, C):
    return pl.pallas_call(
        cross_fwd_kernel,
        out_shape=(SDS((6, 4, 4, 128, 128), BF), SDS((16, 192, 768), BF), SDS((16, 192, 768), BF), SDS((16, 768, 192), BF),
                   SDS((4, 4, 4, 2, 2, 48, 256), BF), SDS((4, 2, 4, 4, 16, 768), BF), SDS((128, 768), F32), SDS((16, 128), F32)),
        in_specs=[VS] * 2 + [HS] * 4, out_specs=(HS,) * 6 + (VS,) * 2, input_output_aliases={4: 4, 5: 5},
        scratch_shapes=[vm(6, 4, 4, 128, 128), vm(16, 192, 768), vm(768, 768), vm(768, 768), vm(768, 768), vm(768, 768),
                        vm(16, 192, 768), vm(16, 192, 768), vm(16, 768, 192), vm(16, 768, 192),
                        vm(6, 4, 4, 144, 128), vm(6, 4, 144, 128), vm(6, 3, 4, 144, 128), vm(6, 3, 144, 128), vf(4, 2, 8, 128),
                        DMA((16,)), DMA((4,)), DMA((6,)), DMA((6, 2, 4)), DMA((6, 2, 4)), DMA((6, 2, 3)), DMA((6, 2, 3)),
                        DMA((3, 1, 4)), DMA((3, 1, 4)), DMA((3, 4)), DMA((3, 4))],
        compiler_params=pltpu.CompilerParams(collective_id=2, has_side_effects=True, vmem_limit_bytes=60 << 20),
        name="cross_forward",
    )(q, lens, memory, A, B, C)


def cross_bwd_kernel(do, st, lens, q_h, k_h, v_h, kt_h, mem_h, A, GB, GC, G_in, dq_ref, gm_h, dw_h, sumE, sumF,
                     qall, doall, stall, wk, wv, K, V, KT, mem, memT, dK, dV, gst, wst, dst, dh1, df1, dh0, df0,
                     accB, accC, sibB, sibC, hB2, hC2, fB2, fC2,
                     q_s, kv_s, mem_s, w_s, gm_s, dw_s, ss, rs, ds_, dr_, fs, fr, fsib_s, fsib_r, floc, sum_s):
    me = where_am_i()
    bar, count = meet(me, "z")

    def load_mem(e):
        return pltpu.make_async_copy(mem_h.at[pl.ds(pl.multiple_of(256 * e, 256), 256)], mem.at[e % 4], mem_s.at[e % 4])

    for e in range(4):
        load_mem(e).start()
    loads = [pltpu.make_async_copy(A.at[10 + i], (wk if i < 2 else wv).at[:, pl.ds(384 * (i % 2), 384)], w_s.at[i]) for i in range(4)]
    loads.append(pltpu.make_async_copy(q_h, qall, q_s))
    for n in range(6):
        doall[n, me["x"], me["y"]] = do[:, 128 * n:128 * n + 128]
    stall[me["x"], me["y"]] = st[...]
    pl.semaphore_wait(bar, count)

    def place(n, at):
        return stall.at[at["x"], at["y"]] if n == 6 else doall.at[n, at["x"], at["y"]]

    plane = Gather(me, PLANE + ("xy",), place, lambda n: place(n, me), ss, rs)
    fhop, ffin = staged("BC", (hB2, hC2, fB2, fC2))
    grads = ffn_place(GB, GC)
    ring = Scatter(me, PARTS_F, {"B": accB, "C": accC}, fhop, ffin, fs, fr, {"B": sibB, "C": sibC},
                   lambda n, at, c: grads(n, {**at, "c": c}), fsib_s, fsib_r, floc, "xy")
    back = Scatter(me, PARTS_D, {"D": dst}, {1: {"D": dh1}, 0: {"D": dh0}}, {1: {"D": df1}, 0: {"D": df0}}, ds_, dr_)
    plane.send(0, (6, 0, 1, 2, 3, 4, 5))
    ring.start()
    for c in loads:
        c.start()

    def turn(a, b):
        @pl.loop(a, b)
        def _(e):
            load_mem(e).wait()
            memT[:, pl.ds(pl.multiple_of(256 * e, 256), 256)] = mem[e % 4].T

            @pl.when(e < 8)
            def _():
                load_mem(e + 4).start()

    turn(0, 1)
    plane.forward(0, (6, 0, 1, 2, 3, 4, 5))
    turn(1, 3)
    plane.send(1, (6, 0, 1))
    plane.send(1, (2, 3))
    plane.send(1, (4, 5))
    ring.merge(0)
    ring.hop(0)
    turn(3, 6)
    plane.forward(1, (6, 0, 1))
    ring.merge(1)
    ring.merge(2)
    plane.forward(1, (2, 3))
    ring.pass_on(0)
    masks = head_masks()
    pos = key_positions()

    def load_kv(g, i, u, which):
        e = ((me["x"] + 2 + i) % 4) * 4 + u
        cols = pl.ds(256 * g, 256)
        src = (k_h.at[e, :, cols], v_h.at[e, :, cols], kt_h.at[e, cols])[which]
        return pltpu.make_async_copy(src, (K, V, KT)[which].at[i % 2, u], kv_s.at[which, i % 2, u])

    def fetch_kv(g, i):
        for u in range(4):
            for w in range(3):
                load_kv(g, i, u, w).start()

    fetch_kv(0, 0)
    for c in loads:
        c.wait()

    def attend(g):
        cols = slice(256 * g, 256 * g + 256)

        @pl.loop(0, 4)
        def _(i):
            @pl.when(i < 3)
            def _():
                fetch_kv(g, i + 1)

            for u in range(4):
                for w in range(3):
                    load_kv(g, i, u, w).wait()
            x = (me["x"] + 2 + i) % 4
            four = [(x * 4 + y, {"x": x, "y": y}) for y in range(4)]
            q4s = [stack_heads(pair_of(qall, g, at), masks) for _, at in four]
            d4s = [stack_heads(pair_of(doall, g, at), masks) for _, at in four]
            sT = [dot(K[i % 2, u], q4s[u], 1, 1) for u in range(4)]
            gT = [dot(V[i % 2, u], d4s[u], 1, 1) for u in range(4)]
            pT, sg = [], []
            for u, (e, at) in enumerate(four):
                live = pos < lens[pl.ds(e, 1), :]
                ps, gs = [], []
                for h in range(4):
                    n = 4 * g + h
                    s = jnp.where(live, sT[u][:, 128 * h:128 * h + 128], NEG)
                    p = jnp.exp(s - stall[at["x"], at["y"], n:n + 1, :])
                    ps.append(p.astype(BF))
                    gs.append((p * (gT[u][:, 128 * h:128 * h + 128] - stall[at["x"], at["y"], 12 + n:13 + n, :])).astype(BF))
                pT.append(jnp.concatenate(ps, axis=1))
                sg.append(jnp.concatenate(gs, axis=1))
            for u, (e, at) in enumerate(four):
                dV[pl.ds(pl.multiple_of(192 * e, 192), 192), cols] = dot(pT[u], d4s[u]).astype(BF)
            for u, (e, at) in enumerate(four):
                dK[pl.ds(pl.multiple_of(192 * e, 192), 192), cols] = dot(sg[u], q4s[u]).astype(BF)
            for u, (e, at) in enumerate(four):
                qT = dot(KT[i % 2, u], sg[u])
                for h in range(4):
                    dst[2 * g + h // 2, at["x"], at["y"], 64 * (h % 2):64 * (h % 2) + 64, :] = qT[64 * h:64 * h + 64, 128 * h:128 * h + 128].astype(BF)

        if g < 2:
            fetch_kv(g + 1, 0)
        back.hop(1, (2 * g, 2 * g + 1))

    plane.finish((6, 0, 1))
    attend(0)
    plane.forward(1, (4, 5))
    plane.finish((2, 3))
    attend(1)
    back.pass_on(1, (0, 1))
    ring.merge(3)
    plane.finish((4, 5))
    attend(2)
    back.pass_on(1, (2, 3))
    back.close(1, (0, 1))
    back.hop(0, (0, 1))

    def gm_copy(e):
        return pltpu.make_async_copy(gst.at[e % 2], gm_h.at[e], gm_s.at[e % 2])

    def mem_grad(a, b):
        @pl.loop(a, b)
        def _(e):
            @pl.when(e > 1)
            def _():
                gm_copy(e - 2).wait()

            rows = pl.ds(pl.multiple_of(384 * e, 384), 384)
            gst[e % 2] = dot(dK[rows, :], wk[...], 1, 1) + dot(dV[rows, :], wv[...], 1, 1)
            gm_copy(e).start()

    def dw_copy(k, r, half):
        rows = pl.ds(pl.multiple_of(256 * r, 256), 256)
        return pltpu.make_async_copy(wst.at[k, :, pl.ds(384 * half, 384)], dw_h.at[10 + 2 * k + half, rows], dw_s.at[k, half])

    def weight_grad(a, b):
        @pl.loop(a, b)
        def _(r):
            for k in range(2):
                @pl.when(r > 0)
                def _():
                    dw_copy(k, r - 1, 0).wait()
                    dw_copy(k, r - 1, 1).wait()

                wst[k] = dot(memT[pl.ds(pl.multiple_of(256 * r, 256), 256), :], (dV if k else dK)[...]).astype(BF)
                dw_copy(k, r, 0).start()
                dw_copy(k, r, 1).start()

    turn(6, 12)
    back.pass_on(1, (4, 5))
    back.close(1, (2, 3))
    back.hop(0, (2, 3))
    back.pass_on(0, (0, 1))
    mem_grad(0, 4)
    back.close(1, (4, 5))
    back.hop(0, (4, 5))
    back.pass_on(0, (2, 3))
    mem_grad(4, 8)
    ring.close(0)
    sums = [pltpu.make_async_copy(accB.at[:, :, :, me["z"]], sumE, sum_s.at[0]), pltpu.make_async_copy(accC.at[me["z"]], sumF, sum_s.at[1])]
    for c in sums:
        c.start()
    back.pass_on(0, (4, 5))
    weight_grad(0, 3)
    for n in range(6):
        dq_ref[:, 128 * n:128 * n + 128] = (0.125 * back.result(n)).T
    for c in sums:
        c.wait()
    gm_copy(6).wait()
    gm_copy(7).wait()
    for k in range(2):
        dw_copy(k, 2, 0).wait()
        dw_copy(k, 2, 1).wait()
    plane.drain()
    ring.drain()
    back.drain()


def cross_bwd(do, st, lens, q_h, k_h, v_h, kt_h, memory, A, GB, GC, GA):
    bB, bC = (48, 256), (16, 768)
    return pl.pallas_call(
        cross_bwd_kernel,
        out_shape=(SDS((128, 768), F32), SDS((8, 384, 768), F32), SDS((16, 768, 384), BF), SDS((2, 4, 4, 48, 256), BF), SDS((4, 4, 16, 768), BF)),
        in_specs=[VS] * 3 + [HS] * 9, out_specs=(VS,) + (HS,) * 4, input_output_aliases={11: 2},
        scratch_shapes=[vm(6, 4, 4, 128, 128), vm(6, 4, 4, 128, 128), vf(4, 4, 24, 128), vm(768, 768), vm(768, 768),
                        vm(2, 4, 192, 256), vm(2, 4, 192, 256), vm(2, 4, 256, 192), vm(4, 256, 768), vm(768, 3072), vm(3072, 768), vm(3072, 768),
                        vf(2, 384, 768), vm(2, 256, 768), vm(6, 4, 4, 128, 128), vm(6, 2, 2, 128, 128), vm(6, 2, 4, 128, 128), vm(6, 2, 128, 128), vm(6, 2, 128, 128),
                        vm(2, 4, 4, 4, *bB), vm(4, 4, 4, *bC), vm(2, 4, 4, 4, *bB), vm(4, 4, 4, *bC), *stage_buffers(LEADS[:2], ((2,), bB), ((), bC)),
                        DMA, DMA((3, 2, 4)), DMA((4,)), DMA((4,)), DMA((2,)), DMA((2, 2)), DMA((7, 2, 4)), DMA((7, 2, 4)), DMA((6, 2, 4)), DMA((6, 2, 4)),
                        DMA((3, 1, 4)), DMA((3, 1, 4)), DMA((3, 4)), DMA((3, 4)), DMA((3, 4)), DMA((2,))],
        compiler_params=pltpu.CompilerParams(collective_id=3, has_side_effects=True, vmem_limit_bytes=60 << 20),
        name="cross_backward",
    )(do, st, lens, q_h, k_h, v_h, kt_h, memory.reshape(3072, 768), A, GB, GC, GA)


def adam_update(master, first, second, grad, rate):
    first_new = beta_one * first + (1.0 - beta_one) * grad
    second_new = beta_two * second + (1.0 - beta_two) * grad * grad
    fix_one = 1.0 - beta_one**STEP
    fix_two = 1.0 - beta_two**STEP
    master_new = master - rate * (
        first_new / fix_one / (jnp.sqrt(second_new / fix_two) + adam_eps) + decay_rate * master
    )
    return (master_new, first_new, second_new, master_new.astype(jnp.bfloat16))


def rms(x):
    return lax.rsqrt(jnp.mean(x * x, axis=-1, keepdims=True) + eps_norm)

def rms_back(x, inv, gain, u):
    scaled = u * gain
    inner = jnp.mean(scaled * x, axis=-1, keepdims=True)
    return inv * scaled - x * inv * inv * inv * inner, jnp.sum(u * x * inv, axis=0, keepdims=True)

def flip(x):
    return jnp.concatenate([x[:, 128 * i:128 * i + 128].T for i in range(x.shape[1] // 128)], axis=0)

def unflip(x):
    return jnp.concatenate([x[128 * i:128 * i + 128, :].T for i in range(x.shape[0] // 128)], axis=1)

def apply_w(h, W, k):
    return jnp.concatenate([dot(h, W[2 * k]), dot(h, W[2 * k + 1])], axis=1)

def apply_wt(u, W, k):
    return dot(u[:, 0:384], W[2 * k], 1, 1) + dot(u[:, 384:768], W[2 * k + 1], 1, 1)

def causal_mask():
    return lax.broadcasted_iota(jnp.int32, (128, 128), 0) <= lax.broadcasted_iota(jnp.int32, (128, 128), 1)

def self_fwd_kernel(x_ref, gains, A, q2, h1, qkv, o1, x1, h2, L1, W, sem):
    loads = [pltpu.make_async_copy(A.at[i], W.at[i], sem.at[i]) for i in range(10)]
    for c in loads:
        c.start()
    x = x_ref[...].astype(F32)
    h = (x * rms(x) * gains[0:1, :]).astype(BF)
    h1[...] = h
    for k in range(3):
        loads[2 * k].wait()
        loads[2 * k + 1].wait()
        full = apply_w(h, W, k)
        qkv[k] = full.astype(BF)
    vT = flip(full).astype(BF)
    masks = head_masks(0.125)
    live = causal_mask()
    outs = []
    for g in range(3):
        cols = slice(256 * g, 256 * g + 256)
        q4 = qkv[0, :, cols]
        sT = dot(qkv[1, :, cols], jnp.concatenate([q4 * m for m in masks], axis=0), 1, 1)
        ps = []
        for n in range(4):
            s = jnp.where(live, sT[:, 128 * n:128 * n + 128], NEG)
            top = jnp.max(s, axis=0, keepdims=True)
            lse = top + jnp.log(jnp.sum(jnp.exp(s - top), axis=0, keepdims=True))
            L1[4 * g + n:4 * g + n + 1, :] = lse
            ps.append(jnp.exp(s - lse).astype(BF))
        oT = dot(vT[256 * g:256 * g + 256, :], jnp.concatenate(ps, axis=1))
        outs += [oT[64 * n:64 * n + 64, 128 * n:128 * n + 128] for n in range(4)]
    o = unflip(jnp.concatenate(outs, axis=0)).astype(BF)
    o1[...] = o
    for c in loads[6:]:
        c.wait()
    x = x + apply_w(o, W, 3)
    x1[...] = x
    h = (x * rms(x) * gains[1:2, :]).astype(BF)
    h2[...] = h
    q2[...] = apply_w(h, W, 4).astype(BF) * jnp.asarray(0.125, BF)

def self_fwd(x, gains, A):
    row = SDS((128, 768), BF)
    return pl.pallas_call(
        self_fwd_kernel,
        out_shape=(row, row, SDS((3, 128, 768), BF), row, SDS((128, 768), F32), row, SDS((16, 128), F32)),
        in_specs=[VS, VS, HS], out_specs=(VS,) * 7,
        scratch_shapes=[pltpu.VMEM((10, 768, 384), BF), pltpu.SemaphoreType.DMA((10,))],
        compiler_params=pltpu.CompilerParams(vmem_limit_bytes=60 << 20),
        name="self_forward",
    )(x, gains, A)

def ffn_kernel(x1, o2, L2, dy_ref, gains, A, B, C, out, do2, st, dx2, gg, GA, GB, GC,
               W7, WB, WC, gA, gB, gC, sw, sb, sc, tb, tc, ta):
    lA = [pltpu.make_async_copy(A.at[14 + i], W7.at[i], sw.at[i]) for i in range(2)]
    lB = [pltpu.make_async_copy(B.at[i], WB.at[i], sb.at[i]) for i in range(16)]
    lC = [pltpu.make_async_copy(C.at[i], WC.at[i], sc.at[i]) for i in range(8)]
    for c in lA:
        c.start()
    for j in range(8):
        lB[j].start()
        lB[8 + j].start()
        lC[j].start()
    o = o2[...]
    ob = o.astype(BF)
    for c in lA:
        c.wait()
    x = x1[...] + apply_w(ob, W7, 0)
    inv = rms(x)
    h = (x * inv * gains[2:3, :]).astype(BF)
    hT = flip(h.astype(F32)).astype(BF)
    df = dy_ref[...]
    y = jnp.zeros((128, 768), F32)
    dh = jnp.zeros((128, 768), F32)
    c0 = 0.7978845608028654
    sB, sC = [], []
    for j0 in range(0, 8, 2):
        js = range(j0, j0 + 2)
        for j in js:
            lB[j].wait()
            lB[8 + j].wait()
            lC[j].wait()
        a_s = [dot(h, WB[j]) for j in js]
        ups = [dot(h, WB[8 + j]) for j in js]
        dms = [dot(df, WC[j], 1, 1) for j in js]
        mids, dgs, dus = [], [], []
        for a, up, dm in zip(a_s, ups, dms):
            t = jnp.tanh(c0 * (a + 0.044715 * a * a * a))
            half = 0.5 * (1.0 + t)
            gel = a * half
            der = half + 0.5 * a * (1.0 - t * t) * (c0 * (1.0 + 0.134145 * a * a))
            mids.append(gel * up)
            dgs.append((dm * up * der).astype(BF))
            dus.append((dm * gel).astype(BF))
        y += dot(jnp.concatenate([m.astype(BF) for m in mids], axis=1), WC[j0:j0 + 2].reshape(2 * 256, 768))
        for n, j in enumerate(js):
            dh += dot(dgs[n], WB[j], 1, 1) + dot(dus[n], WB[8 + j], 1, 1)
        for n, j in enumerate(js):
            gB[j] = dot(hT, dgs[n]).astype(BF)
            gB[8 + j] = dot(hT, dus[n]).astype(BF)
            gC[j] = dot(flip(mids[n]).astype(BF), df).astype(BF)
        for j in js:
            new = [pltpu.make_async_copy(gB.at[j], GB.at[j], tb.at[j]), pltpu.make_async_copy(gB.at[8 + j], GB.at[8 + j], tb.at[8 + j]),
                   pltpu.make_async_copy(gC.at[j], GC.at[j], tc.at[j])]
            for c in new:
                c.start()
            sB += new
    out[...] = (x + y).astype(BF)
    dz, gain = rms_back(x, inv, gains[2:3, :], dh)
    gg[...] = gain
    d = df.astype(F32) + dz
    dx2[...] = d
    dc = d.astype(BF)
    dof = apply_wt(dc, W7, 0).astype(BF)
    do2[...] = dof
    prod = flip(dof.astype(F32) * o)
    st[0:12, :] = L2[0:12, :]
    for n in range(12):
        st[12 + n:13 + n, :] = jnp.sum(prod[64 * n:64 * n + 64, :], axis=0, keepdims=True)
    oT = flip(o).astype(BF)
    sA = []
    for i in range(2):
        gA[i] = dot(oT, dc[:, 384 * i:384 * i + 384]).astype(BF)
        sA.append(pltpu.make_async_copy(gA.at[i], GA.at[14 + i], ta.at[i]))
        sA[-1].start()
    for c in sA + sB + sC:
        c.wait()

def ffn(x1, o2, L2, dy, gains, A, B, C):
    M = lambda *s: pltpu.VMEM(s, BF)
    D = pltpu.SemaphoreType.DMA
    return pl.pallas_call(
        ffn_kernel,
        out_shape=(SDS((128, 768), BF), SDS((128, 768), BF), SDS((24, 128), F32), SDS((128, 768), F32), SDS((1, 768), F32),
                   SDS((16, 768, 384), BF), SDS((16, 768, 256), BF), SDS((8, 256, 768), BF)),
        in_specs=[VS] * 5 + [HS] * 3, out_specs=(VS,) * 5 + (HS,) * 3,
        scratch_shapes=[M(2, 768, 384), M(16, 768, 256), M(8, 256, 768), M(2, 768, 384), M(16, 768, 256), M(8, 256, 768),
                        D((2,)), D((16,)), D((8,)), D((16,)), D((8,)), D((2,))],
        compiler_params=pltpu.CompilerParams(vmem_limit_bytes=60 << 20),
        name="feed_forward",
    )(x1, o2, L2, dy, gains, A, B, C)

def self_bwd_kernel(dq2, h2, x1, dx2, qkv, o1, L1, x_ref, h1, gains, g3, A, GA_in, gm_in, gin, tile, GA, gm,
                    W, G, gb, gmv, sem, gsem, msem):
    loads = [pltpu.make_async_copy(A.at[i], W.at[i], sem.at[i]) for i in range(10)]
    for i in (8, 9, 6, 7, 0, 1, 2, 3, 4, 5):
        loads[i].start()
    def gm_load(e):
        return pltpu.make_async_copy(gm_in.at[e], gmv.at[e], msem.at[e])
    def gm_store(e):
        return pltpu.make_async_copy(gmv.at[e], gm.at[e], msem.at[16 + e])
    for e in range(16):
        gm_load(e).start()
    stores = []
    def weight_grad(k, left, inc):
        for i in range(2):
            n = 2 * k + i
            G[n] = dot(left, inc[:, 384 * i:384 * i + 384]).astype(BF)
            stores.append(pltpu.make_async_copy(G.at[n], GA.at[n], gsem.at[n]))
            stores[-1].start()
    dqb = dq2[...].astype(BF)
    for i in (8, 9, 6, 7):
        loads[i].wait()
    u = apply_wt(dqb, W, 4)
    x = x1[...]
    inv = rms(x)
    dz, gain = rms_back(x, inv, gains[1:2, :], u)
    gb[...] = jnp.zeros((8, 768), F32)
    gb[1:2, :] = gain
    gb[2:3, :] = g3[...]
    d1 = dx2[...] + dz
    da = d1.astype(BF)
    do1 = apply_wt(da, W, 3).astype(BF)
    weight_grad(4, flip(h2[...].astype(F32)).astype(BF), dqb)
    masks = head_masks(0.125)
    ones = head_masks(1.0)
    live = causal_mask()
    kT = flip(qkv[1].astype(F32)).astype(BF)
    qs, ks, vs = [], [], []
    for g in range(3):
        cols = slice(256 * g, 256 * g + 256)
        q4 = qkv[0, :, cols]
        d4 = do1[:, cols]
        q4s = jnp.concatenate([q4 * m for m in masks], axis=0)
        d4s = jnp.concatenate([d4 * m for m in ones], axis=0)
        sT = dot(qkv[1, :, cols], q4s, 1, 1)
        gT = dot(qkv[2, :, cols], d4s, 1, 1)
        ps, gs = [], []
        for n in range(4):
            s = jnp.where(live, sT[:, 128 * n:128 * n + 128], NEG)
            p = jnp.exp(s - L1[4 * g + n:4 * g + n + 1, :])
            gt = gT[:, 128 * n:128 * n + 128]
            ps.append(p.astype(BF))
            gs.append((p * (gt - jnp.sum(p * gt, axis=0, keepdims=True))).astype(BF))
        sg = jnp.concatenate(gs, axis=1)
        vs.append(dot(jnp.concatenate(ps, axis=1), d4s).astype(BF))
        ks.append(dot(sg, q4s).astype(BF))
        qT = dot(kT[256 * g:256 * g + 256, :], sg)
        qs += [qT[64 * n:64 * n + 64, 128 * n:128 * n + 128] for n in range(4)]
    for e in range(16):
        gm_load(e).wait()
        gm_store(e).start()
    inc = [(0.125 * unflip(jnp.concatenate(qs, axis=0))).astype(BF), jnp.concatenate(ks, axis=1), jnp.concatenate(vs, axis=1)]
    weight_grad(3, flip(o1[...].astype(F32)).astype(BF), da)
    for c in loads[:6]:
        c.wait()
    u = apply_wt(inc[0], W, 0) + apply_wt(inc[1], W, 1) + apply_wt(inc[2], W, 2)
    x = x_ref[...].astype(F32)
    inv = rms(x)
    dz, gain = rms_back(x, inv, gains[0:1, :], u)
    gb[0:1, :] = gain
    gin[...] = d1 + dz
    hT = flip(h1[...].astype(F32)).astype(BF)
    for k in range(3):
        weight_grad(k, hT, inc[k])
    lane = lax.broadcasted_iota(jnp.int32, (8, 128), 1)
    for d in range(8):
        lo, sh = 96 * d // 128, 96 * d % 128
        t = pltpu.roll(gb[:, 128 * lo:128 * lo + 128], (128 - sh) % 128, 1)
        if sh > 32:
            nxt = pltpu.roll(gb[:, 128 * lo + 128:128 * lo + 256], (128 - sh) % 128, 1)
            t = jnp.where(lane < 128 - sh, t, nxt)
        tile[d] = jnp.where(lane < 96, t, 0.0)
    for c in stores:
        c.wait()
    for e in range(16):
        gm_store(e).wait()

def self_bwd(dq2, h2, x1, dx2, qkv, o1, L1, x, h1, gains, g3, A, GA, gm):
    D = pltpu.SemaphoreType.DMA
    return pl.pallas_call(
        self_bwd_kernel,
        out_shape=(SDS((128, 768), F32), SDS((8, 8, 128), F32), SDS((16, 768, 384), BF), SDS((16, 192, 768), F32)),
        in_specs=[VS] * 11 + [HS] * 3, out_specs=(VS, VS, HS, HS),
        input_output_aliases={12: 2},
        scratch_shapes=[pltpu.VMEM((10, 768, 384), BF), pltpu.VMEM((10, 768, 384), BF), pltpu.VMEM((8, 768), F32), pltpu.VMEM((16, 192, 768), F32), D((10,)), D((10,)), D((32,))],
        compiler_params=pltpu.CompilerParams(vmem_limit_bytes=60 << 20),
        name="self_backward",
    )(dq2, h2, x1, dx2, qkv, o1, L1, x, h1, gains, g3, A, GA, gm)

def adam_kernel(*refs):
    ins, outs = refs[:16], refs[16:]
    for n in range(4):
        w, m, v, g = ins[4 * n:4 * n + 4]
        grad = g[0:3, 0:6] if n == 3 else g[...]
        for o, val in zip(outs[4 * n:4 * n + 4], adam_update(w[...], m[...], v[...], grad, rate_gain if n == 3 else rate_matrix)):
            o[...] = val

def adam(*args):
    shapes = []
    for n in range(4):
        s = args[4 * n].shape
        shapes += [SDS(s, F32)] * 3 + [SDS(s, BF)]
    return pl.pallas_call(adam_kernel, out_shape=tuple(shapes), in_specs=[VS] * 16, out_specs=(VS,) * 16,
                          compiler_params=pltpu.CompilerParams(vmem_limit_bytes=60 << 20), name="adam")(*args)


def body(
    dec_input,
    memory,
    mem_len,
    grad_out,
    attn_master,
    ffn_in_master,
    ffn_out_master,
    gain_master,
    attn_first,
    ffn_in_first,
    ffn_out_first,
    gain_first,
    attn_second,
    ffn_in_second,
    ffn_out_second,
    gain_second,
):
    swap = lambda a: a.transpose(1, 0, 2)
    attn_t, in_t = swap(attn_master), swap(ffn_in_master)
    gath_a, gath_b, gath_c, gains, lens = gather(attn_t, in_t, ffn_out_master, info_tile(gain_master, mem_len))
    aw = gath_a.reshape(16, 768, 384)
    x = dec_input[0]
    q2, h1, qkv, o1, x1, h2, L1 = self_fwd(x, gains, aw)
    q_all, k_two, v_two, kt_two, gath_b, gath_c, o2, L2 = cross_fwd(q2, lens, memory, aw, gath_b, gath_c)
    out_block, do2, st, dx2, g3, GA, GB, GC = ffn(x1, o2, L2, grad_out[0], gains, aw, gath_b.reshape(16, 768, 256), gath_c.reshape(8, 256, 768))
    dq2, gm, GA, sum_b, sum_c = cross_bwd(
        do2, st, lens, q_all, k_two, v_two, kt_two, memory, aw,
        GB.reshape(4, 4, 4, 2, 2, 48, 256), GC.reshape(4, 2, 4, 4, 16, 768), GA,
    )
    grad_input, tile_g, GA, grad_memory = self_bwd(dq2, h2, x1, dx2, qkv, o1, L1, x, h1, gains, g3, aw, GA, gm.reshape(16, 192, 768))
    share_a, share_b, share_c, share_g = scatter(GA.reshape(4, 4, 4, 2, 3, 32, 384), sum_b, sum_c, tile_g)
    new = adam(
        attn_t, swap(attn_first), swap(attn_second), share_a,
        in_t, swap(ffn_in_first), swap(ffn_in_second), share_b,
        ffn_out_master, ffn_out_first, ffn_out_second, share_c,
        gain_master, gain_first, gain_second, share_g,
    )
    return (out_block[None], grad_input[None], grad_memory, *[swap(a) for a in new[:8]], *new[8:])


def solution(mesh):
    placed = (
        P(("dp", "seq"), None, None),
        P("dp", "seq", None),
        P(("dp", "seq")),
        P(("dp", "seq"), None, None),
        P(None, ("dp", "seq"), None),
        P(None, ("dp", "seq"), None),
        P(("dp", "seq"), None),
        P(None, ("dp", "seq")),
        P(None, ("dp", "seq"), None),
        P(None, ("dp", "seq"), None),
        P(("dp", "seq"), None),
        P(None, ("dp", "seq")),
        P(None, ("dp", "seq"), None),
        P(None, ("dp", "seq"), None),
        P(("dp", "seq"), None),
        P(None, ("dp", "seq")),
    )
    return jax.shard_map(
        body,
        mesh=mesh,
        in_specs=placed,
        out_specs=(
            P(("dp", "seq"), None, None),
            P(("dp", "seq"), None, None),
            P("dp", "seq", None),
            P(None, ("dp", "seq"), None),
            P(None, ("dp", "seq"), None),
            P(None, ("dp", "seq"), None),
            P(None, ("dp", "seq"), None),
            P(None, ("dp", "seq"), None),
            P(None, ("dp", "seq"), None),
            P(None, ("dp", "seq"), None),
            P(None, ("dp", "seq"), None),
            P(("dp", "seq"), None),
            P(("dp", "seq"), None),
            P(("dp", "seq"), None),
            P(("dp", "seq"), None),
            P(None, ("dp", "seq")),
            P(None, ("dp", "seq")),
            P(None, ("dp", "seq")),
            P(None, ("dp", "seq")),
        ),
        check_vma=False,
    )
```

```python
import jax
import jax.numpy as jnp
from jax import lax
from jax.experimental import pallas as pl
from jax.experimental.pallas import tpu as pltpu
from jax.sharding import PartitionSpec as P

eps_norm = 1e-06
beta_one = 0.9
beta_two = 0.999
adam_eps = 1e-08
decay_rate = 0.01
rate_matrix = 0.12
rate_gain = 3.0
STEP = 10
MESH = pl.DeviceIdType.MESH
BF, F32 = jnp.bfloat16, jnp.float32
ALL = slice(None)
NEG = -1e30
PARTS_A = (("A", 0, "xyz"), ("A", 1, "yzx"), ("A", 2, "zxy"))
PARTS_F = (("B", 0, "z"), ("B", 1, "z"), ("C", 0, "z"))
PARTS_G = (("E", 0, "xy"), ("E", 1, "yx"), ("F", 0, "xy"))
PLANE = ("xy", "yx") * 3
PARTS_D = tuple(("D", n, PLANE[n]) for n in range(6))
AXES = {"A": "xyz", "B": "xyz", "C": "zxy", "D": "xy", "E": "xy", "F": "xy"}
STEPS = (2, -1, 1, 0)
VS = pl.BlockSpec(memory_space=pltpu.VMEM)
HS = pl.BlockSpec(memory_space=pltpu.HBM)
SDS = jax.ShapeDtypeStruct
DMA = pltpu.SemaphoreType.DMA


def vm(*shape):
    return pltpu.VMEM(shape, BF)


def vf(*shape):
    return pltpu.VMEM(shape, F32)


def where_am_i():
    dp, sq = lax.axis_index("dp"), lax.axis_index("seq")
    return {"x": sq // 4, "y": sq % 4, "z": dp // 2, "c": dp % 2}


def dev(at):
    return (at["z"] * 2 + at["c"], at["x"] * 4 + at["y"])


def moved(at, axis, step):
    return {**at, axis: (at[axis] + step + 4) % 4}


def offset(me, j, sign=1):
    return {**me, "x": (me["x"] + sign * (j // 4) + 4) % 4, "y": (me["y"] + sign * (j % 4) + 4) % 4}


def sibling_of(me):
    return {**me, "c": 1 - me["c"]}


def remote(src, dst, send, recv, to):
    return pltpu.make_async_remote_copy(src, dst, send, recv, device_id=dev(to), device_id_type=MESH)


def meet(me, column):
    dp, sq = lax.axis_index("dp"), lax.axis_index("seq")
    bar = pltpu.get_barrier_semaphore()
    for i in range(1, 16):
        pl.semaphore_signal(bar, inc=1, device_id=(dp, (sq + i) % 16), device_id_type=MESH)
    if column == "dp":
        for i in range(1, 8):
            pl.semaphore_signal(bar, inc=1, device_id=((dp + i) % 8, sq), device_id_type=MESH)
        return bar, 22
    if column == "z":
        for to in (moved(me, "z", 1), moved(me, "z", -1), sibling_of(me)):
            pl.semaphore_signal(bar, inc=1, device_id=dev(to), device_id_type=MESH)
        return bar, 18
    return bar, 15


def dot(a, b, ca=1, cb=0):
    return lax.dot_general(a, b, (((ca,), (cb,)), ((), ())), preferred_element_type=F32)


class Gather:
    def __init__(self, me, orders, view, own, ss, rs, sib_s=None, sib_r=None, whole=""):
        self.me, self.orders, self.view, self.own, self.whole = me, orders, view, own, whole
        self.ss, self.rs, self.sib_s, self.sib_r = ss, rs, sib_s, sib_r
        self.count, self.last = len(orders), len(orders[0]) - 1

    def group(self, n, t, step, half=None):
        axes = self.whole + self.orders[n][:t]
        at = {**moved(self.me, self.orders[n][t], step), **{a: ALL for a in axes}}
        if half is not None and axes:
            at[axes[0]] = pl.ds(2 * half, 2)
        return at

    def kinds(self, t):
        return (0, 1, 2, 3) if t == self.last else (0, 1, 2)

    def copy(self, n, t, kind, back=0):
        straight = kind < 2 or t < self.last
        step = (1, -1, 2 if straight else 1, -1)[kind]
        dst = self.view(n, self.group(n, t, back) if straight else self.group(n, t, back - step, kind - 2))
        src = self.own(n) if self.own and t == 0 and straight and back == 0 else dst
        return remote(src, dst, self.ss.at[n, t, kind], self.rs.at[n, t, kind], moved(self.me, self.orders[n][t], step))

    def arrived(self, n, t, kind):
        self.copy(n, t, kind, (-1, 1, -2 if t < self.last else -1, 1)[kind]).wait_recv()

    def sibling(self, n, j, c):
        v = self.view(n, {**self.group(n, self.last, (0, -1, 1, 2)[j]), "c": c})
        return remote(v, v, self.sib_s.at[n, j], self.sib_r.at[n, j], sibling_of(self.me))

    def send(self, t, ns=None):
        for n in ns or range(self.count):
            if t:
                for k in range(3):
                    self.arrived(n, t - 1, k)
            for k in (0, 1) if t == self.last else (2, 0, 1):
                self.copy(n, t, k).start()
            if self.sib_s is not None and t == self.last:
                self.sibling(n, 0, self.me["c"]).start()

    def forward(self, ns=None):
        for n in ns or range(self.count):
            for k in (0, 1):
                self.arrived(n, self.last, k)
                self.copy(n, self.last, 2 + k).start()
                if self.sib_s is not None:
                    self.sibling(n, 1 + k, self.me["c"]).start()

    def finish(self, ns=None):
        for n in ns or range(self.count):
            for k in (2, 3):
                self.arrived(n, self.last, k)
            if self.sib_s is not None:
                self.sibling(n, 3, self.me["c"]).start()

    def siblings_in(self):
        for n in range(self.count):
            for j in range(4):
                self.sibling(n, j, 1 - self.me["c"]).wait_recv()

    def drain(self):
        for n in range(self.count):
            for t in range(self.last + 1):
                for k in self.kinds(t):
                    self.copy(n, t, k).wait_send()
            if self.sib_s is not None:
                for j in range(4):
                    self.sibling(n, j, self.me["c"]).wait_send()


class Scatter:
    def __init__(self, me, parts, acc, hop, fin, ss, rs, sib=None, source=None, sib_s=None, sib_r=None, loc_s=None, whole=""):
        self.whole = whole
        self.me, self.parts, self.acc, self.hop_b, self.fin_b = me, parts, acc, hop, fin
        self.ss, self.rs, self.sib, self.source = ss, rs, sib, source
        self.sib_s, self.sib_r, self.loc_s = sib_s, sib_r, loc_s
        self.count, self.last = len(parts), len(parts[0][2]) - 1

    def idx(self, n, at):
        name, p, _ = self.parts[n]
        place = tuple(at[a] for a in AXES[name])
        return place if name in "CF" else (p,) + place

    def slot(self, n):
        name, p, _ = self.parts[n]
        return () if name in "CF" else (p,)

    def done(self, n, t):
        name, _, order = self.parts[n]
        return [a for a in AXES[name] if a in self.whole + order[:t]]

    def group(self, n, t, step, half=None):
        axes = self.done(n, t)
        at = {**moved(self.me, self.parts[n][2][t], step), **{a: ALL for a in axes}}
        if half is not None and axes:
            at[axes[0]] = pl.ds(2 * half, 2)
        return at

    def fins(self, t):
        return 2 if t == self.last else 3

    def refs(self, n, t):
        name = self.parts[n][0]
        return self.acc[name], self.hop_b[name] if t == self.last else None, self.fin_b[t][name]

    def hop_copy(self, n, kind):
        step, t = 1 if kind == 0 else -1, self.last
        a, h, _ = self.refs(n, t)
        return remote(a.at[self.idx(n, self.group(n, t, 2 * step, kind))], h.at[self.slot(n) + (kind,)],
                      self.ss.at[n, t, kind], self.rs.at[n, t, kind], moved(self.me, self.parts[n][2][t], step))

    def fin_copy(self, n, t, kind):
        step = (1, -1, 2)[kind]
        a, _, f = self.refs(n, t)
        return remote(a.at[self.idx(n, self.group(n, t, step))], f.at[self.slot(n) + (kind,)],
                      self.ss.at[n, t, 2 + kind], self.rs.at[n, t, 2 + kind], moved(self.me, self.parts[n][2][t], step))

    def each(self, n, t, at, fn, half=None):
        axes = self.done(n, t)
        sizes, offs = [4] * len(axes), [0] * len(axes)
        if half is not None and axes:
            sizes[0], offs[0] = 2, 2 * half
        total = 1
        for s in sizes:
            total *= s

        def one(i):
            pos, rest = [], i
            for s in sizes[::-1]:
                pos.append(rest % s)
                rest = rest // s
            pos = pos[::-1]
            where = dict(at)
            for a, p, o in zip(axes, pos, offs):
                where[a] = p + o
            fn(self.idx(n, where), tuple(pos))

        if total == 1:
            one(0)
        else:
            pl.loop(0, total, unroll=4)(one)

    def sib_copy(self, n, j):
        at = self.group(n, self.last, STEPS[j])
        return remote(self.source(n, at, 1 - self.me["c"]), self.sib[self.parts[n][0]].at[self.idx(n, at)],
                      self.sib_s.at[n, j], self.sib_r.at[n, j], sibling_of(self.me))

    def loc_copy(self, n, j):
        at = self.group(n, self.last, STEPS[j])
        return pltpu.make_async_copy(self.source(n, at, self.me["c"]), self.acc[self.parts[n][0]].at[self.idx(n, at)], self.loc_s.at[n, j])

    def start(self):
        for j in range(4):
            for n in range(self.count):
                self.sib_copy(n, j).start()
                self.loc_copy(n, j).start()

    def merge(self, j):
        for n in range(self.count):
            self.sib_copy(n, j).wait_recv()
            self.loc_copy(n, j).wait()
            a, b = self.acc[self.parts[n][0]], self.sib[self.parts[n][0]]

            def fn(i, _):
                a[i] = a[i] + b[i]

            self.each(n, self.last, self.group(n, self.last, STEPS[j]), fn)

    def send(self, t, ns=None):
        for n in ns or range(self.count):
            if t == self.last:
                for k in (0, 1):
                    self.hop_copy(n, k).start()
            else:
                for k in (2, 0, 1):
                    self.fin_copy(n, t, k).start()

    def forward(self, ns=None):
        t = self.last
        for n in ns or range(self.count):
            a, h, _ = self.refs(n, t)
            for k in (0, 1):
                self.hop_copy(n, k).wait_recv()

                def fn(i, pos):
                    a[i] = a[i] + h[self.slot(n) + (k,) + pos]

                self.each(n, t, self.group(n, t, 1 if k == 0 else -1), fn, k)
                self.fin_copy(n, t, k).start()

    def close(self, t, ns=None):
        for n in ns or range(self.count):
            for k in range(self.fins(t)):
                self.fin_copy(n, t, k).wait_recv()
            a, _, f = self.refs(n, t)

            def fn(i, pos):
                v = a[i].astype(F32)
                for k in range(self.fins(t)):
                    v = v + f[self.slot(n) + (k,) + pos].astype(F32)
                a[i] = v.astype(BF)

            self.each(n, t, self.group(n, t, 0), fn)

    def result(self, n):
        a, _, f = self.refs(n, 0)
        v = a[self.idx(n, self.me)].astype(F32)
        for k in range(3):
            self.fin_copy(n, 0, k).wait_recv()
            v = v + f[self.slot(n) + (k,)].astype(F32)
        return v

    def drain(self):
        for n in range(self.count):
            if self.sib is not None:
                for j in range(4):
                    self.sib_copy(n, j).wait_send()
            for k in (0, 1):
                self.hop_copy(n, k).wait_send()
            for t in range(self.last + 1):
                for k in range(self.fins(t)):
                    self.fin_copy(n, t, k).wait_send()


LEAD_A = ((2, 2, 4), (2, 4, 4), (3, 4), (3,))
LEAD_D = ((2, 2), (2, 4), (3,))


def stage_buffers(leads, *shapes):
    return [vm(*pre, *lead, *block) for lead in leads for pre, block in shapes]


def staged(names, refs):
    k = len(names)
    got = [dict(zip(names, refs[k * i:k * i + k])) for i in range(len(refs) // k)]
    return got[0], {len(got) - 2 - i: g for i, g in enumerate(got[1:])}


def ffn_place(B, C):
    def place(n, at):
        if n < 2:
            return B.at[at["x"], at["y"], at["z"], at["c"], n]
        return C.at[at["z"], at["c"], at["x"], at["y"]]
    return place


def gather_kernel(attn, wi, wo, info, A, B, C, gains, lens, infos, stage, recv, blk, blkA, blkB, blkC, irecv,
                  fs, fr, ss, rs, sib_s, sib_r, as_, ar_, is_, ir_, ds_, dr_, own_s):
    me = where_am_i()
    dp, sq = lax.axis_index("dp"), lax.axis_index("seq")
    bar, count = meet(me, "dp")
    stage[:, 6:8, :] = jnp.zeros((16, 2, 640), F32)
    for s in range(16):
        stage[s, 0:6, 0:384] = attn[:, s // 2, 384 * (s % 2):384 * (s % 2) + 384]
        stage[s, 0:6, 384:640] = wi[:, s // 8, 256 * (s % 8):256 * (s % 8) + 256]
    pl.semaphore_wait(bar, count)

    def a2a(i):
        peer = (sq + i) % 16
        return pltpu.make_async_remote_copy(stage.at[peer], recv.at[sq], as_.at[i], ar_.at[i], device_id=(dp, peer), device_id_type=MESH)

    def inf(i):
        peer = (sq + i) % 16
        return pltpu.make_async_remote_copy(info, irecv.at[sq], is_.at[i], ir_.at[i], device_id=(dp, peer), device_id_type=MESH)

    for i in range(1, 16):
        a2a(i).start()
    for i in range(1, 16):
        inf(i).start()
    recv[sq] = stage[sq]
    irecv[sq] = info[...]
    blkC[...] = wo[...].astype(BF)
    for i in range(1, 16):
        a2a(i).wait_recv()
    for k in range(16):
        blk[6 * k:6 * k + 6, :] = recv[k, 0:6, :]
    for p in range(3):
        blkA[p] = blk[32 * p:32 * p + 32, 0:384].astype(BF)
    for p in range(2):
        blkB[p] = blk[48 * p:48 * p + 48, 384:640].astype(BF)
    place = lambda n, at: A.at[at["x"], at["y"], at["z"], at["c"], PARTS_A[n][1]]
    ring = Gather(me, [p[2] for p in PARTS_A], place, lambda n: blkA.at[n], ss, rs, sib_s, sib_r)
    place_f = ffn_place(B, C)
    mine = lambda n: blkB.at[n] if n < 2 else blkC
    ring_f = Gather(me, [p[2] for p in PARTS_G], place_f, mine, fs, fr)
    owns = [pltpu.make_async_copy(blkA.at[n], place(n, me), own_s.at[n]) for n in range(3)]
    owns += [pltpu.make_async_copy(mine(n), place_f(n, me), own_s.at[3 + n]) for n in range(3)]
    for o in owns:
        o.start()
    ring.send(0)
    ring_f.send(0)
    for o in owns:
        o.wait()
    ring.send(1)
    ring_f.send(1)
    ring.send(2)
    ring_f.forward()
    for i in range(1, 16):
        inf(i).wait_recv()
    tile = jnp.sum(irecv[...], axis=0)
    infos[dp] = tile

    def dpx(i, back=0):
        v = infos.at[(dp - back + 8) % 8]
        return pltpu.make_async_remote_copy(v, v, ds_.at[i], dr_.at[i], device_id=((dp + i) % 8, sq), device_id_type=MESH)

    for i in range(1, 8):
        dpx(i).start()
    ring.forward()
    for i in range(1, 8):
        dpx(i, i).wait_recv()
    lane = lax.broadcasted_iota(jnp.int32, (8, 128), 1)
    gains[...] = jnp.zeros((8, 768), F32)
    for d in range(8):
        lo, sh = 96 * d // 128, 96 * d % 128
        t = pltpu.roll(jnp.where(lane < 96, infos[d], 0.0), sh, 1)
        gains[:, 128 * lo:128 * lo + 128] += jnp.where(lane >= sh, t, 0.0)
        if sh > 32:
            gains[:, 128 * lo + 128:128 * lo + 256] += jnp.where(lane < sh, t, 0.0)
    pick = lax.broadcasted_iota(jnp.int32, (16, 128), 0) == lax.broadcasted_iota(jnp.int32, (16, 128), 1)
    lens[...] = jnp.broadcast_to(jnp.sum(jnp.where(pick, tile[3:4, :], 0.0), axis=1, keepdims=True), (16, 128))
    ring_f.finish()
    ring.finish()
    ring.siblings_in()
    ring_f.drain()
    for i in range(1, 16):
        a2a(i).wait_send()
        inf(i).wait_send()
    for i in range(1, 8):
        dpx(i).wait_send()
    ring.drain()


def gather(attn, wi, wo, info):
    return pl.pallas_call(
        gather_kernel,
        out_shape=(SDS((4, 4, 4, 2, 3, 32, 384), BF), SDS((4, 4, 4, 2, 2, 48, 256), BF), SDS((4, 2, 4, 4, 16, 768), BF), SDS((8, 768), F32), SDS((16, 128), F32)),
        in_specs=[VS] * 4, out_specs=(HS,) * 3 + (VS,) * 2,
        scratch_shapes=[vf(8, 8, 128), vf(16, 8, 640), vf(16, 8, 640), vf(96, 640), vm(3, 32, 384), vm(2, 48, 256), vm(16, 768), vf(16, 8, 128),
                        DMA((3, 2, 4)), DMA((3, 2, 4)), DMA((3, 3, 4)), DMA((3, 3, 4)), DMA((3, 4)), DMA((3, 4)), DMA((16,)), DMA((16,)), DMA((16,)), DMA((16,)), DMA((8,)), DMA((8,)), DMA((6,))],
        compiler_params=pltpu.CompilerParams(collective_id=0, has_side_effects=True, vmem_limit_bytes=60 << 20),
        name="gather_attention_weights",
    )(attn, wi, wo, info)


def info_tile(gain, mem_len):
    sq = lax.axis_index("seq")
    t = jnp.zeros((8, 128), F32)
    t = lax.dynamic_update_slice(t, gain.astype(BF).astype(F32), (0, 6 * sq))
    return lax.dynamic_update_slice(t, mem_len.astype(F32)[:, None], (3, sq))


def scatter_kernel(GA, sumE, sumF, gg, oA, oB, oC, oG, accA, sibA, h2, f2, f1, f0,
                   accE, accF, hE1, hF1, fE1, fF1, fE0, fF0, blk, stage, recv, gdp, gsum, gsq,
                   ss, rs, sib_s, sib_r, loc_s, as_, ar_, is_, ir_, ds_, dr_, es, er, ld_s):
    me = where_am_i()
    dp, sq = lax.axis_index("dp"), lax.axis_index("seq")
    bar, count = meet(me, "dp")
    loads = [pltpu.make_async_copy(a, b, ld_s.at[i]) for i, (a, b) in enumerate(((sumE, accE), (sumF, accF)))]
    for c in loads:
        c.start()
    pl.semaphore_wait(bar, count)
    hop, fin = staged("A", (h2, f2, f1, f0))
    ring = Scatter(me, PARTS_A, {"A": accA}, hop, fin, ss, rs, {"A": sibA},
                   lambda n, at, c: GA.at[at["x"], at["y"], at["z"], c, n], sib_s, sib_r, loc_s)
    fhop, ffin = staged("EF", (hE1, hF1, fE1, fF1, fE0, fF0))
    ring_f = Scatter(me, PARTS_G, {"E": accE, "F": accF}, fhop, ffin, es, er)
    ring.start()
    for c in loads:
        c.wait()
    ring_f.send(1)

    def dpx(i):
        peer = (dp + i) % 8
        return pltpu.make_async_remote_copy(gg.at[peer], gdp.at[dp], ds_.at[i], dr_.at[i], device_id=(peer, sq), device_id_type=MESH)

    for i in range(1, 8):
        dpx(i).start()
    gdp[dp] = gg[dp]
    ring.merge(0)
    ring.send(2)
    ring.merge(1)
    ring.merge(2)
    ring_f.forward()
    ring.forward()
    ring.merge(3)
    ring_f.close(1)
    ring_f.send(0)
    for i in range(1, 8):
        dpx(i).wait_recv()
    gsum[...] = jnp.sum(gdp[...], axis=0)

    def inf(i):
        peer = (sq + i) % 16
        return pltpu.make_async_remote_copy(gsum, gsq.at[sq], is_.at[i], ir_.at[i], device_id=(dp, peer), device_id_type=MESH)

    for i in range(1, 16):
        inf(i).start()
    gsq[sq] = gsum[...]
    stage[:, 6:8, :] = jnp.zeros((16, 2, 640), F32)
    ring.close(2)
    ring.send(1)
    for n in range(2):
        blk[48 * n:48 * n + 48, 384:640] = ring_f.result(n)
    oC[...] = ring_f.result(2)
    ring.close(1)
    ring.send(0)
    for n in range(3):
        blk[32 * n:32 * n + 32, 0:384] = ring.result(n)
    for k in range(16):
        stage[k, 0:6, :] = blk[6 * k:6 * k + 6, :]

    def a2a(i):
        peer = (sq + i) % 16
        return pltpu.make_async_remote_copy(stage.at[peer], recv.at[sq], as_.at[i], ar_.at[i], device_id=(dp, peer), device_id_type=MESH)

    for i in range(1, 16):
        a2a(i).start()
    recv[sq] = stage[sq]
    for i in range(1, 16):
        inf(i).wait_recv()
    oG[...] = pltpu.roll(jnp.sum(gsq[...], axis=0), (128 - 6 * sq) % 128, 1)
    for i in range(1, 16):
        a2a(i).wait_recv()
    for s in range(16):
        oA[:, s // 2, 384 * (s % 2):384 * (s % 2) + 384] = recv[s, 0:6, 0:384]
        oB[:, s // 8, 256 * (s % 8):256 * (s % 8) + 256] = recv[s, 0:6, 384:640]
    for i in range(1, 8):
        dpx(i).wait_send()
    for i in range(1, 16):
        a2a(i).wait_send()
        inf(i).wait_send()
    ring.drain()
    ring_f.drain()


def scatter(GA, sumE, sumF, gg):
    return pl.pallas_call(
        scatter_kernel,
        out_shape=(SDS((6, 8, 768), F32), SDS((6, 2, 2048), F32), SDS((16, 768), F32), SDS((8, 128), F32)),
        in_specs=[HS, HS, HS, VS], out_specs=(VS,) * 4,
        scratch_shapes=[vm(3, 4, 4, 4, 32, 384), vm(3, 4, 4, 4, 32, 384), *stage_buffers(LEAD_A, ((3,), (32, 384))),
                        vm(2, 4, 4, 48, 256), vm(4, 4, 16, 768), *stage_buffers(LEAD_D, ((2,), (48, 256)), ((), (16, 768))),
                        vf(96, 640), vf(16, 8, 640), vf(16, 8, 640), vf(8, 8, 128), vf(8, 128), vf(16, 8, 128),
                        DMA((3, 3, 5)), DMA((3, 3, 5)), DMA((3, 4)), DMA((3, 4)), DMA((3, 4)),
                        DMA((16,)), DMA((16,)), DMA((16,)), DMA((16,)), DMA((8,)), DMA((8,)), DMA((3, 2, 5)), DMA((3, 2, 5)), DMA((2,))],
        compiler_params=pltpu.CompilerParams(collective_id=1, has_side_effects=True, vmem_limit_bytes=60 << 20),
        name="scatter_attention_grads",
    )(GA, sumE, sumF, gg)


def head_masks(value=1.0):
    lane = lax.broadcasted_iota(jnp.int32, (1, 256), 1)
    return [jnp.where(lane // 64 == h, value, 0.0).astype(BF) for h in range(4)]


def stack_heads(block, masks):
    return jnp.concatenate([block * m for m in masks], axis=0)


def key_positions():
    sq = lax.axis_index("seq")
    return (192 * sq + lax.broadcasted_iota(jnp.int32, (192, 128), 0)).astype(F32)


class Merge:
    def __init__(self, me, src, mid, one, two, ss, rs):
        self.me, self.src, self.mid, self.bufs, self.ss, self.rs = me, src, mid, (one, two), ss, rs

    def block(self, n, a, b):
        return (n, a, b) if n % 2 == 0 else (n, b, a)

    def copy(self, n, t, k):
        axis = PLANE[n][t]
        to = moved(self.me, axis, (1, -1, 2)[k])
        src = self.src.at[self.block(n, to[axis], ALL)] if t == 0 else self.mid.at[n, to[axis]]
        return remote(src, self.bufs[t].at[n, k], self.ss.at[n, t, k], self.rs.at[n, t, k], to)

    def send(self, t, ns):
        for n in ns:
            for k in (2, 0, 1):
                self.copy(n, t, k).start()

    def join(self, blocks):
        rows = [b[128:144, :].astype(F32)[0:8, :] for b in blocks]
        logs = [r + pltpu.roll(r, 6, 0) + pltpu.roll(r, 4, 0) for r in rows]
        top = logs[0]
        for l in logs[1:]:
            top = jnp.maximum(top, l)
        ws = [jnp.exp(l - top) for l in logs]
        total = ws[0] + ws[1] + ws[2] + ws[3]
        inv = 1.0 / total
        out = []
        for h in range(2):
            o = sum(b[64 * h:64 * h + 64, :].astype(F32) * (w * inv)[h:h + 1, :] for b, w in zip(blocks, ws))
            out.append(o)
        return jnp.concatenate(out, axis=0), top + jnp.log(total)

    def middle(self, ns):
        for n in ns:
            for k in range(3):
                self.copy(n, 0, k).wait_recv()
            a = self.me[PLANE[n][0]]

            for b in range(4):
                o, l = self.join([self.src.at[self.block(n, a, b)]] + [self.bufs[0].at[n, k, b] for k in range(3)])
                self.mid[n, b, 0:128, :] = o.astype(BF)
                self.mid[n, b, 128:144, :] = log_tile(l)

    def result(self, n):
        for k in range(3):
            self.copy(n, 1, k).wait_recv()
        return self.join([self.mid.at[n, self.me[PLANE[n][1]]]] + [self.bufs[1].at[n, k] for k in range(3)])

    def drain(self):
        for n in range(6):
            for t in range(2):
                for k in range(3):
                    self.copy(n, t, k).wait_send()


def log_tile(l):
    l = jnp.where(lax.broadcasted_iota(jnp.int32, (8, 128), 0) < 2, l, 0.0)
    high = l.astype(BF).astype(F32)
    middle = (l - high).astype(BF).astype(F32)
    low = l - high - middle
    return jnp.concatenate([high + pltpu.roll(middle, 2, 0) + pltpu.roll(low, 4, 0), jnp.zeros((8, 128), F32)], axis=0).astype(BF)


def pair_of(ref, g, at):
    return jnp.concatenate([ref[2 * g, at["x"], at["y"]], ref[2 * g + 1, at["x"], at["y"]]], axis=1)


def cross_fwd_kernel(q, lens, mem_h, A, B_in, C_in, q_h, k_h, v_h, kt_h, B, C, o_ref, L_ref,
                     qall, mem, wk, wv, wkT, wvT, K, V, KT, VT, ost, mid, one, two, lrow,
                     mem_s, w_s, out_s, ss, rs, os_, or_, fs, fr, fsib_s, fsib_r):
    me = where_am_i()
    bar, count = meet(me, "z")

    def load_mem(e):
        return pltpu.make_async_copy(mem_h.at[e], mem.at[e], mem_s.at[e])

    loads = [pltpu.make_async_copy(A.at[10 + i], (wk if i < 2 else wv).at[:, pl.ds(384 * (i % 2), 384)], w_s.at[i]) for i in range(4)]
    for c in loads:
        c.start()

    @pl.loop(0, 16)
    def _(e):
        load_mem(e).start()

    for n in range(6):
        qall[n, me["x"], me["y"]] = q[:, 128 * n:128 * n + 128]
    lrow[...] = jnp.zeros((4, 2, 8, 128), F32)
    pl.semaphore_wait(bar, count)
    view = lambda n, at: qall.at[n, at["x"], at["y"]]
    plane = Gather(me, PLANE, view, lambda n: view(n, me), ss, rs)
    ring = Gather(me, ("z",) * 3, ffn_place(B, C), None, fs, fr, fsib_s, fsib_r, "xy")
    fold = Merge(me, ost, mid, one, two, os_, or_)
    plane.send(0)
    ring.send(0)
    for c in loads:
        c.wait()
    for i in range(6):
        wvT[:, 128 * i:128 * i + 128] = wv[128 * i:128 * i + 128, :].T

    def project(a, b):
        @pl.loop(a // 2, b // 2)
        def _(i):
            for e in (2 * i, 2 * i + 1):
                load_mem(e).wait()
            K[pl.ds(2 * i, 2)] = dot(mem[pl.ds(2 * i, 2)].reshape(384, 768), wk[...]).astype(BF).reshape(2, 192, 768)
            for e in (2 * i, 2 * i + 1):
                VT[e] = dot(wvT[...], mem[e], 1, 1).astype(BF)

    def project_more(a, b):
        @pl.loop(a // 2, b // 2)
        def _(i):
            V[pl.ds(2 * i, 2)] = dot(mem[pl.ds(2 * i, 2)].reshape(384, 768), wv[...]).astype(BF).reshape(2, 192, 768)
            for e in (2 * i, 2 * i + 1):
                KT[e] = dot(wkT[...], mem[e], 1, 1).astype(BF)

    plane.send(1, (0, 1))
    project(0, 4)
    plane.send(1, (2, 3))
    plane.send(1, (4, 5))
    project(4, 10)
    plane.forward((0, 1))
    plane.forward((2, 3))
    project(10, 16)
    plane.forward((4, 5))
    masks = head_masks()
    pos = key_positions()

    def attend(g):
        cols = slice(256 * g, 256 * g + 256)

        @pl.loop(0, 4)
        def _(i):
            four = [(x, x * 4 + y, {"x": x, "y": y}) for x, y in [(i, y) for y in range(4)]]
            sT = [dot(K[e, :, cols], stack_heads(pair_of(qall, g, at), masks), 1, 1) for _, e, at in four]
            pT, inv = [], []
            for u, (_, e, at) in enumerate(four):
                live = pos < lens[pl.ds(e, 1), :]
                ps = []
                for h in range(4):
                    s = jnp.where(live, sT[u][:, 128 * h:128 * h + 128], NEG)
                    top = jnp.max(s, axis=0, keepdims=True)
                    p = jnp.exp(s - top)
                    tot = jnp.sum(p, axis=0, keepdims=True)
                    lrow[u, h // 2, h % 2:h % 2 + 1, :] = top + jnp.log(tot)
                    ps.append(p.astype(BF))
                    inv.append(1.0 / tot)
                pT.append(jnp.concatenate(ps, axis=1))
            oT = [dot(VT[e, cols, :], p) for (_, e, _), p in zip(four, pT)]
            for u, (_, e, at) in enumerate(four):
                for h in range(4):
                    ost[2 * g + h // 2, at["x"], at["y"], 64 * (h % 2):64 * (h % 2) + 64, :] = (
                        oT[u][64 * h:64 * h + 64, 128 * h:128 * h + 128] * inv[4 * u + h]).astype(BF)
                for h in range(2):
                    ost[2 * g + h, at["x"], at["y"], 128:144, :] = log_tile(lrow[u, h])

        fold.send(0, (2 * g, 2 * g + 1))

    def deliver(g):
        for n in (2 * g, 2 * g + 1):
            o, l = fold.result(n)
            o_ref[:, 128 * n:128 * n + 128] = o.T
            L_ref[2 * n:2 * n + 2, :] = l[0:2, :]

    plane.finish((0, 1))
    attend(0)
    plane.finish((2, 3))
    attend(1)
    fold.middle((0, 1))
    fold.send(1, (0, 1))
    plane.finish((4, 5))
    out_q = pltpu.make_async_copy(qall, q_h, out_s.at[0])
    out_k = pltpu.make_async_copy(K, k_h, out_s.at[1])
    out_q.start()
    out_k.start()
    ring.forward()
    attend(2)
    fold.middle((2, 3))
    fold.send(1, (2, 3))
    for i in range(6):
        wkT[:, 128 * i:128 * i + 128] = wk[128 * i:128 * i + 128, :].T
    project_more(0, 8)
    fold.middle((4, 5))
    fold.send(1, (4, 5))
    low, high = pl.ds(0, 8), pl.ds(8, 8)
    outs = [pltpu.make_async_copy(a.at[k], b.at[k], out_s.at[2 + 2 * i + j])
            for j, k in enumerate((low, high)) for i, (a, b) in enumerate(((V, v_h), (KT, kt_h)))]
    for c in outs[:2]:
        c.start()
    ring.finish()
    project_more(8, 16)
    for c in outs[2:]:
        c.start()
    L_ref[12:16, :] = jnp.zeros((4, 128), F32)
    for g in range(3):
        deliver(g)
    plane.drain()
    fold.drain()
    for c in [out_q, out_k] + outs:
        c.wait()
    ring.siblings_in()
    ring.drain()


def cross_fwd(q, lens, memory, A, B, C):
    return pl.pallas_call(
        cross_fwd_kernel,
        out_shape=(SDS((6, 4, 4, 128, 128), BF), SDS((16, 192, 768), BF), SDS((16, 192, 768), BF), SDS((16, 768, 192), BF),
                   SDS((4, 4, 4, 2, 2, 48, 256), BF), SDS((4, 2, 4, 4, 16, 768), BF), SDS((128, 768), F32), SDS((16, 128), F32)),
        in_specs=[VS] * 2 + [HS] * 4, out_specs=(HS,) * 6 + (VS,) * 2, input_output_aliases={4: 4, 5: 5},
        scratch_shapes=[vm(6, 4, 4, 128, 128), vm(16, 192, 768), vm(768, 768), vm(768, 768), vm(768, 768), vm(768, 768),
                        vm(16, 192, 768), vm(16, 192, 768), vm(16, 768, 192), vm(16, 768, 192),
                        vm(6, 4, 4, 144, 128), vm(6, 4, 144, 128), vm(6, 3, 4, 144, 128), vm(6, 3, 144, 128), vf(4, 2, 8, 128),
                        DMA((16,)), DMA((4,)), DMA((6,)), DMA((6, 2, 4)), DMA((6, 2, 4)), DMA((6, 2, 3)), DMA((6, 2, 3)),
                        DMA((3, 1, 4)), DMA((3, 1, 4)), DMA((3, 4)), DMA((3, 4))],
        compiler_params=pltpu.CompilerParams(collective_id=2, has_side_effects=True, vmem_limit_bytes=60 << 20),
        name="cross_forward",
    )(q, lens, memory, A, B, C)


def cross_bwd_kernel(do, st, lens, q_h, k_h, v_h, kt_h, mem_h, A, GB, GC, G_in, dq_ref, gm_h, dw_h, sumE, sumF,
                     qall, doall, stall, wk, wv, K, V, KT, mem, memT, dK, dV, gst, wst, dst, dh1, df1, df0,
                     accB, accC, sibB, sibC, hB2, hC2, fB2, fC2,
                     q_s, kv_s, mem_s, w_s, gm_s, dw_s, ss, rs, ds_, dr_, fs, fr, fsib_s, fsib_r, floc, sum_s):
    me = where_am_i()
    bar, count = meet(me, "z")

    def load_mem(e):
        return pltpu.make_async_copy(mem_h.at[pl.ds(pl.multiple_of(256 * e, 256), 256)], mem.at[e % 4], mem_s.at[e % 4])

    for e in range(4):
        load_mem(e).start()
    loads = [pltpu.make_async_copy(A.at[10 + i], (wk if i < 2 else wv).at[:, pl.ds(384 * (i % 2), 384)], w_s.at[i]) for i in range(4)]
    loads.append(pltpu.make_async_copy(q_h, qall, q_s))
    for n in range(6):
        doall[n, me["x"], me["y"]] = do[:, 128 * n:128 * n + 128]
    stall[me["x"], me["y"]] = st[...]
    pl.semaphore_wait(bar, count)

    def place(n, at):
        return stall.at[at["x"], at["y"]] if n == 6 else doall.at[n, at["x"], at["y"]]

    plane = Gather(me, PLANE + ("xy",), place, lambda n: place(n, me), ss, rs)
    fhop, ffin = staged("BC", (hB2, hC2, fB2, fC2))
    grads = ffn_place(GB, GC)
    ring = Scatter(me, PARTS_F, {"B": accB, "C": accC}, fhop, ffin, fs, fr, {"B": sibB, "C": sibC},
                   lambda n, at, c: grads(n, {**at, "c": c}), fsib_s, fsib_r, floc, "xy")
    back = Scatter(me, PARTS_D, {"D": dst}, *staged("D", (dh1, df1, df0)), ds_, dr_)
    plane.send(0, (6, 0, 1, 2, 3, 4, 5))
    ring.start()
    for c in loads:
        c.start()

    def turn(a, b):
        @pl.loop(a, b)
        def _(e):
            load_mem(e).wait()
            memT[:, pl.ds(pl.multiple_of(256 * e, 256), 256)] = mem[e % 4].T

            @pl.when(e < 8)
            def _():
                load_mem(e + 4).start()

    turn(0, 3)
    plane.send(1, (6, 0, 1))
    plane.send(1, (2, 3))
    plane.send(1, (4, 5))
    ring.merge(0)
    ring.send(0)
    turn(3, 6)
    plane.forward((6, 0, 1))
    ring.merge(1)
    ring.merge(2)
    plane.forward((2, 3))
    ring.forward()
    masks = head_masks()
    pos = key_positions()

    def load_kv(g, i, u, which):
        e = ((me["x"] + 2 + i) % 4) * 4 + u
        cols = pl.ds(256 * g, 256)
        src = (k_h.at[e, :, cols], v_h.at[e, :, cols], kt_h.at[e, cols])[which]
        return pltpu.make_async_copy(src, (K, V, KT)[which].at[i % 2, u], kv_s.at[which, i % 2, u])

    def fetch_kv(g, i):
        for u in range(4):
            for w in range(3):
                load_kv(g, i, u, w).start()

    fetch_kv(0, 0)
    for c in loads:
        c.wait()

    def attend(g):
        cols = slice(256 * g, 256 * g + 256)

        @pl.loop(0, 4)
        def _(i):
            @pl.when(i < 3)
            def _():
                fetch_kv(g, i + 1)

            for u in range(4):
                for w in range(3):
                    load_kv(g, i, u, w).wait()
            x = (me["x"] + 2 + i) % 4
            four = [(x * 4 + y, {"x": x, "y": y}) for y in range(4)]
            q4s = [stack_heads(pair_of(qall, g, at), masks) for _, at in four]
            d4s = [stack_heads(pair_of(doall, g, at), masks) for _, at in four]
            sT = [dot(K[i % 2, u], q4s[u], 1, 1) for u in range(4)]
            gT = [dot(V[i % 2, u], d4s[u], 1, 1) for u in range(4)]
            pT, sg = [], []
            for u, (e, at) in enumerate(four):
                live = pos < lens[pl.ds(e, 1), :]
                ps, gs = [], []
                for h in range(4):
                    n = 4 * g + h
                    s = jnp.where(live, sT[u][:, 128 * h:128 * h + 128], NEG)
                    p = jnp.exp(s - stall[at["x"], at["y"], n:n + 1, :])
                    ps.append(p.astype(BF))
                    gs.append((p * (gT[u][:, 128 * h:128 * h + 128] - stall[at["x"], at["y"], 12 + n:13 + n, :])).astype(BF))
                pT.append(jnp.concatenate(ps, axis=1))
                sg.append(jnp.concatenate(gs, axis=1))
            for u, (e, at) in enumerate(four):
                dV[pl.ds(pl.multiple_of(192 * e, 192), 192), cols] = dot(pT[u], d4s[u]).astype(BF)
            for u, (e, at) in enumerate(four):
                dK[pl.ds(pl.multiple_of(192 * e, 192), 192), cols] = dot(sg[u], q4s[u]).astype(BF)
            for u, (e, at) in enumerate(four):
                qT = dot(KT[i % 2, u], sg[u])
                for h in range(4):
                    dst[2 * g + h // 2, at["x"], at["y"], 64 * (h % 2):64 * (h % 2) + 64, :] = qT[64 * h:64 * h + 64, 128 * h:128 * h + 128].astype(BF)

        if g < 2:
            fetch_kv(g + 1, 0)
        back.send(1, (2 * g, 2 * g + 1))

    plane.finish((6, 0, 1))
    attend(0)
    plane.forward((4, 5))
    plane.finish((2, 3))
    attend(1)
    back.forward((0, 1))
    ring.merge(3)
    plane.finish((4, 5))
    attend(2)
    back.forward((2, 3))
    back.close(1, (0, 1))
    back.send(0, (0, 1))

    def gm_copy(e):
        return pltpu.make_async_copy(gst.at[e % 2], gm_h.at[e], gm_s.at[e % 2])

    def mem_grad(a, b):
        @pl.loop(a, b)
        def _(e):
            @pl.when(e > 1)
            def _():
                gm_copy(e - 2).wait()

            rows = pl.ds(pl.multiple_of(384 * e, 384), 384)
            gst[e % 2] = dot(dK[rows, :], wk[...], 1, 1) + dot(dV[rows, :], wv[...], 1, 1)
            gm_copy(e).start()

    def dw_copy(k, r, half):
        rows = pl.ds(pl.multiple_of(256 * r, 256), 256)
        return pltpu.make_async_copy(wst.at[k, :, pl.ds(384 * half, 384)], dw_h.at[10 + 2 * k + half, rows], dw_s.at[k, half])

    def weight_grad(a, b):
        @pl.loop(a, b)
        def _(r):
            for k in range(2):
                @pl.when(r > 0)
                def _():
                    dw_copy(k, r - 1, 0).wait()
                    dw_copy(k, r - 1, 1).wait()

                wst[k] = dot(memT[pl.ds(pl.multiple_of(256 * r, 256), 256), :], (dV if k else dK)[...]).astype(BF)
                dw_copy(k, r, 0).start()
                dw_copy(k, r, 1).start()

    turn(6, 12)
    mem_grad(0, 2)
    back.forward((4, 5))
    back.close(1, (2, 3))
    back.send(0, (2, 3))
    mem_grad(2, 8)
    back.close(1, (4, 5))
    back.send(0, (4, 5))
    ring.close(0)
    sums = [pltpu.make_async_copy(accB.at[:, :, :, me["z"]], sumE, sum_s.at[0]), pltpu.make_async_copy(accC.at[me["z"]], sumF, sum_s.at[1])]
    for c in sums:
        c.start()
    weight_grad(0, 3)
    for n in range(6):
        dq_ref[:, 128 * n:128 * n + 128] = (0.125 * back.result(n)).T
    for c in sums:
        c.wait()
    gm_copy(6).wait()
    gm_copy(7).wait()
    for k in range(2):
        dw_copy(k, 2, 0).wait()
        dw_copy(k, 2, 1).wait()
    plane.drain()
    ring.drain()
    back.drain()


def cross_bwd(do, st, lens, q_h, k_h, v_h, kt_h, memory, A, GB, GC, GA):
    bB, bC = (48, 256), (16, 768)
    return pl.pallas_call(
        cross_bwd_kernel,
        out_shape=(SDS((128, 768), F32), SDS((8, 384, 768), F32), SDS((16, 768, 384), BF), SDS((2, 4, 4, 48, 256), BF), SDS((4, 4, 16, 768), BF)),
        in_specs=[VS] * 3 + [HS] * 9, out_specs=(VS,) + (HS,) * 4, input_output_aliases={11: 2},
        scratch_shapes=[vm(6, 4, 4, 128, 128), vm(6, 4, 4, 128, 128), vf(4, 4, 24, 128), vm(768, 768), vm(768, 768),
                        vm(2, 4, 192, 256), vm(2, 4, 192, 256), vm(2, 4, 256, 192), vm(4, 256, 768), vm(768, 3072), vm(3072, 768), vm(3072, 768),
                        vf(2, 384, 768), vm(2, 256, 768), vm(6, 4, 4, 128, 128), *stage_buffers(LEAD_D, ((6,), (128, 128))),
                        vm(2, 4, 4, 4, *bB), vm(4, 4, 4, *bC), vm(2, 4, 4, 4, *bB), vm(4, 4, 4, *bC), *stage_buffers(LEAD_A[:2], ((2,), bB), ((), bC)),
                        DMA, DMA((3, 2, 4)), DMA((4,)), DMA((4,)), DMA((2,)), DMA((2, 2)), DMA((7, 2, 4)), DMA((7, 2, 4)), DMA((6, 2, 5)), DMA((6, 2, 5)),
                        DMA((3, 1, 4)), DMA((3, 1, 4)), DMA((3, 4)), DMA((3, 4)), DMA((3, 4)), DMA((2,))],
        compiler_params=pltpu.CompilerParams(collective_id=3, has_side_effects=True, vmem_limit_bytes=60 << 20),
        name="cross_backward",
    )(do, st, lens, q_h, k_h, v_h, kt_h, memory.reshape(3072, 768), A, GB, GC, GA)


def adam_update(master, first, second, grad, rate):
    first_new = beta_one * first + (1.0 - beta_one) * grad
    second_new = beta_two * second + (1.0 - beta_two) * grad * grad
    fix_one = 1.0 - beta_one**STEP
    fix_two = 1.0 - beta_two**STEP
    master_new = master - rate * (
        first_new / fix_one / (jnp.sqrt(second_new / fix_two) + adam_eps) + decay_rate * master
    )
    return (master_new, first_new, second_new, master_new.astype(jnp.bfloat16))


def rms(x):
    return lax.rsqrt(jnp.mean(x * x, axis=-1, keepdims=True) + eps_norm)

def rms_back(x, inv, gain, u):
    scaled = u * gain
    inner = jnp.mean(scaled * x, axis=-1, keepdims=True)
    return inv * scaled - x * inv * inv * inv * inner, jnp.sum(u * x * inv, axis=0, keepdims=True)

def flip(x):
    return jnp.concatenate([x[:, 128 * i:128 * i + 128].T for i in range(x.shape[1] // 128)], axis=0)

def unflip(x):
    return jnp.concatenate([x[128 * i:128 * i + 128, :].T for i in range(x.shape[0] // 128)], axis=1)

def apply_w(h, W, k):
    return jnp.concatenate([dot(h, W[2 * k]), dot(h, W[2 * k + 1])], axis=1)

def apply_wt(u, W, k):
    return dot(u[:, 0:384], W[2 * k], 1, 1) + dot(u[:, 384:768], W[2 * k + 1], 1, 1)

def causal_mask():
    return lax.broadcasted_iota(jnp.int32, (128, 128), 0) <= lax.broadcasted_iota(jnp.int32, (128, 128), 1)

def self_fwd_kernel(x_ref, gains, A, q2, h1, qkv, o1, x1, h2, L1, W, sem):
    loads = [pltpu.make_async_copy(A.at[i], W.at[i], sem.at[i]) for i in range(10)]
    for c in loads:
        c.start()
    x = x_ref[...].astype(F32)
    h = (x * rms(x) * gains[0:1, :]).astype(BF)
    h1[...] = h
    for k in range(3):
        loads[2 * k].wait()
        loads[2 * k + 1].wait()
        full = apply_w(h, W, k)
        qkv[k] = full.astype(BF)
    vT = flip(full).astype(BF)
    masks = head_masks(0.125)
    live = causal_mask()
    outs = []
    for g in range(3):
        cols = slice(256 * g, 256 * g + 256)
        q4 = qkv[0, :, cols]
        sT = dot(qkv[1, :, cols], jnp.concatenate([q4 * m for m in masks], axis=0), 1, 1)
        ps = []
        for n in range(4):
            s = jnp.where(live, sT[:, 128 * n:128 * n + 128], NEG)
            top = jnp.max(s, axis=0, keepdims=True)
            lse = top + jnp.log(jnp.sum(jnp.exp(s - top), axis=0, keepdims=True))
            L1[4 * g + n:4 * g + n + 1, :] = lse
            ps.append(jnp.exp(s - lse).astype(BF))
        oT = dot(vT[256 * g:256 * g + 256, :], jnp.concatenate(ps, axis=1))
        outs += [oT[64 * n:64 * n + 64, 128 * n:128 * n + 128] for n in range(4)]
    o = unflip(jnp.concatenate(outs, axis=0)).astype(BF)
    o1[...] = o
    for c in loads[6:]:
        c.wait()
    x = x + apply_w(o, W, 3)
    x1[...] = x
    h = (x * rms(x) * gains[1:2, :]).astype(BF)
    h2[...] = h
    q2[...] = apply_w(h, W, 4).astype(BF) * jnp.asarray(0.125, BF)

def self_fwd(x, gains, A):
    row = SDS((128, 768), BF)
    return pl.pallas_call(
        self_fwd_kernel,
        out_shape=(row, row, SDS((3, 128, 768), BF), row, SDS((128, 768), F32), row, SDS((16, 128), F32)),
        in_specs=[VS, VS, HS], out_specs=(VS,) * 7,
        scratch_shapes=[pltpu.VMEM((10, 768, 384), BF), pltpu.SemaphoreType.DMA((10,))],
        compiler_params=pltpu.CompilerParams(vmem_limit_bytes=60 << 20),
        name="self_forward",
    )(x, gains, A)

def ffn_kernel(x1, o2, L2, dy_ref, gains, A, B, C, out, do2, st, dx2, gg, GA, GB, GC,
               W7, WB, WC, gA, gB, gC, sw, sb, sc, tb, tc, ta):
    lA = [pltpu.make_async_copy(A.at[14 + i], W7.at[i], sw.at[i]) for i in range(2)]
    lB = [pltpu.make_async_copy(B.at[i], WB.at[i], sb.at[i]) for i in range(16)]
    lC = [pltpu.make_async_copy(C.at[i], WC.at[i], sc.at[i]) for i in range(8)]
    for c in lA:
        c.start()
    for j in range(8):
        lB[j].start()
        lB[8 + j].start()
        lC[j].start()
    o = o2[...]
    ob = o.astype(BF)
    for c in lA:
        c.wait()
    x = x1[...] + apply_w(ob, W7, 0)
    inv = rms(x)
    h = (x * inv * gains[2:3, :]).astype(BF)
    hT = flip(h.astype(F32)).astype(BF)
    df = dy_ref[...]
    y = jnp.zeros((128, 768), F32)
    dh = jnp.zeros((128, 768), F32)
    c0 = 0.7978845608028654
    sB, sC = [], []
    for j0 in range(0, 8, 2):
        js = range(j0, j0 + 2)
        for j in js:
            lB[j].wait()
            lB[8 + j].wait()
            lC[j].wait()
        a_s = [dot(h, WB[j]) for j in js]
        ups = [dot(h, WB[8 + j]) for j in js]
        dms = [dot(df, WC[j], 1, 1) for j in js]
        mids, dgs, dus = [], [], []
        for a, up, dm in zip(a_s, ups, dms):
            t = jnp.tanh(c0 * (a + 0.044715 * a * a * a))
            half = 0.5 * (1.0 + t)
            gel = a * half
            der = half + 0.5 * a * (1.0 - t * t) * (c0 * (1.0 + 0.134145 * a * a))
            mids.append(gel * up)
            dgs.append((dm * up * der).astype(BF))
            dus.append((dm * gel).astype(BF))
        y += dot(jnp.concatenate([m.astype(BF) for m in mids], axis=1), WC[j0:j0 + 2].reshape(2 * 256, 768))
        for n, j in enumerate(js):
            dh += dot(dgs[n], WB[j], 1, 1) + dot(dus[n], WB[8 + j], 1, 1)
        for n, j in enumerate(js):
            gB[j] = dot(hT, dgs[n]).astype(BF)
            gB[8 + j] = dot(hT, dus[n]).astype(BF)
            gC[j] = dot(flip(mids[n]).astype(BF), df).astype(BF)
        for j in js:
            new = [pltpu.make_async_copy(gB.at[j], GB.at[j], tb.at[j]), pltpu.make_async_copy(gB.at[8 + j], GB.at[8 + j], tb.at[8 + j]),
                   pltpu.make_async_copy(gC.at[j], GC.at[j], tc.at[j])]
            for c in new:
                c.start()
            sB += new
    out[...] = (x + y).astype(BF)
    dz, gain = rms_back(x, inv, gains[2:3, :], dh)
    gg[...] = gain
    d = df.astype(F32) + dz
    dx2[...] = d
    dc = d.astype(BF)
    dof = apply_wt(dc, W7, 0).astype(BF)
    do2[...] = dof
    prod = flip(dof.astype(F32) * o)
    st[0:12, :] = L2[0:12, :]
    for n in range(12):
        st[12 + n:13 + n, :] = jnp.sum(prod[64 * n:64 * n + 64, :], axis=0, keepdims=True)
    oT = flip(o).astype(BF)
    sA = []
    for i in range(2):
        gA[i] = dot(oT, dc[:, 384 * i:384 * i + 384]).astype(BF)
        sA.append(pltpu.make_async_copy(gA.at[i], GA.at[14 + i], ta.at[i]))
        sA[-1].start()
    for c in sA + sB + sC:
        c.wait()

def ffn(x1, o2, L2, dy, gains, A, B, C):
    M = lambda *s: pltpu.VMEM(s, BF)
    D = pltpu.SemaphoreType.DMA
    return pl.pallas_call(
        ffn_kernel,
        out_shape=(SDS((128, 768), BF), SDS((128, 768), BF), SDS((24, 128), F32), SDS((128, 768), F32), SDS((1, 768), F32),
                   SDS((16, 768, 384), BF), SDS((16, 768, 256), BF), SDS((8, 256, 768), BF)),
        in_specs=[VS] * 5 + [HS] * 3, out_specs=(VS,) * 5 + (HS,) * 3,
        scratch_shapes=[M(2, 768, 384), M(16, 768, 256), M(8, 256, 768), M(2, 768, 384), M(16, 768, 256), M(8, 256, 768),
                        D((2,)), D((16,)), D((8,)), D((16,)), D((8,)), D((2,))],
        compiler_params=pltpu.CompilerParams(vmem_limit_bytes=60 << 20),
        name="feed_forward",
    )(x1, o2, L2, dy, gains, A, B, C)

def self_bwd_kernel(dq2, h2, x1, dx2, qkv, o1, L1, x_ref, h1, gains, g3, A, GA_in, gm_in, gin, tile, GA, gm,
                    W, G, gb, gmv, sem, gsem, msem):
    loads = [pltpu.make_async_copy(A.at[i], W.at[i], sem.at[i]) for i in range(10)]
    for i in (8, 9, 6, 7, 0, 1, 2, 3, 4, 5):
        loads[i].start()
    def gm_load(e):
        return pltpu.make_async_copy(gm_in.at[e], gmv.at[e], msem.at[e])
    def gm_store(e):
        return pltpu.make_async_copy(gmv.at[e], gm.at[e], msem.at[16 + e])
    for e in range(16):
        gm_load(e).start()
    stores = []
    def weight_grad(k, left, inc):
        for i in range(2):
            n = 2 * k + i
            G[n] = dot(left, inc[:, 384 * i:384 * i + 384]).astype(BF)
            stores.append(pltpu.make_async_copy(G.at[n], GA.at[n], gsem.at[n]))
            stores[-1].start()
    dqb = dq2[...].astype(BF)
    for i in (8, 9, 6, 7):
        loads[i].wait()
    u = apply_wt(dqb, W, 4)
    x = x1[...]
    inv = rms(x)
    dz, gain = rms_back(x, inv, gains[1:2, :], u)
    gb[...] = jnp.zeros((8, 768), F32)
    gb[1:2, :] = gain
    gb[2:3, :] = g3[...]
    d1 = dx2[...] + dz
    da = d1.astype(BF)
    do1 = apply_wt(da, W, 3).astype(BF)
    weight_grad(4, flip(h2[...].astype(F32)).astype(BF), dqb)
    masks = head_masks(0.125)
    ones = head_masks(1.0)
    live = causal_mask()
    kT = flip(qkv[1].astype(F32)).astype(BF)
    qs, ks, vs = [], [], []
    for g in range(3):
        cols = slice(256 * g, 256 * g + 256)
        q4 = qkv[0, :, cols]
        d4 = do1[:, cols]
        q4s = jnp.concatenate([q4 * m for m in masks], axis=0)
        d4s = jnp.concatenate([d4 * m for m in ones], axis=0)
        sT = dot(qkv[1, :, cols], q4s, 1, 1)
        gT = dot(qkv[2, :, cols], d4s, 1, 1)
        ps, gs = [], []
        for n in range(4):
            s = jnp.where(live, sT[:, 128 * n:128 * n + 128], NEG)
            p = jnp.exp(s - L1[4 * g + n:4 * g + n + 1, :])
            gt = gT[:, 128 * n:128 * n + 128]
            ps.append(p.astype(BF))
            gs.append((p * (gt - jnp.sum(p * gt, axis=0, keepdims=True))).astype(BF))
        sg = jnp.concatenate(gs, axis=1)
        vs.append(dot(jnp.concatenate(ps, axis=1), d4s).astype(BF))
        ks.append(dot(sg, q4s).astype(BF))
        qT = dot(kT[256 * g:256 * g + 256, :], sg)
        qs += [qT[64 * n:64 * n + 64, 128 * n:128 * n + 128] for n in range(4)]
    for e in range(16):
        gm_load(e).wait()
        gm_store(e).start()
    inc = [(0.125 * unflip(jnp.concatenate(qs, axis=0))).astype(BF), jnp.concatenate(ks, axis=1), jnp.concatenate(vs, axis=1)]
    weight_grad(3, flip(o1[...].astype(F32)).astype(BF), da)
    for c in loads[:6]:
        c.wait()
    u = apply_wt(inc[0], W, 0) + apply_wt(inc[1], W, 1) + apply_wt(inc[2], W, 2)
    x = x_ref[...].astype(F32)
    inv = rms(x)
    dz, gain = rms_back(x, inv, gains[0:1, :], u)
    gb[0:1, :] = gain
    gin[...] = d1 + dz
    hT = flip(h1[...].astype(F32)).astype(BF)
    for k in range(3):
        weight_grad(k, hT, inc[k])
    lane = lax.broadcasted_iota(jnp.int32, (8, 128), 1)
    for d in range(8):
        lo, sh = 96 * d // 128, 96 * d % 128
        t = pltpu.roll(gb[:, 128 * lo:128 * lo + 128], (128 - sh) % 128, 1)
        if sh > 32:
            nxt = pltpu.roll(gb[:, 128 * lo + 128:128 * lo + 256], (128 - sh) % 128, 1)
            t = jnp.where(lane < 128 - sh, t, nxt)
        tile[d] = jnp.where(lane < 96, t, 0.0)
    for c in stores:
        c.wait()
    for e in range(16):
        gm_store(e).wait()

def self_bwd(dq2, h2, x1, dx2, qkv, o1, L1, x, h1, gains, g3, A, GA, gm):
    D = pltpu.SemaphoreType.DMA
    return pl.pallas_call(
        self_bwd_kernel,
        out_shape=(SDS((128, 768), F32), SDS((8, 8, 128), F32), SDS((16, 768, 384), BF), SDS((16, 192, 768), F32)),
        in_specs=[VS] * 11 + [HS] * 3, out_specs=(VS, VS, HS, HS),
        input_output_aliases={12: 2},
        scratch_shapes=[pltpu.VMEM((10, 768, 384), BF), pltpu.VMEM((10, 768, 384), BF), pltpu.VMEM((8, 768), F32), pltpu.VMEM((16, 192, 768), F32), D((10,)), D((10,)), D((32,))],
        compiler_params=pltpu.CompilerParams(vmem_limit_bytes=60 << 20),
        name="self_backward",
    )(dq2, h2, x1, dx2, qkv, o1, L1, x, h1, gains, g3, A, GA, gm)

def adam_kernel(*refs):
    ins, outs = refs[:16], refs[16:]
    for n in range(4):
        w, m, v, g = ins[4 * n:4 * n + 4]
        grad = g[0:3, 0:6] if n == 3 else g[...]
        for o, val in zip(outs[4 * n:4 * n + 4], adam_update(w[...], m[...], v[...], grad, rate_gain if n == 3 else rate_matrix)):
            o[...] = val

def adam(*args):
    shapes = []
    for n in range(4):
        s = args[4 * n].shape
        shapes += [SDS(s, F32)] * 3 + [SDS(s, BF)]
    return pl.pallas_call(adam_kernel, out_shape=tuple(shapes), in_specs=[VS] * 16, out_specs=(VS,) * 16,
                          compiler_params=pltpu.CompilerParams(vmem_limit_bytes=60 << 20), name="adam")(*args)


def body(
    dec_input,
    memory,
    mem_len,
    grad_out,
    attn_master,
    ffn_in_master,
    ffn_out_master,
    gain_master,
    attn_first,
    ffn_in_first,
    ffn_out_first,
    gain_first,
    attn_second,
    ffn_in_second,
    ffn_out_second,
    gain_second,
):
    swap = lambda a: a.transpose(1, 0, 2)
    attn_t, in_t = swap(attn_master), swap(ffn_in_master)
    gath_a, gath_b, gath_c, gains, lens = gather(attn_t, in_t, ffn_out_master, info_tile(gain_master, mem_len))
    aw = gath_a.reshape(16, 768, 384)
    x = dec_input[0]
    q2, h1, qkv, o1, x1, h2, L1 = self_fwd(x, gains, aw)
    q_all, k_two, v_two, kt_two, gath_b, gath_c, o2, L2 = cross_fwd(q2, lens, memory, aw, gath_b, gath_c)
    out_block, do2, st, dx2, g3, GA, GB, GC = ffn(x1, o2, L2, grad_out[0], gains, aw, gath_b.reshape(16, 768, 256), gath_c.reshape(8, 256, 768))
    dq2, gm, GA, sum_b, sum_c = cross_bwd(
        do2, st, lens, q_all, k_two, v_two, kt_two, memory, aw,
        GB.reshape(4, 4, 4, 2, 2, 48, 256), GC.reshape(4, 2, 4, 4, 16, 768), GA,
    )
    grad_input, tile_g, GA, grad_memory = self_bwd(dq2, h2, x1, dx2, qkv, o1, L1, x, h1, gains, g3, aw, GA, gm.reshape(16, 192, 768))
    share_a, share_b, share_c, share_g = scatter(GA.reshape(4, 4, 4, 2, 3, 32, 384), sum_b, sum_c, tile_g)
    new = adam(
        attn_t, swap(attn_first), swap(attn_second), share_a,
        in_t, swap(ffn_in_first), swap(ffn_in_second), share_b,
        ffn_out_master, ffn_out_first, ffn_out_second, share_c,
        gain_master, gain_first, gain_second, share_g,
    )
    return (out_block[None], grad_input[None], grad_memory, *[swap(a) for a in new[:8]], *new[8:])


def solution(mesh):
    placed = (
        P(("dp", "seq"), None, None),
        P("dp", "seq", None),
        P(("dp", "seq")),
        P(("dp", "seq"), None, None),
        P(None, ("dp", "seq"), None),
        P(None, ("dp", "seq"), None),
        P(("dp", "seq"), None),
        P(None, ("dp", "seq")),
        P(None, ("dp", "seq"), None),
        P(None, ("dp", "seq"), None),
        P(("dp", "seq"), None),
        P(None, ("dp", "seq")),
        P(None, ("dp", "seq"), None),
        P(None, ("dp", "seq"), None),
        P(("dp", "seq"), None),
        P(None, ("dp", "seq")),
    )
    return jax.shard_map(
        body,
        mesh=mesh,
        in_specs=placed,
        out_specs=(
            P(("dp", "seq"), None, None),
            P(("dp", "seq"), None, None),
            P("dp", "seq", None),
            P(None, ("dp", "seq"), None),
            P(None, ("dp", "seq"), None),
            P(None, ("dp", "seq"), None),
            P(None, ("dp", "seq"), None),
            P(None, ("dp", "seq"), None),
            P(None, ("dp", "seq"), None),
            P(None, ("dp", "seq"), None),
            P(None, ("dp", "seq"), None),
            P(("dp", "seq"), None),
            P(("dp", "seq"), None),
            P(("dp", "seq"), None),
            P(("dp", "seq"), None),
            P(None, ("dp", "seq")),
            P(None, ("dp", "seq")),
            P(None, ("dp", "seq")),
            P(None, ("dp", "seq")),
        ),
        check_vma=False,
    )
```

```python
import jax
import jax.numpy as jnp
from jax import lax
from jax.experimental import pallas as pl
from jax.experimental.pallas import tpu as pltpu
from jax.sharding import PartitionSpec as P

eps_norm = 1e-06
beta_one = 0.9
beta_two = 0.999
adam_eps = 1e-08
decay_rate = 0.01
rate_matrix = 0.12
rate_gain = 3.0
STEP = 10
MESH = pl.DeviceIdType.MESH
BF, F32 = jnp.bfloat16, jnp.float32
ALL = slice(None)
NEG = -1e30
PARTS_A = (("A", 0, "xyz"), ("A", 1, "yzx"), ("A", 2, "zxy"))
PARTS_F = (("B", 0, "z"), ("B", 1, "z"), ("C", 0, "z"))
PARTS_G = (("E", 0, "xy"), ("E", 1, "yx"), ("F", 0, "xy"))
PLANE = ("xy", "yx") * 3
PARTS_D = tuple(("D", n, PLANE[n]) for n in range(6))
AXES = {"A": "xyz", "B": "xyz", "C": "zxy", "D": "xy", "E": "xy", "F": "xy"}
STEPS = (2, -1, 1, 0)
VS = pl.BlockSpec(memory_space=pltpu.VMEM)
HS = pl.BlockSpec(memory_space=pltpu.HBM)
SDS = jax.ShapeDtypeStruct
DMA = pltpu.SemaphoreType.DMA


def vm(*shape):
    return pltpu.VMEM(shape, BF)


def vf(*shape):
    return pltpu.VMEM(shape, F32)


def where_am_i():
    dp, sq = lax.axis_index("dp"), lax.axis_index("seq")
    return {"x": sq // 4, "y": sq % 4, "z": dp // 2, "c": dp % 2}


def dev(at):
    return (at["z"] * 2 + at["c"], at["x"] * 4 + at["y"])


def moved(at, axis, step):
    return {**at, axis: (at[axis] + step + 4) % 4}


def offset(me, j, sign=1):
    return {**me, "x": (me["x"] + sign * (j // 4) + 4) % 4, "y": (me["y"] + sign * (j % 4) + 4) % 4}


def sibling_of(me):
    return {**me, "c": 1 - me["c"]}


def remote(src, dst, send, recv, to):
    return pltpu.make_async_remote_copy(src, dst, send, recv, device_id=dev(to), device_id_type=MESH)


def meet(me, column):
    dp, sq = lax.axis_index("dp"), lax.axis_index("seq")
    bar = pltpu.get_barrier_semaphore()
    for i in range(1, 16):
        pl.semaphore_signal(bar, inc=1, device_id=(dp, (sq + i) % 16), device_id_type=MESH)
    if column == "dp":
        for i in range(1, 8):
            pl.semaphore_signal(bar, inc=1, device_id=((dp + i) % 8, sq), device_id_type=MESH)
        return bar, 22
    if column == "z":
        for to in (moved(me, "z", 1), moved(me, "z", -1), sibling_of(me)):
            pl.semaphore_signal(bar, inc=1, device_id=dev(to), device_id_type=MESH)
        return bar, 18
    return bar, 15


def dot(a, b, ca=1, cb=0):
    return lax.dot_general(a, b, (((ca,), (cb,)), ((), ())), preferred_element_type=F32)


class Gather:
    def __init__(self, me, orders, view, own, ss, rs, sib_s=None, sib_r=None, whole=""):
        self.me, self.orders, self.view, self.own, self.whole = me, orders, view, own, whole
        self.ss, self.rs, self.sib_s, self.sib_r = ss, rs, sib_s, sib_r
        self.count, self.last = len(orders), len(orders[0]) - 1

    def group(self, n, t, step, half=None):
        axes = self.whole + self.orders[n][:t]
        at = {**moved(self.me, self.orders[n][t], step), **{a: ALL for a in axes}}
        if half is not None and axes:
            at[axes[0]] = pl.ds(2 * half, 2)
        return at

    def kinds(self, t):
        return (0, 1, 2, 3) if t == self.last else (0, 1, 2)

    def copy(self, n, t, kind, back=0):
        straight = kind < 2 or t < self.last
        step = (1, -1, 2 if straight else 1, -1)[kind]
        dst = self.view(n, self.group(n, t, back) if straight else self.group(n, t, back - step, kind - 2))
        src = self.own(n) if self.own and t == 0 and straight and back == 0 else dst
        return remote(src, dst, self.ss.at[n, t, kind], self.rs.at[n, t, kind], moved(self.me, self.orders[n][t], step))

    def arrived(self, n, t, kind):
        self.copy(n, t, kind, (-1, 1, -2 if t < self.last else -1, 1)[kind]).wait_recv()

    def sibling(self, n, j, c):
        v = self.view(n, {**self.group(n, self.last, (0, -1, 1, 2)[j]), "c": c})
        return remote(v, v, self.sib_s.at[n, j], self.sib_r.at[n, j], sibling_of(self.me))

    def send(self, t, ns=None):
        for n in ns or range(self.count):
            if t:
                for k in range(3):
                    self.arrived(n, t - 1, k)
            for k in (0, 1) if t == self.last else (2, 0, 1):
                self.copy(n, t, k).start()
            if self.sib_s is not None and t == self.last:
                self.sibling(n, 0, self.me["c"]).start()

    def forward(self, ns=None):
        for n in ns or range(self.count):
            for k in (0, 1):
                self.arrived(n, self.last, k)
                self.copy(n, self.last, 2 + k).start()
                if self.sib_s is not None:
                    self.sibling(n, 1 + k, self.me["c"]).start()

    def finish(self, ns=None):
        for n in ns or range(self.count):
            for k in (2, 3):
                self.arrived(n, self.last, k)
            if self.sib_s is not None:
                self.sibling(n, 3, self.me["c"]).start()

    def siblings_in(self):
        for n in range(self.count):
            for j in range(4):
                self.sibling(n, j, 1 - self.me["c"]).wait_recv()

    def drain(self):
        for n in range(self.count):
            for t in range(self.last + 1):
                for k in self.kinds(t):
                    self.copy(n, t, k).wait_send()
            if self.sib_s is not None:
                for j in range(4):
                    self.sibling(n, j, self.me["c"]).wait_send()


class Scatter:
    def __init__(self, me, parts, acc, hop, fin, ss, rs, sib=None, source=None, sib_s=None, sib_r=None, loc_s=None, whole=""):
        self.whole = whole
        self.me, self.parts, self.acc, self.hop_b, self.fin_b = me, parts, acc, hop, fin
        self.ss, self.rs, self.sib, self.source = ss, rs, sib, source
        self.sib_s, self.sib_r, self.loc_s = sib_s, sib_r, loc_s
        self.count, self.last = len(parts), len(parts[0][2]) - 1

    def idx(self, n, at):
        name, p, _ = self.parts[n]
        place = tuple(at[a] for a in AXES[name])
        return place if name in "CF" else (p,) + place

    def slot(self, n):
        name, p, _ = self.parts[n]
        return () if name in "CF" else (p,)

    def done(self, n, t):
        name, _, order = self.parts[n]
        return [a for a in AXES[name] if a in self.whole + order[:t]]

    def group(self, n, t, step, half=None):
        axes = self.done(n, t)
        at = {**moved(self.me, self.parts[n][2][t], step), **{a: ALL for a in axes}}
        if half is not None and axes:
            at[axes[0]] = pl.ds(2 * half, 2)
        return at

    def fins(self, t):
        return 2 if t == self.last else 3

    def refs(self, n, t):
        name = self.parts[n][0]
        return self.acc[name], self.hop_b[name] if t == self.last else None, self.fin_b[t][name]

    def hop_copy(self, n, kind):
        step, t = 1 if kind == 0 else -1, self.last
        a, h, _ = self.refs(n, t)
        return remote(a.at[self.idx(n, self.group(n, t, 2 * step, kind))], h.at[self.slot(n) + (kind,)],
                      self.ss.at[n, t, kind], self.rs.at[n, t, kind], moved(self.me, self.parts[n][2][t], step))

    def fin_copy(self, n, t, kind):
        step = (1, -1, 2)[kind]
        a, _, f = self.refs(n, t)
        return remote(a.at[self.idx(n, self.group(n, t, step))], f.at[self.slot(n) + (kind,)],
                      self.ss.at[n, t, 2 + kind], self.rs.at[n, t, 2 + kind], moved(self.me, self.parts[n][2][t], step))

    def each(self, n, t, at, fn, half=None):
        axes = self.done(n, t)
        sizes, offs = [4] * len(axes), [0] * len(axes)
        if half is not None and axes:
            sizes[0], offs[0] = 2, 2 * half
        total = 1
        for s in sizes:
            total *= s

        def one(i):
            pos, rest = [], i
            for s in sizes[::-1]:
                pos.append(rest % s)
                rest = rest // s
            pos = pos[::-1]
            where = dict(at)
            for a, p, o in zip(axes, pos, offs):
                where[a] = p + o
            fn(self.idx(n, where), tuple(pos))

        if total == 1:
            one(0)
        else:
            pl.loop(0, total, unroll=4)(one)

    def sib_copy(self, n, j):
        at = self.group(n, self.last, STEPS[j])
        return remote(self.source(n, at, 1 - self.me["c"]), self.sib[self.parts[n][0]].at[self.idx(n, at)],
                      self.sib_s.at[n, j], self.sib_r.at[n, j], sibling_of(self.me))

    def loc_copy(self, n, j):
        at = self.group(n, self.last, STEPS[j])
        return pltpu.make_async_copy(self.source(n, at, self.me["c"]), self.acc[self.parts[n][0]].at[self.idx(n, at)], self.loc_s.at[n, j])

    def start(self):
        for j in range(4):
            for n in range(self.count):
                self.sib_copy(n, j).start()
                self.loc_copy(n, j).start()

    def merge(self, j):
        for n in range(self.count):
            self.sib_copy(n, j).wait_recv()
            self.loc_copy(n, j).wait()
            a, b = self.acc[self.parts[n][0]], self.sib[self.parts[n][0]]

            def fn(i, _):
                a[i] = a[i] + b[i]

            self.each(n, self.last, self.group(n, self.last, STEPS[j]), fn)

    def send(self, t, ns=None):
        for n in ns or range(self.count):
            if t == self.last:
                for k in (0, 1):
                    self.hop_copy(n, k).start()
            else:
                for k in (2, 0, 1):
                    self.fin_copy(n, t, k).start()

    def forward(self, ns=None):
        t = self.last
        for n in ns or range(self.count):
            a, h, _ = self.refs(n, t)
            for k in (0, 1):
                self.hop_copy(n, k).wait_recv()

                def fn(i, pos):
                    a[i] = a[i] + h[self.slot(n) + (k,) + pos]

                self.each(n, t, self.group(n, t, 1 if k == 0 else -1), fn, k)
                self.fin_copy(n, t, k).start()

    def close(self, t, ns=None):
        for n in ns or range(self.count):
            for k in range(self.fins(t)):
                self.fin_copy(n, t, k).wait_recv()
            a, _, f = self.refs(n, t)

            def fn(i, pos):
                v = a[i].astype(F32)
                for k in range(self.fins(t)):
                    v = v + f[self.slot(n) + (k,) + pos].astype(F32)
                a[i] = v.astype(BF)

            self.each(n, t, self.group(n, t, 0), fn)

    def result(self, n):
        a, _, f = self.refs(n, 0)
        v = a[self.idx(n, self.me)].astype(F32)
        for k in range(3):
            self.fin_copy(n, 0, k).wait_recv()
            v = v + f[self.slot(n) + (k,)].astype(F32)
        return v

    def drain(self):
        for n in range(self.count):
            if self.sib is not None:
                for j in range(4):
                    self.sib_copy(n, j).wait_send()
            for k in (0, 1):
                self.hop_copy(n, k).wait_send()
            for t in range(self.last + 1):
                for k in range(self.fins(t)):
                    self.fin_copy(n, t, k).wait_send()


LEAD_A = ((2, 2, 4), (2, 4, 4), (3, 4), (3,))
LEAD_D = ((2, 2), (2, 4), (3,))


def stage_buffers(leads, *shapes):
    return [vm(*pre, *lead, *block) for lead in leads for pre, block in shapes]


def staged(names, refs):
    k = len(names)
    got = [dict(zip(names, refs[k * i:k * i + k])) for i in range(len(refs) // k)]
    return got[0], {len(got) - 2 - i: g for i, g in enumerate(got[1:])}


def ffn_place(B, C):
    def place(n, at):
        if n < 2:
            return B.at[at["x"], at["y"], at["z"], at["c"], n]
        return C.at[at["z"], at["c"], at["x"], at["y"]]
    return place


def info_tile(gain, mem_len):
    sq = lax.axis_index("seq")
    t = jnp.zeros((8, 128), F32)
    t = lax.dynamic_update_slice(t, gain.astype(BF).astype(F32), (0, 6 * sq))
    return lax.dynamic_update_slice(t, mem_len.astype(F32)[:, None], (3, sq))


def scatter_kernel(GA, sumE, sumF, gg, oA, oB, oC, oG, accA, sibA, h2, f2, f1, f0,
                   accE, accF, hE1, hF1, fE1, fF1, fE0, fF0, blk, stage, recv, gdp, gsum,
                   ss, rs, sib_s, sib_r, loc_s, as_, ar_, ds_, dr_, es, er, ld_s):
    me = where_am_i()
    dp, sq = lax.axis_index("dp"), lax.axis_index("seq")
    bar, count = meet(me, "dp")
    loads = [pltpu.make_async_copy(a, b, ld_s.at[i]) for i, (a, b) in enumerate(((sumE, accE), (sumF, accF)))]
    for c in loads:
        c.start()
    pl.semaphore_wait(bar, count)
    hop, fin = staged("A", (h2, f2, f1, f0))
    ring = Scatter(me, PARTS_A, {"A": accA}, hop, fin, ss, rs, {"A": sibA},
                   lambda n, at, c: GA.at[at["x"], at["y"], at["z"], c, n], sib_s, sib_r, loc_s)
    fhop, ffin = staged("EF", (hE1, hF1, fE1, fF1, fE0, fF0))
    ring_f = Scatter(me, PARTS_G, {"E": accE, "F": accF}, fhop, ffin, es, er)
    ring.start()
    for c in loads:
        c.wait()
    ring_f.send(1)

    def dpx(i):
        peer = (dp + i) % 8
        return pltpu.make_async_remote_copy(gg.at[peer], gdp.at[dp], ds_.at[i], dr_.at[i], device_id=(peer, sq), device_id_type=MESH)

    for i in range(1, 8):
        dpx(i).start()
    gdp[dp] = gg[dp]
    ring.merge(0)
    ring.send(2)
    ring.merge(1)
    ring.merge(2)
    ring_f.forward()
    ring.forward()
    ring.merge(3)
    ring_f.close(1)
    ring_f.send(0)
    for i in range(1, 8):
        dpx(i).wait_recv()
    gsum[...] = jnp.sum(gdp[...], axis=0)

    stage[:, 6:8, :] = jnp.zeros((16, 2, 768), F32)
    ring.close(2)
    ring.send(1)
    for n in range(2):
        blk[48 * n:48 * n + 48, 384:640] = ring_f.result(n)
    oC[...] = ring_f.result(2)
    ring.close(1)
    ring.send(0)
    for n in range(3):
        blk[32 * n:32 * n + 32, 0:384] = ring.result(n)
    for k in range(16):
        stage[k, 0:6, 0:640] = blk[6 * k:6 * k + 6, :]
        stage[k, :, 640:768] = gsum[...]

    def a2a(i):
        peer = (sq + i) % 16
        return pltpu.make_async_remote_copy(stage.at[peer], recv.at[sq], as_.at[i], ar_.at[i], device_id=(dp, peer), device_id_type=MESH)

    for i in range(1, 16):
        a2a(i).start()
    recv[sq] = stage[sq]
    for i in range(1, 16):
        a2a(i).wait_recv()
    oG[...] = pltpu.roll(jnp.sum(recv[:, :, 640:768], axis=0), (128 - 6 * sq) % 128, 1)
    for s in range(16):
        oA[:, s // 2, 384 * (s % 2):384 * (s % 2) + 384] = recv[s, 0:6, 0:384]
        oB[:, s // 8, 256 * (s % 8):256 * (s % 8) + 256] = recv[s, 0:6, 384:640]
    for i in range(1, 8):
        dpx(i).wait_send()
    for i in range(1, 16):
        a2a(i).wait_send()
    ring.drain()
    ring_f.drain()


def scatter(GA, sumE, sumF, gg):
    return pl.pallas_call(
        scatter_kernel,
        out_shape=(SDS((6, 8, 768), F32), SDS((6, 2, 2048), F32), SDS((16, 768), F32), SDS((8, 128), F32)),
        in_specs=[HS, HS, HS, VS], out_specs=(VS,) * 4,
        scratch_shapes=[vm(3, 4, 4, 4, 32, 384), vm(3, 4, 4, 4, 32, 384), *stage_buffers(LEAD_A, ((3,), (32, 384))),
                        vm(2, 4, 4, 48, 256), vm(4, 4, 16, 768), *stage_buffers(LEAD_D, ((2,), (48, 256)), ((), (16, 768))),
                        vf(96, 640), vf(16, 8, 768), vf(16, 8, 768), vf(8, 8, 128), vf(8, 128),
                        DMA((3, 3, 5)), DMA((3, 3, 5)), DMA((3, 4)), DMA((3, 4)), DMA((3, 4)),
                        DMA((16,)), DMA((16,)), DMA((8,)), DMA((8,)), DMA((3, 2, 5)), DMA((3, 2, 5)), DMA((2,))],
        compiler_params=pltpu.CompilerParams(collective_id=1, has_side_effects=True, vmem_limit_bytes=60 << 20),
        name="scatter_attention_grads",
    )(GA, sumE, sumF, gg)


def head_masks(value=1.0):
    lane = lax.broadcasted_iota(jnp.int32, (1, 256), 1)
    return [jnp.where(lane // 64 == h, value, 0.0).astype(BF) for h in range(4)]


def stack_heads(block, masks):
    return jnp.concatenate([block * m for m in masks], axis=0)


def key_positions():
    sq = lax.axis_index("seq")
    return (192 * sq + lax.broadcasted_iota(jnp.int32, (192, 128), 0)).astype(F32)


class Merge:
    def __init__(self, me, src, mid, one, two, ss, rs):
        self.me, self.src, self.mid, self.bufs, self.ss, self.rs = me, src, mid, (one, two), ss, rs

    def block(self, n, a, b):
        return (n, a, b) if n % 2 == 0 else (n, b, a)

    def copy(self, n, t, k):
        axis = PLANE[n][t]
        to = moved(self.me, axis, (1, -1, 2)[k])
        src = self.src.at[self.block(n, to[axis], ALL)] if t == 0 else self.mid.at[n, to[axis]]
        return remote(src, self.bufs[t].at[n, k], self.ss.at[n, t, k], self.rs.at[n, t, k], to)

    def send(self, t, ns):
        for n in ns:
            for k in (2, 0, 1):
                self.copy(n, t, k).start()

    def join(self, blocks):
        rows = [b[128:144, :].astype(F32)[0:8, :] for b in blocks]
        logs = [r + pltpu.roll(r, 6, 0) + pltpu.roll(r, 4, 0) for r in rows]
        top = logs[0]
        for l in logs[1:]:
            top = jnp.maximum(top, l)
        ws = [jnp.exp(l - top) for l in logs]
        total = ws[0] + ws[1] + ws[2] + ws[3]
        inv = 1.0 / total
        out = []
        for h in range(2):
            o = sum(b[64 * h:64 * h + 64, :].astype(F32) * (w * inv)[h:h + 1, :] for b, w in zip(blocks, ws))
            out.append(o)
        return jnp.concatenate(out, axis=0), top + jnp.log(total)

    def middle(self, ns):
        for n in ns:
            for k in range(3):
                self.copy(n, 0, k).wait_recv()
            a = self.me[PLANE[n][0]]

            for b in range(4):
                o, l = self.join([self.src.at[self.block(n, a, b)]] + [self.bufs[0].at[n, k, b] for k in range(3)])
                self.mid[n, b, 0:128, :] = o.astype(BF)
                self.mid[n, b, 128:144, :] = log_tile(l)

    def result(self, n):
        for k in range(3):
            self.copy(n, 1, k).wait_recv()
        return self.join([self.mid.at[n, self.me[PLANE[n][1]]]] + [self.bufs[1].at[n, k] for k in range(3)])

    def drain(self):
        for n in range(6):
            for t in range(2):
                for k in range(3):
                    self.copy(n, t, k).wait_send()


def log_tile(l):
    l = jnp.where(lax.broadcasted_iota(jnp.int32, (8, 128), 0) < 2, l, 0.0)
    high = l.astype(BF).astype(F32)
    middle = (l - high).astype(BF).astype(F32)
    low = l - high - middle
    return jnp.concatenate([high + pltpu.roll(middle, 2, 0) + pltpu.roll(low, 4, 0), jnp.zeros((8, 128), F32)], axis=0).astype(BF)


def pair_of(ref, g, at):
    return jnp.concatenate([ref[2 * g, at["x"], at["y"]], ref[2 * g + 1, at["x"], at["y"]]], axis=1)


def rms(x):
    return lax.rsqrt(jnp.mean(x * x, axis=-1, keepdims=True) + eps_norm)

def rms_back(x, inv, gain, u):
    scaled = u * gain
    inner = jnp.mean(scaled * x, axis=-1, keepdims=True)
    return inv * scaled - x * inv * inv * inv * inner, jnp.sum(u * x * inv, axis=0, keepdims=True)

def flip(x):
    return jnp.concatenate([x[:, 128 * i:128 * i + 128].T for i in range(x.shape[1] // 128)], axis=0)

def unflip(x):
    return jnp.concatenate([x[128 * i:128 * i + 128, :].T for i in range(x.shape[0] // 128)], axis=1)

def apply_w(h, W, k):
    return jnp.concatenate([dot(h, W[2 * k]), dot(h, W[2 * k + 1])], axis=1)

def apply_wt(u, W, k):
    return dot(u[:, 0:384], W[2 * k], 1, 1) + dot(u[:, 384:768], W[2 * k + 1], 1, 1)

def causal_mask():
    return lax.broadcasted_iota(jnp.int32, (128, 128), 0) <= lax.broadcasted_iota(jnp.int32, (128, 128), 1)


class Stacked:
    def __init__(self, ref):
        self.ref = ref

    def __getitem__(self, n):
        return self.ref[n].reshape(768, 384)


def self_attention(x_ref, gains, W, loads, q2, h1, qkv, o1, x1, h2, L1):
    x = x_ref[...].astype(F32)
    h = (x * rms(x) * gains[0:1, :]).astype(BF)
    h1[...] = h
    for k in range(3):
        loads[2 * k].wait()
        loads[2 * k + 1].wait()
        full = apply_w(h, W, k)
        qkv[k] = full.astype(BF)
    vT = flip(full).astype(BF)
    masks = head_masks(0.125)
    live = causal_mask()
    outs = []
    for g in range(3):
        cols = slice(256 * g, 256 * g + 256)
        q4 = qkv[0, :, cols]
        sT = dot(qkv[1, :, cols], jnp.concatenate([q4 * m for m in masks], axis=0), 1, 1)
        ps = []
        for n in range(4):
            s = jnp.where(live, sT[:, 128 * n:128 * n + 128], NEG)
            top = jnp.max(s, axis=0, keepdims=True)
            lse = top + jnp.log(jnp.sum(jnp.exp(s - top), axis=0, keepdims=True))
            L1[4 * g + n:4 * g + n + 1, :] = lse
            ps.append(jnp.exp(s - lse).astype(BF))
        oT = dot(vT[256 * g:256 * g + 256, :], jnp.concatenate(ps, axis=1))
        outs += [oT[64 * n:64 * n + 64, 128 * n:128 * n + 128] for n in range(4)]
    o = unflip(jnp.concatenate(outs, axis=0)).astype(BF)
    o1[...] = o
    for c in loads[6:10]:
        c.wait()
    x = x + apply_w(o, W, 3)
    x1[...] = x
    h = (x * rms(x) * gains[1:2, :]).astype(BF)
    h2[...] = h
    q2[...] = apply_w(h, W, 4).astype(BF) * jnp.asarray(0.125, BF)


def forward_kernel(attn, wi, wo, info, x_ref, mem_h, A, B, C, q_h, k_h, v_h, kt_h, gains, lens, h1, qkv, o1, x1, h2, L1, o_ref, L_ref,
                   infos, stage, recv, blk, blkA, blkB, blkC, W, q2,
                   qall, mem, wk, wv, wkT, wvT, K, V, KT, VT, ost, mid, one, two, lrow,
                   fs, fr, ss, rs, sib_s, sib_r, as_, ar_, ds_, dr_, own_s, zs, zr, zsib_s, zsib_r,
                   load_s, mem_s, out_s, ps_, pr_, os_, or_):
    me = where_am_i()
    dp, sq = lax.axis_index("dp"), lax.axis_index("seq")
    bar, count = meet(me, "dp")

    def load_mem(e):
        return pltpu.make_async_copy(mem_h.at[e], mem.at[e], mem_s.at[e])

    @pl.loop(0, 16)
    def _(e):
        load_mem(e).start()

    lrow[...] = jnp.zeros((4, 2, 8, 128), F32)
    stage[:, 6:8, :] = jnp.zeros((16, 2, 768), F32)
    for s in range(16):
        stage[s, 0:6, 0:384] = attn[:, s // 2, 384 * (s % 2):384 * (s % 2) + 384]
        stage[s, :, 640:768] = info[...]
        stage[s, 0:6, 384:640] = wi[:, s // 8, 256 * (s % 8):256 * (s % 8) + 256]
    pl.semaphore_wait(bar, count)

    def a2a(i):
        peer = (sq + i) % 16
        return pltpu.make_async_remote_copy(stage.at[peer], recv.at[sq], as_.at[i], ar_.at[i], device_id=(dp, peer), device_id_type=MESH)

    for i in range(1, 16):
        a2a(i).start()
    recv[sq] = stage[sq]
    blkC[...] = wo[...].astype(BF)
    for i in range(1, 16):
        a2a(i).wait_recv()
    for k in range(16):
        blk[6 * k:6 * k + 6, :] = recv[k, 0:6, 0:640]
    for p in range(3):
        blkA[p] = blk[32 * p:32 * p + 32, 0:384].astype(BF)
    for p in range(2):
        blkB[p] = blk[48 * p:48 * p + 48, 384:640].astype(BF)
    place = lambda n, at: A.at[at["x"], at["y"], at["z"], at["c"], PARTS_A[n][1]]
    ring = Gather(me, [p[2] for p in PARTS_A], place, lambda n: blkA.at[n], ss, rs, sib_s, sib_r)
    place_f = ffn_place(B, C)
    mine = lambda n: blkB.at[n] if n < 2 else blkC
    ring_f = Gather(me, [p[2] for p in PARTS_G], place_f, mine, fs, fr)
    owns = [pltpu.make_async_copy(blkA.at[n], place(n, me), own_s.at[n]) for n in range(3)]
    owns += [pltpu.make_async_copy(mine(n), place_f(n, me), own_s.at[3 + n]) for n in range(3)]
    for o in owns:
        o.start()
    ring.send(0)
    ring_f.send(0)
    for o in owns:
        o.wait()
    ring.send(1)
    ring_f.send(1)
    ring.send(2)
    ring_f.forward()
    tile = jnp.sum(recv[:, :, 640:768], axis=0)
    infos[dp] = tile

    def dpx(i, back=0):
        v = infos.at[(dp - back + 8) % 8]
        return pltpu.make_async_remote_copy(v, v, ds_.at[i], dr_.at[i], device_id=((dp + i) % 8, sq), device_id_type=MESH)

    for i in range(1, 8):
        dpx(i).start()
    ring.forward()
    for i in range(1, 8):
        dpx(i, i).wait_recv()
    lane = lax.broadcasted_iota(jnp.int32, (8, 128), 1)
    gains[...] = jnp.zeros((8, 768), F32)
    for d in range(8):
        lo, sh = 96 * d // 128, 96 * d % 128
        t = pltpu.roll(jnp.where(lane < 96, infos[d], 0.0), sh, 1)
        gains[:, 128 * lo:128 * lo + 128] += jnp.where(lane >= sh, t, 0.0)
        if sh > 32:
            gains[:, 128 * lo + 128:128 * lo + 256] += jnp.where(lane < sh, t, 0.0)
    pick = lax.broadcasted_iota(jnp.int32, (16, 128), 0) == lax.broadcasted_iota(jnp.int32, (16, 128), 1)
    lens[...] = jnp.broadcast_to(jnp.sum(jnp.where(pick, tile[3:4, :], 0.0), axis=1, keepdims=True), (16, 128))
    ring_f.finish()
    ring_z = Gather(me, ("z",) * 3, place_f, None, zs, zr, zsib_s, zsib_r, "xy")
    ring.finish()
    ring.siblings_in()
    block = lambda n: A.at[n // 4, n % 4]
    loads = [pltpu.make_async_copy(block(n), W.at[n], load_s.at[n]) for n in range(10)]
    loads += [pltpu.make_async_copy(block(10 + n), (wk if n < 2 else wv).at[:, :, :, :, pl.ds(384 * (n % 2), 384)], load_s.at[10 + n]) for n in range(4)]
    for c in loads:
        c.start()
    ring_z.send(0)
    self_attention(x_ref, gains, Stacked(W), loads, q2, h1, qkv, o1, x1, h2, L1)
    for n in range(6):
        qall[n, me["x"], me["y"]] = q2[:, 128 * n:128 * n + 128]
    view = lambda n, at: qall.at[n, at["x"], at["y"]]
    plane = Gather(me, PLANE, view, lambda n: view(n, me), ps_, pr_)
    fold = Merge(me, ost, mid, one, two, os_, or_)
    plane.send(0)
    for c in loads[10:]:
        c.wait()
    flat = lambda ref: ref[...].reshape(768, 768)
    for i in range(6):
        wvT[:, 128 * i:128 * i + 128] = flat(wv)[128 * i:128 * i + 128, :].T

    def project(a, b):
        @pl.loop(a // 2, b // 2)
        def _(i):
            for e in (2 * i, 2 * i + 1):
                load_mem(e).wait()
            K[pl.ds(2 * i, 2)] = dot(mem[pl.ds(2 * i, 2)].reshape(384, 768), flat(wk)).astype(BF).reshape(2, 192, 768)
            for e in (2 * i, 2 * i + 1):
                VT[e] = dot(wvT[...], mem[e], 1, 1).astype(BF)

    def project_more(a, b):
        @pl.loop(a // 2, b // 2)
        def _(i):
            V[pl.ds(2 * i, 2)] = dot(mem[pl.ds(2 * i, 2)].reshape(384, 768), flat(wv)).astype(BF).reshape(2, 192, 768)
            for e in (2 * i, 2 * i + 1):
                KT[e] = dot(wkT[...], mem[e], 1, 1).astype(BF)

    plane.send(1, (0, 1))
    project(0, 4)
    plane.send(1, (2, 3))
    plane.send(1, (4, 5))
    project(4, 10)
    plane.forward((0, 1))
    plane.forward((2, 3))
    project(10, 16)
    plane.forward((4, 5))
    masks = head_masks()
    pos = key_positions()

    def attend(g):
        cols = slice(256 * g, 256 * g + 256)

        @pl.loop(0, 4)
        def _(i):
            four = [(x, x * 4 + y, {"x": x, "y": y}) for x, y in [(i, y) for y in range(4)]]
            sT = [dot(K[e, :, cols], stack_heads(pair_of(qall, g, at), masks), 1, 1) for _, e, at in four]
            pT, inv = [], []
            for u, (_, e, at) in enumerate(four):
                live = pos < lens[pl.ds(e, 1), :]
                ps = []
                for h in range(4):
                    s = jnp.where(live, sT[u][:, 128 * h:128 * h + 128], NEG)
                    top = jnp.max(s, axis=0, keepdims=True)
                    p = jnp.exp(s - top)
                    tot = jnp.sum(p, axis=0, keepdims=True)
                    lrow[u, h // 2, h % 2:h % 2 + 1, :] = top + jnp.log(tot)
                    ps.append(p.astype(BF))
                    inv.append(1.0 / tot)
                pT.append(jnp.concatenate(ps, axis=1))
            oT = [dot(VT[e, cols, :], p) for (_, e, _), p in zip(four, pT)]
            for u, (_, e, at) in enumerate(four):
                for h in range(4):
                    ost[2 * g + h // 2, at["x"], at["y"], 64 * (h % 2):64 * (h % 2) + 64, :] = (
                        oT[u][64 * h:64 * h + 64, 128 * h:128 * h + 128] * inv[4 * u + h]).astype(BF)
                for h in range(2):
                    ost[2 * g + h, at["x"], at["y"], 128:144, :] = log_tile(lrow[u, h])

        fold.send(0, (2 * g, 2 * g + 1))

    def deliver(g):
        for n in (2 * g, 2 * g + 1):
            o, l = fold.result(n)
            o_ref[:, 128 * n:128 * n + 128] = o.T
            L_ref[2 * n:2 * n + 2, :] = l[0:2, :]

    plane.finish((0, 1))
    attend(0)
    plane.finish((2, 3))
    attend(1)
    fold.middle((0, 1))
    fold.send(1, (0, 1))
    plane.finish((4, 5))
    out_q = pltpu.make_async_copy(qall, q_h, out_s.at[0])
    out_k = pltpu.make_async_copy(K, k_h, out_s.at[1])
    out_q.start()
    out_k.start()
    ring_z.forward()
    attend(2)
    fold.middle((2, 3))
    fold.send(1, (2, 3))
    for i in range(6):
        wkT[:, 128 * i:128 * i + 128] = flat(wk)[128 * i:128 * i + 128, :].T
    project_more(0, 8)
    fold.middle((4, 5))
    fold.send(1, (4, 5))
    low, high = pl.ds(0, 8), pl.ds(8, 8)
    outs = [pltpu.make_async_copy(a.at[k], b.at[k], out_s.at[2 + 2 * i + j])
            for j, k in enumerate((low, high)) for i, (a, b) in enumerate(((V, v_h), (KT, kt_h)))]
    for c in outs[:2]:
        c.start()
    ring_z.finish()
    project_more(8, 16)
    for c in outs[2:]:
        c.start()
    L_ref[12:16, :] = jnp.zeros((4, 128), F32)
    for g in range(3):
        deliver(g)
    plane.drain()
    fold.drain()
    for c in [out_q, out_k] + outs:
        c.wait()
    ring_z.siblings_in()
    ring_z.drain()
    ring_f.drain()
    ring.drain()
    for i in range(1, 16):
        a2a(i).wait_send()
    for i in range(1, 8):
        dpx(i).wait_send()


def forward(attn, wi, wo, info, x, memory):
    row = SDS((128, 768), BF)
    rowf = SDS((128, 768), F32)
    log = SDS((16, 128), F32)
    return pl.pallas_call(
        forward_kernel,
        out_shape=(SDS((4, 4, 4, 2, 3, 32, 384), BF), SDS((4, 4, 4, 2, 2, 48, 256), BF), SDS((4, 2, 4, 4, 16, 768), BF),
                   SDS((6, 4, 4, 128, 128), BF), SDS((16, 192, 768), BF), SDS((16, 192, 768), BF), SDS((16, 768, 192), BF),
                   SDS((8, 768), F32), log, row, SDS((3, 128, 768), BF), row, rowf, row, log, rowf, log),
        in_specs=[VS] * 5 + [HS], out_specs=(HS,) * 7 + (VS,) * 10,
        scratch_shapes=[vf(8, 8, 128), vf(16, 8, 768), vf(16, 8, 768), vf(96, 640), vm(3, 32, 384), vm(2, 48, 256), vm(16, 768),
                        vm(10, 4, 2, 3, 32, 384), vm(128, 768),
                        vm(6, 4, 4, 128, 128), vm(16, 192, 768), vm(4, 2, 3, 32, 768), vm(4, 2, 3, 32, 768), vm(768, 768), vm(768, 768),
                        vm(16, 192, 768), vm(16, 192, 768), vm(16, 768, 192), vm(16, 768, 192),
                        vm(6, 4, 4, 144, 128), vm(6, 4, 144, 128), vm(6, 3, 4, 144, 128), vm(6, 3, 144, 128), vf(4, 2, 8, 128),
                        DMA((3, 2, 4)), DMA((3, 2, 4)), DMA((3, 3, 4)), DMA((3, 3, 4)), DMA((3, 4)), DMA((3, 4)), DMA((16,)), DMA((16,)), DMA((8,)), DMA((8,)), DMA((6,)),
                        DMA((3, 1, 4)), DMA((3, 1, 4)), DMA((3, 4)), DMA((3, 4)),
                        DMA((14,)), DMA((16,)), DMA((6,)), DMA((6, 2, 4)), DMA((6, 2, 4)), DMA((6, 2, 3)), DMA((6, 2, 3))],
        compiler_params=pltpu.CompilerParams(collective_id=0, has_side_effects=True, vmem_limit_bytes=60 << 20),
        name="forward_attention",
    )(attn, wi, wo, info, x, memory)


def cross_bwd_kernel(do, st, lens, q_h, k_h, v_h, kt_h, mem_h, A, GB, GC, G_in, dq_ref, gm_h, dw_h, sumE, sumF,
                     qall, doall, stall, wk, wv, K, V, KT, mem, memT, dK, dV, gst, wst, dst, dh1, df1, df0,
                     accB, accC, sibB, sibC, hB2, hC2, fB2, fC2,
                     q_s, kv_s, mem_s, w_s, gm_s, dw_s, ss, rs, ds_, dr_, fs, fr, fsib_s, fsib_r, floc, sum_s):
    me = where_am_i()
    bar, count = meet(me, "z")

    def load_mem(e):
        return pltpu.make_async_copy(mem_h.at[pl.ds(pl.multiple_of(256 * e, 256), 256)], mem.at[e % 4], mem_s.at[e % 4])

    for e in range(4):
        load_mem(e).start()
    loads = [pltpu.make_async_copy(A.at[10 + i], (wk if i < 2 else wv).at[:, pl.ds(384 * (i % 2), 384)], w_s.at[i]) for i in range(4)]
    loads.append(pltpu.make_async_copy(q_h, qall, q_s))
    for n in range(6):
        doall[n, me["x"], me["y"]] = do[:, 128 * n:128 * n + 128]
    stall[me["x"], me["y"]] = st[...]
    pl.semaphore_wait(bar, count)

    def place(n, at):
        return stall.at[at["x"], at["y"]] if n == 6 else doall.at[n, at["x"], at["y"]]

    plane = Gather(me, PLANE + ("xy",), place, lambda n: place(n, me), ss, rs)
    fhop, ffin = staged("BC", (hB2, hC2, fB2, fC2))
    grads = ffn_place(GB, GC)
    ring = Scatter(me, PARTS_F, {"B": accB, "C": accC}, fhop, ffin, fs, fr, {"B": sibB, "C": sibC},
                   lambda n, at, c: grads(n, {**at, "c": c}), fsib_s, fsib_r, floc, "xy")
    back = Scatter(me, PARTS_D, {"D": dst}, *staged("D", (dh1, df1, df0)), ds_, dr_)
    plane.send(0, (6, 0, 1, 2, 3, 4, 5))
    ring.start()
    for c in loads:
        c.start()

    def turn(a, b):
        @pl.loop(a, b)
        def _(e):
            load_mem(e).wait()
            memT[:, pl.ds(pl.multiple_of(256 * e, 256), 256)] = mem[e % 4].T

            @pl.when(e < 8)
            def _():
                load_mem(e + 4).start()

    turn(0, 3)
    plane.send(1, (6, 0, 1))
    plane.send(1, (2, 3))
    plane.send(1, (4, 5))
    ring.merge(0)
    ring.send(0)
    turn(3, 6)
    plane.forward((6, 0, 1))
    ring.merge(1)
    ring.merge(2)
    plane.forward((2, 3))
    ring.forward()
    masks = head_masks()
    pos = key_positions()

    def load_kv(g, i, u, which):
        e = ((me["x"] + 2 + i) % 4) * 4 + u
        cols = pl.ds(256 * g, 256)
        src = (k_h.at[e, :, cols], v_h.at[e, :, cols], kt_h.at[e, cols])[which]
        return pltpu.make_async_copy(src, (K, V, KT)[which].at[i % 2, u], kv_s.at[which, i % 2, u])

    def fetch_kv(g, i):
        for u in range(4):
            for w in range(3):
                load_kv(g, i, u, w).start()

    fetch_kv(0, 0)
    for c in loads:
        c.wait()

    def attend(g):
        cols = slice(256 * g, 256 * g + 256)

        @pl.loop(0, 4)
        def _(i):
            @pl.when(i < 3)
            def _():
                fetch_kv(g, i + 1)

            for u in range(4):
                for w in range(3):
                    load_kv(g, i, u, w).wait()
            x = (me["x"] + 2 + i) % 4
            four = [(x * 4 + y, {"x": x, "y": y}) for y in range(4)]
            q4s = [stack_heads(pair_of(qall, g, at), masks) for _, at in four]
            d4s = [stack_heads(pair_of(doall, g, at), masks) for _, at in four]
            sT = [dot(K[i % 2, u], q4s[u], 1, 1) for u in range(4)]
            gT = [dot(V[i % 2, u], d4s[u], 1, 1) for u in range(4)]
            pT, sg = [], []
            for u, (e, at) in enumerate(four):
                live = pos < lens[pl.ds(e, 1), :]
                ps, gs = [], []
                for h in range(4):
                    n = 4 * g + h
                    s = jnp.where(live, sT[u][:, 128 * h:128 * h + 128], NEG)
                    p = jnp.exp(s - stall[at["x"], at["y"], n:n + 1, :])
                    ps.append(p.astype(BF))
                    gs.append((p * (gT[u][:, 128 * h:128 * h + 128] - stall[at["x"], at["y"], 12 + n:13 + n, :])).astype(BF))
                pT.append(jnp.concatenate(ps, axis=1))
                sg.append(jnp.concatenate(gs, axis=1))
            for u, (e, at) in enumerate(four):
                dV[pl.ds(pl.multiple_of(192 * e, 192), 192), cols] = dot(pT[u], d4s[u]).astype(BF)
            for u, (e, at) in enumerate(four):
                dK[pl.ds(pl.multiple_of(192 * e, 192), 192), cols] = dot(sg[u], q4s[u]).astype(BF)
            for u, (e, at) in enumerate(four):
                qT = dot(KT[i % 2, u], sg[u])
                for h in range(4):
                    dst[2 * g + h // 2, at["x"], at["y"], 64 * (h % 2):64 * (h % 2) + 64, :] = qT[64 * h:64 * h + 64, 128 * h:128 * h + 128].astype(BF)

        if g < 2:
            fetch_kv(g + 1, 0)
        back.send(1, (2 * g, 2 * g + 1))

    plane.finish((6, 0, 1))
    attend(0)
    plane.forward((4, 5))
    plane.finish((2, 3))
    attend(1)
    back.forward((0, 1))
    ring.merge(3)
    plane.finish((4, 5))
    attend(2)
    back.forward((2, 3))
    back.close(1, (0, 1))
    back.send(0, (0, 1))

    def gm_copy(e):
        return pltpu.make_async_copy(gst.at[e % 2], gm_h.at[e], gm_s.at[e % 2])

    def mem_grad(a, b):
        @pl.loop(a, b)
        def _(e):
            @pl.when(e > 1)
            def _():
                gm_copy(e - 2).wait()

            rows = pl.ds(pl.multiple_of(384 * e, 384), 384)
            gst[e % 2] = dot(dK[rows, :], wk[...], 1, 1) + dot(dV[rows, :], wv[...], 1, 1)
            gm_copy(e).start()

    def dw_copy(k, r, half):
        rows = pl.ds(pl.multiple_of(256 * r, 256), 256)
        return pltpu.make_async_copy(wst.at[k, :, pl.ds(384 * half, 384)], dw_h.at[10 + 2 * k + half, rows], dw_s.at[k, half])

    def weight_grad(a, b):
        @pl.loop(a, b)
        def _(r):
            for k in range(2):
                @pl.when(r > 0)
                def _():
                    dw_copy(k, r - 1, 0).wait()
                    dw_copy(k, r - 1, 1).wait()

                wst[k] = dot(memT[pl.ds(pl.multiple_of(256 * r, 256), 256), :], (dV if k else dK)[...]).astype(BF)
                dw_copy(k, r, 0).start()
                dw_copy(k, r, 1).start()

    turn(6, 12)
    mem_grad(0, 2)
    back.forward((4, 5))
    back.close(1, (2, 3))
    back.send(0, (2, 3))
    mem_grad(2, 8)
    back.close(1, (4, 5))
    back.send(0, (4, 5))
    ring.close(0)
    sums = [pltpu.make_async_copy(accB.at[:, :, :, me["z"]], sumE, sum_s.at[0]), pltpu.make_async_copy(accC.at[me["z"]], sumF, sum_s.at[1])]
    for c in sums:
        c.start()
    weight_grad(0, 3)
    for n in range(6):
        dq_ref[:, 128 * n:128 * n + 128] = (0.125 * back.result(n)).T
    for c in sums:
        c.wait()
    gm_copy(6).wait()
    gm_copy(7).wait()
    for k in range(2):
        dw_copy(k, 2, 0).wait()
        dw_copy(k, 2, 1).wait()
    plane.drain()
    ring.drain()
    back.drain()


def cross_bwd(do, st, lens, q_h, k_h, v_h, kt_h, memory, A, GB, GC, GA):
    bB, bC = (48, 256), (16, 768)
    return pl.pallas_call(
        cross_bwd_kernel,
        out_shape=(SDS((128, 768), F32), SDS((8, 384, 768), F32), SDS((16, 768, 384), BF), SDS((2, 4, 4, 48, 256), BF), SDS((4, 4, 16, 768), BF)),
        in_specs=[VS] * 3 + [HS] * 9, out_specs=(VS,) + (HS,) * 4, input_output_aliases={11: 2},
        scratch_shapes=[vm(6, 4, 4, 128, 128), vm(6, 4, 4, 128, 128), vf(4, 4, 24, 128), vm(768, 768), vm(768, 768),
                        vm(2, 4, 192, 256), vm(2, 4, 192, 256), vm(2, 4, 256, 192), vm(4, 256, 768), vm(768, 3072), vm(3072, 768), vm(3072, 768),
                        vf(2, 384, 768), vm(2, 256, 768), vm(6, 4, 4, 128, 128), *stage_buffers(LEAD_D, ((6,), (128, 128))),
                        vm(2, 4, 4, 4, *bB), vm(4, 4, 4, *bC), vm(2, 4, 4, 4, *bB), vm(4, 4, 4, *bC), *stage_buffers(LEAD_A[:2], ((2,), bB), ((), bC)),
                        DMA, DMA((3, 2, 4)), DMA((4,)), DMA((4,)), DMA((2,)), DMA((2, 2)), DMA((7, 2, 4)), DMA((7, 2, 4)), DMA((6, 2, 5)), DMA((6, 2, 5)),
                        DMA((3, 1, 4)), DMA((3, 1, 4)), DMA((3, 4)), DMA((3, 4)), DMA((3, 4)), DMA((2,))],
        compiler_params=pltpu.CompilerParams(collective_id=3, has_side_effects=True, vmem_limit_bytes=60 << 20),
        name="cross_backward",
    )(do, st, lens, q_h, k_h, v_h, kt_h, memory.reshape(3072, 768), A, GB, GC, GA)


def adam_update(master, first, second, grad, rate):
    first_new = beta_one * first + (1.0 - beta_one) * grad
    second_new = beta_two * second + (1.0 - beta_two) * grad * grad
    fix_one = 1.0 - beta_one**STEP
    fix_two = 1.0 - beta_two**STEP
    master_new = master - rate * (
        first_new / fix_one / (jnp.sqrt(second_new / fix_two) + adam_eps) + decay_rate * master
    )
    return (master_new, first_new, second_new, master_new.astype(jnp.bfloat16))


def ffn_kernel(x1, o2, L2, dy_ref, gains, A, B, C, out, do2, st, dx2, gg, GA, GB, GC,
               W7, WB, WC, gA, gB, gC, sw, sb, sc, tb, tc, ta):
    lA = [pltpu.make_async_copy(A.at[14 + i], W7.at[i], sw.at[i]) for i in range(2)]
    lB = [pltpu.make_async_copy(B.at[i], WB.at[i], sb.at[i]) for i in range(16)]
    lC = [pltpu.make_async_copy(C.at[i], WC.at[i], sc.at[i]) for i in range(8)]
    for c in lA:
        c.start()
    for j in range(8):
        lB[j].start()
        lB[8 + j].start()
        lC[j].start()
    o = o2[...]
    ob = o.astype(BF)
    for c in lA:
        c.wait()
    x = x1[...] + apply_w(ob, W7, 0)
    inv = rms(x)
    h = (x * inv * gains[2:3, :]).astype(BF)
    hT = flip(h.astype(F32)).astype(BF)
    df = dy_ref[...]
    y = jnp.zeros((128, 768), F32)
    dh = jnp.zeros((128, 768), F32)
    c0 = 0.7978845608028654
    sB, sC = [], []
    for j0 in range(0, 8, 2):
        js = range(j0, j0 + 2)
        for j in js:
            lB[j].wait()
            lB[8 + j].wait()
            lC[j].wait()
        a_s = [dot(h, WB[j]) for j in js]
        ups = [dot(h, WB[8 + j]) for j in js]
        dms = [dot(df, WC[j], 1, 1) for j in js]
        mids, dgs, dus = [], [], []
        for a, up, dm in zip(a_s, ups, dms):
            t = jnp.tanh(c0 * (a + 0.044715 * a * a * a))
            half = 0.5 * (1.0 + t)
            gel = a * half
            der = half + 0.5 * a * (1.0 - t * t) * (c0 * (1.0 + 0.134145 * a * a))
            mids.append(gel * up)
            dgs.append((dm * up * der).astype(BF))
            dus.append((dm * gel).astype(BF))
        y += dot(jnp.concatenate([m.astype(BF) for m in mids], axis=1), WC[j0:j0 + 2].reshape(2 * 256, 768))
        for n, j in enumerate(js):
            dh += dot(dgs[n], WB[j], 1, 1) + dot(dus[n], WB[8 + j], 1, 1)
        for n, j in enumerate(js):
            gB[j] = dot(hT, dgs[n]).astype(BF)
            gB[8 + j] = dot(hT, dus[n]).astype(BF)
            gC[j] = dot(flip(mids[n]).astype(BF), df).astype(BF)
        for j in js:
            new = [pltpu.make_async_copy(gB.at[j], GB.at[j], tb.at[j]), pltpu.make_async_copy(gB.at[8 + j], GB.at[8 + j], tb.at[8 + j]),
                   pltpu.make_async_copy(gC.at[j], GC.at[j], tc.at[j])]
            for c in new:
                c.start()
            sB += new
    out[...] = (x + y).astype(BF)
    dz, gain = rms_back(x, inv, gains[2:3, :], dh)
    gg[...] = gain
    d = df.astype(F32) + dz
    dx2[...] = d
    dc = d.astype(BF)
    dof = apply_wt(dc, W7, 0).astype(BF)
    do2[...] = dof
    prod = flip(dof.astype(F32) * o)
    st[0:12, :] = L2[0:12, :]
    for n in range(12):
        st[12 + n:13 + n, :] = jnp.sum(prod[64 * n:64 * n + 64, :], axis=0, keepdims=True)
    oT = flip(o).astype(BF)
    sA = []
    for i in range(2):
        gA[i] = dot(oT, dc[:, 384 * i:384 * i + 384]).astype(BF)
        sA.append(pltpu.make_async_copy(gA.at[i], GA.at[14 + i], ta.at[i]))
        sA[-1].start()
    for c in sA + sB + sC:
        c.wait()

def ffn(x1, o2, L2, dy, gains, A, B, C):
    M = lambda *s: pltpu.VMEM(s, BF)
    D = pltpu.SemaphoreType.DMA
    return pl.pallas_call(
        ffn_kernel,
        out_shape=(SDS((128, 768), BF), SDS((128, 768), BF), SDS((24, 128), F32), SDS((128, 768), F32), SDS((1, 768), F32),
                   SDS((16, 768, 384), BF), SDS((16, 768, 256), BF), SDS((8, 256, 768), BF)),
        in_specs=[VS] * 5 + [HS] * 3, out_specs=(VS,) * 5 + (HS,) * 3,
        scratch_shapes=[M(2, 768, 384), M(16, 768, 256), M(8, 256, 768), M(2, 768, 384), M(16, 768, 256), M(8, 256, 768),
                        D((2,)), D((16,)), D((8,)), D((16,)), D((8,)), D((2,))],
        compiler_params=pltpu.CompilerParams(vmem_limit_bytes=60 << 20),
        name="feed_forward",
    )(x1, o2, L2, dy, gains, A, B, C)

def self_bwd_kernel(dq2, h2, x1, dx2, qkv, o1, L1, x_ref, h1, gains, g3, A, GA_in, gm_in, gin, tile, GA, gm,
                    W, G, gb, gmv, sem, gsem, msem):
    loads = [pltpu.make_async_copy(A.at[i], W.at[i], sem.at[i]) for i in range(10)]
    for i in (8, 9, 6, 7, 0, 1, 2, 3, 4, 5):
        loads[i].start()
    def gm_load(e):
        return pltpu.make_async_copy(gm_in.at[e], gmv.at[e], msem.at[e])
    def gm_store(e):
        return pltpu.make_async_copy(gmv.at[e], gm.at[e], msem.at[16 + e])
    for e in range(16):
        gm_load(e).start()
    stores = []
    def weight_grad(k, left, inc):
        for i in range(2):
            n = 2 * k + i
            G[n] = dot(left, inc[:, 384 * i:384 * i + 384]).astype(BF)
            stores.append(pltpu.make_async_copy(G.at[n], GA.at[n], gsem.at[n]))
            stores[-1].start()
    dqb = dq2[...].astype(BF)
    for i in (8, 9, 6, 7):
        loads[i].wait()
    u = apply_wt(dqb, W, 4)
    x = x1[...]
    inv = rms(x)
    dz, gain = rms_back(x, inv, gains[1:2, :], u)
    gb[...] = jnp.zeros((8, 768), F32)
    gb[1:2, :] = gain
    gb[2:3, :] = g3[...]
    d1 = dx2[...] + dz
    da = d1.astype(BF)
    do1 = apply_wt(da, W, 3).astype(BF)
    weight_grad(4, flip(h2[...].astype(F32)).astype(BF), dqb)
    masks = head_masks(0.125)
    ones = head_masks(1.0)
    live = causal_mask()
    kT = flip(qkv[1].astype(F32)).astype(BF)
    qs, ks, vs = [], [], []
    for g in range(3):
        cols = slice(256 * g, 256 * g + 256)
        q4 = qkv[0, :, cols]
        d4 = do1[:, cols]
        q4s = jnp.concatenate([q4 * m for m in masks], axis=0)
        d4s = jnp.concatenate([d4 * m for m in ones], axis=0)
        sT = dot(qkv[1, :, cols], q4s, 1, 1)
        gT = dot(qkv[2, :, cols], d4s, 1, 1)
        ps, gs = [], []
        for n in range(4):
            s = jnp.where(live, sT[:, 128 * n:128 * n + 128], NEG)
            p = jnp.exp(s - L1[4 * g + n:4 * g + n + 1, :])
            gt = gT[:, 128 * n:128 * n + 128]
            ps.append(p.astype(BF))
            gs.append((p * (gt - jnp.sum(p * gt, axis=0, keepdims=True))).astype(BF))
        sg = jnp.concatenate(gs, axis=1)
        vs.append(dot(jnp.concatenate(ps, axis=1), d4s).astype(BF))
        ks.append(dot(sg, q4s).astype(BF))
        qT = dot(kT[256 * g:256 * g + 256, :], sg)
        qs += [qT[64 * n:64 * n + 64, 128 * n:128 * n + 128] for n in range(4)]
    for e in range(16):
        gm_load(e).wait()
        gm_store(e).start()
    inc = [(0.125 * unflip(jnp.concatenate(qs, axis=0))).astype(BF), jnp.concatenate(ks, axis=1), jnp.concatenate(vs, axis=1)]
    weight_grad(3, flip(o1[...].astype(F32)).astype(BF), da)
    for c in loads[:6]:
        c.wait()
    u = apply_wt(inc[0], W, 0) + apply_wt(inc[1], W, 1) + apply_wt(inc[2], W, 2)
    x = x_ref[...].astype(F32)
    inv = rms(x)
    dz, gain = rms_back(x, inv, gains[0:1, :], u)
    gb[0:1, :] = gain
    gin[...] = d1 + dz
    hT = flip(h1[...].astype(F32)).astype(BF)
    for k in range(3):
        weight_grad(k, hT, inc[k])
    lane = lax.broadcasted_iota(jnp.int32, (8, 128), 1)
    for d in range(8):
        lo, sh = 96 * d // 128, 96 * d % 128
        t = pltpu.roll(gb[:, 128 * lo:128 * lo + 128], (128 - sh) % 128, 1)
        if sh > 32:
            nxt = pltpu.roll(gb[:, 128 * lo + 128:128 * lo + 256], (128 - sh) % 128, 1)
            t = jnp.where(lane < 128 - sh, t, nxt)
        tile[d] = jnp.where(lane < 96, t, 0.0)
    for c in stores:
        c.wait()
    for e in range(16):
        gm_store(e).wait()

def self_bwd(dq2, h2, x1, dx2, qkv, o1, L1, x, h1, gains, g3, A, GA, gm):
    D = pltpu.SemaphoreType.DMA
    return pl.pallas_call(
        self_bwd_kernel,
        out_shape=(SDS((128, 768), F32), SDS((8, 8, 128), F32), SDS((16, 768, 384), BF), SDS((16, 192, 768), F32)),
        in_specs=[VS] * 11 + [HS] * 3, out_specs=(VS, VS, HS, HS),
        input_output_aliases={12: 2},
        scratch_shapes=[pltpu.VMEM((10, 768, 384), BF), pltpu.VMEM((10, 768, 384), BF), pltpu.VMEM((8, 768), F32), pltpu.VMEM((16, 192, 768), F32), D((10,)), D((10,)), D((32,))],
        compiler_params=pltpu.CompilerParams(vmem_limit_bytes=60 << 20),
        name="self_backward",
    )(dq2, h2, x1, dx2, qkv, o1, L1, x, h1, gains, g3, A, GA, gm)

def adam_kernel(*refs):
    ins, outs = refs[:16], refs[16:]
    for n in range(4):
        w, m, v, g = ins[4 * n:4 * n + 4]
        grad = g[0:3, 0:6] if n == 3 else g[...]
        for o, val in zip(outs[4 * n:4 * n + 4], adam_update(w[...], m[...], v[...], grad, rate_gain if n == 3 else rate_matrix)):
            o[...] = val

def adam(*args):
    shapes = []
    for n in range(4):
        s = args[4 * n].shape
        shapes += [SDS(s, F32)] * 3 + [SDS(s, BF)]
    return pl.pallas_call(adam_kernel, out_shape=tuple(shapes), in_specs=[VS] * 16, out_specs=(VS,) * 16,
                          compiler_params=pltpu.CompilerParams(vmem_limit_bytes=60 << 20), name="adam")(*args)


def body(
    dec_input,
    memory,
    mem_len,
    grad_out,
    attn_master,
    ffn_in_master,
    ffn_out_master,
    gain_master,
    attn_first,
    ffn_in_first,
    ffn_out_first,
    gain_first,
    attn_second,
    ffn_in_second,
    ffn_out_second,
    gain_second,
):
    swap = lambda a: a.transpose(1, 0, 2)
    attn_t, in_t = swap(attn_master), swap(ffn_in_master)
    x = dec_input[0]
    (gath_a, gath_b, gath_c, q_all, k_two, v_two, kt_two, gains, lens, h1, qkv, o1, x1, h2, L1, o2, L2) = forward(
        attn_t, in_t, ffn_out_master, info_tile(gain_master, mem_len), x, memory
    )
    aw = gath_a.reshape(16, 768, 384)
    out_block, do2, st, dx2, g3, GA, GB, GC = ffn(x1, o2, L2, grad_out[0], gains, aw, gath_b.reshape(16, 768, 256), gath_c.reshape(8, 256, 768))
    dq2, gm, GA, sum_b, sum_c = cross_bwd(
        do2, st, lens, q_all, k_two, v_two, kt_two, memory, aw,
        GB.reshape(4, 4, 4, 2, 2, 48, 256), GC.reshape(4, 2, 4, 4, 16, 768), GA,
    )
    grad_input, tile_g, GA, grad_memory = self_bwd(dq2, h2, x1, dx2, qkv, o1, L1, x, h1, gains, g3, aw, GA, gm.reshape(16, 192, 768))
    share_a, share_b, share_c, share_g = scatter(GA.reshape(4, 4, 4, 2, 3, 32, 384), sum_b, sum_c, tile_g)
    new = adam(
        attn_t, swap(attn_first), swap(attn_second), share_a,
        in_t, swap(ffn_in_first), swap(ffn_in_second), share_b,
        ffn_out_master, ffn_out_first, ffn_out_second, share_c,
        gain_master, gain_first, gain_second, share_g,
    )
    return (out_block[None], grad_input[None], grad_memory, *[swap(a) for a in new[:8]], *new[8:])


def solution(mesh):
    placed = (
        P(("dp", "seq"), None, None),
        P("dp", "seq", None),
        P(("dp", "seq")),
        P(("dp", "seq"), None, None),
        P(None, ("dp", "seq"), None),
        P(None, ("dp", "seq"), None),
        P(("dp", "seq"), None),
        P(None, ("dp", "seq")),
        P(None, ("dp", "seq"), None),
        P(None, ("dp", "seq"), None),
        P(("dp", "seq"), None),
        P(None, ("dp", "seq")),
        P(None, ("dp", "seq"), None),
        P(None, ("dp", "seq"), None),
        P(("dp", "seq"), None),
        P(None, ("dp", "seq")),
    )
    return jax.shard_map(
        body,
        mesh=mesh,
        in_specs=placed,
        out_specs=(
            P(("dp", "seq"), None, None),
            P(("dp", "seq"), None, None),
            P("dp", "seq", None),
            P(None, ("dp", "seq"), None),
            P(None, ("dp", "seq"), None),
            P(None, ("dp", "seq"), None),
            P(None, ("dp", "seq"), None),
            P(None, ("dp", "seq"), None),
            P(None, ("dp", "seq"), None),
            P(None, ("dp", "seq"), None),
            P(None, ("dp", "seq"), None),
            P(("dp", "seq"), None),
            P(("dp", "seq"), None),
            P(("dp", "seq"), None),
            P(("dp", "seq"), None),
            P(None, ("dp", "seq")),
            P(None, ("dp", "seq")),
            P(None, ("dp", "seq")),
            P(None, ("dp", "seq")),
        ),
        check_vma=False,
    )
```

```python
import jax
import jax.numpy as jnp
from jax import lax
from jax.experimental import pallas as pl
from jax.experimental.pallas import tpu as pltpu
from jax.sharding import PartitionSpec as P

eps_norm = 1e-06
beta_one = 0.9
beta_two = 0.999
adam_eps = 1e-08
decay_rate = 0.01
rate_matrix = 0.12
rate_gain = 3.0
STEP = 10
MESH = pl.DeviceIdType.MESH
BF, F32 = jnp.bfloat16, jnp.float32
ALL = slice(None)
NEG = -1e30
PARTS_A = (("A", 0, "xyz"), ("A", 1, "yzx"), ("A", 2, "zxy"))
PARTS_F = (("B", 0, "z"), ("B", 1, "z"), ("C", 0, "z"))
PARTS_G = (("E", 0, "xy"), ("E", 1, "yx"), ("F", 0, "xy"))
PLANE = ("xy", "yx") * 3
PARTS_D = tuple(("D", n, PLANE[n]) for n in range(6))
AXES = {"A": "xyz", "B": "xyz", "C": "zxy", "D": "xy", "E": "xy", "F": "xy"}
STEPS = (2, -1, 1, 0)
VS = pl.BlockSpec(memory_space=pltpu.VMEM)
HS = pl.BlockSpec(memory_space=pltpu.HBM)
SDS = jax.ShapeDtypeStruct
DMA = pltpu.SemaphoreType.DMA


def vm(*shape):
    return pltpu.VMEM(shape, BF)


def vf(*shape):
    return pltpu.VMEM(shape, F32)


def where_am_i():
    dp, sq = lax.axis_index("dp"), lax.axis_index("seq")
    return {"x": sq // 4, "y": sq % 4, "z": dp // 2, "c": dp % 2}


def dev(at):
    return (at["z"] * 2 + at["c"], at["x"] * 4 + at["y"])


def moved(at, axis, step):
    return {**at, axis: (at[axis] + step + 4) % 4}


def offset(me, j, sign=1):
    return {**me, "x": (me["x"] + sign * (j // 4) + 4) % 4, "y": (me["y"] + sign * (j % 4) + 4) % 4}


def sibling_of(me):
    return {**me, "c": 1 - me["c"]}


def remote(src, dst, send, recv, to):
    return pltpu.make_async_remote_copy(src, dst, send, recv, device_id=dev(to), device_id_type=MESH)


def meet(me, column):
    dp, sq = lax.axis_index("dp"), lax.axis_index("seq")
    bar = pltpu.get_barrier_semaphore()
    for i in range(1, 16):
        pl.semaphore_signal(bar, inc=1, device_id=(dp, (sq + i) % 16), device_id_type=MESH)
    if column == "dp":
        for i in range(1, 8):
            pl.semaphore_signal(bar, inc=1, device_id=((dp + i) % 8, sq), device_id_type=MESH)
        return bar, 22
    if column == "z":
        for to in (moved(me, "z", 1), moved(me, "z", -1), sibling_of(me)):
            pl.semaphore_signal(bar, inc=1, device_id=dev(to), device_id_type=MESH)
        return bar, 18
    return bar, 15


def dot(a, b, ca=1, cb=0):
    return lax.dot_general(a, b, (((ca,), (cb,)), ((), ())), preferred_element_type=F32)


class Gather:
    def __init__(self, me, orders, view, own, ss, rs, sib_s=None, sib_r=None, whole=""):
        self.me, self.orders, self.view, self.own, self.whole = me, orders, view, own, whole
        self.ss, self.rs, self.sib_s, self.sib_r = ss, rs, sib_s, sib_r
        self.count, self.last = len(orders), len(orders[0]) - 1

    def group(self, n, t, step, half=None):
        axes = self.whole + self.orders[n][:t]
        at = {**moved(self.me, self.orders[n][t], step), **{a: ALL for a in axes}}
        if half is not None and axes:
            at[axes[0]] = pl.ds(2 * half, 2)
        return at

    def kinds(self, t):
        return (0, 1, 2, 3) if t == self.last else (0, 1, 2)

    def copy(self, n, t, kind, back=0):
        straight = kind < 2 or t < self.last
        step = (1, -1, 2 if straight else 1, -1)[kind]
        dst = self.view(n, self.group(n, t, back) if straight else self.group(n, t, back - step, kind - 2))
        src = self.own(n) if self.own and t == 0 and straight and back == 0 else dst
        return remote(src, dst, self.ss.at[n, t, kind], self.rs.at[n, t, kind], moved(self.me, self.orders[n][t], step))

    def arrived(self, n, t, kind):
        self.copy(n, t, kind, (-1, 1, -2 if t < self.last else -1, 1)[kind]).wait_recv()

    def sibling(self, n, j, c):
        v = self.view(n, {**self.group(n, self.last, (0, -1, 1, 2)[j]), "c": c})
        return remote(v, v, self.sib_s.at[n, j], self.sib_r.at[n, j], sibling_of(self.me))

    def send(self, t, ns=None):
        for n in ns or range(self.count):
            if t:
                for k in range(3):
                    self.arrived(n, t - 1, k)
            for k in (0, 1) if t == self.last else (2, 0, 1):
                self.copy(n, t, k).start()
            if self.sib_s is not None and t == self.last:
                self.sibling(n, 0, self.me["c"]).start()

    def forward(self, ns=None):
        for n in ns or range(self.count):
            for k in (0, 1):
                self.arrived(n, self.last, k)
                self.copy(n, self.last, 2 + k).start()
                if self.sib_s is not None:
                    self.sibling(n, 1 + k, self.me["c"]).start()

    def finish(self, ns=None):
        for n in ns or range(self.count):
            for k in (2, 3):
                self.arrived(n, self.last, k)
            if self.sib_s is not None:
                self.sibling(n, 3, self.me["c"]).start()

    def siblings_in(self):
        for n in range(self.count):
            for j in range(4):
                self.sibling(n, j, 1 - self.me["c"]).wait_recv()

    def drain(self):
        for n in range(self.count):
            for t in range(self.last + 1):
                for k in self.kinds(t):
                    self.copy(n, t, k).wait_send()
            if self.sib_s is not None:
                for j in range(4):
                    self.sibling(n, j, self.me["c"]).wait_send()


class Scatter:
    def __init__(self, me, parts, acc, hop, fin, ss, rs, sib=None, source=None, sib_s=None, sib_r=None, loc_s=None, whole=""):
        self.whole = whole
        self.me, self.parts, self.acc, self.hop_b, self.fin_b = me, parts, acc, hop, fin
        self.ss, self.rs, self.sib, self.source = ss, rs, sib, source
        self.sib_s, self.sib_r, self.loc_s = sib_s, sib_r, loc_s
        self.count, self.last = len(parts), len(parts[0][2]) - 1

    def idx(self, n, at):
        name, p, _ = self.parts[n]
        place = tuple(at[a] for a in AXES[name])
        return place if name in "CF" else (p,) + place

    def slot(self, n):
        name, p, _ = self.parts[n]
        return () if name in "CF" else (p,)

    def done(self, n, t):
        name, _, order = self.parts[n]
        return [a for a in AXES[name] if a in self.whole + order[:t]]

    def group(self, n, t, step, half=None):
        axes = self.done(n, t)
        at = {**moved(self.me, self.parts[n][2][t], step), **{a: ALL for a in axes}}
        if half is not None and axes:
            at[axes[0]] = pl.ds(2 * half, 2)
        return at

    def fins(self, t):
        return 2 if t == self.last else 3

    def refs(self, n, t):
        name = self.parts[n][0]
        return self.acc[name], self.hop_b[name] if t == self.last else None, self.fin_b[t][name]

    def hop_copy(self, n, kind):
        step, t = 1 if kind == 0 else -1, self.last
        a, h, _ = self.refs(n, t)
        return remote(a.at[self.idx(n, self.group(n, t, 2 * step, kind))], h.at[self.slot(n) + (kind,)],
                      self.ss.at[n, t, kind], self.rs.at[n, t, kind], moved(self.me, self.parts[n][2][t], step))

    def fin_copy(self, n, t, kind):
        step = (1, -1, 2)[kind]
        a, _, f = self.refs(n, t)
        return remote(a.at[self.idx(n, self.group(n, t, step))], f.at[self.slot(n) + (kind,)],
                      self.ss.at[n, t, 2 + kind], self.rs.at[n, t, 2 + kind], moved(self.me, self.parts[n][2][t], step))

    def each(self, n, t, at, fn, half=None):
        axes = self.done(n, t)
        sizes, offs = [4] * len(axes), [0] * len(axes)
        if half is not None and axes:
            sizes[0], offs[0] = 2, 2 * half
        total = 1
        for s in sizes:
            total *= s

        def one(i):
            pos, rest = [], i
            for s in sizes[::-1]:
                pos.append(rest % s)
                rest = rest // s
            pos = pos[::-1]
            where = dict(at)
            for a, p, o in zip(axes, pos, offs):
                where[a] = p + o
            fn(self.idx(n, where), tuple(pos))

        if total == 1:
            one(0)
        else:
            pl.loop(0, total, unroll=4)(one)

    def sib_copy(self, n, j):
        at = self.group(n, self.last, STEPS[j])
        return remote(self.source(n, at, 1 - self.me["c"]), self.sib[self.parts[n][0]].at[self.idx(n, at)],
                      self.sib_s.at[n, j], self.sib_r.at[n, j], sibling_of(self.me))

    def loc_copy(self, n, j):
        at = self.group(n, self.last, STEPS[j])
        return pltpu.make_async_copy(self.source(n, at, self.me["c"]), self.acc[self.parts[n][0]].at[self.idx(n, at)], self.loc_s.at[n, j])

    def start(self):
        for j in range(4):
            for n in range(self.count):
                self.sib_copy(n, j).start()
                self.loc_copy(n, j).start()

    def merge(self, j):
        for n in range(self.count):
            self.sib_copy(n, j).wait_recv()
            self.loc_copy(n, j).wait()
            a, b = self.acc[self.parts[n][0]], self.sib[self.parts[n][0]]

            def fn(i, _):
                a[i] = a[i] + b[i]

            self.each(n, self.last, self.group(n, self.last, STEPS[j]), fn)

    def send(self, t, ns=None):
        for n in ns or range(self.count):
            if t == self.last:
                for k in (0, 1):
                    self.hop_copy(n, k).start()
            else:
                for k in (2, 0, 1):
                    self.fin_copy(n, t, k).start()

    def forward(self, ns=None):
        t = self.last
        for n in ns or range(self.count):
            a, h, _ = self.refs(n, t)
            for k in (0, 1):
                self.hop_copy(n, k).wait_recv()

                def fn(i, pos):
                    a[i] = a[i] + h[self.slot(n) + (k,) + pos]

                self.each(n, t, self.group(n, t, 1 if k == 0 else -1), fn, k)
                self.fin_copy(n, t, k).start()

    def close(self, t, ns=None):
        for n in ns or range(self.count):
            for k in range(self.fins(t)):
                self.fin_copy(n, t, k).wait_recv()
            a, _, f = self.refs(n, t)

            def fn(i, pos):
                v = a[i].astype(F32)
                for k in range(self.fins(t)):
                    v = v + f[self.slot(n) + (k,) + pos].astype(F32)
                a[i] = v.astype(BF)

            self.each(n, t, self.group(n, t, 0), fn)

    def result(self, n):
        a, _, f = self.refs(n, 0)
        v = a[self.idx(n, self.me)].astype(F32)
        for k in range(3):
            self.fin_copy(n, 0, k).wait_recv()
            v = v + f[self.slot(n) + (k,)].astype(F32)
        return v

    def drain(self):
        for n in range(self.count):
            if self.sib is not None:
                for j in range(4):
                    self.sib_copy(n, j).wait_send()
            for k in (0, 1):
                self.hop_copy(n, k).wait_send()
            for t in range(self.last + 1):
                for k in range(self.fins(t)):
                    self.fin_copy(n, t, k).wait_send()


LEAD_A = ((2, 2, 4), (2, 4, 4), (3, 4), (3,))
LEAD_D = ((2, 2), (2, 4), (3,))


def stage_buffers(leads, *shapes):
    return [vm(*pre, *lead, *block) for lead in leads for pre, block in shapes]


def staged(names, refs):
    k = len(names)
    got = [dict(zip(names, refs[k * i:k * i + k])) for i in range(len(refs) // k)]
    return got[0], {len(got) - 2 - i: g for i, g in enumerate(got[1:])}


def ffn_place(B, C):
    def place(n, at):
        if n < 2:
            return B.at[at["x"], at["y"], at["z"], at["c"], n]
        return C.at[at["z"], at["c"], at["x"], at["y"]]
    return place


def scatter_kernel(GA, sumE, sumF, gg, oA, oB, oC, oG, accA, sibA, h2, f2, f1, f0,
                   accE, accF, hE1, hF1, fE1, fF1, fE0, fF0, blk, stage, recv, gdp, gsum,
                   ss, rs, sib_s, sib_r, loc_s, as_, ar_, ds_, dr_, es, er, ld_s):
    me = where_am_i()
    dp, sq = lax.axis_index("dp"), lax.axis_index("seq")
    bar, count = meet(me, "dp")
    loads = [pltpu.make_async_copy(a, b, ld_s.at[i]) for i, (a, b) in enumerate(((sumE, accE), (sumF, accF)))]
    for c in loads:
        c.start()
    pl.semaphore_wait(bar, count)
    hop, fin = staged("A", (h2, f2, f1, f0))
    ring = Scatter(me, PARTS_A, {"A": accA}, hop, fin, ss, rs, {"A": sibA},
                   lambda n, at, c: GA.at[at["x"], at["y"], at["z"], c, n], sib_s, sib_r, loc_s)
    fhop, ffin = staged("EF", (hE1, hF1, fE1, fF1, fE0, fF0))
    ring_f = Scatter(me, PARTS_G, {"E": accE, "F": accF}, fhop, ffin, es, er)
    ring.start()
    for c in loads:
        c.wait()
    ring_f.send(1)

    def dpx(i):
        peer = (dp + i) % 8
        return pltpu.make_async_remote_copy(gg.at[peer], gdp.at[dp], ds_.at[i], dr_.at[i], device_id=(peer, sq), device_id_type=MESH)

    for i in range(1, 8):
        dpx(i).start()
    gdp[dp] = gg[dp]
    ring.merge(0)
    ring.send(2)
    ring.merge(1)
    ring.merge(2)
    ring_f.forward()
    ring.forward()
    ring.merge(3)
    ring_f.close(1)
    ring_f.send(0)
    for i in range(1, 8):
        dpx(i).wait_recv()
    gsum[...] = jnp.sum(gdp[...], axis=0)

    stage[:, 6:8, :] = jnp.zeros((16, 2, 768), F32)
    ring.close(2)
    ring.send(1)
    for n in range(2):
        blk[48 * n:48 * n + 48, 384:640] = ring_f.result(n)
    oC[...] = ring_f.result(2)
    ring.close(1)
    ring.send(0)
    for n in range(3):
        blk[32 * n:32 * n + 32, 0:384] = ring.result(n)
    for k in range(16):
        stage[k, 0:6, 0:640] = blk[6 * k:6 * k + 6, :]
        stage[k, :, 640:768] = gsum[...]

    def a2a(i):
        peer = (sq + i) % 16
        return pltpu.make_async_remote_copy(stage.at[peer], recv.at[sq], as_.at[i], ar_.at[i], device_id=(dp, peer), device_id_type=MESH)

    for i in range(1, 16):
        a2a(i).start()
    recv[sq] = stage[sq]
    for i in range(1, 16):
        a2a(i).wait_recv()
    oG[...] = pltpu.roll(jnp.sum(recv[:, :, 640:768], axis=0), (128 - 6 * sq) % 128, 1)
    for s in range(16):
        oA[:, s // 2, 384 * (s % 2):384 * (s % 2) + 384] = recv[s, 0:6, 0:384]
        oB[:, s // 8, 256 * (s % 8):256 * (s % 8) + 256] = recv[s, 0:6, 384:640]
    for i in range(1, 8):
        dpx(i).wait_send()
    for i in range(1, 16):
        a2a(i).wait_send()
    ring.drain()
    ring_f.drain()


def scatter(GA, sumE, sumF, gg):
    return pl.pallas_call(
        scatter_kernel,
        out_shape=(SDS((6, 8, 768), F32), SDS((6, 2, 2048), F32), SDS((16, 768), F32), SDS((8, 128), F32)),
        in_specs=[HS, HS, HS, VS], out_specs=(VS,) * 4,
        scratch_shapes=[vm(3, 4, 4, 4, 32, 384), vm(3, 4, 4, 4, 32, 384), *stage_buffers(LEAD_A, ((3,), (32, 384))),
                        vm(2, 4, 4, 48, 256), vm(4, 4, 16, 768), *stage_buffers(LEAD_D, ((2,), (48, 256)), ((), (16, 768))),
                        vf(96, 640), vf(16, 8, 768), vf(16, 8, 768), vf(8, 8, 128), vf(8, 128),
                        DMA((3, 3, 5)), DMA((3, 3, 5)), DMA((3, 4)), DMA((3, 4)), DMA((3, 4)),
                        DMA((16,)), DMA((16,)), DMA((8,)), DMA((8,)), DMA((3, 2, 5)), DMA((3, 2, 5)), DMA((2,))],
        compiler_params=pltpu.CompilerParams(collective_id=1, has_side_effects=True, vmem_limit_bytes=60 << 20),
        name="scatter_attention_grads",
    )(GA, sumE, sumF, gg)


def head_masks(value=1.0):
    lane = lax.broadcasted_iota(jnp.int32, (1, 256), 1)
    return [jnp.where(lane // 64 == h, value, 0.0).astype(BF) for h in range(4)]


def stack_heads(block, masks):
    return jnp.concatenate([block * m for m in masks], axis=0)


def key_positions():
    sq = lax.axis_index("seq")
    return (192 * sq + lax.broadcasted_iota(jnp.int32, (192, 128), 0)).astype(F32)


class Merge:
    def __init__(self, me, src, mid, one, two, ss, rs):
        self.me, self.src, self.mid, self.bufs, self.ss, self.rs = me, src, mid, (one, two), ss, rs

    def block(self, n, a, b):
        return (n, a, b) if n % 2 == 0 else (n, b, a)

    def copy(self, n, t, k):
        axis = PLANE[n][t]
        to = moved(self.me, axis, (1, -1, 2)[k])
        src = self.src.at[self.block(n, to[axis], ALL)] if t == 0 else self.mid.at[n, to[axis]]
        return remote(src, self.bufs[t].at[n, k], self.ss.at[n, t, k], self.rs.at[n, t, k], to)

    def send(self, t, ns):
        for n in ns:
            for k in (2, 0, 1):
                self.copy(n, t, k).start()

    def join(self, blocks):
        rows = [b[128:144, :].astype(F32)[0:8, :] for b in blocks]
        logs = [r + pltpu.roll(r, 6, 0) + pltpu.roll(r, 4, 0) for r in rows]
        top = logs[0]
        for l in logs[1:]:
            top = jnp.maximum(top, l)
        ws = [jnp.exp(l - top) for l in logs]
        total = ws[0] + ws[1] + ws[2] + ws[3]
        inv = 1.0 / total
        out = []
        for h in range(2):
            o = sum(b[64 * h:64 * h + 64, :].astype(F32) * (w * inv)[h:h + 1, :] for b, w in zip(blocks, ws))
            out.append(o)
        return jnp.concatenate(out, axis=0), top + jnp.log(total)

    def middle(self, ns):
        for n in ns:
            for k in range(3):
                self.copy(n, 0, k).wait_recv()
            a = self.me[PLANE[n][0]]

            for b in range(4):
                o, l = self.join([self.src.at[self.block(n, a, b)]] + [self.bufs[0].at[n, k, b] for k in range(3)])
                self.mid[n, b, 0:128, :] = o.astype(BF)
                self.mid[n, b, 128:144, :] = log_tile(l)

    def result(self, n):
        for k in range(3):
            self.copy(n, 1, k).wait_recv()
        return self.join([self.mid.at[n, self.me[PLANE[n][1]]]] + [self.bufs[1].at[n, k] for k in range(3)])

    def drain(self):
        for n in range(6):
            for t in range(2):
                for k in range(3):
                    self.copy(n, t, k).wait_send()


def log_tile(l):
    l = jnp.where(lax.broadcasted_iota(jnp.int32, (8, 128), 0) < 2, l, 0.0)
    high = l.astype(BF).astype(F32)
    middle = (l - high).astype(BF).astype(F32)
    low = l - high - middle
    return jnp.concatenate([high + pltpu.roll(middle, 2, 0) + pltpu.roll(low, 4, 0), jnp.zeros((8, 128), F32)], axis=0).astype(BF)


def pair_of(ref, g, at):
    return jnp.concatenate([ref[2 * g, at["x"], at["y"]], ref[2 * g + 1, at["x"], at["y"]]], axis=1)


def rms(x):
    return lax.rsqrt(jnp.mean(x * x, axis=-1, keepdims=True) + eps_norm)

def rms_back(x, inv, gain, u):
    scaled = u * gain
    inner = jnp.mean(scaled * x, axis=-1, keepdims=True)
    return inv * scaled - x * inv * inv * inv * inner, jnp.sum(u * x * inv, axis=0, keepdims=True)

def flip(x):
    return jnp.concatenate([x[:, 128 * i:128 * i + 128].T for i in range(x.shape[1] // 128)], axis=0)

def unflip(x):
    return jnp.concatenate([x[128 * i:128 * i + 128, :].T for i in range(x.shape[0] // 128)], axis=1)

def apply_w(h, W, k):
    return jnp.concatenate([dot(h, W[2 * k]), dot(h, W[2 * k + 1])], axis=1)

def apply_wt(u, W, k):
    return dot(u[:, 0:384], W[2 * k], 1, 1) + dot(u[:, 384:768], W[2 * k + 1], 1, 1)

def causal_mask():
    return lax.broadcasted_iota(jnp.int32, (128, 128), 0) <= lax.broadcasted_iota(jnp.int32, (128, 128), 1)


class Stacked:
    def __init__(self, ref):
        self.ref = ref

    def __getitem__(self, n):
        return self.ref[n].reshape(768, 384)


def self_attention(x_ref, gains, W, loads, q2, h1, qkv, o1, x1, h2, L1):
    x = x_ref[...].astype(F32)
    h = (x * rms(x) * gains[0:1, :]).astype(BF)
    h1[...] = h
    for k in range(3):
        loads[2 * k].wait()
        loads[2 * k + 1].wait()
        full = apply_w(h, W, k)
        qkv[k] = full.astype(BF)
    vT = flip(full).astype(BF)
    masks = head_masks(0.125)
    live = causal_mask()
    outs = []
    for g in range(3):
        cols = slice(256 * g, 256 * g + 256)
        q4 = qkv[0, :, cols]
        sT = dot(qkv[1, :, cols], jnp.concatenate([q4 * m for m in masks], axis=0), 1, 1)
        ps = []
        for n in range(4):
            s = jnp.where(live, sT[:, 128 * n:128 * n + 128], NEG)
            top = jnp.max(s, axis=0, keepdims=True)
            lse = top + jnp.log(jnp.sum(jnp.exp(s - top), axis=0, keepdims=True))
            L1[4 * g + n:4 * g + n + 1, :] = lse
            ps.append(jnp.exp(s - lse).astype(BF))
        oT = dot(vT[256 * g:256 * g + 256, :], jnp.concatenate(ps, axis=1))
        outs += [oT[64 * n:64 * n + 64, 128 * n:128 * n + 128] for n in range(4)]
    o = unflip(jnp.concatenate(outs, axis=0)).astype(BF)
    o1[...] = o
    for c in loads[6:10]:
        c.wait()
    x = x + apply_w(o, W, 3)
    x1[...] = x
    h = (x * rms(x) * gains[1:2, :]).astype(BF)
    h2[...] = h
    q2[...] = apply_w(h, W, 4).astype(BF) * jnp.asarray(0.125, BF)


def forward_kernel(attn, wi, wo, gain, length, x_ref, mem_h, A, B, C, q_h, k_h, v_h, kt_h, gains, lens, h1, qkv, o1, x1, h2, L1, o_ref, L_ref,
                   infos, info, stage, recv, blk, blkA, blkB, blkC, W, q2,
                   qall, mem, wk, wv, wkT, wvT, K, V, KT, VT, ost, mid, one, two, lrow,
                   fs, fr, ss, rs, sib_s, sib_r, as_, ar_, ds_, dr_, own_s, zs, zr, zsib_s, zsib_r,
                   load_s, mem_s, out_s, ps_, pr_, os_, or_):
    me = where_am_i()
    dp, sq = lax.axis_index("dp"), lax.axis_index("seq")
    bar, count = meet(me, "dp")

    def load_mem(e):
        return pltpu.make_async_copy(mem_h.at[e], mem.at[e], mem_s.at[e])

    @pl.loop(0, 16)
    def _(e):
        load_mem(e).start()

    lrow[...] = jnp.zeros((4, 2, 8, 128), F32)
    info[...] = jnp.zeros((8, 128), F32)
    info[0:3, 0:6] = gain[...].astype(BF).astype(F32)
    spot = (lax.broadcasted_iota(jnp.int32, (8, 128), 0) == 3) & (lax.broadcasted_iota(jnp.int32, (8, 128), 1) == sq)
    info[...] = pltpu.roll(info[...], 6 * sq, 1) + jnp.where(spot, length[...].astype(F32), 0.0)
    stage[:, 6:8, :] = jnp.zeros((16, 2, 768), F32)
    for s in range(16):
        stage[s, 0:6, 0:384] = attn[:, s // 2, 384 * (s % 2):384 * (s % 2) + 384]
        stage[s, :, 640:768] = info[...]
        stage[s, 0:6, 384:640] = wi[:, s // 8, 256 * (s % 8):256 * (s % 8) + 256]
    pl.semaphore_wait(bar, count)

    def a2a(i):
        peer = (sq + i) % 16
        return pltpu.make_async_remote_copy(stage.at[peer], recv.at[sq], as_.at[i], ar_.at[i], device_id=(dp, peer), device_id_type=MESH)

    for i in range(1, 16):
        a2a(i).start()
    recv[sq] = stage[sq]
    blkC[...] = wo[...].astype(BF)
    for i in range(1, 16):
        a2a(i).wait_recv()
    for k in range(16):
        blk[6 * k:6 * k + 6, :] = recv[k, 0:6, 0:640]
    for p in range(3):
        blkA[p] = blk[32 * p:32 * p + 32, 0:384].astype(BF)
    for p in range(2):
        blkB[p] = blk[48 * p:48 * p + 48, 384:640].astype(BF)
    place = lambda n, at: A.at[at["x"], at["y"], at["z"], at["c"], PARTS_A[n][1]]
    ring = Gather(me, [p[2] for p in PARTS_A], place, lambda n: blkA.at[n], ss, rs, sib_s, sib_r)
    place_f = ffn_place(B, C)
    mine = lambda n: blkB.at[n] if n < 2 else blkC
    ring_f = Gather(me, [p[2] for p in PARTS_G], place_f, mine, fs, fr)
    owns = [pltpu.make_async_copy(blkA.at[n], place(n, me), own_s.at[n]) for n in range(3)]
    owns += [pltpu.make_async_copy(mine(n), place_f(n, me), own_s.at[3 + n]) for n in range(3)]
    for o in owns:
        o.start()
    ring.send(0)
    ring_f.send(0)
    for o in owns:
        o.wait()
    ring.send(1)
    ring_f.send(1)
    ring.send(2)
    ring_f.forward()
    tile = jnp.sum(recv[:, :, 640:768], axis=0)
    infos[dp] = tile

    def dpx(i, back=0):
        v = infos.at[(dp - back + 8) % 8]
        return pltpu.make_async_remote_copy(v, v, ds_.at[i], dr_.at[i], device_id=((dp + i) % 8, sq), device_id_type=MESH)

    for i in range(1, 8):
        dpx(i).start()
    ring.forward()
    for i in range(1, 8):
        dpx(i, i).wait_recv()
    lane = lax.broadcasted_iota(jnp.int32, (8, 128), 1)
    gains[...] = jnp.zeros((8, 768), F32)
    for d in range(8):
        lo, sh = 96 * d // 128, 96 * d % 128
        t = pltpu.roll(jnp.where(lane < 96, infos[d], 0.0), sh, 1)
        gains[:, 128 * lo:128 * lo + 128] += jnp.where(lane >= sh, t, 0.0)
        if sh > 32:
            gains[:, 128 * lo + 128:128 * lo + 256] += jnp.where(lane < sh, t, 0.0)
    pick = lax.broadcasted_iota(jnp.int32, (16, 128), 0) == lax.broadcasted_iota(jnp.int32, (16, 128), 1)
    lens[...] = jnp.broadcast_to(jnp.sum(jnp.where(pick, tile[3:4, :], 0.0), axis=1, keepdims=True), (16, 128))
    ring_f.finish()
    ring_z = Gather(me, ("z",) * 3, place_f, None, zs, zr, zsib_s, zsib_r, "xy")
    ring.finish()
    ring.siblings_in()
    block = lambda n: A.at[n // 4, n % 4]
    loads = [pltpu.make_async_copy(block(n), W.at[n], load_s.at[n]) for n in range(10)]
    loads += [pltpu.make_async_copy(block(10 + n), (wk if n < 2 else wv).at[:, :, :, :, pl.ds(384 * (n % 2), 384)], load_s.at[10 + n]) for n in range(4)]
    for c in loads:
        c.start()
    self_attention(x_ref, gains, Stacked(W), loads, q2, h1, qkv, o1, x1, h2, L1)
    for n in range(6):
        qall[n, me["x"], me["y"]] = q2[:, 128 * n:128 * n + 128]
    view = lambda n, at: qall.at[n, at["x"], at["y"]]
    plane = Gather(me, PLANE, view, lambda n: view(n, me), ps_, pr_)
    fold = Merge(me, ost, mid, one, two, os_, or_)
    plane.send(0)
    ring_z.send(0)
    for c in loads[10:]:
        c.wait()
    flat = lambda ref: ref[...].reshape(768, 768)
    for i in range(6):
        wvT[:, 128 * i:128 * i + 128] = flat(wv)[128 * i:128 * i + 128, :].T

    def project(a, b):
        @pl.loop(a // 2, b // 2)
        def _(i):
            for e in (2 * i, 2 * i + 1):
                load_mem(e).wait()
            K[pl.ds(2 * i, 2)] = dot(mem[pl.ds(2 * i, 2)].reshape(384, 768), flat(wk)).astype(BF).reshape(2, 192, 768)
            for e in (2 * i, 2 * i + 1):
                VT[e] = dot(wvT[...], mem[e], 1, 1).astype(BF)

    def project_more(a, b):
        @pl.loop(a // 2, b // 2)
        def _(i):
            V[pl.ds(2 * i, 2)] = dot(mem[pl.ds(2 * i, 2)].reshape(384, 768), flat(wv)).astype(BF).reshape(2, 192, 768)
            for e in (2 * i, 2 * i + 1):
                KT[e] = dot(wkT[...], mem[e], 1, 1).astype(BF)

    plane.send(1, (0, 1))
    project(0, 4)
    plane.send(1, (2, 3))
    plane.send(1, (4, 5))
    project(4, 10)
    plane.forward((0, 1))
    plane.forward((2, 3))
    project(10, 16)
    plane.forward((4, 5))
    masks = head_masks()
    pos = key_positions()

    def attend(g):
        cols = slice(256 * g, 256 * g + 256)

        @pl.loop(0, 4)
        def _(i):
            four = [(x, x * 4 + y, {"x": x, "y": y}) for x, y in [(i, y) for y in range(4)]]
            sT = [dot(K[e, :, cols], stack_heads(pair_of(qall, g, at), masks), 1, 1) for _, e, at in four]
            pT, inv = [], []
            for u, (_, e, at) in enumerate(four):
                live = pos < lens[pl.ds(e, 1), :]
                ps = []
                for h in range(4):
                    s = jnp.where(live, sT[u][:, 128 * h:128 * h + 128], NEG)
                    top = jnp.max(s, axis=0, keepdims=True)
                    p = jnp.exp(s - top)
                    tot = jnp.sum(p, axis=0, keepdims=True)
                    lrow[u, h // 2, h % 2:h % 2 + 1, :] = top + jnp.log(tot)
                    ps.append(p.astype(BF))
                    inv.append(1.0 / tot)
                pT.append(jnp.concatenate(ps, axis=1))
            oT = [dot(VT[e, cols, :], p) for (_, e, _), p in zip(four, pT)]
            for u, (_, e, at) in enumerate(four):
                for h in range(4):
                    ost[2 * g + h // 2, at["x"], at["y"], 64 * (h % 2):64 * (h % 2) + 64, :] = (
                        oT[u][64 * h:64 * h + 64, 128 * h:128 * h + 128] * inv[4 * u + h]).astype(BF)
                for h in range(2):
                    ost[2 * g + h, at["x"], at["y"], 128:144, :] = log_tile(lrow[u, h])

        fold.send(0, (2 * g, 2 * g + 1))

    def deliver(g):
        for n in (2 * g, 2 * g + 1):
            o, l = fold.result(n)
            o_ref[:, 128 * n:128 * n + 128] = o.T
            L_ref[2 * n:2 * n + 2, :] = l[0:2, :]

    plane.finish((0, 1))
    attend(0)
    plane.finish((2, 3))
    attend(1)
    fold.middle((0, 1))
    fold.send(1, (0, 1))
    plane.finish((4, 5))
    out_q = pltpu.make_async_copy(qall, q_h, out_s.at[0])
    out_k = pltpu.make_async_copy(K, k_h, out_s.at[1])
    out_q.start()
    out_k.start()
    ring_z.forward()
    attend(2)
    fold.middle((2, 3))
    fold.send(1, (2, 3))
    for i in range(6):
        wkT[:, 128 * i:128 * i + 128] = flat(wk)[128 * i:128 * i + 128, :].T
    project_more(0, 8)
    fold.middle((4, 5))
    fold.send(1, (4, 5))
    low, high = pl.ds(0, 8), pl.ds(8, 8)
    outs = [pltpu.make_async_copy(a.at[k], b.at[k], out_s.at[2 + 2 * i + j])
            for j, k in enumerate((low, high)) for i, (a, b) in enumerate(((V, v_h), (KT, kt_h)))]
    for c in outs[:2]:
        c.start()
    ring_z.finish()
    project_more(8, 16)
    for c in outs[2:]:
        c.start()
    L_ref[12:16, :] = jnp.zeros((4, 128), F32)
    for g in range(3):
        deliver(g)
    plane.drain()
    fold.drain()
    for c in [out_q, out_k] + outs:
        c.wait()
    ring_z.siblings_in()
    ring_z.drain()
    ring_f.drain()
    ring.drain()
    for i in range(1, 16):
        a2a(i).wait_send()
    for i in range(1, 8):
        dpx(i).wait_send()


def forward(attn, wi, wo, gain, length, x, memory):
    row = SDS((128, 768), BF)
    rowf = SDS((128, 768), F32)
    log = SDS((16, 128), F32)
    return pl.pallas_call(
        forward_kernel,
        out_shape=(SDS((4, 4, 4, 2, 3, 32, 384), BF), SDS((4, 4, 4, 2, 2, 48, 256), BF), SDS((4, 2, 4, 4, 16, 768), BF),
                   SDS((6, 4, 4, 128, 128), BF), SDS((16, 192, 768), BF), SDS((16, 192, 768), BF), SDS((16, 768, 192), BF),
                   SDS((8, 768), F32), log, row, SDS((3, 128, 768), BF), row, rowf, row, log, rowf, log),
        in_specs=[VS] * 6 + [HS], out_specs=(HS,) * 7 + (VS,) * 10,
        scratch_shapes=[vf(8, 8, 128), vf(8, 128), vf(16, 8, 768), vf(16, 8, 768), vf(96, 640), vm(3, 32, 384), vm(2, 48, 256), vm(16, 768),
                        vm(10, 4, 2, 3, 32, 384), vm(128, 768),
                        vm(6, 4, 4, 128, 128), vm(16, 192, 768), vm(4, 2, 3, 32, 768), vm(4, 2, 3, 32, 768), vm(768, 768), vm(768, 768),
                        vm(16, 192, 768), vm(16, 192, 768), vm(16, 768, 192), vm(16, 768, 192),
                        vm(6, 4, 4, 144, 128), vm(6, 4, 144, 128), vm(6, 3, 4, 144, 128), vm(6, 3, 144, 128), vf(4, 2, 8, 128),
                        DMA((3, 2, 4)), DMA((3, 2, 4)), DMA((3, 3, 4)), DMA((3, 3, 4)), DMA((3, 4)), DMA((3, 4)), DMA((16,)), DMA((16,)), DMA((8,)), DMA((8,)), DMA((6,)),
                        DMA((3, 1, 4)), DMA((3, 1, 4)), DMA((3, 4)), DMA((3, 4)),
                        DMA((14,)), DMA((16,)), DMA((6,)), DMA((6, 2, 4)), DMA((6, 2, 4)), DMA((6, 2, 3)), DMA((6, 2, 3))],
        compiler_params=pltpu.CompilerParams(collective_id=0, has_side_effects=True, vmem_limit_bytes=60 << 20),
        name="forward_attention",
    )(attn, wi, wo, gain, length, x, memory)


def cross_bwd_kernel(do, st, lens, q_h, k_h, v_h, kt_h, mem_h, A, GB, GC, G_in, dq_ref, gm_h, dw_h, sumE, sumF,
                     qall, doall, stall, wk, wv, K, V, KT, mem, memT, dK, dV, gst, wst, dst, dh1, df1, df0,
                     accB, accC, sibB, sibC, hB2, hC2, fB2, fC2,
                     q_s, kv_s, mem_s, w_s, gm_s, dw_s, ss, rs, ds_, dr_, fs, fr, fsib_s, fsib_r, floc, sum_s):
    me = where_am_i()
    bar, count = meet(me, "z")

    def load_mem(e):
        return pltpu.make_async_copy(mem_h.at[pl.ds(pl.multiple_of(256 * e, 256), 256)], mem.at[e % 4], mem_s.at[e % 4])

    for e in range(4):
        load_mem(e).start()
    loads = [pltpu.make_async_copy(A.at[10 + i], (wk if i < 2 else wv).at[:, pl.ds(384 * (i % 2), 384)], w_s.at[i]) for i in range(4)]
    loads.append(pltpu.make_async_copy(q_h, qall, q_s))
    for n in range(6):
        doall[n, me["x"], me["y"]] = do[:, 128 * n:128 * n + 128]
    stall[me["x"], me["y"]] = st[...]
    pl.semaphore_wait(bar, count)

    def place(n, at):
        return stall.at[at["x"], at["y"]] if n == 6 else doall.at[n, at["x"], at["y"]]

    plane = Gather(me, PLANE + ("xy",), place, lambda n: place(n, me), ss, rs)
    fhop, ffin = staged("BC", (hB2, hC2, fB2, fC2))
    grads = ffn_place(GB, GC)
    ring = Scatter(me, PARTS_F, {"B": accB, "C": accC}, fhop, ffin, fs, fr, {"B": sibB, "C": sibC},
                   lambda n, at, c: grads(n, {**at, "c": c}), fsib_s, fsib_r, floc, "xy")
    back = Scatter(me, PARTS_D, {"D": dst}, *staged("D", (dh1, df1, df0)), ds_, dr_)
    plane.send(0, (6, 0, 1, 2, 3, 4, 5))
    ring.start()
    for c in loads:
        c.start()

    def turn(a, b):
        @pl.loop(a, b)
        def _(e):
            load_mem(e).wait()
            memT[:, pl.ds(pl.multiple_of(256 * e, 256), 256)] = mem[e % 4].T

            @pl.when(e < 8)
            def _():
                load_mem(e + 4).start()

    turn(0, 3)
    plane.send(1, (6, 0, 1))
    plane.send(1, (2, 3))
    plane.send(1, (4, 5))
    turn(3, 6)
    ring.merge(0)
    ring.send(0)
    plane.forward((6, 0, 1))
    plane.forward((2, 3))
    ring.merge(1)
    ring.merge(2)
    masks = head_masks()
    pos = key_positions()

    def load_kv(g, i, u, which):
        e = ((me["x"] + 2 + i) % 4) * 4 + u
        cols = pl.ds(256 * g, 256)
        src = (k_h.at[e, :, cols], v_h.at[e, :, cols], kt_h.at[e, cols])[which]
        return pltpu.make_async_copy(src, (K, V, KT)[which].at[i % 2, u], kv_s.at[which, i % 2, u])

    def fetch_kv(g, i):
        for u in range(4):
            for w in range(3):
                load_kv(g, i, u, w).start()

    fetch_kv(0, 0)
    for c in loads:
        c.wait()

    def attend(g):
        cols = slice(256 * g, 256 * g + 256)

        @pl.loop(0, 4)
        def _(i):
            @pl.when(i < 3)
            def _():
                fetch_kv(g, i + 1)

            for u in range(4):
                for w in range(3):
                    load_kv(g, i, u, w).wait()
            x = (me["x"] + 2 + i) % 4
            four = [(x * 4 + y, {"x": x, "y": y}) for y in range(4)]
            q4s = [stack_heads(pair_of(qall, g, at), masks) for _, at in four]
            d4s = [stack_heads(pair_of(doall, g, at), masks) for _, at in four]
            sT = [dot(K[i % 2, u], q4s[u], 1, 1) for u in range(4)]
            gT = [dot(V[i % 2, u], d4s[u], 1, 1) for u in range(4)]
            pT, sg = [], []
            for u, (e, at) in enumerate(four):
                live = pos < lens[pl.ds(e, 1), :]
                ps, gs = [], []
                for h in range(4):
                    n = 4 * g + h
                    s = jnp.where(live, sT[u][:, 128 * h:128 * h + 128], NEG)
                    p = jnp.exp(s - stall[at["x"], at["y"], n:n + 1, :])
                    ps.append(p.astype(BF))
                    gs.append((p * (gT[u][:, 128 * h:128 * h + 128] - stall[at["x"], at["y"], 12 + n:13 + n, :])).astype(BF))
                pT.append(jnp.concatenate(ps, axis=1))
                sg.append(jnp.concatenate(gs, axis=1))
            for u, (e, at) in enumerate(four):
                dV[pl.ds(pl.multiple_of(192 * e, 192), 192), cols] = dot(pT[u], d4s[u]).astype(BF)
            for u, (e, at) in enumerate(four):
                dK[pl.ds(pl.multiple_of(192 * e, 192), 192), cols] = dot(sg[u], q4s[u]).astype(BF)
            for u, (e, at) in enumerate(four):
                qT = dot(KT[i % 2, u], sg[u])
                for h in range(4):
                    dst[2 * g + h // 2, at["x"], at["y"], 64 * (h % 2):64 * (h % 2) + 64, :] = qT[64 * h:64 * h + 64, 128 * h:128 * h + 128].astype(BF)

        if g < 2:
            fetch_kv(g + 1, 0)
        back.send(1, (2 * g, 2 * g + 1))

    plane.finish((6, 0, 1))
    attend(0)
    ring.forward()
    plane.forward((4, 5))
    plane.finish((2, 3))
    attend(1)
    back.forward((0, 1))
    ring.merge(3)
    plane.finish((4, 5))
    attend(2)
    back.forward((2, 3))
    back.close(1, (0, 1))
    back.send(0, (0, 1))

    def gm_copy(e):
        return pltpu.make_async_copy(gst.at[e % 2], gm_h.at[e], gm_s.at[e % 2])

    def mem_grad(a, b):
        @pl.loop(a, b)
        def _(e):
            @pl.when(e > 1)
            def _():
                gm_copy(e - 2).wait()

            rows = pl.ds(pl.multiple_of(384 * e, 384), 384)
            gst[e % 2] = dot(dK[rows, :], wk[...], 1, 1) + dot(dV[rows, :], wv[...], 1, 1)
            gm_copy(e).start()

    def dw_copy(k, r, half):
        rows = pl.ds(pl.multiple_of(256 * r, 256), 256)
        return pltpu.make_async_copy(wst.at[k, :, pl.ds(384 * half, 384)], dw_h.at[10 + 2 * k + half, rows], dw_s.at[k, half])

    def weight_grad(a, b):
        @pl.loop(a, b)
        def _(r):
            for k in range(2):
                @pl.when(r > 0)
                def _():
                    dw_copy(k, r - 1, 0).wait()
                    dw_copy(k, r - 1, 1).wait()

                wst[k] = dot(memT[pl.ds(pl.multiple_of(256 * r, 256), 256), :], (dV if k else dK)[...]).astype(BF)
                dw_copy(k, r, 0).start()
                dw_copy(k, r, 1).start()

    turn(6, 12)
    mem_grad(0, 2)
    back.forward((4, 5))
    back.close(1, (2, 3))
    back.send(0, (2, 3))
    mem_grad(2, 8)
    back.close(1, (4, 5))
    back.send(0, (4, 5))
    ring.close(0)
    sums = [pltpu.make_async_copy(accB.at[:, :, :, me["z"]], sumE, sum_s.at[0]), pltpu.make_async_copy(accC.at[me["z"]], sumF, sum_s.at[1])]
    for c in sums:
        c.start()
    weight_grad(0, 3)
    for n in range(6):
        dq_ref[:, 128 * n:128 * n + 128] = (0.125 * back.result(n)).T
    for c in sums:
        c.wait()
    gm_copy(6).wait()
    gm_copy(7).wait()
    for k in range(2):
        dw_copy(k, 2, 0).wait()
        dw_copy(k, 2, 1).wait()
    plane.drain()
    ring.drain()
    back.drain()


def cross_bwd(do, st, lens, q_h, k_h, v_h, kt_h, memory, A, GB, GC, GA):
    bB, bC = (48, 256), (16, 768)
    return pl.pallas_call(
        cross_bwd_kernel,
        out_shape=(SDS((128, 768), F32), SDS((8, 384, 768), F32), SDS((16, 768, 384), BF), SDS((2, 4, 4, 48, 256), BF), SDS((4, 4, 16, 768), BF)),
        in_specs=[VS] * 3 + [HS] * 9, out_specs=(VS,) + (HS,) * 4, input_output_aliases={11: 2},
        scratch_shapes=[vm(6, 4, 4, 128, 128), vm(6, 4, 4, 128, 128), vf(4, 4, 24, 128), vm(768, 768), vm(768, 768),
                        vm(2, 4, 192, 256), vm(2, 4, 192, 256), vm(2, 4, 256, 192), vm(4, 256, 768), vm(768, 3072), vm(3072, 768), vm(3072, 768),
                        vf(2, 384, 768), vm(2, 256, 768), vm(6, 4, 4, 128, 128), *stage_buffers(LEAD_D, ((6,), (128, 128))),
                        vm(2, 4, 4, 4, *bB), vm(4, 4, 4, *bC), vm(2, 4, 4, 4, *bB), vm(4, 4, 4, *bC), *stage_buffers(LEAD_A[:2], ((2,), bB), ((), bC)),
                        DMA, DMA((3, 2, 4)), DMA((4,)), DMA((4,)), DMA((2,)), DMA((2, 2)), DMA((7, 2, 4)), DMA((7, 2, 4)), DMA((6, 2, 5)), DMA((6, 2, 5)),
                        DMA((3, 1, 4)), DMA((3, 1, 4)), DMA((3, 4)), DMA((3, 4)), DMA((3, 4)), DMA((2,))],
        compiler_params=pltpu.CompilerParams(collective_id=3, has_side_effects=True, vmem_limit_bytes=60 << 20),
        name="cross_backward",
    )(do, st, lens, q_h, k_h, v_h, kt_h, memory.reshape(3072, 768), A, GB, GC, GA)


def adam_update(master, first, second, grad, rate):
    first_new = beta_one * first + (1.0 - beta_one) * grad
    second_new = beta_two * second + (1.0 - beta_two) * grad * grad
    fix_one = 1.0 - beta_one**STEP
    fix_two = 1.0 - beta_two**STEP
    master_new = master - rate * (
        first_new / fix_one / (jnp.sqrt(second_new / fix_two) + adam_eps) + decay_rate * master
    )
    return (master_new, first_new, second_new, master_new.astype(jnp.bfloat16))


def ffn_kernel(x1, o2, L2, dy_ref, gains, A, B, C, out, do2, st, dx2, gg, GA, GB, GC,
               W7, WB, WC, gA, gB, gC, sw, sb, sc, tb, tc, ta):
    lA = [pltpu.make_async_copy(A.at[14 + i], W7.at[i], sw.at[i]) for i in range(2)]
    lB = [pltpu.make_async_copy(B.at[i], WB.at[i], sb.at[i]) for i in range(16)]
    lC = [pltpu.make_async_copy(C.at[i], WC.at[i], sc.at[i]) for i in range(8)]
    for c in lA:
        c.start()
    for j in range(8):
        lB[j].start()
        lB[8 + j].start()
        lC[j].start()
    o = o2[...]
    ob = o.astype(BF)
    for c in lA:
        c.wait()
    x = x1[...] + apply_w(ob, W7, 0)
    inv = rms(x)
    h = (x * inv * gains[2:3, :]).astype(BF)
    hT = flip(h.astype(F32)).astype(BF)
    df = dy_ref[...]
    y = jnp.zeros((128, 768), F32)
    dh = jnp.zeros((128, 768), F32)
    c0 = 0.7978845608028654
    sB, sC = [], []
    for j0 in range(0, 8, 2):
        js = range(j0, j0 + 2)
        for j in js:
            lB[j].wait()
            lB[8 + j].wait()
            lC[j].wait()
        a_s = [dot(h, WB[j]) for j in js]
        ups = [dot(h, WB[8 + j]) for j in js]
        dms = [dot(df, WC[j], 1, 1) for j in js]
        mids, dgs, dus = [], [], []
        for a, up, dm in zip(a_s, ups, dms):
            t = jnp.tanh(c0 * (a + 0.044715 * a * a * a))
            half = 0.5 * (1.0 + t)
            gel = a * half
            der = half + 0.5 * a * (1.0 - t * t) * (c0 * (1.0 + 0.134145 * a * a))
            mids.append(gel * up)
            dgs.append((dm * up * der).astype(BF))
            dus.append((dm * gel).astype(BF))
        y += dot(jnp.concatenate([m.astype(BF) for m in mids], axis=1), WC[j0:j0 + 2].reshape(2 * 256, 768))
        for n, j in enumerate(js):
            dh += dot(dgs[n], WB[j], 1, 1) + dot(dus[n], WB[8 + j], 1, 1)
        for n, j in enumerate(js):
            gB[j] = dot(hT, dgs[n]).astype(BF)
            gB[8 + j] = dot(hT, dus[n]).astype(BF)
            gC[j] = dot(flip(mids[n]).astype(BF), df).astype(BF)
        for j in js:
            new = [pltpu.make_async_copy(gB.at[j], GB.at[j], tb.at[j]), pltpu.make_async_copy(gB.at[8 + j], GB.at[8 + j], tb.at[8 + j]),
                   pltpu.make_async_copy(gC.at[j], GC.at[j], tc.at[j])]
            for c in new:
                c.start()
            sB += new
    out[...] = (x + y).astype(BF)
    dz, gain = rms_back(x, inv, gains[2:3, :], dh)
    gg[...] = gain
    d = df.astype(F32) + dz
    dx2[...] = d
    dc = d.astype(BF)
    dof = apply_wt(dc, W7, 0).astype(BF)
    do2[...] = dof
    prod = flip(dof.astype(F32) * o)
    st[0:12, :] = L2[0:12, :]
    for n in range(12):
        st[12 + n:13 + n, :] = jnp.sum(prod[64 * n:64 * n + 64, :], axis=0, keepdims=True)
    oT = flip(o).astype(BF)
    sA = []
    for i in range(2):
        gA[i] = dot(oT, dc[:, 384 * i:384 * i + 384]).astype(BF)
        sA.append(pltpu.make_async_copy(gA.at[i], GA.at[14 + i], ta.at[i]))
        sA[-1].start()
    for c in sA + sB + sC:
        c.wait()

def ffn(x1, o2, L2, dy, gains, A, B, C):
    M = lambda *s: pltpu.VMEM(s, BF)
    D = pltpu.SemaphoreType.DMA
    return pl.pallas_call(
        ffn_kernel,
        out_shape=(SDS((128, 768), BF), SDS((128, 768), BF), SDS((24, 128), F32), SDS((128, 768), F32), SDS((1, 768), F32),
                   SDS((16, 768, 384), BF), SDS((16, 768, 256), BF), SDS((8, 256, 768), BF)),
        in_specs=[VS] * 5 + [HS] * 3, out_specs=(VS,) * 5 + (HS,) * 3,
        scratch_shapes=[M(2, 768, 384), M(16, 768, 256), M(8, 256, 768), M(2, 768, 384), M(16, 768, 256), M(8, 256, 768),
                        D((2,)), D((16,)), D((8,)), D((16,)), D((8,)), D((2,))],
        compiler_params=pltpu.CompilerParams(vmem_limit_bytes=60 << 20),
        name="feed_forward",
    )(x1, o2, L2, dy, gains, A, B, C)

def self_bwd_kernel(dq2, h2, x1, dx2, qkv, o1, L1, x_ref, h1, gains, g3, A, GA_in, gm_in, gin, tile, GA, gm,
                    W, G, gb, gmv, sem, gsem, msem):
    loads = [pltpu.make_async_copy(A.at[i], W.at[i], sem.at[i]) for i in range(10)]
    for i in (8, 9, 6, 7, 0, 1, 2, 3, 4, 5):
        loads[i].start()
    def gm_load(e):
        return pltpu.make_async_copy(gm_in.at[e], gmv.at[e], msem.at[e])
    def gm_store(e):
        return pltpu.make_async_copy(gmv.at[e], gm.at[e], msem.at[16 + e])
    for e in range(16):
        gm_load(e).start()
    stores = []
    def weight_grad(k, left, inc):
        for i in range(2):
            n = 2 * k + i
            G[n] = dot(left, inc[:, 384 * i:384 * i + 384]).astype(BF)
            stores.append(pltpu.make_async_copy(G.at[n], GA.at[n], gsem.at[n]))
            stores[-1].start()
    dqb = dq2[...].astype(BF)
    for i in (8, 9, 6, 7):
        loads[i].wait()
    u = apply_wt(dqb, W, 4)
    x = x1[...]
    inv = rms(x)
    dz, gain = rms_back(x, inv, gains[1:2, :], u)
    gb[...] = jnp.zeros((8, 768), F32)
    gb[1:2, :] = gain
    gb[2:3, :] = g3[...]
    d1 = dx2[...] + dz
    da = d1.astype(BF)
    do1 = apply_wt(da, W, 3).astype(BF)
    weight_grad(4, flip(h2[...].astype(F32)).astype(BF), dqb)
    masks = head_masks(0.125)
    ones = head_masks(1.0)
    live = causal_mask()
    kT = flip(qkv[1].astype(F32)).astype(BF)
    qs, ks, vs = [], [], []
    for g in range(3):
        cols = slice(256 * g, 256 * g + 256)
        q4 = qkv[0, :, cols]
        d4 = do1[:, cols]
        q4s = jnp.concatenate([q4 * m for m in masks], axis=0)
        d4s = jnp.concatenate([d4 * m for m in ones], axis=0)
        sT = dot(qkv[1, :, cols], q4s, 1, 1)
        gT = dot(qkv[2, :, cols], d4s, 1, 1)
        ps, gs = [], []
        for n in range(4):
            s = jnp.where(live, sT[:, 128 * n:128 * n + 128], NEG)
            p = jnp.exp(s - L1[4 * g + n:4 * g + n + 1, :])
            gt = gT[:, 128 * n:128 * n + 128]
            ps.append(p.astype(BF))
            gs.append((p * (gt - jnp.sum(p * gt, axis=0, keepdims=True))).astype(BF))
        sg = jnp.concatenate(gs, axis=1)
        vs.append(dot(jnp.concatenate(ps, axis=1), d4s).astype(BF))
        ks.append(dot(sg, q4s).astype(BF))
        qT = dot(kT[256 * g:256 * g + 256, :], sg)
        qs += [qT[64 * n:64 * n + 64, 128 * n:128 * n + 128] for n in range(4)]
    for e in range(16):
        gm_load(e).wait()
        gm_store(e).start()
    inc = [(0.125 * unflip(jnp.concatenate(qs, axis=0))).astype(BF), jnp.concatenate(ks, axis=1), jnp.concatenate(vs, axis=1)]
    weight_grad(3, flip(o1[...].astype(F32)).astype(BF), da)
    for c in loads[:6]:
        c.wait()
    u = apply_wt(inc[0], W, 0) + apply_wt(inc[1], W, 1) + apply_wt(inc[2], W, 2)
    x = x_ref[...].astype(F32)
    inv = rms(x)
    dz, gain = rms_back(x, inv, gains[0:1, :], u)
    gb[0:1, :] = gain
    gin[...] = d1 + dz
    hT = flip(h1[...].astype(F32)).astype(BF)
    for k in range(3):
        weight_grad(k, hT, inc[k])
    lane = lax.broadcasted_iota(jnp.int32, (8, 128), 1)
    for d in range(8):
        lo, sh = 96 * d // 128, 96 * d % 128
        t = pltpu.roll(gb[:, 128 * lo:128 * lo + 128], (128 - sh) % 128, 1)
        if sh > 32:
            nxt = pltpu.roll(gb[:, 128 * lo + 128:128 * lo + 256], (128 - sh) % 128, 1)
            t = jnp.where(lane < 128 - sh, t, nxt)
        tile[d] = jnp.where(lane < 96, t, 0.0)
    for c in stores:
        c.wait()
    for e in range(16):
        gm_store(e).wait()

def self_bwd(dq2, h2, x1, dx2, qkv, o1, L1, x, h1, gains, g3, A, GA, gm):
    D = pltpu.SemaphoreType.DMA
    return pl.pallas_call(
        self_bwd_kernel,
        out_shape=(SDS((128, 768), F32), SDS((8, 8, 128), F32), SDS((16, 768, 384), BF), SDS((16, 192, 768), F32)),
        in_specs=[VS] * 11 + [HS] * 3, out_specs=(VS, VS, HS, HS),
        input_output_aliases={12: 2},
        scratch_shapes=[pltpu.VMEM((10, 768, 384), BF), pltpu.VMEM((10, 768, 384), BF), pltpu.VMEM((8, 768), F32), pltpu.VMEM((16, 192, 768), F32), D((10,)), D((10,)), D((32,))],
        compiler_params=pltpu.CompilerParams(vmem_limit_bytes=60 << 20),
        name="self_backward",
    )(dq2, h2, x1, dx2, qkv, o1, L1, x, h1, gains, g3, A, GA, gm)

def adam_kernel(*refs):
    ins, outs = refs[:16], refs[16:]
    for n in range(4):
        w, m, v, g = ins[4 * n:4 * n + 4]
        grad = g[0:3, 0:6] if n == 3 else g[...]
        for o, val in zip(outs[4 * n:4 * n + 4], adam_update(w[...], m[...], v[...], grad, rate_gain if n == 3 else rate_matrix)):
            o[...] = val

def adam(*args):
    shapes = []
    for n in range(4):
        s = args[4 * n].shape
        shapes += [SDS(s, F32)] * 3 + [SDS(s, BF)]
    return pl.pallas_call(adam_kernel, out_shape=tuple(shapes), in_specs=[VS] * 16, out_specs=(VS,) * 16,
                          compiler_params=pltpu.CompilerParams(vmem_limit_bytes=60 << 20), name="adam")(*args)


def body(
    dec_input,
    memory,
    mem_len,
    grad_out,
    attn_master,
    ffn_in_master,
    ffn_out_master,
    gain_master,
    attn_first,
    ffn_in_first,
    ffn_out_first,
    gain_first,
    attn_second,
    ffn_in_second,
    ffn_out_second,
    gain_second,
):
    swap = lambda a: a.transpose(1, 0, 2)
    attn_t, in_t = swap(attn_master), swap(ffn_in_master)
    x = dec_input[0]
    (gath_a, gath_b, gath_c, q_all, k_two, v_two, kt_two, gains, lens, h1, qkv, o1, x1, h2, L1, o2, L2) = forward(
        attn_t, in_t, ffn_out_master, gain_master, mem_len.reshape(1, 1), x, memory
    )
    aw = gath_a.reshape(16, 768, 384)
    out_block, do2, st, dx2, g3, GA, GB, GC = ffn(x1, o2, L2, grad_out[0], gains, aw, gath_b.reshape(16, 768, 256), gath_c.reshape(8, 256, 768))
    dq2, gm, GA, sum_b, sum_c = cross_bwd(
        do2, st, lens, q_all, k_two, v_two, kt_two, memory, aw,
        GB.reshape(4, 4, 4, 2, 2, 48, 256), GC.reshape(4, 2, 4, 4, 16, 768), GA,
    )
    grad_input, tile_g, GA, grad_memory = self_bwd(dq2, h2, x1, dx2, qkv, o1, L1, x, h1, gains, g3, aw, GA, gm.reshape(16, 192, 768))
    share_a, share_b, share_c, share_g = scatter(GA.reshape(4, 4, 4, 2, 3, 32, 384), sum_b, sum_c, tile_g)
    new = adam(
        attn_t, swap(attn_first), swap(attn_second), share_a,
        in_t, swap(ffn_in_first), swap(ffn_in_second), share_b,
        ffn_out_master, ffn_out_first, ffn_out_second, share_c,
        gain_master, gain_first, gain_second, share_g,
    )
    return (out_block[None], grad_input[None], grad_memory, *[swap(a) for a in new[:8]], *new[8:])


def solution(mesh):
    placed = (
        P(("dp", "seq"), None, None),
        P("dp", "seq", None),
        P(("dp", "seq")),
        P(("dp", "seq"), None, None),
        P(None, ("dp", "seq"), None),
        P(None, ("dp", "seq"), None),
        P(("dp", "seq"), None),
        P(None, ("dp", "seq")),
        P(None, ("dp", "seq"), None),
        P(None, ("dp", "seq"), None),
        P(("dp", "seq"), None),
        P(None, ("dp", "seq")),
        P(None, ("dp", "seq"), None),
        P(None, ("dp", "seq"), None),
        P(("dp", "seq"), None),
        P(None, ("dp", "seq")),
    )
    return jax.shard_map(
        body,
        mesh=mesh,
        in_specs=placed,
        out_specs=(
            P(("dp", "seq"), None, None),
            P(("dp", "seq"), None, None),
            P("dp", "seq", None),
            P(None, ("dp", "seq"), None),
            P(None, ("dp", "seq"), None),
            P(None, ("dp", "seq"), None),
            P(None, ("dp", "seq"), None),
            P(None, ("dp", "seq"), None),
            P(None, ("dp", "seq"), None),
            P(None, ("dp", "seq"), None),
            P(None, ("dp", "seq"), None),
            P(("dp", "seq"), None),
            P(("dp", "seq"), None),
            P(("dp", "seq"), None),
            P(("dp", "seq"), None),
            P(None, ("dp", "seq")),
            P(None, ("dp", "seq")),
            P(None, ("dp", "seq")),
            P(None, ("dp", "seq")),
        ),
        check_vma=False,
    )
```

```python
import jax
import jax.numpy as jnp
from jax import lax
from jax.experimental import pallas as pl
from jax.experimental.pallas import tpu as pltpu
from jax.sharding import PartitionSpec as P

eps_norm = 1e-06
beta_one = 0.9
beta_two = 0.999
adam_eps = 1e-08
decay_rate = 0.01
rate_matrix = 0.12
rate_gain = 3.0
STEP = 10
MESH = pl.DeviceIdType.MESH
BF, F32 = jnp.bfloat16, jnp.float32
ALL = slice(None)
NEG = -1e30
PARTS_A = (("A", 0, "xyz"), ("A", 1, "yzx"), ("A", 2, "zxy"))
PARTS_F = (("B", 0, "z"), ("B", 1, "z"), ("C", 0, "z"))
PARTS_G = (("E", 0, "xy"), ("E", 1, "yx"), ("F", 0, "xy"))
PLANE = ("xy", "yx") * 3
PARTS_D = tuple(("D", n, PLANE[n]) for n in range(6))
AXES = {"A": "xyz", "B": "xyz", "C": "zxy", "D": "xy", "E": "xy", "F": "xy"}
STEPS = (2, -1, 1, 0)
VS = pl.BlockSpec(memory_space=pltpu.VMEM)
HS = pl.BlockSpec(memory_space=pltpu.HBM)
SDS = jax.ShapeDtypeStruct
DMA = pltpu.SemaphoreType.DMA


def vm(*shape):
    return pltpu.VMEM(shape, BF)


def vf(*shape):
    return pltpu.VMEM(shape, F32)


def where_am_i():
    dp, sq = lax.axis_index("dp"), lax.axis_index("seq")
    return {"x": sq // 4, "y": sq % 4, "z": dp // 2, "c": dp % 2}


def dev(at):
    return (at["z"] * 2 + at["c"], at["x"] * 4 + at["y"])


def moved(at, axis, step):
    return {**at, axis: (at[axis] + step + 4) % 4}


def offset(me, j, sign=1):
    return {**me, "x": (me["x"] + sign * (j // 4) + 4) % 4, "y": (me["y"] + sign * (j % 4) + 4) % 4}


def sibling_of(me):
    return {**me, "c": 1 - me["c"]}


def remote(src, dst, send, recv, to):
    return pltpu.make_async_remote_copy(src, dst, send, recv, device_id=dev(to), device_id_type=MESH)


def meet(me, column):
    dp, sq = lax.axis_index("dp"), lax.axis_index("seq")
    bar = pltpu.get_barrier_semaphore()
    for i in range(1, 16):
        pl.semaphore_signal(bar, inc=1, device_id=(dp, (sq + i) % 16), device_id_type=MESH)
    if column == "dp":
        for i in range(1, 8):
            pl.semaphore_signal(bar, inc=1, device_id=((dp + i) % 8, sq), device_id_type=MESH)
        return bar, 22
    if column == "z":
        for to in (moved(me, "z", 1), moved(me, "z", -1), sibling_of(me)):
            pl.semaphore_signal(bar, inc=1, device_id=dev(to), device_id_type=MESH)
        return bar, 18
    return bar, 15


def dot(a, b, ca=1, cb=0):
    return lax.dot_general(a, b, (((ca,), (cb,)), ((), ())), preferred_element_type=F32)


class Gather:
    def __init__(self, me, orders, view, own, ss, rs, sib_s=None, sib_r=None, whole=""):
        self.me, self.orders, self.view, self.own, self.whole = me, orders, view, own, whole
        self.ss, self.rs, self.sib_s, self.sib_r = ss, rs, sib_s, sib_r
        self.count, self.last = len(orders), len(orders[0]) - 1

    def group(self, n, t, step, half=None):
        axes = self.whole + self.orders[n][:t]
        at = {**moved(self.me, self.orders[n][t], step), **{a: ALL for a in axes}}
        if half is not None and axes:
            at[axes[0]] = pl.ds(2 * half, 2)
        return at

    def kinds(self, t):
        return (0, 1, 2, 3) if t == self.last else (0, 1, 2)

    def copy(self, n, t, kind, back=0):
        straight = kind < 2 or t < self.last
        step = (1, -1, 2 if straight else 1, -1)[kind]
        dst = self.view(n, self.group(n, t, back) if straight else self.group(n, t, back - step, kind - 2))
        src = self.own(n) if self.own and t == 0 and straight and back == 0 else dst
        return remote(src, dst, self.ss.at[n, t, kind], self.rs.at[n, t, kind], moved(self.me, self.orders[n][t], step))

    def arrived(self, n, t, kind):
        self.copy(n, t, kind, (-1, 1, -2 if t < self.last else -1, 1)[kind]).wait_recv()

    def sibling(self, n, j, c):
        v = self.view(n, {**self.group(n, self.last, (0, -1, 1, 2)[j]), "c": c})
        return remote(v, v, self.sib_s.at[n, j], self.sib_r.at[n, j], sibling_of(self.me))

    def send(self, t, ns=None):
        for n in ns or range(self.count):
            if t:
                for k in range(3):
                    self.arrived(n, t - 1, k)
            for k in (0, 1) if t == self.last else (2, 0, 1):
                self.copy(n, t, k).start()
            if self.sib_s is not None and t == self.last:
                self.sibling(n, 0, self.me["c"]).start()

    def forward(self, ns=None):
        for n in ns or range(self.count):
            for k in (0, 1):
                self.arrived(n, self.last, k)
                self.copy(n, self.last, 2 + k).start()
                if self.sib_s is not None:
                    self.sibling(n, 1 + k, self.me["c"]).start()

    def finish(self, ns=None):
        for n in ns or range(self.count):
            for k in (2, 3):
                self.arrived(n, self.last, k)
            if self.sib_s is not None:
                self.sibling(n, 3, self.me["c"]).start()

    def siblings_in(self):
        for n in range(self.count):
            for j in range(4):
                self.sibling(n, j, 1 - self.me["c"]).wait_recv()

    def drain(self):
        for n in range(self.count):
            for t in range(self.last + 1):
                for k in self.kinds(t):
                    self.copy(n, t, k).wait_send()
            if self.sib_s is not None:
                for j in range(4):
                    self.sibling(n, j, self.me["c"]).wait_send()


class Scatter:
    def __init__(self, me, parts, acc, hop, fin, ss, rs, sib=None, source=None, sib_s=None, sib_r=None, loc_s=None, whole=""):
        self.whole = whole
        self.me, self.parts, self.acc, self.hop_b, self.fin_b = me, parts, acc, hop, fin
        self.ss, self.rs, self.sib, self.source = ss, rs, sib, source
        self.sib_s, self.sib_r, self.loc_s = sib_s, sib_r, loc_s
        self.count, self.last = len(parts), len(parts[0][2]) - 1

    def idx(self, n, at):
        name, p, _ = self.parts[n]
        place = tuple(at[a] for a in AXES[name])
        return place if name in "CF" else (p,) + place

    def slot(self, n):
        name, p, _ = self.parts[n]
        return () if name in "CF" else (p,)

    def done(self, n, t):
        name, _, order = self.parts[n]
        return [a for a in AXES[name] if a in self.whole + order[:t]]

    def group(self, n, t, step, half=None):
        axes = self.done(n, t)
        at = {**moved(self.me, self.parts[n][2][t], step), **{a: ALL for a in axes}}
        if half is not None and axes:
            at[axes[0]] = pl.ds(2 * half, 2)
        return at

    def fins(self, t):
        return 2 if t == self.last else 3

    def refs(self, n, t):
        name = self.parts[n][0]
        return self.acc[name], self.hop_b[name] if t == self.last else None, self.fin_b[t][name]

    def hop_copy(self, n, kind):
        step, t = 1 if kind == 0 else -1, self.last
        a, h, _ = self.refs(n, t)
        return remote(a.at[self.idx(n, self.group(n, t, 2 * step, kind))], h.at[self.slot(n) + (kind,)],
                      self.ss.at[n, t, kind], self.rs.at[n, t, kind], moved(self.me, self.parts[n][2][t], step))

    def fin_copy(self, n, t, kind):
        step = (1, -1, 2)[kind]
        a, _, f = self.refs(n, t)
        return remote(a.at[self.idx(n, self.group(n, t, step))], f.at[self.slot(n) + (kind,)],
                      self.ss.at[n, t, 2 + kind], self.rs.at[n, t, 2 + kind], moved(self.me, self.parts[n][2][t], step))

    def each(self, n, t, at, fn, half=None):
        axes = self.done(n, t)
        sizes, offs = [4] * len(axes), [0] * len(axes)
        if half is not None and axes:
            sizes[0], offs[0] = 2, 2 * half
        total = 1
        for s in sizes:
            total *= s

        def one(i):
            pos, rest = [], i
            for s in sizes[::-1]:
                pos.append(rest % s)
                rest = rest // s
            pos = pos[::-1]
            where = dict(at)
            for a, p, o in zip(axes, pos, offs):
                where[a] = p + o
            fn(self.idx(n, where), tuple(pos))

        if total == 1:
            one(0)
        else:
            pl.loop(0, total, unroll=4)(one)

    def sib_copy(self, n, j):
        at = self.group(n, self.last, STEPS[j])
        return remote(self.source(n, at, 1 - self.me["c"]), self.sib[self.parts[n][0]].at[self.idx(n, at)],
                      self.sib_s.at[n, j], self.sib_r.at[n, j], sibling_of(self.me))

    def loc_copy(self, n, j):
        at = self.group(n, self.last, STEPS[j])
        return pltpu.make_async_copy(self.source(n, at, self.me["c"]), self.acc[self.parts[n][0]].at[self.idx(n, at)], self.loc_s.at[n, j])

    def start(self):
        for j in range(4):
            for n in range(self.count):
                self.sib_copy(n, j).start()
                self.loc_copy(n, j).start()

    def merge(self, j):
        for n in range(self.count):
            self.sib_copy(n, j).wait_recv()
            self.loc_copy(n, j).wait()
            a, b = self.acc[self.parts[n][0]], self.sib[self.parts[n][0]]

            def fn(i, _):
                a[i] = a[i] + b[i]

            self.each(n, self.last, self.group(n, self.last, STEPS[j]), fn)

    def send(self, t, ns=None):
        for n in ns or range(self.count):
            if t == self.last:
                for k in (0, 1):
                    self.hop_copy(n, k).start()
            else:
                for k in (2, 0, 1):
                    self.fin_copy(n, t, k).start()

    def forward(self, ns=None):
        t = self.last
        for n in ns or range(self.count):
            a, h, _ = self.refs(n, t)
            for k in (0, 1):
                self.hop_copy(n, k).wait_recv()

                def fn(i, pos):
                    a[i] = a[i] + h[self.slot(n) + (k,) + pos]

                self.each(n, t, self.group(n, t, 1 if k == 0 else -1), fn, k)
                self.fin_copy(n, t, k).start()

    def close(self, t, ns=None):
        for n in ns or range(self.count):
            for k in range(self.fins(t)):
                self.fin_copy(n, t, k).wait_recv()
            a, _, f = self.refs(n, t)

            def fn(i, pos):
                v = a[i].astype(F32)
                for k in range(self.fins(t)):
                    v = v + f[self.slot(n) + (k,) + pos].astype(F32)
                a[i] = v.astype(BF)

            self.each(n, t, self.group(n, t, 0), fn)

    def result(self, n):
        a, _, f = self.refs(n, 0)
        v = a[self.idx(n, self.me)].astype(F32)
        for k in range(3):
            self.fin_copy(n, 0, k).wait_recv()
            v = v + f[self.slot(n) + (k,)].astype(F32)
        return v

    def drain(self):
        for n in range(self.count):
            if self.sib is not None:
                for j in range(4):
                    self.sib_copy(n, j).wait_send()
            for k in (0, 1):
                self.hop_copy(n, k).wait_send()
            for t in range(self.last + 1):
                for k in range(self.fins(t)):
                    self.fin_copy(n, t, k).wait_send()


LEAD_A = ((2, 2, 4), (2, 4, 4), (3, 4), (3,))
LEAD_D = ((2, 2), (2, 4), (3,))


def stage_buffers(leads, *shapes):
    return [vm(*pre, *lead, *block) for lead in leads for pre, block in shapes]


def staged(names, refs):
    k = len(names)
    got = [dict(zip(names, refs[k * i:k * i + k])) for i in range(len(refs) // k)]
    return got[0], {len(got) - 2 - i: g for i, g in enumerate(got[1:])}


def ffn_place(B, C):
    def place(n, at):
        if n < 2:
            return B.at[at["x"], at["y"], at["z"], at["c"], n]
        return C.at[at["z"], at["c"], at["x"], at["y"]]
    return place


def scatter_kernel(GA, sumE, sumF, gg, oA, oB, oC, oG, accA, sibA, h2, f2, f1, f0,
                   accE, accF, hE1, hF1, fE1, fF1, fE0, fF0, blk, stage, recv, gdp, gsum,
                   ss, rs, sib_s, sib_r, loc_s, as_, ar_, ds_, dr_, es, er, ld_s):
    me = where_am_i()
    dp, sq = lax.axis_index("dp"), lax.axis_index("seq")
    bar, count = meet(me, "dp")
    loads = [pltpu.make_async_copy(a, b, ld_s.at[i]) for i, (a, b) in enumerate(((sumE, accE), (sumF, accF)))]
    for c in loads:
        c.start()
    pl.semaphore_wait(bar, count)
    hop, fin = staged("A", (h2, f2, f1, f0))
    ring = Scatter(me, PARTS_A, {"A": accA}, hop, fin, ss, rs, {"A": sibA},
                   lambda n, at, c: GA.at[at["x"], at["y"], at["z"], c, n], sib_s, sib_r, loc_s)
    fhop, ffin = staged("EF", (hE1, hF1, fE1, fF1, fE0, fF0))
    ring_f = Scatter(me, PARTS_G, {"E": accE, "F": accF}, fhop, ffin, es, er)
    ring.start()
    for c in loads:
        c.wait()
    ring_f.send(1)

    def dpx(i):
        peer = (dp + i) % 8
        return pltpu.make_async_remote_copy(gg.at[peer], gdp.at[dp], ds_.at[i], dr_.at[i], device_id=(peer, sq), device_id_type=MESH)

    for i in range(1, 8):
        dpx(i).start()
    gdp[dp] = gg[dp]
    ring.merge(0)
    ring.send(2)
    ring.merge(1)
    ring.merge(2)
    ring_f.forward()
    ring.forward()
    ring.merge(3)
    ring_f.close(1)
    ring_f.send(0)
    for i in range(1, 8):
        dpx(i).wait_recv()
    gsum[...] = jnp.sum(gdp[...], axis=0)

    stage[:, 6:8, :] = jnp.zeros((16, 2, 768), F32)
    ring.close(2)
    ring.send(1)
    for n in range(2):
        blk[48 * n:48 * n + 48, 384:640] = ring_f.result(n)
    oC[...] = ring_f.result(2)
    ring.close(1)
    ring.send(0)
    for n in range(3):
        blk[32 * n:32 * n + 32, 0:384] = ring.result(n)
    for k in range(16):
        stage[k, 0:6, 0:640] = blk[6 * k:6 * k + 6, :]
        stage[k, :, 640:768] = gsum[...]

    def a2a(i):
        peer = (sq + i) % 16
        return pltpu.make_async_remote_copy(stage.at[peer], recv.at[sq], as_.at[i], ar_.at[i], device_id=(dp, peer), device_id_type=MESH)

    for i in range(1, 16):
        a2a(i).start()
    recv[sq] = stage[sq]
    for i in range(1, 16):
        a2a(i).wait_recv()
    oG[...] = pltpu.roll(jnp.sum(recv[:, :, 640:768], axis=0), (128 - 6 * sq) % 128, 1)
    for s in range(16):
        oA[:, s // 2, 384 * (s % 2):384 * (s % 2) + 384] = recv[s, 0:6, 0:384]
        oB[:, s // 8, 256 * (s % 8):256 * (s % 8) + 256] = recv[s, 0:6, 384:640]
    for i in range(1, 8):
        dpx(i).wait_send()
    for i in range(1, 16):
        a2a(i).wait_send()
    ring.drain()
    ring_f.drain()


def scatter(GA, sumE, sumF, gg):
    return pl.pallas_call(
        scatter_kernel,
        out_shape=(SDS((6, 8, 768), F32), SDS((6, 2, 2048), F32), SDS((16, 768), F32), SDS((8, 128), F32)),
        in_specs=[HS, HS, HS, VS], out_specs=(VS,) * 4,
        scratch_shapes=[vm(3, 4, 4, 4, 32, 384), vm(3, 4, 4, 4, 32, 384), *stage_buffers(LEAD_A, ((3,), (32, 384))),
                        vm(2, 4, 4, 48, 256), vm(4, 4, 16, 768), *stage_buffers(LEAD_D, ((2,), (48, 256)), ((), (16, 768))),
                        vf(96, 640), vf(16, 8, 768), vf(16, 8, 768), vf(8, 8, 128), vf(8, 128),
                        DMA((3, 3, 5)), DMA((3, 3, 5)), DMA((3, 4)), DMA((3, 4)), DMA((3, 4)),
                        DMA((16,)), DMA((16,)), DMA((8,)), DMA((8,)), DMA((3, 2, 5)), DMA((3, 2, 5)), DMA((2,))],
        compiler_params=pltpu.CompilerParams(collective_id=1, has_side_effects=True, vmem_limit_bytes=60 << 20),
        name="scatter_attention_grads",
    )(GA, sumE, sumF, gg)


def head_masks(value=1.0):
    lane = lax.broadcasted_iota(jnp.int32, (1, 256), 1)
    return [jnp.where(lane // 64 == h, value, 0.0).astype(BF) for h in range(4)]


def stack_heads(block, masks):
    return jnp.concatenate([block * m for m in masks], axis=0)


def key_positions():
    sq = lax.axis_index("seq")
    return (192 * sq + lax.broadcasted_iota(jnp.int32, (192, 128), 0)).astype(F32)


class Merge:
    def __init__(self, me, src, mid, one, two, ss, rs):
        self.me, self.src, self.mid, self.bufs, self.ss, self.rs = me, src, mid, (one, two), ss, rs

    def block(self, n, a, b):
        return (n, a, b) if n % 2 == 0 else (n, b, a)

    def copy(self, n, t, k):
        axis = PLANE[n][t]
        to = moved(self.me, axis, (1, -1, 2)[k])
        src = self.src.at[self.block(n, to[axis], ALL)] if t == 0 else self.mid.at[n, to[axis]]
        return remote(src, self.bufs[t].at[n, k], self.ss.at[n, t, k], self.rs.at[n, t, k], to)

    def send(self, t, ns):
        for n in ns:
            for k in (2, 0, 1):
                self.copy(n, t, k).start()

    def join(self, blocks):
        rows = [b[128:144, :].astype(F32)[0:8, :] for b in blocks]
        logs = [r + pltpu.roll(r, 6, 0) + pltpu.roll(r, 4, 0) for r in rows]
        top = logs[0]
        for l in logs[1:]:
            top = jnp.maximum(top, l)
        ws = [jnp.exp(l - top) for l in logs]
        total = ws[0] + ws[1] + ws[2] + ws[3]
        inv = 1.0 / total
        out = []
        for h in range(2):
            o = sum(b[64 * h:64 * h + 64, :].astype(F32) * (w * inv)[h:h + 1, :] for b, w in zip(blocks, ws))
            out.append(o)
        return jnp.concatenate(out, axis=0), top + jnp.log(total)

    def middle(self, ns):
        for n in ns:
            for k in range(3):
                self.copy(n, 0, k).wait_recv()
            a = self.me[PLANE[n][0]]

            for b in range(4):
                o, l = self.join([self.src.at[self.block(n, a, b)]] + [self.bufs[0].at[n, k, b] for k in range(3)])
                self.mid[n, b, 0:128, :] = o.astype(BF)
                self.mid[n, b, 128:144, :] = log_tile(l)

    def result(self, n):
        for k in range(3):
            self.copy(n, 1, k).wait_recv()
        return self.join([self.mid.at[n, self.me[PLANE[n][1]]]] + [self.bufs[1].at[n, k] for k in range(3)])

    def drain(self):
        for n in range(6):
            for t in range(2):
                for k in range(3):
                    self.copy(n, t, k).wait_send()


def log_tile(l):
    l = jnp.where(lax.broadcasted_iota(jnp.int32, (8, 128), 0) < 2, l, 0.0)
    high = l.astype(BF).astype(F32)
    middle = (l - high).astype(BF).astype(F32)
    low = l - high - middle
    return jnp.concatenate([high + pltpu.roll(middle, 2, 0) + pltpu.roll(low, 4, 0), jnp.zeros((8, 128), F32)], axis=0).astype(BF)


def pair_of(ref, g, at):
    return jnp.concatenate([ref[2 * g, at["x"], at["y"]], ref[2 * g + 1, at["x"], at["y"]]], axis=1)


def rms(x):
    return lax.rsqrt(jnp.mean(x * x, axis=-1, keepdims=True) + eps_norm)

def rms_back(x, inv, gain, u):
    scaled = u * gain
    inner = jnp.mean(scaled * x, axis=-1, keepdims=True)
    return inv * scaled - x * inv * inv * inv * inner, jnp.sum(u * x * inv, axis=0, keepdims=True)

def flip(x):
    return jnp.concatenate([x[:, 128 * i:128 * i + 128].T for i in range(x.shape[1] // 128)], axis=0)

def unflip(x):
    return jnp.concatenate([x[128 * i:128 * i + 128, :].T for i in range(x.shape[0] // 128)], axis=1)

def apply_w(h, W, k):
    return jnp.concatenate([dot(h, W[2 * k]), dot(h, W[2 * k + 1])], axis=1)

def apply_wt(u, W, k):
    return dot(u[:, 0:384], W[2 * k], 1, 1) + dot(u[:, 384:768], W[2 * k + 1], 1, 1)

def causal_mask():
    return lax.broadcasted_iota(jnp.int32, (128, 128), 0) <= lax.broadcasted_iota(jnp.int32, (128, 128), 1)


class Stacked:
    def __init__(self, ref):
        self.ref = ref

    def __getitem__(self, n):
        return self.ref[n].reshape(768, 384)


def self_attention(x_ref, gains, W, loads, q2, h1, qkv, o1, x1, h2, L1):
    x = x_ref[...].astype(F32)
    h = (x * rms(x) * gains[0:1, :]).astype(BF)
    h1[...] = h
    for k in range(3):
        loads[2 * k].wait()
        loads[2 * k + 1].wait()
        full = apply_w(h, W, k)
        qkv[k] = full.astype(BF)
    vT = flip(full).astype(BF)
    masks = head_masks(0.125)
    live = causal_mask()
    outs = []
    for g in range(3):
        cols = slice(256 * g, 256 * g + 256)
        q4 = qkv[0, :, cols]
        sT = dot(qkv[1, :, cols], jnp.concatenate([q4 * m for m in masks], axis=0), 1, 1)
        ps = []
        for n in range(4):
            s = jnp.where(live, sT[:, 128 * n:128 * n + 128], NEG)
            top = jnp.max(s, axis=0, keepdims=True)
            lse = top + jnp.log(jnp.sum(jnp.exp(s - top), axis=0, keepdims=True))
            L1[4 * g + n:4 * g + n + 1, :] = lse
            ps.append(jnp.exp(s - lse).astype(BF))
        oT = dot(vT[256 * g:256 * g + 256, :], jnp.concatenate(ps, axis=1))
        outs += [oT[64 * n:64 * n + 64, 128 * n:128 * n + 128] for n in range(4)]
    o = unflip(jnp.concatenate(outs, axis=0)).astype(BF)
    o1[...] = o
    for c in loads[6:10]:
        c.wait()
    x = x + apply_w(o, W, 3)
    x1[...] = x
    h = (x * rms(x) * gains[1:2, :]).astype(BF)
    h2[...] = h
    q2[...] = apply_w(h, W, 4).astype(BF) * jnp.asarray(0.125, BF)


def forward_kernel(attn, wi, wo, gain, length, x_ref, mem_h, A, B, C, q_h, k_h, v_h, kt_h, gains, lens, h1, qkv, o1, x1, h2, L1, o_ref, L_ref,
                   infos, info, stage, recv, blk, blkA, blkB, blkC, W, q2,
                   qall, mem, wk, wv, wkT, wvT, K, V, KT, VT, ost, mid, one, two, lrow,
                   fs, fr, ss, rs, sib_s, sib_r, as_, ar_, ds_, dr_, own_s, zs, zr, zsib_s, zsib_r,
                   load_s, mem_s, out_s, ps_, pr_, os_, or_):
    me = where_am_i()
    dp, sq = lax.axis_index("dp"), lax.axis_index("seq")
    bar, count = meet(me, "dp")

    def load_mem(e):
        return pltpu.make_async_copy(mem_h.at[e], mem.at[e], mem_s.at[e])

    @pl.loop(0, 16)
    def _(e):
        load_mem(e).start()

    lrow[...] = jnp.zeros((4, 2, 8, 128), F32)
    info[...] = jnp.zeros((8, 128), F32)
    info[0:3, 0:6] = gain[...].astype(BF).astype(F32)
    spot = (lax.broadcasted_iota(jnp.int32, (8, 128), 0) == 3) & (lax.broadcasted_iota(jnp.int32, (8, 128), 1) == sq)
    info[...] = pltpu.roll(info[...], 6 * sq, 1) + jnp.where(spot, length[...].astype(F32), 0.0)
    stage[:, 6:8, :] = jnp.zeros((16, 2, 768), F32)
    for s in range(16):
        stage[s, 0:6, 0:384] = attn[:, s // 2, 384 * (s % 2):384 * (s % 2) + 384]
        stage[s, :, 640:768] = info[...]
        stage[s, 0:6, 384:640] = wi[:, s // 8, 256 * (s % 8):256 * (s % 8) + 256]
    pl.semaphore_wait(bar, count)

    def a2a(i):
        peer = (sq + i) % 16
        return pltpu.make_async_remote_copy(stage.at[peer], recv.at[sq], as_.at[i], ar_.at[i], device_id=(dp, peer), device_id_type=MESH)

    for i in range(1, 16):
        a2a(i).start()
    recv[sq] = stage[sq]
    blkC[...] = wo[...].astype(BF)
    for i in range(1, 16):
        a2a(i).wait_recv()
    for k in range(16):
        blk[6 * k:6 * k + 6, :] = recv[k, 0:6, 0:640]
    for p in range(3):
        blkA[p] = blk[32 * p:32 * p + 32, 0:384].astype(BF)
    for p in range(2):
        blkB[p] = blk[48 * p:48 * p + 48, 384:640].astype(BF)
    place = lambda n, at: A.at[at["x"], at["y"], at["z"], at["c"], PARTS_A[n][1]]
    ring = Gather(me, [p[2] for p in PARTS_A], place, lambda n: blkA.at[n], ss, rs, sib_s, sib_r)
    place_f = ffn_place(B, C)
    mine = lambda n: blkB.at[n] if n < 2 else blkC
    ring_f = Gather(me, [p[2] for p in PARTS_G], place_f, mine, fs, fr)
    owns = [pltpu.make_async_copy(blkA.at[n], place(n, me), own_s.at[n]) for n in range(3)]
    owns += [pltpu.make_async_copy(mine(n), place_f(n, me), own_s.at[3 + n]) for n in range(3)]
    for o in owns:
        o.start()
    ring.send(0)
    ring_f.send(0)
    for o in owns:
        o.wait()
    ring.send(1)
    ring_f.send(1)
    ring.send(2)
    ring_f.forward()
    tile = jnp.sum(recv[:, :, 640:768], axis=0)
    infos[dp] = tile

    def dpx(i, back=0):
        v = infos.at[(dp - back + 8) % 8]
        return pltpu.make_async_remote_copy(v, v, ds_.at[i], dr_.at[i], device_id=((dp + i) % 8, sq), device_id_type=MESH)

    for i in range(1, 8):
        dpx(i).start()
    ring.forward()
    for i in range(1, 8):
        dpx(i, i).wait_recv()
    lane = lax.broadcasted_iota(jnp.int32, (8, 128), 1)
    gains[...] = jnp.zeros((8, 768), F32)
    for d in range(8):
        lo, sh = 96 * d // 128, 96 * d % 128
        t = pltpu.roll(jnp.where(lane < 96, infos[d], 0.0), sh, 1)
        gains[:, 128 * lo:128 * lo + 128] += jnp.where(lane >= sh, t, 0.0)
        if sh > 32:
            gains[:, 128 * lo + 128:128 * lo + 256] += jnp.where(lane < sh, t, 0.0)
    pick = lax.broadcasted_iota(jnp.int32, (16, 128), 0) == lax.broadcasted_iota(jnp.int32, (16, 128), 1)
    lens[...] = jnp.broadcast_to(jnp.sum(jnp.where(pick, tile[3:4, :], 0.0), axis=1, keepdims=True), (16, 128))
    ring_f.finish()
    ring_z = Gather(me, ("z",) * 3, place_f, None, zs, zr, zsib_s, zsib_r, "xy")
    ring.finish()
    ring.siblings_in()
    block = lambda n: A.at[n // 4, n % 4]
    loads = [pltpu.make_async_copy(block(n), W.at[n], load_s.at[n]) for n in range(10)]
    loads += [pltpu.make_async_copy(block(10 + n), (wk if n < 2 else wv).at[:, :, :, :, pl.ds(384 * (n % 2), 384)], load_s.at[10 + n]) for n in range(4)]
    for c in loads:
        c.start()
    self_attention(x_ref, gains, Stacked(W), loads, q2, h1, qkv, o1, x1, h2, L1)
    for n in range(6):
        qall[n, me["x"], me["y"]] = q2[:, 128 * n:128 * n + 128]
    view = lambda n, at: qall.at[n, at["x"], at["y"]]
    plane = Gather(me, PLANE, view, lambda n: view(n, me), ps_, pr_)
    fold = Merge(me, ost, mid, one, two, os_, or_)
    plane.send(0)
    ring_z.send(0)
    for c in loads[10:]:
        c.wait()
    flat = lambda ref: ref[...].reshape(768, 768)
    for i in range(6):
        wvT[:, 128 * i:128 * i + 128] = flat(wv)[128 * i:128 * i + 128, :].T

    def project(a, b):
        @pl.loop(a // 2, b // 2)
        def _(i):
            for e in (2 * i, 2 * i + 1):
                load_mem(e).wait()
            K[pl.ds(2 * i, 2)] = dot(mem[pl.ds(2 * i, 2)].reshape(384, 768), flat(wk)).astype(BF).reshape(2, 192, 768)
            for e in (2 * i, 2 * i + 1):
                VT[e] = dot(wvT[...], mem[e], 1, 1).astype(BF)

    def project_more(a, b):
        @pl.loop(a // 2, b // 2)
        def _(i):
            V[pl.ds(2 * i, 2)] = dot(mem[pl.ds(2 * i, 2)].reshape(384, 768), flat(wv)).astype(BF).reshape(2, 192, 768)
            for e in (2 * i, 2 * i + 1):
                KT[e] = dot(wkT[...], mem[e], 1, 1).astype(BF)

    plane.send(1, (0, 1))
    project(0, 4)
    plane.send(1, (2, 3))
    plane.send(1, (4, 5))
    project(4, 10)
    plane.forward((0, 1))
    plane.forward((2, 3))
    project(10, 16)
    plane.forward((4, 5))
    masks = head_masks()
    pos = key_positions()

    def attend(g):
        cols = slice(256 * g, 256 * g + 256)

        @pl.loop(0, 4)
        def _(i):
            four = [(x, x * 4 + y, {"x": x, "y": y}) for x, y in [(i, y) for y in range(4)]]
            sT = [dot(K[e, :, cols], stack_heads(pair_of(qall, g, at), masks), 1, 1) for _, e, at in four]
            pT, inv = [], []
            for u, (_, e, at) in enumerate(four):
                live = pos < lens[pl.ds(e, 1), :]
                ps = []
                for h in range(4):
                    s = jnp.where(live, sT[u][:, 128 * h:128 * h + 128], NEG)
                    top = jnp.max(s, axis=0, keepdims=True)
                    p = jnp.exp(s - top)
                    tot = jnp.sum(p, axis=0, keepdims=True)
                    lrow[u, h // 2, h % 2:h % 2 + 1, :] = top + jnp.log(tot)
                    ps.append(p.astype(BF))
                    inv.append(1.0 / tot)
                pT.append(jnp.concatenate(ps, axis=1))
            oT = [dot(VT[e, cols, :], p) for (_, e, _), p in zip(four, pT)]
            for u, (_, e, at) in enumerate(four):
                for h in range(4):
                    ost[2 * g + h // 2, at["x"], at["y"], 64 * (h % 2):64 * (h % 2) + 64, :] = (
                        oT[u][64 * h:64 * h + 64, 128 * h:128 * h + 128] * inv[4 * u + h]).astype(BF)
                for h in range(2):
                    ost[2 * g + h, at["x"], at["y"], 128:144, :] = log_tile(lrow[u, h])

        fold.send(0, (2 * g, 2 * g + 1))

    def deliver(g):
        for n in (2 * g, 2 * g + 1):
            o, l = fold.result(n)
            o_ref[:, 128 * n:128 * n + 128] = o.T
            L_ref[2 * n:2 * n + 2, :] = l[0:2, :]

    plane.finish((0, 1))
    attend(0)
    plane.finish((2, 3))
    attend(1)
    fold.middle((0, 1))
    fold.send(1, (0, 1))
    plane.finish((4, 5))
    out_q = pltpu.make_async_copy(qall, q_h, out_s.at[0])
    out_k = pltpu.make_async_copy(K, k_h, out_s.at[1])
    out_q.start()
    out_k.start()
    ring_z.forward()
    attend(2)
    fold.middle((2, 3))
    fold.send(1, (2, 3))
    for i in range(6):
        wkT[:, 128 * i:128 * i + 128] = flat(wk)[128 * i:128 * i + 128, :].T
    project_more(0, 8)
    fold.middle((4, 5))
    fold.send(1, (4, 5))
    low, high = pl.ds(0, 8), pl.ds(8, 8)
    outs = [pltpu.make_async_copy(a.at[k], b.at[k], out_s.at[2 + 2 * i + j])
            for j, k in enumerate((low, high)) for i, (a, b) in enumerate(((V, v_h), (KT, kt_h)))]
    for c in outs[:2]:
        c.start()
    ring_z.finish()
    project_more(8, 16)
    for c in outs[2:]:
        c.start()
    L_ref[12:16, :] = jnp.zeros((4, 128), F32)
    for g in range(3):
        deliver(g)
    plane.drain()
    fold.drain()
    for c in [out_q, out_k] + outs:
        c.wait()
    ring_z.siblings_in()
    ring_z.drain()
    ring_f.drain()
    ring.drain()
    for i in range(1, 16):
        a2a(i).wait_send()
    for i in range(1, 8):
        dpx(i).wait_send()


def forward(attn, wi, wo, gain, length, x, memory):
    row = SDS((128, 768), BF)
    rowf = SDS((128, 768), F32)
    log = SDS((16, 128), F32)
    return pl.pallas_call(
        forward_kernel,
        out_shape=(SDS((4, 4, 4, 2, 3, 32, 384), BF), SDS((4, 4, 4, 2, 2, 48, 256), BF), SDS((4, 2, 4, 4, 16, 768), BF),
                   SDS((6, 4, 4, 128, 128), BF), SDS((16, 192, 768), BF), SDS((16, 192, 768), BF), SDS((16, 768, 192), BF),
                   SDS((8, 768), F32), log, row, SDS((3, 128, 768), BF), row, rowf, row, log, rowf, log),
        in_specs=[VS] * 6 + [HS], out_specs=(HS,) * 7 + (VS,) * 10,
        scratch_shapes=[vf(8, 8, 128), vf(8, 128), vf(16, 8, 768), vf(16, 8, 768), vf(96, 640), vm(3, 32, 384), vm(2, 48, 256), vm(16, 768),
                        vm(10, 4, 2, 3, 32, 384), vm(128, 768),
                        vm(6, 4, 4, 128, 128), vm(16, 192, 768), vm(4, 2, 3, 32, 768), vm(4, 2, 3, 32, 768), vm(768, 768), vm(768, 768),
                        vm(16, 192, 768), vm(16, 192, 768), vm(16, 768, 192), vm(16, 768, 192),
                        vm(6, 4, 4, 144, 128), vm(6, 4, 144, 128), vm(6, 3, 4, 144, 128), vm(6, 3, 144, 128), vf(4, 2, 8, 128),
                        DMA((3, 2, 4)), DMA((3, 2, 4)), DMA((3, 3, 4)), DMA((3, 3, 4)), DMA((3, 4)), DMA((3, 4)), DMA((16,)), DMA((16,)), DMA((8,)), DMA((8,)), DMA((6,)),
                        DMA((3, 1, 4)), DMA((3, 1, 4)), DMA((3, 4)), DMA((3, 4)),
                        DMA((14,)), DMA((16,)), DMA((6,)), DMA((6, 2, 4)), DMA((6, 2, 4)), DMA((6, 2, 3)), DMA((6, 2, 3))],
        compiler_params=pltpu.CompilerParams(collective_id=0, has_side_effects=True, vmem_limit_bytes=60 << 20),
        name="forward_attention",
    )(attn, wi, wo, gain, length, x, memory)


def cross_bwd_kernel(do, st, lens, q_h, k_h, v_h, kt_h, mem_h, A, GB, GC, G_in, dq_ref, gm_h, dw_h, sumE, sumF,
                     qall, doall, stall, wk, wv, K, V, KT, mem, memT, dK, dV, gst, wst, dst, dh1, df1, df0,
                     accB, accC, sibB, sibC, hB2, hC2, fB2, fC2,
                     q_s, kv_s, mem_s, w_s, gm_s, dw_s, ss, rs, ds_, dr_, fs, fr, fsib_s, fsib_r, floc, sum_s):
    me = where_am_i()
    bar, count = meet(me, "z")

    def load_mem(e):
        return pltpu.make_async_copy(mem_h.at[pl.ds(pl.multiple_of(256 * e, 256), 256)], mem.at[e % 4], mem_s.at[e % 4])

    for e in range(4):
        load_mem(e).start()
    loads = [pltpu.make_async_copy(A.at[10 + i], (wk if i < 2 else wv).at[:, pl.ds(384 * (i % 2), 384)], w_s.at[i]) for i in range(4)]
    loads.append(pltpu.make_async_copy(q_h, qall, q_s))
    for n in range(6):
        doall[n, me["x"], me["y"]] = do[:, 128 * n:128 * n + 128]
    stall[me["x"], me["y"]] = st[...]
    pl.semaphore_wait(bar, count)

    def place(n, at):
        return stall.at[at["x"], at["y"]] if n == 6 else doall.at[n, at["x"], at["y"]]

    plane = Gather(me, PLANE + ("xy",), place, lambda n: place(n, me), ss, rs)
    fhop, ffin = staged("BC", (hB2, hC2, fB2, fC2))
    grads = ffn_place(GB, GC)
    ring = Scatter(me, PARTS_F, {"B": accB, "C": accC}, fhop, ffin, fs, fr, {"B": sibB, "C": sibC},
                   lambda n, at, c: grads(n, {**at, "c": c}), fsib_s, fsib_r, floc, "xy")
    back = Scatter(me, PARTS_D, {"D": dst}, *staged("D", (dh1, df1, df0)), ds_, dr_)
    plane.send(0, (6, 0, 1, 2, 3, 4, 5))
    ring.start()
    for c in loads:
        c.start()

    def turn(a, b):
        @pl.loop(a, b)
        def _(e):
            load_mem(e).wait()
            memT[:, pl.ds(pl.multiple_of(256 * e, 256), 256)] = mem[e % 4].T

            @pl.when(e < 8)
            def _():
                load_mem(e + 4).start()

    turn(0, 3)
    plane.send(1, (6, 0, 1))
    plane.send(1, (2, 3))
    plane.send(1, (4, 5))
    turn(3, 6)
    ring.merge(0)
    ring.send(0)
    plane.forward((6, 0, 1))
    plane.forward((2, 3))
    ring.merge(1)
    ring.merge(2)
    masks = head_masks()
    pos = key_positions()

    def load_kv(g, i, u, which):
        e = ((me["x"] + 2 + i) % 4) * 4 + u
        cols = pl.ds(256 * g, 256)
        src = (k_h.at[e, :, cols], v_h.at[e, :, cols], kt_h.at[e, cols])[which]
        return pltpu.make_async_copy(src, (K, V, KT)[which].at[i % 2, u], kv_s.at[which, i % 2, u])

    def fetch_kv(g, i):
        for u in range(4):
            for w in range(3):
                load_kv(g, i, u, w).start()

    fetch_kv(0, 0)
    for c in loads:
        c.wait()

    def attend(g):
        cols = slice(256 * g, 256 * g + 256)

        @pl.loop(0, 4)
        def _(i):
            @pl.when(i < 3)
            def _():
                fetch_kv(g, i + 1)

            for u in range(4):
                for w in range(3):
                    load_kv(g, i, u, w).wait()
            x = (me["x"] + 2 + i) % 4
            four = [(x * 4 + y, {"x": x, "y": y}) for y in range(4)]
            q4s = [stack_heads(pair_of(qall, g, at), masks) for _, at in four]
            d4s = [stack_heads(pair_of(doall, g, at), masks) for _, at in four]
            sT = [dot(K[i % 2, u], q4s[u], 1, 1) for u in range(4)]
            gT = [dot(V[i % 2, u], d4s[u], 1, 1) for u in range(4)]
            pT, sg = [], []
            for u, (e, at) in enumerate(four):
                live = pos < lens[pl.ds(e, 1), :]
                ps, gs = [], []
                for h in range(4):
                    n = 4 * g + h
                    s = jnp.where(live, sT[u][:, 128 * h:128 * h + 128], NEG)
                    p = jnp.exp(s - stall[at["x"], at["y"], n:n + 1, :])
                    ps.append(p.astype(BF))
                    gs.append((p * (gT[u][:, 128 * h:128 * h + 128] - stall[at["x"], at["y"], 12 + n:13 + n, :])).astype(BF))
                pT.append(jnp.concatenate(ps, axis=1))
                sg.append(jnp.concatenate(gs, axis=1))
            for u, (e, at) in enumerate(four):
                dV[pl.ds(pl.multiple_of(192 * e, 192), 192), cols] = dot(pT[u], d4s[u]).astype(BF)
            for u, (e, at) in enumerate(four):
                dK[pl.ds(pl.multiple_of(192 * e, 192), 192), cols] = dot(sg[u], q4s[u]).astype(BF)
            for u, (e, at) in enumerate(four):
                qT = dot(KT[i % 2, u], sg[u])
                for h in range(4):
                    dst[2 * g + h // 2, at["x"], at["y"], 64 * (h % 2):64 * (h % 2) + 64, :] = qT[64 * h:64 * h + 64, 128 * h:128 * h + 128].astype(BF)

        if g < 2:
            fetch_kv(g + 1, 0)
        back.send(1, (2 * g, 2 * g + 1))

    plane.finish((6, 0, 1))
    attend(0)
    ring.forward()
    plane.forward((4, 5))
    plane.finish((2, 3))
    attend(1)
    back.forward((0, 1))
    ring.merge(3)
    plane.finish((4, 5))
    attend(2)
    back.forward((2, 3))
    back.close(1, (0, 1))
    back.send(0, (0, 1))

    def gm_copy(e):
        return pltpu.make_async_copy(gst.at[e % 2], gm_h.at[e], gm_s.at[e % 2])

    def mem_grad(a, b):
        @pl.loop(a, b)
        def _(e):
            @pl.when(e > 1)
            def _():
                gm_copy(e - 2).wait()

            rows = pl.ds(pl.multiple_of(384 * e, 384), 384)
            gst[e % 2] = dot(dK[rows, :], wk[...], 1, 1) + dot(dV[rows, :], wv[...], 1, 1)
            gm_copy(e).start()

    def dw_copy(k, r, half):
        rows = pl.ds(pl.multiple_of(256 * r, 256), 256)
        return pltpu.make_async_copy(wst.at[k, :, pl.ds(384 * half, 384)], dw_h.at[10 + 2 * k + half, rows], dw_s.at[k, half])

    def weight_grad(a, b):
        @pl.loop(a, b)
        def _(r):
            for k in range(2):
                @pl.when(r > 0)
                def _():
                    dw_copy(k, r - 1, 0).wait()
                    dw_copy(k, r - 1, 1).wait()

                wst[k] = dot(memT[pl.ds(pl.multiple_of(256 * r, 256), 256), :], (dV if k else dK)[...]).astype(BF)
                dw_copy(k, r, 0).start()
                dw_copy(k, r, 1).start()

    turn(6, 12)
    mem_grad(0, 2)
    back.forward((4, 5))
    back.close(1, (2, 3))
    back.send(0, (2, 3))
    mem_grad(2, 8)
    weight_grad(0, 1)
    back.close(1, (4, 5))
    back.send(0, (4, 5))
    weight_grad(1, 2)
    ring.close(0)
    sums = [pltpu.make_async_copy(accB.at[:, :, :, me["z"]], sumE, sum_s.at[0]), pltpu.make_async_copy(accC.at[me["z"]], sumF, sum_s.at[1])]
    for c in sums:
        c.start()
    weight_grad(2, 3)
    for n in range(6):
        dq_ref[:, 128 * n:128 * n + 128] = (0.125 * back.result(n)).T
    for c in sums:
        c.wait()
    gm_copy(6).wait()
    gm_copy(7).wait()
    for k in range(2):
        dw_copy(k, 2, 0).wait()
        dw_copy(k, 2, 1).wait()
    plane.drain()
    ring.drain()
    back.drain()


def cross_bwd(do, st, lens, q_h, k_h, v_h, kt_h, memory, A, GB, GC, GA):
    bB, bC = (48, 256), (16, 768)
    return pl.pallas_call(
        cross_bwd_kernel,
        out_shape=(SDS((128, 768), F32), SDS((8, 384, 768), F32), SDS((16, 768, 384), BF), SDS((2, 4, 4, 48, 256), BF), SDS((4, 4, 16, 768), BF)),
        in_specs=[VS] * 3 + [HS] * 9, out_specs=(VS,) + (HS,) * 4, input_output_aliases={11: 2},
        scratch_shapes=[vm(6, 4, 4, 128, 128), vm(6, 4, 4, 128, 128), vf(4, 4, 24, 128), vm(768, 768), vm(768, 768),
                        vm(2, 4, 192, 256), vm(2, 4, 192, 256), vm(2, 4, 256, 192), vm(4, 256, 768), vm(768, 3072), vm(3072, 768), vm(3072, 768),
                        vf(2, 384, 768), vm(2, 256, 768), vm(6, 4, 4, 128, 128), *stage_buffers(LEAD_D, ((6,), (128, 128))),
                        vm(2, 4, 4, 4, *bB), vm(4, 4, 4, *bC), vm(2, 4, 4, 4, *bB), vm(4, 4, 4, *bC), *stage_buffers(LEAD_A[:2], ((2,), bB), ((), bC)),
                        DMA, DMA((3, 2, 4)), DMA((4,)), DMA((4,)), DMA((2,)), DMA((2, 2)), DMA((7, 2, 4)), DMA((7, 2, 4)), DMA((6, 2, 5)), DMA((6, 2, 5)),
                        DMA((3, 1, 4)), DMA((3, 1, 4)), DMA((3, 4)), DMA((3, 4)), DMA((3, 4)), DMA((2,))],
        compiler_params=pltpu.CompilerParams(collective_id=3, has_side_effects=True, vmem_limit_bytes=60 << 20),
        name="cross_backward",
    )(do, st, lens, q_h, k_h, v_h, kt_h, memory.reshape(3072, 768), A, GB, GC, GA)


def adam_update(master, first, second, grad, rate):
    first_new = beta_one * first + (1.0 - beta_one) * grad
    second_new = beta_two * second + (1.0 - beta_two) * grad * grad
    fix_one = 1.0 - beta_one**STEP
    fix_two = 1.0 - beta_two**STEP
    master_new = master - rate * (
        first_new / fix_one / (jnp.sqrt(second_new / fix_two) + adam_eps) + decay_rate * master
    )
    return (master_new, first_new, second_new, master_new.astype(jnp.bfloat16))


def ffn_kernel(x1, o2, L2, dy_ref, gains, A, B, C, out, do2, st, dx2, gg, GA, GB, GC,
               W7, WB, WC, gA, gB, gC, sw, sb, sc, tb, tc, ta):
    lA = [pltpu.make_async_copy(A.at[14 + i], W7.at[i], sw.at[i]) for i in range(2)]
    lB = [pltpu.make_async_copy(B.at[i], WB.at[i], sb.at[i]) for i in range(16)]
    lC = [pltpu.make_async_copy(C.at[i], WC.at[i], sc.at[i]) for i in range(8)]
    for c in lA:
        c.start()
    for j in range(8):
        lB[j].start()
        lB[8 + j].start()
        lC[j].start()
    o = o2[...]
    ob = o.astype(BF)
    for c in lA:
        c.wait()
    x = x1[...] + apply_w(ob, W7, 0)
    inv = rms(x)
    h = (x * inv * gains[2:3, :]).astype(BF)
    hT = flip(h.astype(F32)).astype(BF)
    df = dy_ref[...]
    y = jnp.zeros((128, 768), F32)
    dh = jnp.zeros((128, 768), F32)
    c0 = 0.7978845608028654
    sB, sC = [], []
    for j0 in range(0, 8, 2):
        js = range(j0, j0 + 2)
        for j in js:
            lB[j].wait()
            lB[8 + j].wait()
            lC[j].wait()
        a_s = [dot(h, WB[j]) for j in js]
        ups = [dot(h, WB[8 + j]) for j in js]
        dms = [dot(df, WC[j], 1, 1) for j in js]
        mids, dgs, dus = [], [], []
        for a, up, dm in zip(a_s, ups, dms):
            t = jnp.tanh(c0 * (a + 0.044715 * a * a * a))
            half = 0.5 * (1.0 + t)
            gel = a * half
            der = half + 0.5 * a * (1.0 - t * t) * (c0 * (1.0 + 0.134145 * a * a))
            mids.append(gel * up)
            dgs.append((dm * up * der).astype(BF))
            dus.append((dm * gel).astype(BF))
        y += dot(jnp.concatenate([m.astype(BF) for m in mids], axis=1), WC[j0:j0 + 2].reshape(2 * 256, 768))
        for n, j in enumerate(js):
            dh += dot(dgs[n], WB[j], 1, 1) + dot(dus[n], WB[8 + j], 1, 1)
        for n, j in enumerate(js):
            gB[j] = dot(hT, dgs[n]).astype(BF)
            gB[8 + j] = dot(hT, dus[n]).astype(BF)
            gC[j] = dot(flip(mids[n]).astype(BF), df).astype(BF)
        for j in js:
            new = [pltpu.make_async_copy(gB.at[j], GB.at[j], tb.at[j]), pltpu.make_async_copy(gB.at[8 + j], GB.at[8 + j], tb.at[8 + j]),
                   pltpu.make_async_copy(gC.at[j], GC.at[j], tc.at[j])]
            for c in new:
                c.start()
            sB += new
    out[...] = (x + y).astype(BF)
    dz, gain = rms_back(x, inv, gains[2:3, :], dh)
    gg[...] = gain
    d = df.astype(F32) + dz
    dx2[...] = d
    dc = d.astype(BF)
    dof = apply_wt(dc, W7, 0).astype(BF)
    do2[...] = dof
    prod = flip(dof.astype(F32) * o)
    st[0:12, :] = L2[0:12, :]
    for n in range(12):
        st[12 + n:13 + n, :] = jnp.sum(prod[64 * n:64 * n + 64, :], axis=0, keepdims=True)
    oT = flip(o).astype(BF)
    sA = []
    for i in range(2):
        gA[i] = dot(oT, dc[:, 384 * i:384 * i + 384]).astype(BF)
        sA.append(pltpu.make_async_copy(gA.at[i], GA.at[14 + i], ta.at[i]))
        sA[-1].start()
    for c in sA + sB + sC:
        c.wait()

def ffn(x1, o2, L2, dy, gains, A, B, C):
    M = lambda *s: pltpu.VMEM(s, BF)
    D = pltpu.SemaphoreType.DMA
    return pl.pallas_call(
        ffn_kernel,
        out_shape=(SDS((128, 768), BF), SDS((128, 768), BF), SDS((24, 128), F32), SDS((128, 768), F32), SDS((1, 768), F32),
                   SDS((16, 768, 384), BF), SDS((16, 768, 256), BF), SDS((8, 256, 768), BF)),
        in_specs=[VS] * 5 + [HS] * 3, out_specs=(VS,) * 5 + (HS,) * 3,
        scratch_shapes=[M(2, 768, 384), M(16, 768, 256), M(8, 256, 768), M(2, 768, 384), M(16, 768, 256), M(8, 256, 768),
                        D((2,)), D((16,)), D((8,)), D((16,)), D((8,)), D((2,))],
        compiler_params=pltpu.CompilerParams(vmem_limit_bytes=60 << 20),
        name="feed_forward",
    )(x1, o2, L2, dy, gains, A, B, C)

def self_bwd_kernel(dq2, h2, x1, dx2, qkv, o1, L1, x_ref, h1, gains, g3, A, GA_in, gm_in, gin, tile, GA, gm,
                    W, G, gb, gmv, sem, gsem, msem):
    loads = [pltpu.make_async_copy(A.at[i], W.at[i], sem.at[i]) for i in range(10)]
    for i in (8, 9, 6, 7, 0, 1, 2, 3, 4, 5):
        loads[i].start()
    def gm_load(e):
        return pltpu.make_async_copy(gm_in.at[e], gmv.at[e], msem.at[e])
    def gm_store(e):
        return pltpu.make_async_copy(gmv.at[e], gm.at[e], msem.at[16 + e])
    for e in range(16):
        gm_load(e).start()
    stores = []
    def weight_grad(k, left, inc):
        for i in range(2):
            n = 2 * k + i
            G[n] = dot(left, inc[:, 384 * i:384 * i + 384]).astype(BF)
            stores.append(pltpu.make_async_copy(G.at[n], GA.at[n], gsem.at[n]))
            stores[-1].start()
    dqb = dq2[...].astype(BF)
    for i in (8, 9, 6, 7):
        loads[i].wait()
    u = apply_wt(dqb, W, 4)
    x = x1[...]
    inv = rms(x)
    dz, gain = rms_back(x, inv, gains[1:2, :], u)
    gb[...] = jnp.zeros((8, 768), F32)
    gb[1:2, :] = gain
    gb[2:3, :] = g3[...]
    d1 = dx2[...] + dz
    da = d1.astype(BF)
    do1 = apply_wt(da, W, 3).astype(BF)
    weight_grad(4, flip(h2[...].astype(F32)).astype(BF), dqb)
    for e in range(16):
        gm_load(e).wait()
        gm_store(e).start()
    masks = head_masks(0.125)
    ones = head_masks(1.0)
    live = causal_mask()
    kT = flip(qkv[1].astype(F32)).astype(BF)
    qs, ks, vs = [], [], []
    for g in range(3):
        cols = slice(256 * g, 256 * g + 256)
        q4 = qkv[0, :, cols]
        d4 = do1[:, cols]
        q4s = jnp.concatenate([q4 * m for m in masks], axis=0)
        d4s = jnp.concatenate([d4 * m for m in ones], axis=0)
        sT = dot(qkv[1, :, cols], q4s, 1, 1)
        gT = dot(qkv[2, :, cols], d4s, 1, 1)
        ps, gs = [], []
        for n in range(4):
            s = jnp.where(live, sT[:, 128 * n:128 * n + 128], NEG)
            p = jnp.exp(s - L1[4 * g + n:4 * g + n + 1, :])
            gt = gT[:, 128 * n:128 * n + 128]
            ps.append(p.astype(BF))
            gs.append((p * (gt - jnp.sum(p * gt, axis=0, keepdims=True))).astype(BF))
        sg = jnp.concatenate(gs, axis=1)
        vs.append(dot(jnp.concatenate(ps, axis=1), d4s).astype(BF))
        ks.append(dot(sg, q4s).astype(BF))
        qT = dot(kT[256 * g:256 * g + 256, :], sg)
        qs += [qT[64 * n:64 * n + 64, 128 * n:128 * n + 128] for n in range(4)]
    inc = [(0.125 * unflip(jnp.concatenate(qs, axis=0))).astype(BF), jnp.concatenate(ks, axis=1), jnp.concatenate(vs, axis=1)]
    weight_grad(3, flip(o1[...].astype(F32)).astype(BF), da)
    for c in loads[:6]:
        c.wait()
    u = apply_wt(inc[0], W, 0) + apply_wt(inc[1], W, 1) + apply_wt(inc[2], W, 2)
    x = x_ref[...].astype(F32)
    inv = rms(x)
    dz, gain = rms_back(x, inv, gains[0:1, :], u)
    gb[0:1, :] = gain
    gin[...] = d1 + dz
    hT = flip(h1[...].astype(F32)).astype(BF)
    for k in range(3):
        weight_grad(k, hT, inc[k])
    lane = lax.broadcasted_iota(jnp.int32, (8, 128), 1)
    for d in range(8):
        lo, sh = 96 * d // 128, 96 * d % 128
        t = pltpu.roll(gb[:, 128 * lo:128 * lo + 128], (128 - sh) % 128, 1)
        if sh > 32:
            nxt = pltpu.roll(gb[:, 128 * lo + 128:128 * lo + 256], (128 - sh) % 128, 1)
            t = jnp.where(lane < 128 - sh, t, nxt)
        tile[d] = jnp.where(lane < 96, t, 0.0)
    for c in stores:
        c.wait()
    for e in range(16):
        gm_store(e).wait()

def self_bwd(dq2, h2, x1, dx2, qkv, o1, L1, x, h1, gains, g3, A, GA, gm):
    D = pltpu.SemaphoreType.DMA
    return pl.pallas_call(
        self_bwd_kernel,
        out_shape=(SDS((128, 768), F32), SDS((8, 8, 128), F32), SDS((16, 768, 384), BF), SDS((16, 192, 768), F32)),
        in_specs=[VS] * 11 + [HS] * 3, out_specs=(VS, VS, HS, HS),
        input_output_aliases={12: 2},
        scratch_shapes=[pltpu.VMEM((10, 768, 384), BF), pltpu.VMEM((10, 768, 384), BF), pltpu.VMEM((8, 768), F32), pltpu.VMEM((16, 192, 768), F32), D((10,)), D((10,)), D((32,))],
        compiler_params=pltpu.CompilerParams(vmem_limit_bytes=60 << 20),
        name="self_backward",
    )(dq2, h2, x1, dx2, qkv, o1, L1, x, h1, gains, g3, A, GA, gm)

def adam_kernel(*refs):
    ins, outs = refs[:16], refs[16:]
    for n in range(4):
        w, m, v, g = ins[4 * n:4 * n + 4]
        grad = g[0:3, 0:6] if n == 3 else g[...]
        for o, val in zip(outs[4 * n:4 * n + 4], adam_update(w[...], m[...], v[...], grad, rate_gain if n == 3 else rate_matrix)):
            o[...] = val

def adam(*args):
    shapes = []
    for n in range(4):
        s = args[4 * n].shape
        shapes += [SDS(s, F32)] * 3 + [SDS(s, BF)]
    return pl.pallas_call(adam_kernel, out_shape=tuple(shapes), in_specs=[VS] * 16, out_specs=(VS,) * 16,
                          compiler_params=pltpu.CompilerParams(vmem_limit_bytes=60 << 20), name="adam")(*args)


def body(
    dec_input,
    memory,
    mem_len,
    grad_out,
    attn_master,
    ffn_in_master,
    ffn_out_master,
    gain_master,
    attn_first,
    ffn_in_first,
    ffn_out_first,
    gain_first,
    attn_second,
    ffn_in_second,
    ffn_out_second,
    gain_second,
):
    swap = lambda a: a.transpose(1, 0, 2)
    attn_t, in_t = swap(attn_master), swap(ffn_in_master)
    x = dec_input[0]
    (gath_a, gath_b, gath_c, q_all, k_two, v_two, kt_two, gains, lens, h1, qkv, o1, x1, h2, L1, o2, L2) = forward(
        attn_t, in_t, ffn_out_master, gain_master, mem_len.reshape(1, 1), x, memory
    )
    aw = gath_a.reshape(16, 768, 384)
    out_block, do2, st, dx2, g3, GA, GB, GC = ffn(x1, o2, L2, grad_out[0], gains, aw, gath_b.reshape(16, 768, 256), gath_c.reshape(8, 256, 768))
    dq2, gm, GA, sum_b, sum_c = cross_bwd(
        do2, st, lens, q_all, k_two, v_two, kt_two, memory, aw,
        GB.reshape(4, 4, 4, 2, 2, 48, 256), GC.reshape(4, 2, 4, 4, 16, 768), GA,
    )
    grad_input, tile_g, GA, grad_memory = self_bwd(dq2, h2, x1, dx2, qkv, o1, L1, x, h1, gains, g3, aw, GA, gm.reshape(16, 192, 768))
    share_a, share_b, share_c, share_g = scatter(GA.reshape(4, 4, 4, 2, 3, 32, 384), sum_b, sum_c, tile_g)
    new = adam(
        attn_t, swap(attn_first), swap(attn_second), share_a,
        in_t, swap(ffn_in_first), swap(ffn_in_second), share_b,
        ffn_out_master, ffn_out_first, ffn_out_second, share_c,
        gain_master, gain_first, gain_second, share_g,
    )
    return (out_block[None], grad_input[None], grad_memory, *[swap(a) for a in new[:8]], *new[8:])


def solution(mesh):
    placed = (
        P(("dp", "seq"), None, None),
        P("dp", "seq", None),
        P(("dp", "seq")),
        P(("dp", "seq"), None, None),
        P(None, ("dp", "seq"), None),
        P(None, ("dp", "seq"), None),
        P(("dp", "seq"), None),
        P(None, ("dp", "seq")),
        P(None, ("dp", "seq"), None),
        P(None, ("dp", "seq"), None),
        P(("dp", "seq"), None),
        P(None, ("dp", "seq")),
        P(None, ("dp", "seq"), None),
        P(None, ("dp", "seq"), None),
        P(("dp", "seq"), None),
        P(None, ("dp", "seq")),
    )
    return jax.shard_map(
        body,
        mesh=mesh,
        in_specs=placed,
        out_specs=(
            P(("dp", "seq"), None, None),
            P(("dp", "seq"), None, None),
            P("dp", "seq", None),
            P(None, ("dp", "seq"), None),
            P(None, ("dp", "seq"), None),
            P(None, ("dp", "seq"), None),
            P(None, ("dp", "seq"), None),
            P(None, ("dp", "seq"), None),
            P(None, ("dp", "seq"), None),
            P(None, ("dp", "seq"), None),
            P(None, ("dp", "seq"), None),
            P(("dp", "seq"), None),
            P(("dp", "seq"), None),
            P(("dp", "seq"), None),
            P(("dp", "seq"), None),
            P(None, ("dp", "seq")),
            P(None, ("dp", "seq")),
            P(None, ("dp", "seq")),
            P(None, ("dp", "seq")),
        ),
        check_vma=False,
    )
```
